32 devices in a mesh: groups: 2 (over x), ctx: 16 (over z, y, core).
Axes of the slice: x: 2, y: 2, z: 4, core: 2. Of those that a mesh axis runs over, the one named last changes fastest.
Arguments:
- queries: bfloat16 [8192, 1024], P(('groups', 'ctx')), parts along dimension 0, may hold values from -5 to 5
- keys: bfloat16 [8192, 1024], P(('groups', 'ctx')), parts along dimension 0, may hold values from -5 to 5
- values: bfloat16 [8192, 1024], P(('groups', 'ctx')), parts along dimension 0, may hold values from -5 to 5
- grad_self: bfloat16 [8192, 1024], P(('groups', 'ctx')), parts along dimension 0, may hold values from -5 to 5
- doc_ids: int32 [8192], P('groups'), parts along dimension 0, may hold values from 0 to 31, never falling along the last dimension, each value on 1 to 512 neighbouring positions
- cross_queries: bfloat16 [8192, 1024], P(('groups', 'ctx')), parts along dimension 0, may hold values from -5 to 5
- grad_cross: bfloat16 [8192, 1024], P(('groups', 'ctx')), parts along dimension 0, may hold values from -5 to 5
- pool_kv: bfloat16 [2, 64, 128, 1024], P(None, ('groups', 'ctx')), parts along dimension 1, may hold values from -5 to 5
- neighbour_ids: int32 [128, 2], P(('groups', 'ctx')), parts along dimension 0, may hold values from 0 to 31, as said below
Outputs:
- grad_queries: bfloat16 [8192, 1024], P(('groups', 'ctx')), parts along dimension 0
- grad_keys: bfloat16 [8192, 1024], P(('groups', 'ctx')), parts along dimension 0
- grad_values: bfloat16 [8192, 1024], P(('groups', 'ctx')), parts along dimension 0
- grad_cross_queries: bfloat16 [8192, 1024], P(('groups', 'ctx')), parts along dimension 0
- grad_pool: bfloat16 [2, 64, 128, 1024], P(None, ('groups', 'ctx')), parts along dimension 1
The draws below stay inside these ranges and needn't reach their ends.
There are 2 independent parts, one for each index of `groups`. The reference program is written for one: setup_inputs(seed, part) draws one part's arguments, and reference() takes and returns one part's arrays. A program takes and returns all parts, laid end to end along the dimension named above; each array names one. Nothing has to cross between parts.
Inputs may be any that keep to these rules, and one draw needn't show every extreme that they name: `doc_ids`: document numbers never fall along the tokens; a document spans 1 to 512 tokens. `neighbour_ids`: encoding e is owned by device e // 2 of the loop; the encodings of stretch c are owned by the device holding stretch c (c // 4) or by one of the two devices beside it on the loop, which wraps around.
All inputs are finite; a program needn't handle non-finite values.
Results may differ from the reference program's by a relative error of at most 0.0086.
Values may be sent and summed in bfloat16 or wider, within the bound.
No kernel may reach another device: no remote copies, remote signals or barrier semaphores. Data moves between devices by JAX's collectives and lax.ppermute only.
A program may use at most 128 MiB of HBM per device.

```python
import math
import jax
import jax.numpy as jnp
import numpy as np
from jax import lax

HEADS = 8
HEAD_DIM = 128
STRETCH = 64
NBRS = 2
NBR_TOK = 128
REACH = 2
TOK_DEV = 256
ENC_DEV = 2
TOKENS = 4096
STRETCHES = 64
CH_DEV = 4
ENCS = 32
HD = 1024
DOC_MOST = 512
DOCS = 32
N_CTX = 16


def base_field(key, shape):
    return jnp.clip(jax.random.normal(key, shape), -4.5, 4.5)


def drawn_queries(key, salt):
    field = base_field(jax.random.fold_in(key, salt), (TOKENS, HD))
    return field.astype(jnp.bfloat16)


def draw_queries(key, part):
    return drawn_queries(key, 11)


def draw_cross_queries(key, part):
    return drawn_queries(key, 13)


def draw_keys(key, part):
    field = base_field(jax.random.fold_in(key, 17), (TOKENS, HD))
    return field.astype(jnp.bfloat16)


def draw_pool_kv(key, part):
    key_part = base_field(jax.random.fold_in(key, 19), (ENCS, NBR_TOK, HD))
    value_part = base_field(jax.random.fold_in(key, 23), (ENCS, NBR_TOK, HD))
    return jnp.stack([key_part, value_part]).astype(jnp.bfloat16)


def draw_neighbour_ids(key, part):
    loop_size = ENCS // ENC_DEV
    stretch_index = jnp.arange(STRETCHES, dtype=jnp.int32)
    device = stretch_index // CH_DEV
    shifts = jax.random.randint(jax.random.fold_in(key, 41), (STRETCHES, NBRS), -1, 2)
    slot_index = jax.random.randint(jax.random.fold_in(key, 43), (STRETCHES, NBRS), 0, ENC_DEV)
    owners = (device[:, None] + shifts) % loop_size
    chosen = owners * ENC_DEV + slot_index
    chosen = chosen.at[0, 0].set(ENCS - 1).at[0, NBRS - 1].set(0)
    return chosen.astype(jnp.int32)


def level_of(key, extent, shards, low, high):
    loudness = 1.0
    for position, shards_of in shards:
        draws = jax.random.uniform(jax.random.fold_in(jax.random.fold_in(key, 6), position), (shards_of,), jnp.float32, low / len(shards), high / len(shards))
        loudness = loudness * jnp.repeat(jnp.exp(draws), extent[position] // shards_of).reshape((-1,) + (1,) * (len(extent) - 1 - position))
    return loudness


def length_profile(number_of, total, reach, skew):
    portions = [(1 << 20) // math.isqrt(rank ** skew) + 1 for rank in range(2, number_of + 1)]
    spare, given = total - reach - (number_of - 1), [1] * (number_of - 1)
    while spare > 0:
        movable = [i for i in range(number_of - 1) if given[i] < reach]
        whole, remaining = sum([portions[i] for i in movable]), spare
        for i in movable:
            more = min(reach - given[i], max(1, remaining * portions[i] // whole), spare)
            given[i] = given[i] + more
            spare = spare - more
    return np.array([reach] + given)


def uneven_parts(own_key, amount, total, reach, skew):
    if amount == 2:
        one = jax.random.randint(own_key, (), max(1, total - reach), min(reach, total - 1) + 1)
        return jnp.stack([one, total - one])
    sizes = jnp.asarray(length_profile(amount, total, reach, skew), jnp.int32)
    twos = (amount - 1) // 2
    giver, receiver = sizes[1:1 + 2 * twos:2], sizes[2:2 + 2 * twos:2]
    slack = jnp.minimum(giver - 1, reach - receiver)
    moved = jax.random.randint(jax.random.fold_in(own_key, 1), (twos,), 0, 1 << 20) % (slack + 1)
    sizes = sizes.at[1:1 + 2 * twos:2].set(giver - moved).at[2:2 + 2 * twos:2].set(receiver + moved)
    return sizes[jax.random.permutation(jax.random.fold_in(own_key, 2), amount)]


def scatter_about(own_key, shape, scale, reach, split=(), held_as=jnp.bfloat16):
    loudness = level_of(own_key, shape, split, -0.22, 0.18) if split else 1.0
    array = jax.random.normal(own_key, shape, jnp.float32) * scale * loudness
    return jnp.minimum(jnp.maximum(array, -reach), reach).astype(held_as)


def setup_inputs(seed: int = 0, part: int = 0) -> dict:
    splits = jax.random.split(jax.random.key(seed), 10)
    own_keys = jax.random.split(jax.random.fold_in(splits[9], part), 10)
    queries = draw_queries(jax.random.fold_in(jax.random.fold_in(splits[9], part), 71), part)
    keys = draw_keys(jax.random.fold_in(jax.random.fold_in(splits[9], part), 71), part)
    values = scatter_about(own_keys[2], (TOKENS, HD), 1.0, 5.0, ((0, 16),))
    grad_self = scatter_about(own_keys[3], (TOKENS, HD), 1.0, 5.0, ((0, 16),))
    doc_ids = jnp.searchsorted(jnp.cumsum(uneven_parts(own_keys[4], DOCS, TOKENS, DOC_MOST, 2)), jnp.arange(TOKENS), side="right").astype(jnp.int32)
    cross_queries = draw_cross_queries(jax.random.fold_in(jax.random.fold_in(splits[9], part), 71), part)
    grad_cross = scatter_about(own_keys[6], (TOKENS, HD), 1.0, 5.0, ((0, 16),))
    pool_kv = draw_pool_kv(jax.random.fold_in(jax.random.fold_in(splits[9], part), 71), part)
    neighbour_ids = draw_neighbour_ids(jax.random.fold_in(jax.random.fold_in(splits[9], part), 71), part)
    return {"queries": queries, "keys": keys, "values": values, "grad_self": grad_self, "doc_ids": doc_ids, "cross_queries": cross_queries, "grad_cross": grad_cross, "pool_kv": pool_kv, "neighbour_ids": neighbour_ids}


def rounded(numbers):
    return lax.optimization_barrier(numbers.astype(jnp.bfloat16)).astype(jnp.float32)


def head_pass(query_rows, key_rows, value_rows, grad_rows, allowed):
    factor = HEAD_DIM ** -0.5
    scores = jnp.dot(query_rows, key_rows.T, preferred_element_type=jnp.float32) * factor
    scores = jnp.where(allowed, scores, -jnp.inf)
    row_peak = jnp.max(scores, axis=1, keepdims=True)
    weights = jnp.exp(scores - row_peak)
    probs = weights / jnp.sum(weights, axis=1, keepdims=True)
    probs_low = probs.astype(jnp.bfloat16)
    output = jnp.dot(probs_low, value_rows, preferred_element_type=jnp.float32)
    delta = jnp.sum(grad_rows.astype(jnp.float32) * output, axis=1, keepdims=True)
    grad_probs = jnp.dot(grad_rows, value_rows.T, preferred_element_type=jnp.float32)
    grad_scores = (probs * (grad_probs - delta)).astype(jnp.bfloat16)
    grad_query = jnp.dot(grad_scores, key_rows, preferred_element_type=jnp.float32) * factor
    grad_key = jnp.dot(grad_scores.T, query_rows, preferred_element_type=jnp.float32) * factor
    grad_value = jnp.dot(probs_low.T, grad_rows, preferred_element_type=jnp.float32)
    return grad_query, grad_key, grad_value


def block_pass(query_rows, key_rows, value_rows, grad_rows, allowed):
    result_sets = []
    for head_index in range(HEADS):
        low_col = head_index * HEAD_DIM
        high_col = low_col + HEAD_DIM
        result_sets.append(head_pass(query_rows[:, low_col:high_col], key_rows[:, low_col:high_col], value_rows[:, low_col:high_col], grad_rows[:, low_col:high_col], allowed))
    return tuple(jnp.concatenate([result_set[column] for result_set in result_sets], axis=1) for column in range(3))


def cross_pass(stretch_q, stretch_kv, stretch_g):
    count, width_q, _ = stretch_q.shape
    width_k = stretch_kv.shape[2]
    query4 = stretch_q.reshape(count, width_q, HEADS, HEAD_DIM).astype(jnp.float32)
    key4 = stretch_kv[0].reshape(count, width_k, HEADS, HEAD_DIM).astype(jnp.float32)
    value4 = stretch_kv[1].reshape(count, width_k, HEADS, HEAD_DIM).astype(jnp.float32)
    grad4 = stretch_g.reshape(count, width_q, HEADS, HEAD_DIM).astype(jnp.float32)
    factor = HEAD_DIM ** -0.5
    scores = jnp.einsum("cqhd,ckhd->chqk", query4, key4) * factor
    row_peak = jnp.max(scores, axis=3, keepdims=True)
    weights = jnp.exp(scores - row_peak)
    probs = weights / jnp.sum(weights, axis=3, keepdims=True)
    probs_low = probs.astype(jnp.bfloat16).astype(jnp.float32)
    output = jnp.einsum("chqk,ckhd->cqhd", probs_low, value4)
    delta = jnp.sum(grad4 * output, axis=3).transpose(0, 2, 1)[..., None]
    grad_probs = jnp.einsum("cqhd,ckhd->chqk", grad4, value4)
    grad_scores = (probs * (grad_probs - delta)).astype(jnp.bfloat16).astype(jnp.float32)
    grad_query = jnp.einsum("chqk,ckhd->cqhd", grad_scores, key4) * factor
    grad_key = jnp.einsum("chqk,cqhd->ckhd", grad_scores, query4) * factor
    grad_value = jnp.einsum("chqk,cqhd->ckhd", probs_low, grad4)
    return grad_query.reshape(count, width_q, HD), grad_key.reshape(count, width_k, HD), grad_value.reshape(count, width_k, HD)


def reference(queries, keys, values, grad_self, doc_ids, cross_queries, grad_cross, pool_kv, neighbour_ids):
    window_rows = (REACH + 1) * TOK_DEV
    pad_keys = jnp.pad(keys, ((REACH * TOK_DEV, 0), (0, 0)))
    pad_values = jnp.pad(values, ((REACH * TOK_DEV, 0), (0, 0)))
    pad_ids = jnp.pad(doc_ids, (REACH * TOK_DEV, 0), constant_values=-1)
    row_pos = jnp.arange(TOK_DEV, dtype=jnp.int32)[:, None]
    col_pos = jnp.arange(window_rows, dtype=jnp.int32)[None, :] - REACH * TOK_DEV
    causal = col_pos <= row_pos

    def self_step(carry, block):
        acc_keys, acc_values = carry
        first_row = (block * TOK_DEV).astype(jnp.int32)
        query_rows = lax.dynamic_slice_in_dim(queries, first_row, TOK_DEV, 0)
        grad_rows = lax.dynamic_slice_in_dim(grad_self, first_row, TOK_DEV, 0)
        key_rows = lax.dynamic_slice_in_dim(pad_keys, first_row, window_rows, 0)
        value_rows = lax.dynamic_slice_in_dim(pad_values, first_row, window_rows, 0)
        query_ids = lax.dynamic_slice_in_dim(doc_ids, first_row, TOK_DEV, 0)
        key_ids = lax.dynamic_slice_in_dim(pad_ids, first_row, window_rows, 0)
        allowed = causal & (key_ids[None, :] == query_ids[:, None])
        grad_q, grad_k, grad_v = block_pass(query_rows, key_rows, value_rows, grad_rows, allowed)
        terms_k = [rounded(grad_k[(REACH - distance) * TOK_DEV:(REACH - distance + 1) * TOK_DEV]) for distance in range(REACH + 1)]
        terms_v = [rounded(grad_v[(REACH - distance) * TOK_DEV:(REACH - distance + 1) * TOK_DEV]) for distance in range(REACH + 1)]
        done_k = acc_keys[REACH - 1] + terms_k[REACH]
        done_v = acc_values[REACH - 1] + terms_v[REACH]
        next_k = tuple([terms_k[0]] + [acc_keys[slot_index - 1] + terms_k[slot_index] for slot_index in range(1, REACH)])
        next_v = tuple([terms_v[0]] + [acc_values[slot_index - 1] + terms_v[slot_index] for slot_index in range(1, REACH)])
        return (next_k, next_v), (grad_q.astype(jnp.bfloat16), done_k, done_v)

    zero_block = jnp.zeros((TOK_DEV, HD), jnp.float32)
    start_carry = (tuple(zero_block for slot_index in range(REACH)), tuple(zero_block for slot_index in range(REACH)))
    blocks = jnp.arange(N_CTX, dtype=jnp.int32)
    (last_k, last_v), (grad_q_all, done_k_all, done_v_all) = lax.scan(self_step, start_carry, blocks)
    grad_queries = grad_q_all.reshape(TOKENS, HD)
    tail_k = [last_k[slot_index] for slot_index in range(REACH - 1, -1, -1)]
    tail_v = [last_v[slot_index] for slot_index in range(REACH - 1, -1, -1)]
    grad_keys = jnp.concatenate([done_k_all[REACH:].reshape(-1, HD)] + tail_k, axis=0).astype(jnp.bfloat16)
    grad_values = jnp.concatenate([done_v_all[REACH:].reshape(-1, HD)] + tail_v, axis=0).astype(jnp.bfloat16)

    def cross_step(acc_pool, block):
        first_row = (block * TOK_DEV).astype(jnp.int32)
        query_rows = lax.dynamic_slice_in_dim(cross_queries, first_row, TOK_DEV, 0).reshape(CH_DEV, STRETCH, HD)
        grad_rows = lax.dynamic_slice_in_dim(grad_cross, first_row, TOK_DEV, 0).reshape(CH_DEV, STRETCH, HD)
        chosen_ids = lax.dynamic_slice_in_dim(neighbour_ids, (block * CH_DEV).astype(jnp.int32), CH_DEV, 0)
        flat_ids = chosen_ids.reshape(-1)
        chosen = jnp.take(pool_kv, flat_ids, axis=1).reshape(2, CH_DEV, NBRS * NBR_TOK, HD)
        grad_q, grad_k, grad_v = cross_pass(query_rows, chosen, grad_rows)
        relative = (flat_ids // ENC_DEV - block + 1) % N_CTX
        local_ids = (relative * ENC_DEV + flat_ids % ENC_DEV).astype(jnp.int32)
        stacked = jnp.stack([grad_k, grad_v]).reshape(2, CH_DEV * NBRS, NBR_TOK, HD)
        window = jnp.zeros((2, 3 * ENC_DEV, NBR_TOK, HD), jnp.float32).at[:, local_ids].add(stacked)
        window = rounded(window).reshape(2, 3, ENC_DEV, NBR_TOK, HD)
        for side in range(3):
            acc_pool = acc_pool.at[:, (block - 1 + side) % N_CTX].add(window[:, side])
        return acc_pool, grad_q.reshape(TOK_DEV, HD).astype(jnp.bfloat16)

    start_pool = jnp.zeros((2, N_CTX, ENC_DEV, NBR_TOK, HD), jnp.float32)
    acc_pool, grad_cq_all = lax.scan(cross_step, start_pool, blocks)
    grad_cross_queries = grad_cq_all.reshape(TOKENS, HD)
    grad_pool = acc_pool.reshape(2, ENCS, NBR_TOK, HD).astype(jnp.bfloat16)
    return grad_queries, grad_keys, grad_values, grad_cross_queries, grad_pool
```

```python
import functools
import math

import jax
import jax.numpy as jnp
from jax import lax
from jax.experimental import pallas as pl
from jax.experimental.pallas import tpu as pltpu
from jax.sharding import PartitionSpec as P

HEADS = 8
HEAD_DIM = 128
STRETCH = 64
NBRS = 2
NBR_TOK = 128
REACH = 2
FACTOR = HEAD_DIM ** (-0.5)
MASKED = -1e30


def pairs_to(axis, steps, wrap=False, parity=None):
    count = lax.axis_size(axis)
    pairs = []
    for source in range(count):
        target = source + steps
        if parity is not None and source % 2 != parity:
            continue
        if wrap:
            pairs.append((source, target % count))
        elif 0 <= target < count:
            pairs.append((source, target))
    return pairs


def send(value, steps, wrap=False, parity=None):
    return lax.ppermute(value, "ctx", pairs_to("ctx", steps, wrap, parity))


def attend(bias, q, g, k, v):
    f32 = jnp.float32
    last = (((1,), (1,)), ((), ()))
    s = lax.dot_general(k, q, last, preferred_element_type=f32) * FACTOR + bias
    peak = jnp.max(s, axis=0, keepdims=True)
    e = jnp.exp(s - peak)
    p = e * (1.0 / jnp.sum(e, axis=0, keepdims=True))
    pb = p.astype(jnp.bfloat16)
    dp = lax.dot_general(v, g, last, preferred_element_type=f32)
    delta = jnp.sum(pb.astype(f32) * dp, axis=0, keepdims=True)
    ds = (p * (dp - delta)).astype(jnp.bfloat16)
    dv = jnp.dot(pb, g, preferred_element_type=f32)
    dk = jnp.dot(ds, q, preferred_element_type=f32) * FACTOR
    first = (((0,), (0,)), ((), ()))
    dq = lax.dot_general(ds, k, first, preferred_element_type=f32) * FACTOR
    return dq, dk, dv


def store(refs, dk, dv):
    rows = dk.shape[0] // len(refs)
    for index, ref in enumerate(refs):
        ref[0] = dk[index * rows : (index + 1) * rows].astype(jnp.bfloat16)
        ref[1] = dv[index * rows : (index + 1) * rows].astype(jnp.bfloat16)


def self_kernel(
    bias, q, g, k2a, k2b, k1, k0, v2a, v2b, v1, v0, dq_ref, kv2, kv1, kv0
):
    k = jnp.concatenate([k2a[...] + k2b[...], k1[...], k0[...]], axis=0)
    v = jnp.concatenate([v2a[...] + v2b[...], v1[...], v0[...]], axis=0)
    dq, dk, dv = attend(bias[...], q[...], g[...], k, v)
    dq_ref[...] = dq.astype(jnp.bfloat16)
    store((kv2, kv1, kv0), dk, dv)


def cross_kernel(bias, q, g, low, own, high, dq_ref, kv_low, kv_own, kv_high):
    k = jnp.concatenate([low[0], own[0], high[0]], axis=0)
    v = jnp.concatenate([low[1], own[1], high[1]], axis=0)
    dq, dk, dv = attend(bias[...], q[...], g[...], k, v)
    dq_ref[...] = dq.astype(jnp.bfloat16)
    store((kv_low, kv_own, kv_high), dk, dv)


def attention_call(kernel, name, bias, rows_in, pairs_in):
    rows, width = rows_in[0].shape
    keys = bias.shape[0]
    part = keys // 3
    row_spec = lambda r: pl.BlockSpec((r, HEAD_DIM), lambda h: (0, h))
    pair_spec = lambda r: pl.BlockSpec((2, r, HEAD_DIM), lambda h: (0, 0, h))
    bf16 = jnp.bfloat16
    return pl.pallas_call(
        kernel,
        name=name,
        grid=(width // HEAD_DIM,),
        in_specs=[pl.BlockSpec(bias.shape, lambda h: (0, 0))]
        + [row_spec(x.shape[0]) for x in rows_in]
        + [pair_spec(x.shape[1]) for x in pairs_in],
        out_specs=[row_spec(rows)] + [pair_spec(part)] * 3,
        out_shape=[jax.ShapeDtypeStruct((rows, width), bf16)]
        + [jax.ShapeDtypeStruct((2, part, width), bf16)] * 3,
        compiler_params=pltpu.CompilerParams(vmem_limit_bytes=40 << 20),
        cost_estimate=pl.CostEstimate(
            flops=10 * rows * keys * width,
            transcendentals=rows * keys * (width // HEAD_DIM),
            bytes_accessed=2 * width * (4 * rows + 8 * keys),
        ),
    )(bias, *rows_in, *pairs_in)


def body(
    queries, keys, values, grad_self, doc_ids, cross_queries, grad_cross, pool_kv, neighbour_ids
):
    f32 = jnp.float32
    tok_rows, width = queries.shape
    loop_size = lax.axis_size("ctx")
    my_index = lax.axis_index("ctx")
    enc_dev = pool_kv.shape[1]
    pool = pool_kv.reshape(2, enc_dev * NBR_TOK, width)

    low = send(pool, 1, wrap=True)
    high = send(pool, -1, wrap=True)
    k1, v1 = send((keys, values), 1)
    k2a, v2a = send((keys, values), 2, parity=0)
    k2b, v2b = send((k1, v1), 1, parity=0)

    window = (REACH + 1) * tok_rows
    padded_ids = jnp.pad(doc_ids, (REACH * tok_rows, 0), constant_values=-1)
    first_row = my_index * tok_rows
    query_ids = lax.dynamic_slice_in_dim(doc_ids, first_row, tok_rows, 0)
    key_ids = lax.dynamic_slice_in_dim(padded_ids, first_row, window, 0)
    row_pos = jnp.arange(tok_rows, dtype=jnp.int32)[None, :]
    col_pos = jnp.arange(window, dtype=jnp.int32)[:, None] - REACH * tok_rows
    allowed = (col_pos <= row_pos) & (key_ids[:, None] == query_ids[None, :])
    self_bias = jnp.where(allowed, 0.0, MASKED).astype(f32)

    relative = (neighbour_ids // enc_dev - my_index + 1) % loop_size
    local_ids = relative * enc_dev + neighbour_ids % enc_dev
    slots = jnp.arange(3 * enc_dev, dtype=jnp.int32)
    times = jnp.sum((local_ids[None] == slots[:, None, None]).astype(jnp.int32), axis=2)
    small = jnp.where(times == 0, MASKED, jnp.where(times == 1, 0.0, math.log(2.0))).astype(f32)
    cross_bias = jnp.repeat(jnp.repeat(small, NBR_TOK, axis=0), STRETCH, axis=1)

    grad_cq, pool_low, pool_own, pool_high = attention_call(
        cross_kernel, "cross_attention", cross_bias, (cross_queries, grad_cross), (low, pool, high)
    )
    back_low = send(pool_low, -1, wrap=True)
    back_high = send(pool_high, 1, wrap=True)

    grad_q, part2, part1, part0 = attention_call(
        self_kernel,
        "self_attention",
        self_bias,
        (queries, grad_self, k2a, k2b, k1, keys, v2a, v2b, v1, values),
        (),
    )
    from2 = send(part2, -2, parity=0)
    odd2 = send(part2, -1, parity=1)
    part1 = (part1.astype(f32) + odd2.astype(f32)).astype(jnp.bfloat16)
    from1 = send(part1, -1)

    grad_pool = (pool_own.astype(f32) + back_low.astype(f32) + back_high.astype(f32)).astype(
        jnp.bfloat16
    )
    total = part0.astype(f32) + from1.astype(f32) + from2.astype(f32)
    return (
        grad_q,
        total[0].astype(jnp.bfloat16),
        total[1].astype(jnp.bfloat16),
        grad_cq,
        grad_pool.reshape(pool_kv.shape),
    )


def solution(mesh):
    rows = P(("groups", "ctx"), None)
    pool = P(None, ("groups", "ctx"), None, None)
    return jax.shard_map(
        body,
        mesh=mesh,
        in_specs=(rows, rows, rows, rows, P("groups"), rows, rows, pool, rows),
        out_specs=(rows, rows, rows, rows, pool),
        check_vma=False,
    )
```

```python
import functools
import math

import jax
import jax.numpy as jnp
from jax import lax
from jax.experimental import pallas as pl
from jax.experimental.pallas import tpu as pltpu
from jax.sharding import PartitionSpec as P

HEADS = 8
HEAD_DIM = 128
STRETCH = 64
NBRS = 2
NBR_TOK = 128
REACH = 2
FACTOR = HEAD_DIM ** (-0.5)
MASKED = -1e30


def pairs_to(axis, steps, wrap=False, parity=None):
    count = lax.axis_size(axis)
    pairs = []
    for source in range(count):
        target = source + steps
        if parity is not None and source % 2 != parity:
            continue
        if wrap:
            pairs.append((source, target % count))
        elif 0 <= target < count:
            pairs.append((source, target))
    return pairs


def send(value, steps, wrap=False, parity=None):
    return lax.ppermute(value, "ctx", pairs_to("ctx", steps, wrap, parity))


def attend(bias, q, g, k, v):
    f32 = jnp.float32
    last = (((1,), (1,)), ((), ()))
    s = lax.dot_general(k, q, last, preferred_element_type=f32) * FACTOR + bias
    peak = jnp.max(s, axis=0, keepdims=True)
    e = jnp.exp(s - peak)
    p = e * (1.0 / jnp.sum(e, axis=0, keepdims=True))
    pb = p.astype(jnp.bfloat16)
    dp = lax.dot_general(v, g, last, preferred_element_type=f32)
    delta = jnp.sum(pb.astype(f32) * dp, axis=0, keepdims=True)
    ds = (p * (dp - delta)).astype(jnp.bfloat16)
    dv = jnp.dot(pb, g, preferred_element_type=f32)
    dk = jnp.dot(ds, q, preferred_element_type=f32) * FACTOR
    first = (((0,), (0,)), ((), ()))
    dq = lax.dot_general(ds, k, first, preferred_element_type=f32) * FACTOR
    return dq, dk, dv


def store(refs, dk, dv):
    rows = dk.shape[0] // len(refs)
    for index, ref in enumerate(refs):
        ref[0] = dk[index * rows : (index + 1) * rows].astype(jnp.bfloat16)
        ref[1] = dv[index * rows : (index + 1) * rows].astype(jnp.bfloat16)


def self_kernel(bias, q, g, k0, v0, two_a, two_b, one, dq_ref, kv2, kv1, kv0):
    k = jnp.concatenate([two_a[0] + two_b[0], one[0], k0[...]], axis=0)
    v = jnp.concatenate([two_a[1] + two_b[1], one[1], v0[...]], axis=0)
    dq, dk, dv = attend(bias[...], q[...], g[...], k, v)
    dq_ref[...] = dq.astype(jnp.bfloat16)
    store((kv2, kv1, kv0), dk, dv)


def cross_kernel(bias, q, g, low, own, high, dq_ref, kv_low, kv_own, kv_high):
    k = jnp.concatenate([low[0], own[0], high[0]], axis=0)
    v = jnp.concatenate([low[1], own[1], high[1]], axis=0)
    dq, dk, dv = attend(bias[...], q[...], g[...], k, v)
    dq_ref[...] = dq.astype(jnp.bfloat16)
    store((kv_low, kv_own, kv_high), dk, dv)


def attention_call(kernel, name, bias, rows_in, pairs_in):
    rows, width = rows_in[0].shape
    keys = bias.shape[0]
    part = keys // 3
    row_spec = lambda r: pl.BlockSpec((r, HEAD_DIM), lambda h: (0, h))
    pair_spec = lambda r: pl.BlockSpec((2, r, HEAD_DIM), lambda h: (0, 0, h))
    bf16 = jnp.bfloat16
    return pl.pallas_call(
        kernel,
        name=name,
        grid=(width // HEAD_DIM,),
        in_specs=[pl.BlockSpec(bias.shape, lambda h: (0, 0))]
        + [row_spec(x.shape[0]) for x in rows_in]
        + [pair_spec(x.shape[1]) for x in pairs_in],
        out_specs=[row_spec(rows)] + [pair_spec(part)] * 3,
        out_shape=[jax.ShapeDtypeStruct((rows, width), bf16)]
        + [jax.ShapeDtypeStruct((2, part, width), bf16)] * 3,
        compiler_params=pltpu.CompilerParams(vmem_limit_bytes=60 << 20),
        cost_estimate=pl.CostEstimate(
            flops=60 * rows * keys * width,
            transcendentals=rows * keys * (width // HEAD_DIM),
            bytes_accessed=2 * width * (4 * rows + 8 * keys),
        ),
    )(bias, *rows_in, *pairs_in)


def body(
    queries, keys, values, grad_self, doc_ids, cross_queries, grad_cross, pool_kv, neighbour_ids
):
    f32 = jnp.float32
    tok_rows, width = queries.shape
    loop_size = lax.axis_size("ctx")
    my_index = lax.axis_index("ctx")
    enc_dev = pool_kv.shape[1]
    pool = pool_kv.reshape(2, enc_dev * NBR_TOK, width)

    low = send(pool, 1, wrap=True)
    high = send(pool, -1, wrap=True)

    window = (REACH + 1) * tok_rows
    padded_ids = jnp.pad(doc_ids, (REACH * tok_rows, 0), constant_values=-1)
    first_row = my_index * tok_rows
    query_ids = lax.dynamic_slice_in_dim(doc_ids, first_row, tok_rows, 0)
    key_ids = lax.dynamic_slice_in_dim(padded_ids, first_row, window, 0)
    row_pos = jnp.arange(tok_rows, dtype=jnp.int32)[None, :]
    col_pos = jnp.arange(window, dtype=jnp.int32)[:, None] - REACH * tok_rows
    allowed = (col_pos <= row_pos) & (key_ids[:, None] == query_ids[None, :])
    self_bias = jnp.where(allowed, 0.0, MASKED).astype(f32)

    neighbour_ids, low, high = lax.optimization_barrier((neighbour_ids, low, high))
    relative = (neighbour_ids // enc_dev - my_index + 1) % loop_size
    local_ids = relative * enc_dev + neighbour_ids % enc_dev
    slots = jnp.arange(3 * enc_dev, dtype=jnp.int32)
    times = jnp.sum((local_ids[None] == slots[:, None, None]).astype(jnp.int32), axis=2)
    small = jnp.where(times == 0, MASKED, jnp.where(times == 1, 0.0, math.log(2.0))).astype(f32)
    cross_bias = jnp.repeat(jnp.repeat(small, NBR_TOK, axis=0), STRETCH, axis=1)

    own_kv = jnp.stack([keys, values])
    one = send(own_kv, 1)
    two_a = send(own_kv, 2, parity=0)
    two_b = send(one, 1, parity=0)

    grad_cq, pool_low, pool_own, pool_high = attention_call(
        cross_kernel, "cross_attention", cross_bias, (cross_queries, grad_cross), (low, pool, high)
    )
    back_low = send(pool_low, -1, wrap=True)
    back_high = send(pool_high, 1, wrap=True)

    self_bias, pool_own = lax.optimization_barrier((self_bias, pool_own))
    grad_q, part2, part1, part0 = attention_call(
        self_kernel,
        "self_attention",
        self_bias,
        (queries, grad_self, keys, values),
        (two_a, two_b, one),
    )
    from2 = send(part2, -2, parity=0)
    odd2 = send(part2, -1, parity=1)
    part1 = (part1.astype(f32) + odd2.astype(f32)).astype(jnp.bfloat16)
    grad_pool = (pool_own.astype(f32) + back_low.astype(f32) + back_high.astype(f32)).astype(
        jnp.bfloat16
    )
    part1, grad_pool = lax.optimization_barrier((part1, grad_pool))
    from1 = send(part1, -1)
    total = part0.astype(f32) + from1.astype(f32) + from2.astype(f32)
    return (
        grad_q,
        total[0].astype(jnp.bfloat16),
        total[1].astype(jnp.bfloat16),
        grad_cq,
        grad_pool.reshape(pool_kv.shape),
    )


def solution(mesh):
    rows = P(("groups", "ctx"), None)
    pool = P(None, ("groups", "ctx"), None, None)
    return jax.shard_map(
        body,
        mesh=mesh,
        in_specs=(rows, rows, rows, rows, P("groups"), rows, rows, pool, rows),
        out_specs=(rows, rows, rows, rows, pool),
        check_vma=False,
    )
```

```python
import functools
import math

import jax
import jax.numpy as jnp
from jax import lax
from jax.experimental import pallas as pl
from jax.experimental.pallas import tpu as pltpu
from jax.sharding import PartitionSpec as P

HEADS = 8
HEAD_DIM = 128
HALF = HEADS // 2
WIDE = HALF * HEAD_DIM
STRETCH = 64
NBR_TOK = 128
ROWS = 256
EXTRA = 16
FACTOR = HEAD_DIM ** (-0.5)
MASKED = -1e30
BF16 = jnp.bfloat16
F32 = jnp.float32


def send(value, target_of, wrap):
    count = lax.axis_size("ctx")
    pairs = []
    for source in range(count):
        target = target_of(source)
        if wrap:
            pairs.append((source, target % count))
        elif 0 <= target < count:
            pairs.append((source, target))
    return lax.ppermute(value, "ctx", pairs)


def swap(d):
    return d ^ 1


def outward(d):
    return d - 2 if d % 2 == 0 else d + 2


def inward(d):
    return d + 2 if d % 2 == 0 else d - 2


def across(d):
    return d - 1 if d % 2 == 0 else d + 1


def spec(rows, row_block=0, cols=HEAD_DIM):
    return pl.BlockSpec((rows, cols), lambda h, info: (row_block, h))


def own_spec(lead=()):
    zeros = (0,) * len(lead)
    return pl.BlockSpec(
        lead + (ROWS, HEAD_DIM), lambda h, info: zeros + (0, info[0] % 2 * HALF + h)
    )


def other_spec(lead=()):
    zeros = (0,) * len(lead)
    return pl.BlockSpec(
        lead + (ROWS, HEAD_DIM), lambda h, info: zeros + (0, (1 - info[0] % 2) * HALF + h)
    )


def whole_spec(shape, index=None):
    index = (0,) * len(shape) if index is None else index
    return pl.BlockSpec(shape, lambda h, *info: index)


def stat_spec(rows):
    return pl.BlockSpec((1, 8, rows), lambda h, info: (h, 0, 0))


def call(kernel, name, info, in_specs, inputs, out_specs, outs, steps=HALF, flops=0, prefetch=None):
    prefetch = (info,) if prefetch is None else prefetch
    return pl.pallas_call(
        kernel,
        name=name,
        grid_spec=pltpu.PrefetchScalarGridSpec(
            num_scalar_prefetch=len(prefetch),
            grid=(steps,),
            in_specs=in_specs,
            out_specs=out_specs,
        ),
        out_shape=[jax.ShapeDtypeStruct(shape, dtype) for shape, dtype in outs],
        compiler_params=pltpu.CompilerParams(vmem_limit_bytes=60 << 20),
        cost_estimate=pl.CostEstimate(flops=flops, transcendentals=0, bytes_accessed=4 << 20),
    )(*prefetch, *inputs)


def dot_last(a, b):
    return lax.dot_general(a, b, (((1,), (1,)), ((), ())), preferred_element_type=F32)


def dot_first(a, b):
    return lax.dot_general(a, b, (((0,), (0,)), ((), ())), preferred_element_type=F32)


def dot(a, b):
    return jnp.dot(a, b, preferred_element_type=F32)


def both(a, b):
    return jnp.concatenate([a, b], axis=0)


def weight_rows(times):
    log_two = jnp.where(times > 1.5, math.log(2.0), 0.0)
    return jnp.where(times < 0.5, MASKED, log_two)


def slot_pair(ref, first, core, second=None):
    times = ref[...].astype(F32)[:, :ROWS]
    low = times[first : first + 2]
    if second is None:
        return weight_rows(low)
    return weight_rows(jnp.where(core == 0, low, times[second : second + 2]))


def add_rows(s, rows):
    parts = [
        s[e * NBR_TOK : (e + 1) * NBR_TOK] + rows[e : e + 1] for e in range(s.shape[0] // NBR_TOK)
    ]
    return jnp.concatenate(parts, axis=0)


def partial_stats(s, dp):
    peak = jnp.max(s, axis=0, keepdims=True)
    e = jnp.exp(s - peak)
    return e, peak, jnp.sum(e, axis=0, keepdims=True), jnp.sum(e * dp, axis=0, keepdims=True)


def stat_rows(a, b, c):
    return jnp.concatenate([a, b, c, jnp.zeros((5, a.shape[1]), F32)], axis=0)[None]


def merge(stats, mine):
    t_peak, t_total, t_moment = stats[0, 0:1], stats[0, 1:2], stats[0, 2:3]
    peak, total, moment = mine
    top = jnp.maximum(t_peak, peak)
    t_scale = jnp.exp(t_peak - top)
    scale = jnp.exp(peak - top)
    full = t_total * t_scale + total * scale
    inverse = jnp.where(full > 0, 1.0 / full, 0.0)
    delta = (t_moment * t_scale + moment * scale) * inverse
    return top, inverse, delta, scale * inverse


def gradients(p, dp, delta, q, g, k):
    pb = p.astype(BF16)
    ds = (p * (dp - delta)).astype(BF16)
    return dot_first(ds, k) * FACTOR, dot(ds, q) * FACTOR, dot(pb, g)


def pack_kernel(enc_dev, loop, info, ids, *refs):
    qm, gm, xqm, xgm, q, g, k, v, xq, xg, pool, swap_ref, xm, xo, sm, so = refs
    me = info[0]
    shape = (EXTRA, HEAD_DIM)
    row = lax.broadcasted_iota(jnp.int32, shape, 0)
    lane = lax.broadcasted_iota(jnp.int32, shape, 1) + pl.program_id(0) * HEAD_DIM
    times = jnp.zeros(shape, F32)
    for s in range(ids.shape[0]):
        for n in range(ids.shape[1]):
            relative = lax.rem(ids[s, n] // enc_dev - me + 1 + loop, loop)
            local = relative * enc_dev + lax.rem(ids[s, n], enc_dev)
            hit = (row == local) & (lane >= s * STRETCH) & (lane < (s + 1) * STRETCH)
            times = times + jnp.where(hit, 1.0, 0.0)
    times = times.astype(BF16)
    for index, ref in enumerate((q, g, k, v, xq, xg)):
        swap_ref[index * ROWS : (index + 1) * ROWS] = ref[...]
    swap_ref[6 * ROWS : 7 * ROWS] = pool[0]
    swap_ref[7 * ROWS : 8 * ROWS] = pool[1]
    swap_ref[8 * ROWS :] = times
    for out, first, second in ((xm, xqm, xgm), (xo, xq, xg), (sm, qm, gm), (so, q, g)):
        out[0:ROWS] = first[...]
        out[ROWS : 2 * ROWS] = second[...]
    xm[2 * ROWS :] = times
    xo[2 * ROWS :] = times


def local_self(bias, q, g, k, v, pq, pg, pk, pv):
    qs, gs = both(q[...], pq[...]), both(g[...], pg[...])
    ks, vs = both(k[...], pk[...]), both(v[...], pv[...])
    return dot_last(ks, qs) * FACTOR + bias[...], dot_last(vs, gs), qs, gs, ks


def local_cross(core, w, pw, q, g, pool, pq, pg, pk, pv):
    qs, gs = both(q[...], pq[...]), both(g[...], pg[...])
    ks, vs = both(pool[0], pk[...]), both(pool[1], pv[...])
    own = both(slot_pair(w, 2, core), slot_pair(w, 4, core, 0))
    partner = both(slot_pair(pw, 0, core, 4), slot_pair(pw, 2, core))
    s = add_rows(dot_last(ks, qs) * FACTOR, jnp.concatenate([own, partner], axis=1))
    return s, dot_last(vs, gs), qs, gs, ks


def self_stats_kernel(info, *refs):
    s, dp, _, _, _ = local_self(*refs[:-1])
    refs[-1][...] = stat_rows(*partial_stats(s, dp)[1:])


def cross_stats_kernel(info, *refs):
    s, dp, _, _, _ = local_cross(info[0] % 2, *refs[:-2])
    stats = stat_rows(*partial_stats(s, dp)[1:])
    refs[-2][...] = stats[:, :, :ROWS]
    refs[-1][...] = stats[:, :, ROWS:]


def self_remote_kernel(
    info, bias, sq, sg, cq, cg, k, v, pk, pv, stats, dq_same, dq_cross, kv_ref, out_stats
):
    qs, gs = both(sq[...], cq[...]), both(sg[...], cg[...])
    ks, vs = both(k[...], pk[...]), both(v[...], pv[...])
    s, dp = dot_last(ks, qs) * FACTOR + bias[...], dot_last(vs, gs)
    e, *mine = partial_stats(s, dp)
    top, inverse, delta, scale = merge(stats[...], mine)
    dq, dk, dv = gradients(e * scale, dp, delta, qs, gs, ks)
    dq_same[...] = dq[:ROWS].astype(BF16)
    dq_cross[...] = dq[ROWS:].astype(BF16)
    kv_ref[: 2 * ROWS] = dk.astype(BF16)
    kv_ref[2 * ROWS :] = dv.astype(BF16)
    out_stats[...] = stat_rows(top, inverse, delta)


def cross_remote_kernel(
    info, sw, cw, sq, sg, cq, cg, pool, pk, pv, s_stats, c_stats, *outs
):
    dq_same, dq_cross, kv_ref, out_same, out_cross = outs
    core = info[0] % 2
    jobs = (
        (cq, cg, pool[0], pool[1], slot_pair(cw, 4, core, 0), c_stats, dq_cross, out_cross, 0),
        (sq, sg, pk[...], pv[...], slot_pair(sw, 0, core, 4), s_stats, dq_same, out_same, 1),
    )
    for q, g, k, v, rows, stats, dq_ref, out_stats, place in jobs:
        s, dp = add_rows(dot_last(k, q[...]) * FACTOR, rows), dot_last(v, g[...])
        e, *mine = partial_stats(s, dp)
        top, inverse, delta, scale = merge(stats[...], mine)
        dq, dk, dv = gradients(e * scale, dp, delta, q[...], g[...], k)
        dq_ref[...] = dq.astype(BF16)
        kv_ref[place * ROWS : (place + 1) * ROWS] = dk.astype(BF16)
        kv_ref[(2 + place) * ROWS : (3 + place) * ROWS] = dv.astype(BF16)
        out_stats[...] = stat_rows(top, inverse, delta)


def finish_local(parts, top, inverse, delta, kv_ref, mine, theirs):
    s, dp, qs, gs, ks = parts
    dq, dk, dv = gradients(jnp.exp(s - top) * inverse, dp, delta, qs, gs, ks)
    dk = dk + kv_ref[: 2 * ROWS].astype(F32)
    dv = dv + kv_ref[2 * ROWS :].astype(F32)
    for index, grad in enumerate((dq, dk, dv)):
        mine[index * ROWS : (index + 1) * ROWS] = grad[:ROWS].astype(BF16)
        theirs[index * ROWS : (index + 1) * ROWS] = grad[ROWS:].astype(BF16)


def self_local_kernel(info, *refs):
    stats_ref, own_ref, kv_ref, mine, theirs = refs[-5:]
    stats, local = stats_ref[0], own_ref[0]
    first = info[0] < 2
    inverse = 1.0 / local[1:2]
    top = jnp.where(first, local[0:1], stats[0:1])
    delta = jnp.where(first, local[2:3] * inverse, stats[2:3])
    inverse = jnp.where(first, inverse, stats[1:2])
    finish_local(local_self(*refs[:-5]), top, inverse, delta, kv_ref, mine, theirs)


def cross_local_kernel(info, *refs):
    own_ref, partner_ref, kv_ref, mine, theirs = refs[-5:]
    stats = jnp.concatenate([own_ref[0], partner_ref[0]], axis=1)
    parts = local_cross(info[0] % 2, *refs[:-5])
    finish_local(parts, stats[0:1], stats[1:2], stats[2:3], kv_ref, mine, theirs)


def final_kernel(info, mine, theirs, dq_mine, dq_theirs, *outs):
    def write(source, extra):
        dq = source[:ROWS].astype(F32) + extra[...].astype(F32)
        outs[0][...] = dq.astype(BF16)
        if len(outs) == 3:
            outs[1][...] = source[ROWS : 2 * ROWS]
            outs[2][...] = source[2 * ROWS :]
        else:
            outs[1][0] = source[ROWS : 2 * ROWS]
            outs[1][1] = source[2 * ROWS :]

    @pl.when(pl.program_id(0) == 0)
    def _():
        write(mine, dq_mine)

    @pl.when(pl.program_id(0) == 1)
    def _():
        write(theirs, dq_theirs)


def assemble(name, info, mine, theirs, dq_mine, dq_theirs, pooled):
    half = lambda h, info: (info[0] + h) % 2
    rows_out = pl.BlockSpec((ROWS, WIDE), lambda h, info: (0, half(h, info)))
    pool_out = pl.BlockSpec((2, ROWS, WIDE), lambda h, info: (0, 0, half(h, info)))
    full = ((ROWS, 2 * WIDE), BF16)
    if pooled:
        out_specs, outs = [rows_out, pool_out], [full, ((2, ROWS, 2 * WIDE), BF16)]
    else:
        out_specs, outs = [rows_out] * 3, [full] * 3
    return call(
        final_kernel,
        name,
        info,
        [whole_spec((3 * ROWS, WIDE))] * 2 + [whole_spec((ROWS, WIDE))] * 2,
        (mine, theirs, dq_mine, dq_theirs),
        out_specs,
        outs,
        steps=2,
    )


def body(
    queries, keys, values, grad_self, doc_ids, cross_queries, grad_cross, pool_kv, neighbour_ids
):
    loop = lax.axis_size("ctx")
    me = lax.axis_index("ctx").astype(jnp.int32)
    info = jnp.full((1,), me, jnp.int32)
    enc_dev = pool_kv.shape[1]
    width = queries.shape[1]
    pool = pool_kv.reshape(2, ROWS, width)
    hd = HEAD_DIM
    gig = 10**9

    two = lambda: pl.BlockSpec((2 * ROWS + EXTRA, hd), lambda h, *info: (0, h))
    pair = lambda: pl.BlockSpec((2 * ROWS, hd), lambda h, *info: (0, h))
    mine_spec = pl.BlockSpec((ROWS, hd), lambda h, info, ids: (0, info[0] % 2 * HALF + h))
    their_spec = pl.BlockSpec((ROWS, hd), lambda h, info, ids: (0, (1 - info[0] % 2) * HALF + h))
    their_pool = pl.BlockSpec(
        (2, ROWS, hd), lambda h, info, ids: (0, 0, (1 - info[0] % 2) * HALF + h)
    )
    swap_rows = 8 * ROWS + EXTRA
    packed, x_mine, x_other, s_mine, s_other = call(
        functools.partial(pack_kernel, enc_dev, loop),
        "pack",
        info,
        [mine_spec] * 4 + [their_spec] * 6 + [their_pool],
        (queries, grad_self, cross_queries, grad_cross)
        + (queries, grad_self, keys, values, cross_queries, grad_cross, pool),
        [pl.BlockSpec((swap_rows, hd), lambda h, *info: (0, h)), two(), two(), pair(), pair()],
        [((swap_rows, WIDE), BF16)]
        + [((2 * ROWS + EXTRA, WIDE), BF16)] * 2
        + [((2 * ROWS, WIDE), BF16)] * 2,
        prefetch=(info, neighbour_ids),
    )
    partner = send(packed, swap, False)
    x_same = send(x_mine, outward, True)
    x_cross = send(x_other, across, True)

    ids_of = lambda d: lax.dynamic_slice_in_dim(doc_ids, d * ROWS, ROWS, 0)
    span = jnp.arange(ROWS, dtype=jnp.int32)
    beside = me + 1 - 2 * (me % 2)
    key_ids = jnp.concatenate([ids_of(me), ids_of(beside)])
    key_pos = jnp.concatenate([span + me * ROWS, span + beside * ROWS])
    far_ids = jnp.concatenate([ids_of(me + 2), ids_of(beside + 2)])
    same_doc = key_ids[:, None] == key_ids[None, :]
    local_ok = same_doc & (key_pos[:, None] <= key_pos[None, :])
    far_ok = (key_ids[:, None] == far_ids[None, :]) & (me + 2 < loop)
    local_bias = jnp.where(local_ok, 0.0, MASKED).astype(F32)
    far_bias = jnp.where(far_ok, 0.0, MASKED).astype(F32)

    bias_spec = whole_spec((2 * ROWS, 2 * ROWS))
    self_specs = [bias_spec] + [own_spec()] * 4 + [spec(ROWS, j) for j in range(4)]
    self_args = (local_bias, queries, grad_self, keys, values) + (partner,) * 4
    mine_w = whole_spec((EXTRA, WIDE), (2 * ROWS // EXTRA, 0))
    partner_w = whole_spec((EXTRA, WIDE), (8 * ROWS // EXTRA, 0))
    cross_specs = (
        [mine_w, partner_w, own_spec(), own_spec(), own_spec((2,))]
        + [spec(ROWS, j) for j in range(4, 8)]
    )
    cross_args = (x_mine, partner, cross_queries, grad_cross, pool) + (partner,) * 4
    stat = lambda rows: ((HALF, 8, rows), F32)

    x_own, x_partner = call(
        cross_stats_kernel, "cross_stats", info, cross_specs, cross_args,
        [stat_spec(ROWS)] * 2, [stat(ROWS)] * 2, flops=4 * gig,
    )
    t_same = send(x_own, outward, True)
    t_cross = send(x_partner, inward, True)
    s_mine, s_other, x_own = lax.optimization_barrier((s_mine, s_other, x_own))
    s_same = send(s_mine, lambda d: d - 2, False)
    s_cross = send(s_other, lambda d: (d - 2) ^ 1, False)

    (s_own,) = call(
        self_stats_kernel, "self_stats", info, self_specs, self_args,
        [stat_spec(2 * ROWS)], [stat(2 * ROWS)], flops=4 * gig,
    )
    t_self = send(s_own, lambda d: d - 2, False)

    kv_out = spec(4 * ROWS)
    kv_shape = ((4 * ROWS, WIDE), BF16)
    q_shape = ((ROWS, WIDE), BF16)
    xd_same, xd_cross, x_kv, x_fin_same, x_fin_cross = call(
        cross_remote_kernel, "cross_remote", info,
        [mine_w, mine_w, spec(ROWS, 0), spec(ROWS, 1), spec(ROWS, 0), spec(ROWS, 1)]
        + [own_spec((2,)), spec(ROWS, 6), spec(ROWS, 7), stat_spec(ROWS), stat_spec(ROWS)],
        (x_same, x_cross, x_same, x_same, x_cross, x_cross, pool, partner, partner, t_same, t_cross),
        [spec(ROWS), spec(ROWS), kv_out, stat_spec(ROWS), stat_spec(ROWS)],
        [q_shape, q_shape, kv_shape, stat(ROWS), stat(ROWS)], flops=6 * gig,
    )
    f_own = send(x_fin_same, inward, True)
    f_partner = send(x_fin_cross, outward, True)
    xr_same = send(xd_same, inward, True)
    xr_cross = send(xd_cross, across, True)

    sd_same, sd_cross, s_kv, s_fin = call(
        self_remote_kernel, "self_remote", info,
        [bias_spec, spec(ROWS, 0), spec(ROWS, 1), spec(ROWS, 0), spec(ROWS, 1)]
        + [own_spec(), own_spec(), spec(ROWS, 2), spec(ROWS, 3), stat_spec(2 * ROWS)],
        (far_bias, s_same, s_same, s_cross, s_cross, keys, values, partner, partner, t_self),
        [spec(ROWS), spec(ROWS), kv_out, stat_spec(2 * ROWS)],
        [q_shape, q_shape, kv_shape, stat(2 * ROWS)], flops=8 * gig,
    )
    f_self = send(s_fin, lambda d: d + 2, False)
    sr_same = send(sd_same, lambda d: d + 2, False)
    sr_cross = send(sd_cross, lambda d: (d + 2) ^ 1, False)

    half_out = spec(3 * ROWS)
    half_shape = ((3 * ROWS, WIDE), BF16)
    x_keep, x_give = call(
        cross_local_kernel, "cross_local", info,
        cross_specs + [stat_spec(ROWS), stat_spec(ROWS), spec(4 * ROWS)],
        cross_args + (f_own, f_partner, x_kv),
        [half_out] * 2, [half_shape] * 2, flops=8 * gig,
    )
    x_take = send(x_give, swap, False)
    s_keep, s_give = call(
        self_local_kernel, "self_local", info,
        self_specs + [stat_spec(2 * ROWS), stat_spec(2 * ROWS), spec(4 * ROWS)],
        self_args + (f_self, s_own, s_kv),
        [half_out] * 2, [half_shape] * 2, flops=8 * gig,
    )
    s_take = send(s_give, swap, False)
    grad_cq, grad_pool = assemble("cross_final", info, x_keep, x_take, xr_same, xr_cross, True)
    grad_q, grad_k, grad_v = assemble("self_final", info, s_keep, s_take, sr_same, sr_cross, False)
    return grad_q, grad_k, grad_v, grad_cq, grad_pool.reshape(pool_kv.shape)


def solution(mesh):
    rows = P(("groups", "ctx"), None)
    pool = P(None, ("groups", "ctx"), None, None)
    return jax.shard_map(
        body,
        mesh=mesh,
        in_specs=(rows, rows, rows, rows, P("groups"), rows, rows, pool, rows),
        out_specs=(rows, rows, rows, rows, pool),
        check_vma=False,
    )
```

```python
import functools
import math

import jax
import jax.numpy as jnp
from jax import lax
from jax.experimental import pallas as pl
from jax.experimental.pallas import tpu as pltpu
from jax.sharding import PartitionSpec as P

HEADS = 8
HEAD_DIM = 128
HALF = HEADS // 2
WIDE = HALF * HEAD_DIM
STRETCH = 64
NBR_TOK = 128
ROWS = 256
EXTRA = 16
STATS = 32
FACTOR = HEAD_DIM ** (-0.5)
MASKED = -1e30
BF16 = jnp.bfloat16
F32 = jnp.float32


def send(value, target_of, wrap):
    count = lax.axis_size("ctx")
    pairs = []
    for source in range(count):
        target = target_of(source)
        if wrap:
            pairs.append((source, target % count))
        elif 0 <= target < count:
            pairs.append((source, target))
    return lax.ppermute(value, "ctx", pairs)


def swap(d):
    return d ^ 1


def outward(d):
    return d - 2 if d % 2 == 0 else d + 2


def inward(d):
    return d + 2 if d % 2 == 0 else d - 2


def across(d):
    return d - 1 if d % 2 == 0 else d + 1


def spec(rows, row_block=0, cols=HEAD_DIM):
    return pl.BlockSpec((rows, cols), lambda h, info: (row_block, h))


def own_spec(lead=()):
    zeros = (0,) * len(lead)
    return pl.BlockSpec(
        lead + (ROWS, HEAD_DIM), lambda h, info: zeros + (0, info[0] % 2 * HALF + h)
    )


def other_spec(lead=()):
    zeros = (0,) * len(lead)
    return pl.BlockSpec(
        lead + (ROWS, HEAD_DIM), lambda h, info: zeros + (0, (1 - info[0] % 2) * HALF + h)
    )


def whole_spec(shape, index=None):
    index = (0,) * len(shape) if index is None else index
    return pl.BlockSpec(shape, lambda h, *info: index)


def stat_spec(rows):
    return pl.BlockSpec((1, 8, rows), lambda h, info: (h, 0, 0))


def call(kernel, name, info, in_specs, inputs, out_specs, outs, steps=HALF, flops=0, prefetch=None):
    prefetch = (info,) if prefetch is None else prefetch
    return pl.pallas_call(
        kernel,
        name=name,
        grid_spec=pltpu.PrefetchScalarGridSpec(
            num_scalar_prefetch=len(prefetch),
            grid=(steps,),
            in_specs=in_specs,
            out_specs=out_specs,
        ),
        out_shape=[jax.ShapeDtypeStruct(shape, dtype) for shape, dtype in outs],
        compiler_params=pltpu.CompilerParams(vmem_limit_bytes=63 << 20),
        cost_estimate=pl.CostEstimate(flops=flops, transcendentals=0, bytes_accessed=0),
    )(*prefetch, *inputs)


def dot_last(a, b):
    return lax.dot_general(a, b, (((1,), (1,)), ((), ())), preferred_element_type=F32)


def dot_first(a, b):
    return lax.dot_general(a, b, (((0,), (0,)), ((), ())), preferred_element_type=F32)


def dot(a, b):
    return jnp.dot(a, b, preferred_element_type=F32)


def both(a, b):
    return jnp.concatenate([a, b], axis=0)


def weight_rows(times):
    log_two = jnp.where(times > 1.5, math.log(2.0), 0.0)
    return jnp.where(times < 0.5, MASKED, log_two)


def slot_pair(ref, first, core, second=None):
    times = ref[...].astype(F32)[:, :ROWS]
    low = times[first : first + 2]
    if second is None:
        return weight_rows(low)
    return weight_rows(jnp.where(core == 0, low, times[second : second + 2]))


def add_rows(s, rows):
    parts = [
        s[e * NBR_TOK : (e + 1) * NBR_TOK] + rows[e : e + 1] for e in range(s.shape[0] // NBR_TOK)
    ]
    return jnp.concatenate(parts, axis=0)


def partial_stats(s, dp):
    peak = jnp.max(s, axis=0, keepdims=True)
    e = jnp.exp(s - peak)
    return e, peak, jnp.sum(e, axis=0, keepdims=True), jnp.sum(e * dp, axis=0, keepdims=True)


def stat_rows(a, b, c):
    return jnp.concatenate([a, b, c, jnp.zeros((5, a.shape[1]), F32)], axis=0)[None]


def merge(stats, mine):
    t_peak, t_total, t_moment = stats[0, 0:1], stats[0, 1:2], stats[0, 2:3]
    peak, total, moment = mine
    top = jnp.maximum(t_peak, peak)
    t_scale = jnp.exp(t_peak - top)
    scale = jnp.exp(peak - top)
    full = t_total * t_scale + total * scale
    inverse = jnp.where(full > 0, 1.0 / full, 0.0)
    delta = (t_moment * t_scale + moment * scale) * inverse
    return top, inverse, delta, scale * inverse


def gradients(p, dp, delta, q, g, k):
    pb = p.astype(BF16)
    ds = (p * (dp - delta)).astype(BF16)
    return dot_first(ds, k) * FACTOR, dot(ds, q) * FACTOR, dot(pb, g)


def pack_kernel(enc_dev, loop, info, ids_ref, *refs):
    qm, gm, xqm, xgm, q, g, k, v, xq, xg, pool, swap_ref, xm, xo, sm, so = refs
    shape = (EXTRA, xm.shape[1])
    row = lax.broadcasted_iota(jnp.int32, shape, 0)
    lane = lax.broadcasted_iota(jnp.int32, shape, 1) + pl.program_id(0) * shape[1]
    ids = ids_ref[...]
    owner = ids // enc_dev
    relative = owner - info[0] + 1
    relative = jnp.where(relative < 0, relative + loop, relative)
    relative = jnp.where(relative >= loop, relative - loop, relative)
    slots = relative * enc_dev + ids - owner * enc_dev
    times = jnp.zeros(shape, F32)
    for n in range(ids.shape[0]):
        for s in range(ids.shape[1]):
            hit = (row == slots[n : n + 1, s : s + 1]) & (lane // STRETCH == s)
            times = times + jnp.where(hit, 1.0, 0.0)
    times = times.astype(BF16)
    for index, ref in enumerate((q, g, k, v, xq, xg)):
        swap_ref[index * ROWS : (index + 1) * ROWS] = ref[...]
    swap_ref[6 * ROWS : 7 * ROWS] = pool[0]
    swap_ref[7 * ROWS : 8 * ROWS] = pool[1]
    swap_ref[8 * ROWS :] = times
    for out, first, second in ((xm, xqm, xgm), (xo, xq, xg), (sm, qm, gm), (so, q, g)):
        out[0:ROWS] = first[...]
        out[ROWS : 2 * ROWS] = second[...]
    xm[2 * ROWS :] = times
    xo[2 * ROWS :] = times


def ordered(core, a, b):
    return jnp.where(core == 0, a, b), jnp.where(core == 0, b, a)


def split3(x):
    high = x.astype(BF16)
    rest = x - high.astype(F32)
    middle = rest.astype(BF16)
    return [high, middle, (rest - middle.astype(F32)).astype(BF16)]


def put_stats(ref, stats):
    rows = []
    for low in range(0, stats[0].shape[1], HEAD_DIM):
        for x in stats:
            rows += split3(x[:, low : low + HEAD_DIM])
    rows.append(jnp.zeros((ref.shape[0] - ROWS - len(rows), HEAD_DIM), BF16))
    ref[ROWS:] = jnp.concatenate(rows, axis=0)


def take_stats(ref, lanes):
    x = ref[...].astype(F32)
    stats = []
    for index in range(3):
        parts = []
        for low in range(3 * index, 9 * (lanes // HEAD_DIM), 9):
            parts.append(x[low : low + 1] + x[low + 1 : low + 2] + x[low + 2 : low + 3])
        stats.append(jnp.concatenate(parts, axis=1))
    return stats


def wide_scores(keys_x, keys_y, values_x, values_y, qs, gs, bias):
    sx = dot_last(keys_x, qs) * FACTOR + bias[:ROWS]
    sy = dot_last(keys_y, qs[ROWS:]) * FACTOR + bias[ROWS:, ROWS:]
    return sx, sy, dot_last(values_x, gs), dot_last(values_y, gs[ROWS:])


def wide_stats(sx, sy, dpx, dpy):
    peak = jnp.max(sx, axis=0, keepdims=True)
    peak_y = jnp.maximum(peak[:, ROWS:], jnp.max(sy, axis=0, keepdims=True))
    peak = jnp.concatenate([peak[:, :ROWS], peak_y], axis=1)
    ex, ey = jnp.exp(sx - peak), jnp.exp(sy - peak_y)
    widen = lambda a, b: jnp.concatenate([a[:, :ROWS], a[:, ROWS:] + b], axis=1)
    add = lambda a: jnp.sum(a, axis=0, keepdims=True)
    return ex, ey, peak, widen(add(ex), add(ey)), widen(add(ex * dpx), add(ey * dpy))


def wide_gradients(px, py, dpx, dpy, delta, qs, gs, kx, ky):
    pbx, pby = px.astype(BF16), py.astype(BF16)
    dsx = (px * (dpx - delta)).astype(BF16)
    dsy = (py * (dpy - delta[:, ROWS:])).astype(BF16)
    dq_z = dot_first(dsx[:, :ROWS], kx) * FACTOR
    dq_y = dot_first(both(dsx[:, ROWS:], dsy), both(kx, ky)) * FACTOR
    dkx, dky = dot(dsx, qs) * FACTOR, dot(dsy, qs[ROWS:]) * FACTOR
    return dq_z, dq_y, dkx, dky, dot(pbx, gs), dot(pby, gs[ROWS:])


def local_self(core, bias, q, g, k, v, pq, pg, pk, pv):
    q0, q1 = ordered(core, q[...], pq[...])
    g0, g1 = ordered(core, g[...], pg[...])
    k0, k1 = ordered(core, k[...], pk[...])
    v0, v1 = ordered(core, v[...], pv[...])
    qs, gs = both(q0, q1), both(g0, g1)
    return wide_scores(k0, k1, v0, v1, qs, gs, bias[...]), qs, gs, k0, k1


def local_cross(core, w, pw, q, g, pool, pq, pg, pk, pv):
    qs, gs = both(q[...], pq[...]), both(g[...], pg[...])
    ks, vs = both(pool[0], pk[...]), both(pool[1], pv[...])
    own = both(slot_pair(w, 2, core), slot_pair(w, 4, core, 0))
    partner = both(slot_pair(pw, 0, core, 4), slot_pair(pw, 2, core))
    s = add_rows(dot_last(ks, qs) * FACTOR, jnp.concatenate([own, partner], axis=1))
    return s, dot_last(vs, gs), qs, gs, ks


def self_stats_kernel(info, *refs):
    scores = local_self(info[0] % 2, *refs[:-1])[0]
    refs[-1][...] = stat_rows(*wide_stats(*scores)[2:])


def cross_stats_kernel(info, *refs):
    s, dp, _, _, _ = local_cross(info[0] % 2, *refs[:-2])
    stats = stat_rows(*partial_stats(s, dp)[1:])
    refs[-2][...] = stats[:, :, :ROWS]
    refs[-1][...] = stats[:, :, ROWS:]


def self_remote_kernel(
    info, bias, sq, sg, cq, cg, k, v, pk, pv, stats, dq_same, dq_cross, kv_ref
):
    core = info[0] % 2
    q0, q1 = ordered(core, sq[...], cq[...])
    g0, g1 = ordered(core, sg[...], cg[...])
    k0, k1 = ordered(core, k[...], pk[...])
    v0, v1 = ordered(core, v[...], pv[...])
    qs, gs = both(q1, q0), both(g1, g0)
    sx, sy, dpx, dpy = wide_scores(k1, k0, v1, v0, qs, gs, bias[...])
    ex, ey, *mine = wide_stats(sx, sy, dpx, dpy)
    known = stats[...]
    known = jnp.concatenate([known[:, :, ROWS:], known[:, :, :ROWS]], axis=2)
    top, inverse, delta, scale = merge(known, mine)
    px, py = ex * scale, ey * scale[:, ROWS:]
    dq1, dq0, dk1, dk0, dv1, dv0 = wide_gradients(px, py, dpx, dpy, delta, qs, gs, k1, k0)
    same, cross = ordered(core, dq0, dq1)
    dq_same[:ROWS] = same.astype(BF16)
    put_stats(dq_same, (top, inverse, delta))
    dq_cross[...] = cross.astype(BF16)
    for index, grad in enumerate(ordered(core, dk0, dk1) + ordered(core, dv0, dv1)):
        kv_ref[index * ROWS : (index + 1) * ROWS] = grad.astype(BF16)


def cross_remote_kernel(
    info, sw, cw, sq, sg, cq, cg, pool, pk, pv, s_stats, c_stats, *outs
):
    dq_same, dq_cross, kv_ref = outs
    core = info[0] % 2
    jobs = (
        (cq, cg, pool[0], pool[1], slot_pair(cw, 4, core, 0), c_stats, dq_cross, 0),
        (sq, sg, pk[...], pv[...], slot_pair(sw, 0, core, 4), s_stats, dq_same, 1),
    )
    for q, g, k, v, rows, stats, dq_ref, place in jobs:
        s, dp = add_rows(dot_last(k, q[...]) * FACTOR, rows), dot_last(v, g[...])
        e, *mine = partial_stats(s, dp)
        top, inverse, delta, scale = merge(stats[...], mine)
        dq, dk, dv = gradients(e * scale, dp, delta, q[...], g[...], k)
        dq_ref[:ROWS] = dq.astype(BF16)
        put_stats(dq_ref, (top, inverse, delta))
        kv_ref[place * ROWS : (place + 1) * ROWS] = dk.astype(BF16)
        kv_ref[(2 + place) * ROWS : (3 + place) * ROWS] = dv.astype(BF16)


def self_local_kernel(info, *refs):
    stats_ref, dq_ref, own_ref, kv_ref, mine, theirs = refs[-6:]
    local = own_ref[0]
    core = info[0] % 2
    first = info[0] < 2
    stats = take_stats(stats_ref, 2 * ROWS)
    stats = [jnp.concatenate([x[:, ROWS:], x[:, :ROWS]], axis=1) for x in stats]
    inverse = 1.0 / local[1:2]
    top = jnp.where(first, local[0:1], stats[0])
    delta = jnp.where(first, local[2:3] * inverse, stats[2])
    inverse = jnp.where(first, inverse, stats[1])
    (sx, sy, dpx, dpy), qs, gs, k0, k1 = local_self(core, *refs[:-6])
    px = jnp.exp(sx - top) * inverse
    py = jnp.exp(sy - top[:, ROWS:]) * inverse[:, ROWS:]
    dq0, dq1, dk0, dk1, dv0, dv1 = wide_gradients(px, py, dpx, dpy, delta, qs, gs, k0, k1)
    grads = (ordered(core, dq0, dq1), ordered(core, dk0, dk1), ordered(core, dv0, dv1))
    for index, pair in enumerate(grads):
        for out, place, grad in ((mine, 0, pair[0]), (theirs, 1, pair[1])):
            if index == 0 and place == 0:
                grad = grad + dq_ref[...].astype(F32)
            if index > 0:
                low = (2 * index - 2 + place) * ROWS
                grad = grad + kv_ref[low : low + ROWS].astype(F32)
            out[index * ROWS : (index + 1) * ROWS] = grad.astype(BF16)


def cross_local_kernel(info, *refs):
    own_stats, partner_stats, own_dq, partner_dq, kv_ref, mine, theirs = refs[-7:]
    own, partner = take_stats(own_stats, ROWS), take_stats(partner_stats, ROWS)
    top, inverse, delta = [jnp.concatenate([own[i], partner[i]], axis=1) for i in range(3)]
    s, dp, qs, gs, ks = local_cross(info[0] % 2, *refs[:-7])
    dq, dk, dv = gradients(jnp.exp(s - top) * inverse, dp, delta, qs, gs, ks)
    dq = dq + both(own_dq[...], partner_dq[...]).astype(F32)
    dk = dk + kv_ref[: 2 * ROWS].astype(F32)
    dv = dv + kv_ref[2 * ROWS :].astype(F32)
    for index, grad in enumerate((dq, dk, dv)):
        mine[index * ROWS : (index + 1) * ROWS] = grad[:ROWS].astype(BF16)
        theirs[index * ROWS : (index + 1) * ROWS] = grad[ROWS:].astype(BF16)


def self_final_kernel(info, mine, theirs, dq_theirs, *outs):
    def write(source, dq):
        outs[0][...] = dq.astype(BF16)
        outs[1][...] = source[ROWS : 2 * ROWS]
        outs[2][...] = source[2 * ROWS :]

    @pl.when(pl.program_id(0) == 0)
    def _():
        write(mine, mine[:ROWS])

    @pl.when(pl.program_id(0) == 1)
    def _():
        write(theirs, theirs[:ROWS].astype(F32) + dq_theirs[...].astype(F32))


def cross_final_kernel(info, mine, theirs, dq_out, pool_out):
    def write(source):
        dq_out[...] = source[:ROWS]
        pool_out[0] = source[ROWS : 2 * ROWS]
        pool_out[1] = source[2 * ROWS :]

    pl.when(pl.program_id(0) == 0)(lambda: write(mine))
    pl.when(pl.program_id(0) == 1)(lambda: write(theirs))


def assemble(kernel, name, info, inputs, pooled):
    half = lambda h, info: (info[0] + h) % 2
    rows_out = pl.BlockSpec((ROWS, WIDE), lambda h, info: (0, half(h, info)))
    pool_out = pl.BlockSpec((2, ROWS, WIDE), lambda h, info: (0, 0, half(h, info)))
    full = ((ROWS, 2 * WIDE), BF16)
    if pooled:
        out_specs, outs = [rows_out, pool_out], [full, ((2, ROWS, 2 * WIDE), BF16)]
    else:
        out_specs, outs = [rows_out] * 3, [full] * 3
    in_specs = [whole_spec(x.shape) for x in inputs]
    return call(kernel, name, info, in_specs, inputs, out_specs, outs, steps=2)


def body(
    queries, keys, values, grad_self, doc_ids, cross_queries, grad_cross, pool_kv, neighbour_ids
):
    loop = lax.axis_size("ctx")
    me = lax.axis_index("ctx").astype(jnp.int32)
    info = jnp.full((1,), me, jnp.int32)
    enc_dev = pool_kv.shape[1]
    width = queries.shape[1]
    pool = pool_kv.reshape(2, ROWS, width)
    flops_l, flops_x, flops_s = 0, 0, 0

    cols = WIDE // 2
    block = lambda rows: pl.BlockSpec((rows, cols), lambda h, info: (0, h))
    mine_spec = pl.BlockSpec((ROWS, cols), lambda h, info: (0, info[0] % 2 * 2 + h))
    their_spec = pl.BlockSpec((ROWS, cols), lambda h, info: (0, (1 - info[0] % 2) * 2 + h))
    their_pool = pl.BlockSpec((2, ROWS, cols), lambda h, info: (0, 0, (1 - info[0] % 2) * 2 + h))
    sizes = (8 * ROWS + EXTRA, 2 * ROWS + EXTRA, 2 * ROWS + EXTRA, 2 * ROWS, 2 * ROWS)
    packed, x_mine, x_other, s_mine, s_other = call(
        functools.partial(pack_kernel, enc_dev, loop),
        "pack",
        info,
        [whole_spec(neighbour_ids.shape[::-1])] + [mine_spec] * 4 + [their_spec] * 6 + [their_pool],
        (neighbour_ids.T, queries, grad_self, cross_queries, grad_cross)
        + (queries, grad_self, keys, values, cross_queries, grad_cross, pool),
        [block(rows) for rows in sizes],
        [((rows, WIDE), BF16) for rows in sizes],
        steps=2,
    )
    partner = send(packed, swap, False)
    x_same = send(x_mine, outward, True)
    x_cross = send(x_other, across, True)

    ids_of = lambda d: lax.dynamic_slice_in_dim(doc_ids, d * ROWS, ROWS, 0)
    span = jnp.arange(ROWS, dtype=jnp.int32)
    base = me // 2 * 2
    places = jnp.concatenate([span + base * ROWS, span + (base + 1) * ROWS])
    near0, near1, far0, far1 = [ids_of(base + j) for j in range(4)]
    near = jnp.concatenate([near0, near1])
    near_flip = jnp.concatenate([near1, near0])
    far_flip = jnp.concatenate([far1, far0])
    local_ok = (near[:, None] == near[None, :]) & (places[:, None] <= places[None, :])
    far_ok = (near_flip[:, None] == far_flip[None, :]) & (base + 2 < loop)
    local_bias = jnp.where(local_ok, 0.0, MASKED).astype(F32)
    far_bias = jnp.where(far_ok, 0.0, MASKED).astype(F32)

    bias_spec = whole_spec((2 * ROWS, 2 * ROWS))
    self_specs = [bias_spec] + [own_spec()] * 4 + [spec(ROWS, j) for j in range(4)]
    self_args = (local_bias, queries, grad_self, keys, values) + (partner,) * 4
    mine_w = whole_spec((EXTRA, WIDE), (2 * ROWS // EXTRA, 0))
    partner_w = whole_spec((EXTRA, WIDE), (8 * ROWS // EXTRA, 0))
    cross_specs = (
        [mine_w, partner_w, own_spec(), own_spec(), own_spec((2,))]
        + [spec(ROWS, j) for j in range(4, 8)]
    )
    cross_args = (x_mine, partner, cross_queries, grad_cross, pool) + (partner,) * 4
    stat = lambda rows: ((HALF, 8, rows), F32)

    x_own, x_partner = call(
        cross_stats_kernel, "cross_stats", info, cross_specs, cross_args,
        [stat_spec(ROWS)] * 2, [stat(ROWS)] * 2, flops=flops_l,
    )
    t_same = send(x_own, outward, True)
    t_cross = send(x_partner, inward, True)
    s_mine, s_other, x_own = lax.optimization_barrier((s_mine, s_other, x_own))
    s_same = send(s_mine, lambda d: d - 2, False)
    s_cross = send(s_other, lambda d: (d - 2) ^ 1, False)

    (s_own,) = call(
        self_stats_kernel, "self_stats", info, self_specs, self_args,
        [stat_spec(2 * ROWS)], [stat(2 * ROWS)], flops=flops_l,
    )
    t_self = send(s_own, lambda d: d - 2, False)

    kv_out = spec(4 * ROWS)
    kv_shape = ((4 * ROWS, WIDE), BF16)
    q_shape = ((ROWS, WIDE), BF16)
    tagged = spec(ROWS + STATS)
    tagged_shape = ((ROWS + STATS, WIDE), BF16)
    xd_same, xd_cross, x_kv = call(
        cross_remote_kernel, "cross_remote", info,
        [mine_w, mine_w, spec(ROWS, 0), spec(ROWS, 1), spec(ROWS, 0), spec(ROWS, 1)]
        + [own_spec((2,)), spec(ROWS, 6), spec(ROWS, 7), stat_spec(ROWS), stat_spec(ROWS)],
        (x_same, x_cross, x_same, x_same, x_cross, x_cross, pool, partner, partner, t_same, t_cross),
        [tagged, tagged, kv_out],
        [tagged_shape, tagged_shape, kv_shape], flops=flops_x,
    )
    xr_same = send(xd_same, inward, True)
    xr_cross = send(xd_cross, outward, True)

    far_bias, x_kv = lax.optimization_barrier((far_bias, x_kv))
    sd_same, sd_cross, s_kv = call(
        self_remote_kernel, "self_remote", info,
        [bias_spec, spec(ROWS, 0), spec(ROWS, 1), spec(ROWS, 0), spec(ROWS, 1)]
        + [own_spec(), own_spec(), spec(ROWS, 2), spec(ROWS, 3), stat_spec(2 * ROWS)],
        (far_bias, s_same, s_same, s_cross, s_cross, keys, values, partner, partner, t_self),
        [spec(ROWS + 2 * STATS), spec(ROWS), kv_out],
        [((ROWS + 2 * STATS, WIDE), BF16), q_shape, kv_shape], flops=flops_s,
    )
    sr_same = send(sd_same, lambda d: d + 2, False)
    sr_cross = send(sd_cross, lambda d: (d + 2) ^ 1, False)

    half_out = spec(3 * ROWS)
    half_shape = ((3 * ROWS, WIDE), BF16)
    x_keep, x_give = call(
        cross_local_kernel, "cross_local", info,
        cross_specs
        + [spec(STATS, ROWS // STATS), spec(STATS, ROWS // STATS), spec(ROWS), spec(ROWS)]
        + [spec(4 * ROWS)],
        cross_args + (xr_same, xr_cross, xr_same, xr_cross, x_kv),
        [half_out] * 2, [half_shape] * 2, flops=0,
    )
    x_take = send(x_give, swap, False)
    s_keep, s_give = call(
        self_local_kernel, "self_local", info,
        self_specs
        + [spec(2 * STATS, ROWS // (2 * STATS)), spec(ROWS), stat_spec(2 * ROWS), spec(4 * ROWS)],
        self_args + (sr_same, sr_same, s_own, s_kv),
        [half_out] * 2, [half_shape] * 2, flops=flops_s,
    )
    s_take = send(s_give, swap, False)
    grad_cq, grad_pool = assemble(cross_final_kernel, "cross_final", info, (x_keep, x_take), True)
    grad_q, grad_k, grad_v = assemble(
        self_final_kernel, "self_final", info, (s_keep, s_take, sr_cross), False
    )
    return grad_q, grad_k, grad_v, grad_cq, grad_pool.reshape(pool_kv.shape)


def solution(mesh):
    rows = P(("groups", "ctx"), None)
    pool = P(None, ("groups", "ctx"), None, None)
    return jax.shard_map(
        body,
        mesh=mesh,
        in_specs=(rows, rows, rows, rows, P("groups"), rows, rows, pool, rows),
        out_specs=(rows, rows, rows, rows, pool),
        check_vma=False,
    )
```

```python
import functools
import math

import jax
import jax.numpy as jnp
from jax import lax
from jax.experimental import pallas as pl
from jax.experimental.pallas import tpu as pltpu
from jax.sharding import PartitionSpec as P

HEADS = 8
HEAD_DIM = 128
HALF = HEADS // 2
WIDE = HALF * HEAD_DIM
STRETCH = 64
NBR_TOK = 128
ROWS = 256
EXTRA = 16
STATS = 32
LONG = 12 * 10**9
FACTOR = HEAD_DIM ** (-0.5)
MASKED = -1e30
BF16 = jnp.bfloat16
F32 = jnp.float32


def send(value, target_of, wrap):
    count = lax.axis_size("ctx")
    pairs = []
    for source in range(count):
        target = target_of(source)
        if wrap:
            pairs.append((source, target % count))
        elif 0 <= target < count:
            pairs.append((source, target))
    return lax.ppermute(value, "ctx", pairs)


def swap(d):
    return d ^ 1


def outward(d):
    return d - 2 if d % 2 == 0 else d + 2


def inward(d):
    return d + 2 if d % 2 == 0 else d - 2


def across(d):
    return d - 1 if d % 2 == 0 else d + 1


def spec(rows, row_block=0, cols=HEAD_DIM):
    return pl.BlockSpec((rows, cols), lambda h, info: (row_block, h))


def own_spec(lead=()):
    zeros = (0,) * len(lead)
    return pl.BlockSpec(
        lead + (ROWS, HEAD_DIM), lambda h, info: zeros + (0, info[0] % 2 * HALF + h)
    )


def other_spec(lead=()):
    zeros = (0,) * len(lead)
    return pl.BlockSpec(
        lead + (ROWS, HEAD_DIM), lambda h, info: zeros + (0, (1 - info[0] % 2) * HALF + h)
    )


def whole_spec(shape, index=None):
    index = (0,) * len(shape) if index is None else index
    return pl.BlockSpec(shape, lambda h, *info: index)


def stat_spec(rows):
    return pl.BlockSpec((1, 8, rows), lambda h, info: (h, 0, 0))


def call(kernel, name, info, in_specs, inputs, out_specs, outs, steps=HALF, flops=0, prefetch=None):
    prefetch = (info,) if prefetch is None else prefetch
    return pl.pallas_call(
        kernel,
        name=name,
        grid_spec=pltpu.PrefetchScalarGridSpec(
            num_scalar_prefetch=len(prefetch),
            grid=(steps,),
            in_specs=in_specs,
            out_specs=out_specs,
        ),
        out_shape=[jax.ShapeDtypeStruct(shape, dtype) for shape, dtype in outs],
        compiler_params=pltpu.CompilerParams(vmem_limit_bytes=63 << 20),
        cost_estimate=pl.CostEstimate(flops=flops, transcendentals=0, bytes_accessed=0),
    )(*prefetch, *inputs)


def dot_last(a, b):
    return lax.dot_general(a, b, (((1,), (1,)), ((), ())), preferred_element_type=F32)


def dot_first(a, b):
    return lax.dot_general(a, b, (((0,), (0,)), ((), ())), preferred_element_type=F32)


def dot(a, b):
    return jnp.dot(a, b, preferred_element_type=F32)


def both(a, b):
    return jnp.concatenate([a, b], axis=0)


def weight_rows(times):
    log_two = jnp.where(times > 1.5, math.log(2.0), 0.0)
    return jnp.where(times < 0.5, MASKED, log_two)


def slot_pair(ref, first, core, second=None):
    times = ref[...].astype(F32)[:, :ROWS]
    low = times[first : first + 2]
    if second is None:
        return weight_rows(low)
    return weight_rows(jnp.where(core == 0, low, times[second : second + 2]))


def add_rows(s, rows):
    parts = [
        s[e * NBR_TOK : (e + 1) * NBR_TOK] + rows[e : e + 1] for e in range(s.shape[0] // NBR_TOK)
    ]
    return jnp.concatenate(parts, axis=0)


def partial_stats(s, dp):
    peak = jnp.max(s, axis=0, keepdims=True)
    e = jnp.exp(s - peak)
    return e, peak, jnp.sum(e, axis=0, keepdims=True), jnp.sum(e * dp, axis=0, keepdims=True)


def stat_rows(a, b, c):
    return jnp.concatenate([a, b, c, jnp.zeros((5, a.shape[1]), F32)], axis=0)[None]


def merge(stats, mine):
    t_peak, t_total, t_moment = stats[0, 0:1], stats[0, 1:2], stats[0, 2:3]
    peak, total, moment = mine
    top = jnp.maximum(t_peak, peak)
    t_scale = jnp.exp(t_peak - top)
    scale = jnp.exp(peak - top)
    full = t_total * t_scale + total * scale
    inverse = jnp.where(full > 0, 1.0 / full, 0.0)
    delta = (t_moment * t_scale + moment * scale) * inverse
    return top, inverse, delta, scale * inverse


def gradients(p, dp, delta, q, g, k):
    pb = p.astype(BF16)
    ds = (p * (dp - delta)).astype(BF16)
    return dot_first(ds, k) * FACTOR, dot(ds, q) * FACTOR, dot(pb, g)


def pack_kernel(enc_dev, loop, info, ids_ref, *refs):
    qm, gm, xqm, xgm, q, g, k, v, xq, xg, pool, swap_ref, xm, xo, sm, so = refs
    shape = (EXTRA, xm.shape[1])
    row = lax.broadcasted_iota(jnp.int32, shape, 0)
    lane = lax.broadcasted_iota(jnp.int32, shape, 1) + pl.program_id(0) * shape[1]
    ids = ids_ref[...]
    owner = ids // enc_dev
    relative = owner - info[0] + 1
    relative = jnp.where(relative < 0, relative + loop, relative)
    relative = jnp.where(relative >= loop, relative - loop, relative)
    slots = relative * enc_dev + ids - owner * enc_dev
    times = jnp.zeros(shape, F32)
    for n in range(ids.shape[0]):
        for s in range(ids.shape[1]):
            hit = (row == slots[n : n + 1, s : s + 1]) & (lane // STRETCH == s)
            times = times + jnp.where(hit, 1.0, 0.0)
    times = times.astype(BF16)
    for index, ref in enumerate((q, g, k, v, xq, xg)):
        swap_ref[index * ROWS : (index + 1) * ROWS] = ref[...]
    swap_ref[6 * ROWS : 7 * ROWS] = pool[0]
    swap_ref[7 * ROWS : 8 * ROWS] = pool[1]
    swap_ref[8 * ROWS :] = times
    for out, first, second in ((xm, xqm, xgm), (xo, xq, xg), (sm, qm, gm), (so, q, g)):
        out[0:ROWS] = first[...]
        out[ROWS : 2 * ROWS] = second[...]
    xm[2 * ROWS :] = times
    xo[2 * ROWS :] = times


def ordered(core, a, b):
    return jnp.where(core == 0, a, b), jnp.where(core == 0, b, a)


def split3(x):
    high = x.astype(BF16)
    rest = x - high.astype(F32)
    middle = rest.astype(BF16)
    return [high, middle, (rest - middle.astype(F32)).astype(BF16)]


def put_stats(ref, stats):
    rows = []
    for low in range(0, stats[0].shape[1], HEAD_DIM):
        for x in stats:
            rows += split3(x[:, low : low + HEAD_DIM])
    rows.append(jnp.zeros((ref.shape[0] - ROWS - len(rows), HEAD_DIM), BF16))
    ref[ROWS:] = jnp.concatenate(rows, axis=0)


def take_stats(ref, lanes):
    x = ref[...].astype(F32)
    stats = []
    for index in range(3):
        parts = []
        for low in range(3 * index, 9 * (lanes // HEAD_DIM), 9):
            parts.append(x[low : low + 1] + x[low + 1 : low + 2] + x[low + 2 : low + 3])
        stats.append(jnp.concatenate(parts, axis=1))
    return stats


def wide_scores(keys_x, keys_y, values_x, values_y, qs, gs, bias):
    sx = dot_last(keys_x, qs) * FACTOR + bias[:ROWS]
    sy = dot_last(keys_y, qs[ROWS:]) * FACTOR + bias[ROWS:, ROWS:]
    return sx, sy, dot_last(values_x, gs), dot_last(values_y, gs[ROWS:])


def wide_stats(sx, sy, dpx, dpy):
    peak = jnp.max(sx, axis=0, keepdims=True)
    peak_y = jnp.maximum(peak[:, ROWS:], jnp.max(sy, axis=0, keepdims=True))
    peak = jnp.concatenate([peak[:, :ROWS], peak_y], axis=1)
    ex, ey = jnp.exp(sx - peak), jnp.exp(sy - peak_y)
    widen = lambda a, b: jnp.concatenate([a[:, :ROWS], a[:, ROWS:] + b], axis=1)
    add = lambda a: jnp.sum(a, axis=0, keepdims=True)
    return ex, ey, peak, widen(add(ex), add(ey)), widen(add(ex * dpx), add(ey * dpy))


def wide_gradients(px, py, dpx, dpy, delta, qs, gs, kx, ky):
    pbx, pby = px.astype(BF16), py.astype(BF16)
    dsx = (px * (dpx - delta)).astype(BF16)
    dsy = (py * (dpy - delta[:, ROWS:])).astype(BF16)
    dq_z = dot_first(dsx[:, :ROWS], kx) * FACTOR
    dq_y = dot_first(both(dsx[:, ROWS:], dsy), both(kx, ky)) * FACTOR
    dkx, dky = dot(dsx, qs) * FACTOR, dot(dsy, qs[ROWS:]) * FACTOR
    return dq_z, dq_y, dkx, dky, dot(pbx, gs), dot(pby, gs[ROWS:])


def local_self(core, bias, q, g, k, v, pq, pg, pk, pv):
    q0, q1 = ordered(core, q[...], pq[...])
    g0, g1 = ordered(core, g[...], pg[...])
    k0, k1 = ordered(core, k[...], pk[...])
    v0, v1 = ordered(core, v[...], pv[...])
    qs, gs = both(q0, q1), both(g0, g1)
    return wide_scores(k0, k1, v0, v1, qs, gs, bias[...]), qs, gs, k0, k1


def local_cross(core, w, pw, q, g, pool, pq, pg, pk, pv):
    qs, gs = both(q[...], pq[...]), both(g[...], pg[...])
    ks, vs = both(pool[0], pk[...]), both(pool[1], pv[...])
    own = both(slot_pair(w, 2, core), slot_pair(w, 4, core, 0))
    partner = both(slot_pair(pw, 0, core, 4), slot_pair(pw, 2, core))
    s = add_rows(dot_last(ks, qs) * FACTOR, jnp.concatenate([own, partner], axis=1))
    return s, dot_last(vs, gs), qs, gs, ks


def self_stats_kernel(info, *refs):
    scores = local_self(info[0] % 2, *refs[:-1])[0]
    refs[-1][...] = stat_rows(*wide_stats(*scores)[2:])


def cross_stats_kernel(info, *refs):
    s, dp, _, _, _ = local_cross(info[0] % 2, *refs[:-2])
    stats = stat_rows(*partial_stats(s, dp)[1:])
    refs[-2][...] = stats[:, :, :ROWS]
    refs[-1][...] = stats[:, :, ROWS:]


def self_remote_kernel(
    info, bias, sq, sg, cq, cg, k, v, pk, pv, stats, dq_same, dq_cross, kv_ref, out_stats
):
    core = info[0] % 2
    q0, q1 = ordered(core, sq[...], cq[...])
    g0, g1 = ordered(core, sg[...], cg[...])
    k0, k1 = ordered(core, k[...], pk[...])
    v0, v1 = ordered(core, v[...], pv[...])
    qs, gs = both(q1, q0), both(g1, g0)
    sx, sy, dpx, dpy = wide_scores(k1, k0, v1, v0, qs, gs, bias[...])
    ex, ey, *mine = wide_stats(sx, sy, dpx, dpy)
    known = stats[...]
    known = jnp.concatenate([known[:, :, ROWS:], known[:, :, :ROWS]], axis=2)
    top, inverse, delta, scale = merge(known, mine)
    px, py = ex * scale, ey * scale[:, ROWS:]
    dq1, dq0, dk1, dk0, dv1, dv0 = wide_gradients(px, py, dpx, dpy, delta, qs, gs, k1, k0)
    same, cross = ordered(core, dq0, dq1)
    dq_same[...] = same.astype(BF16)
    dq_cross[...] = cross.astype(BF16)
    for index, grad in enumerate(ordered(core, dk0, dk1) + ordered(core, dv0, dv1)):
        kv_ref[index * ROWS : (index + 1) * ROWS] = grad.astype(BF16)
    out_stats[...] = stat_rows(top, inverse, delta)


def cross_remote_kernel(
    info, sw, cw, sq, sg, cq, cg, pool, pk, pv, s_stats, c_stats, *outs
):
    dq_same, dq_cross, kv_ref = outs
    core = info[0] % 2
    jobs = (
        (cq, cg, pool[0], pool[1], slot_pair(cw, 4, core, 0), c_stats, dq_cross, 0),
        (sq, sg, pk[...], pv[...], slot_pair(sw, 0, core, 4), s_stats, dq_same, 1),
    )
    for q, g, k, v, rows, stats, dq_ref, place in jobs:
        s, dp = add_rows(dot_last(k, q[...]) * FACTOR, rows), dot_last(v, g[...])
        e, *mine = partial_stats(s, dp)
        top, inverse, delta, scale = merge(stats[...], mine)
        dq, dk, dv = gradients(e * scale, dp, delta, q[...], g[...], k)
        dq_ref[:ROWS] = dq.astype(BF16)
        put_stats(dq_ref, (top, inverse, delta))
        kv_ref[place * ROWS : (place + 1) * ROWS] = dk.astype(BF16)
        kv_ref[(2 + place) * ROWS : (3 + place) * ROWS] = dv.astype(BF16)


def self_local_kernel(info, *refs):
    stats_ref, own_ref, kv_ref, mine, theirs = refs[-5:]
    local = own_ref[0]
    core = info[0] % 2
    first = info[0] < 2
    stats = stats_ref[0]
    stats = jnp.concatenate([stats[:, ROWS:], stats[:, :ROWS]], axis=1)
    inverse = 1.0 / local[1:2]
    top = jnp.where(first, local[0:1], stats[0:1])
    delta = jnp.where(first, local[2:3] * inverse, stats[2:3])
    inverse = jnp.where(first, inverse, stats[1:2])
    (sx, sy, dpx, dpy), qs, gs, k0, k1 = local_self(core, *refs[:-5])
    px = jnp.exp(sx - top) * inverse
    py = jnp.exp(sy - top[:, ROWS:]) * inverse[:, ROWS:]
    dq0, dq1, dk0, dk1, dv0, dv1 = wide_gradients(px, py, dpx, dpy, delta, qs, gs, k0, k1)
    grads = (ordered(core, dq0, dq1), ordered(core, dk0, dk1), ordered(core, dv0, dv1))
    for index, pair in enumerate(grads):
        for out, place, grad in ((mine, 0, pair[0]), (theirs, 1, pair[1])):
            if index > 0:
                low = (2 * index - 2 + place) * ROWS
                grad = grad + kv_ref[low : low + ROWS].astype(F32)
            out[index * ROWS : (index + 1) * ROWS] = grad.astype(BF16)


def cross_local_kernel(info, *refs):
    own_stats, partner_stats, own_dq, partner_dq, kv_ref, mine, theirs = refs[-7:]
    own, partner = take_stats(own_stats, ROWS), take_stats(partner_stats, ROWS)
    top, inverse, delta = [jnp.concatenate([own[i], partner[i]], axis=1) for i in range(3)]
    s, dp, qs, gs, ks = local_cross(info[0] % 2, *refs[:-7])
    dq, dk, dv = gradients(jnp.exp(s - top) * inverse, dp, delta, qs, gs, ks)
    dq = dq + both(own_dq[...], partner_dq[...]).astype(F32)
    dk = dk + kv_ref[: 2 * ROWS].astype(F32)
    dv = dv + kv_ref[2 * ROWS :].astype(F32)
    for index, grad in enumerate((dq, dk, dv)):
        mine[index * ROWS : (index + 1) * ROWS] = grad[:ROWS].astype(BF16)
        theirs[index * ROWS : (index + 1) * ROWS] = grad[ROWS:].astype(BF16)


def self_final_kernel(info, mine, theirs, dq_mine, dq_theirs, *outs):
    def write(source, extra):
        dq = source[:ROWS].astype(F32) + extra[...].astype(F32)
        outs[0][...] = dq.astype(BF16)
        outs[1][...] = source[ROWS : 2 * ROWS]
        outs[2][...] = source[2 * ROWS :]

    pl.when(pl.program_id(0) == 0)(lambda: write(mine, dq_mine))
    pl.when(pl.program_id(0) == 1)(lambda: write(theirs, dq_theirs))


def cross_final_kernel(info, mine, theirs, dq_out, pool_out):
    def write(source):
        dq_out[...] = source[:ROWS]
        pool_out[0] = source[ROWS : 2 * ROWS]
        pool_out[1] = source[2 * ROWS :]

    pl.when(pl.program_id(0) == 0)(lambda: write(mine))
    pl.when(pl.program_id(0) == 1)(lambda: write(theirs))


def assemble(kernel, name, info, inputs, pooled):
    half = lambda h, info: (info[0] + h) % 2
    rows_out = pl.BlockSpec((ROWS, WIDE), lambda h, info: (0, half(h, info)))
    pool_out = pl.BlockSpec((2, ROWS, WIDE), lambda h, info: (0, 0, half(h, info)))
    full = ((ROWS, 2 * WIDE), BF16)
    if pooled:
        out_specs, outs = [rows_out, pool_out], [full, ((2, ROWS, 2 * WIDE), BF16)]
    else:
        out_specs, outs = [rows_out] * 3, [full] * 3
    in_specs = [whole_spec(x.shape) for x in inputs]
    return call(kernel, name, info, in_specs, inputs, out_specs, outs, steps=2)


def body(
    queries, keys, values, grad_self, doc_ids, cross_queries, grad_cross, pool_kv, neighbour_ids
):
    loop = lax.axis_size("ctx")
    me = lax.axis_index("ctx").astype(jnp.int32)
    info = jnp.full((1,), me, jnp.int32)
    enc_dev = pool_kv.shape[1]
    width = queries.shape[1]
    pool = pool_kv.reshape(2, ROWS, width)

    cols = WIDE // 2
    block = lambda rows: pl.BlockSpec((rows, cols), lambda h, info: (0, h))
    mine_spec = pl.BlockSpec((ROWS, cols), lambda h, info: (0, info[0] % 2 * 2 + h))
    their_spec = pl.BlockSpec((ROWS, cols), lambda h, info: (0, (1 - info[0] % 2) * 2 + h))
    their_pool = pl.BlockSpec((2, ROWS, cols), lambda h, info: (0, 0, (1 - info[0] % 2) * 2 + h))
    sizes = (8 * ROWS + EXTRA, 2 * ROWS + EXTRA, 2 * ROWS + EXTRA, 2 * ROWS, 2 * ROWS)
    packed, x_mine, x_other, s_mine, s_other = call(
        functools.partial(pack_kernel, enc_dev, loop),
        "pack",
        info,
        [whole_spec(neighbour_ids.shape[::-1])] + [mine_spec] * 4 + [their_spec] * 6 + [their_pool],
        (neighbour_ids.T, queries, grad_self, cross_queries, grad_cross)
        + (queries, grad_self, keys, values, cross_queries, grad_cross, pool),
        [block(rows) for rows in sizes],
        [((rows, WIDE), BF16) for rows in sizes],
        steps=2,
    )
    partner = send(packed, swap, False)
    x_same = send(x_mine, outward, True)
    x_cross = send(x_other, across, True)

    ids_of = lambda d: lax.dynamic_slice_in_dim(doc_ids, d * ROWS, ROWS, 0)
    span = jnp.arange(ROWS, dtype=jnp.int32)
    base = me // 2 * 2
    places = jnp.concatenate([span + base * ROWS, span + (base + 1) * ROWS])
    near0, near1, far0, far1 = [ids_of(base + j) for j in range(4)]
    near = jnp.concatenate([near0, near1])
    near_flip = jnp.concatenate([near1, near0])
    far_flip = jnp.concatenate([far1, far0])
    local_ok = (near[:, None] == near[None, :]) & (places[:, None] <= places[None, :])
    far_ok = (near_flip[:, None] == far_flip[None, :]) & (base + 2 < loop)
    local_bias = jnp.where(local_ok, 0.0, MASKED).astype(F32)
    far_bias = jnp.where(far_ok, 0.0, MASKED).astype(F32)

    bias_spec = whole_spec((2 * ROWS, 2 * ROWS))
    self_specs = [bias_spec] + [own_spec()] * 4 + [spec(ROWS, j) for j in range(4)]
    self_args = (local_bias, queries, grad_self, keys, values) + (partner,) * 4
    mine_w = whole_spec((EXTRA, WIDE), (2 * ROWS // EXTRA, 0))
    partner_w = whole_spec((EXTRA, WIDE), (8 * ROWS // EXTRA, 0))
    cross_specs = (
        [mine_w, partner_w, own_spec(), own_spec(), own_spec((2,))]
        + [spec(ROWS, j) for j in range(4, 8)]
    )
    cross_args = (x_mine, partner, cross_queries, grad_cross, pool) + (partner,) * 4
    stat = lambda rows: ((HALF, 8, rows), F32)

    x_own, x_partner = call(
        cross_stats_kernel, "cross_stats", info, cross_specs, cross_args,
        [stat_spec(ROWS)] * 2, [stat(ROWS)] * 2, flops=0,
    )
    t_same = send(x_own, outward, True)
    t_cross = send(x_partner, inward, True)
    local_bias, x_own = lax.optimization_barrier((local_bias, x_own))
    self_args = (local_bias,) + self_args[1:]
    (s_own,) = call(
        self_stats_kernel, "self_stats", info, self_specs, self_args,
        [stat_spec(2 * ROWS)], [stat(2 * ROWS)], flops=0,
    )
    t_self = send(s_own, lambda d: d - 2, False)
    s_mine, s_other, x_same, x_cross, s_own = lax.optimization_barrier(
        (s_mine, s_other, x_same, x_cross, s_own)
    )
    s_same = send(s_mine, lambda d: d - 2, False)
    s_cross = send(s_other, lambda d: (d - 2) ^ 1, False)


    kv_out = spec(4 * ROWS)
    kv_shape = ((4 * ROWS, WIDE), BF16)
    q_shape = ((ROWS, WIDE), BF16)
    tagged = spec(ROWS + STATS)
    tagged_shape = ((ROWS + STATS, WIDE), BF16)
    xd_same, xd_cross, x_kv = call(
        cross_remote_kernel, "cross_remote", info,
        [mine_w, mine_w, spec(ROWS, 0), spec(ROWS, 1), spec(ROWS, 0), spec(ROWS, 1)]
        + [own_spec((2,)), spec(ROWS, 6), spec(ROWS, 7), stat_spec(ROWS), stat_spec(ROWS)],
        (x_same, x_cross, x_same, x_same, x_cross, x_cross, pool, partner, partner, t_same, t_cross),
        [tagged, tagged, kv_out],
        [tagged_shape, tagged_shape, kv_shape], flops=0,
    )
    xr_same = send(xd_same, inward, True)
    xr_cross = send(xd_cross, outward, True)

    far_bias, x_kv = lax.optimization_barrier((far_bias, x_kv))
    sd_same, sd_cross, s_kv, s_fin = call(
        self_remote_kernel, "self_remote", info,
        [bias_spec, spec(ROWS, 0), spec(ROWS, 1), spec(ROWS, 0), spec(ROWS, 1)]
        + [own_spec(), own_spec(), spec(ROWS, 2), spec(ROWS, 3), stat_spec(2 * ROWS)],
        (far_bias, s_same, s_same, s_cross, s_cross, keys, values, partner, partner, t_self),
        [spec(ROWS), spec(ROWS), kv_out, stat_spec(2 * ROWS)],
        [q_shape, q_shape, kv_shape, stat(2 * ROWS)], flops=LONG,
    )
    f_self = send(s_fin, lambda d: d + 2, False)
    sr_same = send(sd_same, lambda d: d + 2, False)
    sr_cross = send(sd_cross, lambda d: (d + 2) ^ 1, False)

    half_out = spec(3 * ROWS)
    half_shape = ((3 * ROWS, WIDE), BF16)
    x_keep, x_give = call(
        cross_local_kernel, "cross_local", info,
        cross_specs
        + [spec(STATS, ROWS // STATS), spec(STATS, ROWS // STATS), spec(ROWS), spec(ROWS)]
        + [spec(4 * ROWS)],
        cross_args + (xr_same, xr_cross, xr_same, xr_cross, x_kv),
        [half_out] * 2, [half_shape] * 2, flops=LONG,
    )
    x_take = send(x_give, swap, False)
    s_kv, x_keep = lax.optimization_barrier((s_kv, x_keep))
    s_keep, s_give = call(
        self_local_kernel, "self_local", info,
        self_specs
        + [stat_spec(2 * ROWS), stat_spec(2 * ROWS), spec(4 * ROWS)],
        self_args + (f_self, s_own, s_kv),
        [half_out] * 2, [half_shape] * 2, flops=0,
    )
    s_give, sr_same, sr_cross = lax.optimization_barrier((s_give, sr_same, sr_cross))
    s_take = send(s_give, swap, False)
    grad_cq, grad_pool = assemble(cross_final_kernel, "cross_final", info, (x_keep, x_take), True)
    grad_q, grad_k, grad_v = assemble(
        self_final_kernel, "self_final", info, (s_keep, s_take, sr_same, sr_cross), False
    )
    return grad_q, grad_k, grad_v, grad_cq, grad_pool.reshape(pool_kv.shape)


def solution(mesh):
    rows = P(("groups", "ctx"), None)
    pool = P(None, ("groups", "ctx"), None, None)
    return jax.shard_map(
        body,
        mesh=mesh,
        in_specs=(rows, rows, rows, rows, P("groups"), rows, rows, pool, rows),
        out_specs=(rows, rows, rows, rows, pool),
        check_vma=False,
    )
```

```python
import functools
import math

import jax
import jax.numpy as jnp
from jax import lax
from jax.experimental import pallas as pl
from jax.experimental.pallas import tpu as pltpu
from jax.sharding import PartitionSpec as P

HEADS = 8
HEAD_DIM = 128
HALF = HEADS // 2
WIDE = HALF * HEAD_DIM
STRETCH = 64
NBR_TOK = 128
ROWS = 256
EXTRA = 16
STATS = 32
LONG = 12 * 10**9
FACTOR = HEAD_DIM ** (-0.5)
MASKED = -1e30
BF16 = jnp.bfloat16
F32 = jnp.float32


def send(value, target_of, wrap):
    count = lax.axis_size("ctx")
    pairs = []
    for source in range(count):
        target = target_of(source)
        if wrap:
            pairs.append((source, target % count))
        elif 0 <= target < count:
            pairs.append((source, target))
    return lax.ppermute(value, "ctx", pairs)


def swap(d):
    return d ^ 1


def outward(d):
    return d - 2 if d % 2 == 0 else d + 2


def inward(d):
    return d + 2 if d % 2 == 0 else d - 2


def across(d):
    return d - 1 if d % 2 == 0 else d + 1


def spec(rows, row_block=0, cols=HEAD_DIM):
    return pl.BlockSpec((rows, cols), lambda h, info: (row_block, h))


def own_spec(lead=()):
    zeros = (0,) * len(lead)
    return pl.BlockSpec(
        lead + (ROWS, HEAD_DIM), lambda h, info: zeros + (0, info[0] % 2 * HALF + h)
    )


def other_spec(lead=()):
    zeros = (0,) * len(lead)
    return pl.BlockSpec(
        lead + (ROWS, HEAD_DIM), lambda h, info: zeros + (0, (1 - info[0] % 2) * HALF + h)
    )


def whole_spec(shape, index=None):
    index = (0,) * len(shape) if index is None else index
    return pl.BlockSpec(shape, lambda h, *info: index)


def stat_spec(rows):
    return pl.BlockSpec((1, 8, rows), lambda h, info: (h, 0, 0))


def call(kernel, name, info, in_specs, inputs, out_specs, outs, steps=HALF, flops=0, prefetch=None):
    prefetch = (info,) if prefetch is None else prefetch
    return pl.pallas_call(
        kernel,
        name=name,
        grid_spec=pltpu.PrefetchScalarGridSpec(
            num_scalar_prefetch=len(prefetch),
            grid=(steps,),
            in_specs=in_specs,
            out_specs=out_specs,
        ),
        out_shape=[jax.ShapeDtypeStruct(shape, dtype) for shape, dtype in outs],
        compiler_params=pltpu.CompilerParams(vmem_limit_bytes=63 << 20),
        cost_estimate=pl.CostEstimate(flops=flops, transcendentals=0, bytes_accessed=0),
    )(*prefetch, *inputs)


def dot_last(a, b):
    return lax.dot_general(a, b, (((1,), (1,)), ((), ())), preferred_element_type=F32)


def dot_first(a, b):
    return lax.dot_general(a, b, (((0,), (0,)), ((), ())), preferred_element_type=F32)


def dot(a, b):
    return jnp.dot(a, b, preferred_element_type=F32)


def both(a, b):
    return jnp.concatenate([a, b], axis=0)


def weight_rows(times):
    log_two = jnp.where(times > 1.5, math.log(2.0), 0.0)
    return jnp.where(times < 0.5, MASKED, log_two)


def slot_pair(ref, first, core, second=None):
    times = ref[...].astype(F32)[:, :ROWS]
    low = times[first : first + 2]
    if second is None:
        return weight_rows(low)
    return weight_rows(jnp.where(core == 0, low, times[second : second + 2]))


def add_rows(s, rows):
    parts = [
        s[e * NBR_TOK : (e + 1) * NBR_TOK] + rows[e : e + 1] for e in range(s.shape[0] // NBR_TOK)
    ]
    return jnp.concatenate(parts, axis=0)


def partial_stats(s, dp):
    peak = jnp.max(s, axis=0, keepdims=True)
    e = jnp.exp(s - peak)
    return e, peak, jnp.sum(e, axis=0, keepdims=True), jnp.sum(e * dp, axis=0, keepdims=True)


def stat_rows(a, b, c):
    return jnp.concatenate([a, b, c, jnp.zeros((5, a.shape[1]), F32)], axis=0)[None]


def merge(stats, mine):
    t_peak, t_total, t_moment = stats[0, 0:1], stats[0, 1:2], stats[0, 2:3]
    peak, total, moment = mine
    top = jnp.maximum(t_peak, peak)
    t_scale = jnp.exp(t_peak - top)
    scale = jnp.exp(peak - top)
    full = t_total * t_scale + total * scale
    inverse = jnp.where(full > 0, 1.0 / full, 0.0)
    delta = (t_moment * t_scale + moment * scale) * inverse
    return top, inverse, delta, scale * inverse


def gradients(p, dp, delta, q, g, k):
    pb = p.astype(BF16)
    ds = (p * (dp - delta)).astype(BF16)
    return dot_first(ds, k) * FACTOR, dot(ds, q) * FACTOR, dot(pb, g)


def pack_kernel(enc_dev, loop, info, ids_ref, *refs):
    qm, gm, xqm, xgm, q, g, k, v, xq, xg, pool, swap_ref, xm, xo, sm, so = refs
    shape = (EXTRA, xm.shape[1])
    row = lax.broadcasted_iota(jnp.int32, shape, 0)
    lane = lax.broadcasted_iota(jnp.int32, shape, 1) + pl.program_id(0) * shape[1]
    ids = ids_ref[...]
    owner = ids // enc_dev
    relative = owner - info[0] + 1
    relative = jnp.where(relative < 0, relative + loop, relative)
    relative = jnp.where(relative >= loop, relative - loop, relative)
    slots = relative * enc_dev + ids - owner * enc_dev
    times = jnp.zeros(shape, F32)
    for n in range(ids.shape[0]):
        for s in range(ids.shape[1]):
            hit = (row == slots[n : n + 1, s : s + 1]) & (lane // STRETCH == s)
            times = times + jnp.where(hit, 1.0, 0.0)
    times = times.astype(BF16)
    for index, ref in enumerate((q, g, k, v, xq, xg)):
        swap_ref[index * ROWS : (index + 1) * ROWS] = ref[...]
    swap_ref[6 * ROWS : 7 * ROWS] = pool[0]
    swap_ref[7 * ROWS : 8 * ROWS] = pool[1]
    swap_ref[8 * ROWS :] = times
    for out, first, second in ((xm, xqm, xgm), (xo, xq, xg), (sm, qm, gm), (so, q, g)):
        out[0:ROWS] = first[...]
        out[ROWS : 2 * ROWS] = second[...]
    xm[2 * ROWS :] = times
    xo[2 * ROWS :] = times


def ordered(core, a, b):
    return jnp.where(core == 0, a, b), jnp.where(core == 0, b, a)


def split3(x):
    high = x.astype(BF16)
    rest = x - high.astype(F32)
    middle = rest.astype(BF16)
    return [high, middle, (rest - middle.astype(F32)).astype(BF16)]


def put_stats(ref, stats):
    rows = []
    for low in range(0, stats[0].shape[1], HEAD_DIM):
        for x in stats:
            rows += split3(x[:, low : low + HEAD_DIM])
    rows.append(jnp.zeros((ref.shape[0] - ROWS - len(rows), HEAD_DIM), BF16))
    ref[ROWS:] = jnp.concatenate(rows, axis=0)


def take_stats(ref, lanes):
    x = ref[...].astype(F32)
    stats = []
    for index in range(3):
        parts = []
        for low in range(3 * index, 9 * (lanes // HEAD_DIM), 9):
            parts.append(x[low : low + 1] + x[low + 1 : low + 2] + x[low + 2 : low + 3])
        stats.append(jnp.concatenate(parts, axis=1))
    return stats


def wide_scores(keys_x, keys_y, values_x, values_y, qs, gs, bias):
    sx = dot_last(keys_x, qs) * FACTOR + bias[:ROWS]
    sy = dot_last(keys_y, qs[ROWS:]) * FACTOR + bias[ROWS:, ROWS:]
    return sx, sy, dot_last(values_x, gs), dot_last(values_y, gs[ROWS:])


def wide_stats(sx, sy, dpx, dpy):
    peak = jnp.max(sx, axis=0, keepdims=True)
    peak_y = jnp.maximum(peak[:, ROWS:], jnp.max(sy, axis=0, keepdims=True))
    peak = jnp.concatenate([peak[:, :ROWS], peak_y], axis=1)
    ex, ey = jnp.exp(sx - peak), jnp.exp(sy - peak_y)
    widen = lambda a, b: jnp.concatenate([a[:, :ROWS], a[:, ROWS:] + b], axis=1)
    add = lambda a: jnp.sum(a, axis=0, keepdims=True)
    return ex, ey, peak, widen(add(ex), add(ey)), widen(add(ex * dpx), add(ey * dpy))


def wide_gradients(px, py, dpx, dpy, delta, qs, gs, kx, ky):
    pbx, pby = px.astype(BF16), py.astype(BF16)
    dsx = (px * (dpx - delta)).astype(BF16)
    dsy = (py * (dpy - delta[:, ROWS:])).astype(BF16)
    dq_z = dot_first(dsx[:, :ROWS], kx) * FACTOR
    dq_y = dot_first(both(dsx[:, ROWS:], dsy), both(kx, ky)) * FACTOR
    dkx, dky = dot(dsx, qs) * FACTOR, dot(dsy, qs[ROWS:]) * FACTOR
    return dq_z, dq_y, dkx, dky, dot(pbx, gs), dot(pby, gs[ROWS:])


def local_self(core, bias, q, g, k, v, pq, pg, pk, pv):
    q0, q1 = ordered(core, q[...], pq[...])
    g0, g1 = ordered(core, g[...], pg[...])
    k0, k1 = ordered(core, k[...], pk[...])
    v0, v1 = ordered(core, v[...], pv[...])
    qs, gs = both(q0, q1), both(g0, g1)
    return wide_scores(k0, k1, v0, v1, qs, gs, bias[...]), qs, gs, k0, k1


def local_cross(core, w, pw, q, g, pool, pq, pg, pk, pv):
    qs, gs = both(q[...], pq[...]), both(g[...], pg[...])
    ks, vs = both(pool[0], pk[...]), both(pool[1], pv[...])
    own = both(slot_pair(w, 2, core), slot_pair(w, 4, core, 0))
    partner = both(slot_pair(pw, 0, core, 4), slot_pair(pw, 2, core))
    s = add_rows(dot_last(ks, qs) * FACTOR, jnp.concatenate([own, partner], axis=1))
    return s, dot_last(vs, gs), qs, gs, ks


def self_stats_kernel(info, *refs):
    scores = local_self(info[0] % 2, *refs[:-1])[0]
    refs[-1][...] = stat_rows(*wide_stats(*scores)[2:])


def cross_stats_kernel(info, *refs):
    s, dp, _, _, _ = local_cross(info[0] % 2, *refs[:-2])
    stats = stat_rows(*partial_stats(s, dp)[1:])
    refs[-2][...] = stats[:, :, :ROWS]
    refs[-1][...] = stats[:, :, ROWS:]


def self_remote_kernel(
    info, bias, sq, sg, cq, cg, k, v, pk, pv, stats, dq_same, dq_cross, kv_ref, out_stats
):
    core = info[0] % 2
    q0, q1 = ordered(core, sq[...], cq[...])
    g0, g1 = ordered(core, sg[...], cg[...])
    k0, k1 = ordered(core, k[...], pk[...])
    v0, v1 = ordered(core, v[...], pv[...])
    qs, gs = both(q1, q0), both(g1, g0)
    sx, sy, dpx, dpy = wide_scores(k1, k0, v1, v0, qs, gs, bias[...])
    ex, ey, *mine = wide_stats(sx, sy, dpx, dpy)
    known = stats[...]
    known = jnp.concatenate([known[:, :, ROWS:], known[:, :, :ROWS]], axis=2)
    top, inverse, delta, scale = merge(known, mine)
    px, py = ex * scale, ey * scale[:, ROWS:]
    dq1, dq0, dk1, dk0, dv1, dv0 = wide_gradients(px, py, dpx, dpy, delta, qs, gs, k1, k0)
    same, cross = ordered(core, dq0, dq1)
    dq_same[...] = same.astype(BF16)
    dq_cross[...] = cross.astype(BF16)
    for index, grad in enumerate(ordered(core, dk0, dk1) + ordered(core, dv0, dv1)):
        kv_ref[index * ROWS : (index + 1) * ROWS] = grad.astype(BF16)
    out_stats[...] = stat_rows(top, inverse, delta)


def cross_remote_kernel(
    info, sw, cw, sq, sg, cq, cg, pool, pk, pv, s_stats, c_stats, *outs
):
    dq_same, dq_cross, kv_ref = outs
    core = info[0] % 2
    jobs = (
        (cq, cg, pool[0], pool[1], slot_pair(cw, 4, core, 0), c_stats, dq_cross, 0),
        (sq, sg, pk[...], pv[...], slot_pair(sw, 0, core, 4), s_stats, dq_same, 1),
    )
    for q, g, k, v, rows, stats, dq_ref, place in jobs:
        s, dp = add_rows(dot_last(k, q[...]) * FACTOR, rows), dot_last(v, g[...])
        e, *mine = partial_stats(s, dp)
        top, inverse, delta, scale = merge(stats[...], mine)
        dq, dk, dv = gradients(e * scale, dp, delta, q[...], g[...], k)
        dq_ref[:ROWS] = dq.astype(BF16)
        put_stats(dq_ref, (top, inverse, delta))
        kv_ref[place * ROWS : (place + 1) * ROWS] = dk.astype(BF16)
        kv_ref[(2 + place) * ROWS : (3 + place) * ROWS] = dv.astype(BF16)


def self_local_kernel(info, *refs):
    stats_ref, own_ref, kv_ref, mine, theirs = refs[-5:]
    local = own_ref[0]
    core = info[0] % 2
    first = info[0] < 2
    stats = stats_ref[0]
    stats = jnp.concatenate([stats[:, ROWS:], stats[:, :ROWS]], axis=1)
    inverse = 1.0 / local[1:2]
    top = jnp.where(first, local[0:1], stats[0:1])
    delta = jnp.where(first, local[2:3] * inverse, stats[2:3])
    inverse = jnp.where(first, inverse, stats[1:2])
    (sx, sy, dpx, dpy), qs, gs, k0, k1 = local_self(core, *refs[:-5])
    px = jnp.exp(sx - top) * inverse
    py = jnp.exp(sy - top[:, ROWS:]) * inverse[:, ROWS:]
    dq0, dq1, dk0, dk1, dv0, dv1 = wide_gradients(px, py, dpx, dpy, delta, qs, gs, k0, k1)
    grads = (ordered(core, dq0, dq1), ordered(core, dk0, dk1), ordered(core, dv0, dv1))
    for index, pair in enumerate(grads):
        for out, place, grad in ((mine, 0, pair[0]), (theirs, 1, pair[1])):
            if index > 0:
                low = (2 * index - 2 + place) * ROWS
                grad = grad + kv_ref[low : low + ROWS].astype(F32)
            out[index * ROWS : (index + 1) * ROWS] = grad.astype(BF16)


def cross_local_kernel(info, *refs):
    own_stats, partner_stats, own_dq, partner_dq, kv_ref, mine, theirs = refs[-7:]
    own, partner = take_stats(own_stats, ROWS), take_stats(partner_stats, ROWS)
    top, inverse, delta = [jnp.concatenate([own[i], partner[i]], axis=1) for i in range(3)]
    s, dp, qs, gs, ks = local_cross(info[0] % 2, *refs[:-7])
    dq, dk, dv = gradients(jnp.exp(s - top) * inverse, dp, delta, qs, gs, ks)
    dq = dq + both(own_dq[...], partner_dq[...]).astype(F32)
    dk = dk + kv_ref[: 2 * ROWS].astype(F32)
    dv = dv + kv_ref[2 * ROWS :].astype(F32)
    for index, grad in enumerate((dq, dk, dv)):
        mine[index * ROWS : (index + 1) * ROWS] = grad[:ROWS].astype(BF16)
        theirs[index * ROWS : (index + 1) * ROWS] = grad[ROWS:].astype(BF16)


def self_final_kernel(info, mine, theirs, dq_mine, dq_theirs, *outs):
    def write(source, extra):
        dq = source[:ROWS].astype(F32) + extra[...].astype(F32)
        outs[0][...] = dq.astype(BF16)
        outs[1][...] = source[ROWS : 2 * ROWS]
        outs[2][...] = source[2 * ROWS :]

    pl.when(pl.program_id(0) == 0)(lambda: write(mine, dq_mine))
    pl.when(pl.program_id(0) == 1)(lambda: write(theirs, dq_theirs))


def cross_final_kernel(info, mine, theirs, dq_out, pool_out):
    def write(source):
        dq_out[...] = source[:ROWS]
        pool_out[0] = source[ROWS : 2 * ROWS]
        pool_out[1] = source[2 * ROWS :]

    pl.when(pl.program_id(0) == 0)(lambda: write(mine))
    pl.when(pl.program_id(0) == 1)(lambda: write(theirs))


def assemble(kernel, name, info, inputs, pooled):
    half = lambda h, info: (info[0] + h) % 2
    rows_out = pl.BlockSpec((ROWS, WIDE), lambda h, info: (0, half(h, info)))
    pool_out = pl.BlockSpec((2, ROWS, WIDE), lambda h, info: (0, 0, half(h, info)))
    full = ((ROWS, 2 * WIDE), BF16)
    if pooled:
        out_specs, outs = [rows_out, pool_out], [full, ((2, ROWS, 2 * WIDE), BF16)]
    else:
        out_specs, outs = [rows_out] * 3, [full] * 3
    in_specs = [whole_spec(x.shape) for x in inputs]
    return call(kernel, name, info, in_specs, inputs, out_specs, outs, steps=2)


def body(
    queries, keys, values, grad_self, doc_ids, cross_queries, grad_cross, pool_kv, neighbour_ids
):
    loop = lax.axis_size("ctx")
    me = lax.axis_index("ctx").astype(jnp.int32)
    info = jnp.full((1,), me, jnp.int32)
    enc_dev = pool_kv.shape[1]
    width = queries.shape[1]
    pool = pool_kv.reshape(2, ROWS, width)

    cols = WIDE // 2
    block = lambda rows: pl.BlockSpec((rows, cols), lambda h, info: (0, h))
    mine_spec = pl.BlockSpec((ROWS, cols), lambda h, info: (0, info[0] % 2 * 2 + h))
    their_spec = pl.BlockSpec((ROWS, cols), lambda h, info: (0, (1 - info[0] % 2) * 2 + h))
    their_pool = pl.BlockSpec((2, ROWS, cols), lambda h, info: (0, 0, (1 - info[0] % 2) * 2 + h))
    sizes = (8 * ROWS + EXTRA, 2 * ROWS + EXTRA, 2 * ROWS + EXTRA, 2 * ROWS, 2 * ROWS)
    packed, x_mine, x_other, s_mine, s_other = call(
        functools.partial(pack_kernel, enc_dev, loop),
        "pack",
        info,
        [whole_spec(neighbour_ids.shape[::-1])] + [mine_spec] * 4 + [their_spec] * 6 + [their_pool],
        (neighbour_ids.T, queries, grad_self, cross_queries, grad_cross)
        + (queries, grad_self, keys, values, cross_queries, grad_cross, pool),
        [block(rows) for rows in sizes],
        [((rows, WIDE), BF16) for rows in sizes],
        steps=2,
    )
    partner = send(packed, swap, False)
    x_same = send(x_mine, outward, True)
    x_cross = send(x_other, across, True)

    ids_of = lambda d: lax.dynamic_slice_in_dim(doc_ids, d * ROWS, ROWS, 0)
    span = jnp.arange(ROWS, dtype=jnp.int32)
    base = me // 2 * 2
    places = jnp.concatenate([span + base * ROWS, span + (base + 1) * ROWS])
    near0, near1, far0, far1 = [ids_of(base + j) for j in range(4)]
    near = jnp.concatenate([near0, near1])
    near_flip = jnp.concatenate([near1, near0])
    far_flip = jnp.concatenate([far1, far0])
    local_ok = (near[:, None] == near[None, :]) & (places[:, None] <= places[None, :])
    far_ok = (near_flip[:, None] == far_flip[None, :]) & (base + 2 < loop)
    local_bias = jnp.where(local_ok, 0.0, MASKED).astype(F32)
    far_bias = jnp.where(far_ok, 0.0, MASKED).astype(F32)

    bias_spec = whole_spec((2 * ROWS, 2 * ROWS))
    self_specs = [bias_spec] + [own_spec()] * 4 + [spec(ROWS, j) for j in range(4)]
    self_args = (local_bias, queries, grad_self, keys, values) + (partner,) * 4
    mine_w = whole_spec((EXTRA, WIDE), (2 * ROWS // EXTRA, 0))
    partner_w = whole_spec((EXTRA, WIDE), (8 * ROWS // EXTRA, 0))
    cross_specs = (
        [mine_w, partner_w, own_spec(), own_spec(), own_spec((2,))]
        + [spec(ROWS, j) for j in range(4, 8)]
    )
    cross_args = (x_mine, partner, cross_queries, grad_cross, pool) + (partner,) * 4
    stat = lambda rows: ((HALF, 8, rows), F32)

    x_own, x_partner = call(
        cross_stats_kernel, "cross_stats", info, cross_specs, cross_args,
        [stat_spec(ROWS)] * 2, [stat(ROWS)] * 2, flops=0,
    )
    t_same = send(x_own, outward, True)
    t_cross = send(x_partner, inward, True)
    local_bias, x_own = lax.optimization_barrier((local_bias, x_own))
    self_args = (local_bias,) + self_args[1:]
    (s_own,) = call(
        self_stats_kernel, "self_stats", info, self_specs, self_args,
        [stat_spec(2 * ROWS)], [stat(2 * ROWS)], flops=0,
    )
    t_self = send(s_own, lambda d: d - 2, False)
    s_mine, s_other, x_same, x_cross, t_same, t_cross, s_own = lax.optimization_barrier(
        (s_mine, s_other, x_same, x_cross, t_same, t_cross, s_own)
    )
    s_same = send(s_mine, lambda d: d - 2, False)
    s_cross = send(s_other, lambda d: (d - 2) ^ 1, False)


    kv_out = spec(4 * ROWS)
    kv_shape = ((4 * ROWS, WIDE), BF16)
    q_shape = ((ROWS, WIDE), BF16)
    tagged = spec(ROWS + STATS)
    tagged_shape = ((ROWS + STATS, WIDE), BF16)
    xd_same, xd_cross, x_kv = call(
        cross_remote_kernel, "cross_remote", info,
        [mine_w, mine_w, spec(ROWS, 0), spec(ROWS, 1), spec(ROWS, 0), spec(ROWS, 1)]
        + [own_spec((2,)), spec(ROWS, 6), spec(ROWS, 7), stat_spec(ROWS), stat_spec(ROWS)],
        (x_same, x_cross, x_same, x_same, x_cross, x_cross, pool, partner, partner, t_same, t_cross),
        [tagged, tagged, kv_out],
        [tagged_shape, tagged_shape, kv_shape], flops=0,
    )
    xr_same = send(xd_same, inward, True)
    xr_cross = send(xd_cross, outward, True)

    far_bias, x_kv = lax.optimization_barrier((far_bias, x_kv))
    sd_same, sd_cross, s_kv, s_fin = call(
        self_remote_kernel, "self_remote", info,
        [bias_spec, spec(ROWS, 0), spec(ROWS, 1), spec(ROWS, 0), spec(ROWS, 1)]
        + [own_spec(), own_spec(), spec(ROWS, 2), spec(ROWS, 3), stat_spec(2 * ROWS)],
        (far_bias, s_same, s_same, s_cross, s_cross, keys, values, partner, partner, t_self),
        [spec(ROWS), spec(ROWS), kv_out, stat_spec(2 * ROWS)],
        [q_shape, q_shape, kv_shape, stat(2 * ROWS)], flops=LONG,
    )
    f_self = send(s_fin, lambda d: d + 2, False)
    sr_same = send(sd_same, lambda d: d + 2, False)
    sr_cross = send(sd_cross, lambda d: (d + 2) ^ 1, False)

    half_out = spec(3 * ROWS)
    half_shape = ((3 * ROWS, WIDE), BF16)
    x_keep, x_give = call(
        cross_local_kernel, "cross_local", info,
        cross_specs
        + [spec(STATS, ROWS // STATS), spec(STATS, ROWS // STATS), spec(ROWS), spec(ROWS)]
        + [spec(4 * ROWS)],
        cross_args + (xr_same, xr_cross, xr_same, xr_cross, x_kv),
        [half_out] * 2, [half_shape] * 2, flops=LONG,
    )
    x_take = send(x_give, swap, False)
    s_kv, x_keep = lax.optimization_barrier((s_kv, x_keep))
    s_keep, s_give = call(
        self_local_kernel, "self_local", info,
        self_specs
        + [stat_spec(2 * ROWS), stat_spec(2 * ROWS), spec(4 * ROWS)],
        self_args + (f_self, s_own, s_kv),
        [half_out] * 2, [half_shape] * 2, flops=0,
    )
    s_give, sr_same, sr_cross = lax.optimization_barrier((s_give, sr_same, sr_cross))
    s_take = send(s_give, swap, False)
    grad_cq, grad_pool = assemble(cross_final_kernel, "cross_final", info, (x_keep, x_take), True)
    grad_q, grad_k, grad_v = assemble(
        self_final_kernel, "self_final", info, (s_keep, s_take, sr_same, sr_cross), False
    )
    return grad_q, grad_k, grad_v, grad_cq, grad_pool.reshape(pool_kv.shape)


def solution(mesh):
    rows = P(("groups", "ctx"), None)
    pool = P(None, ("groups", "ctx"), None, None)
    return jax.shard_map(
        body,
        mesh=mesh,
        in_specs=(rows, rows, rows, rows, P("groups"), rows, rows, pool, rows),
        out_specs=(rows, rows, rows, rows, pool),
        check_vma=False,
    )
```

```python
import functools
import math

import jax
import jax.numpy as jnp
from jax import lax
from jax.experimental import pallas as pl
from jax.experimental.pallas import tpu as pltpu
from jax.sharding import PartitionSpec as P

HEADS = 8
HEAD_DIM = 128
HALF = HEADS // 2
WIDE = HALF * HEAD_DIM
STRETCH = 64
NBR_TOK = 128
ROWS = 256
EXTRA = 16
LONG = 12 * 10**9
FACTOR = HEAD_DIM ** (-0.5)
MASKED = -1e30
BF16 = jnp.bfloat16
F32 = jnp.float32


def send(value, target_of, wrap):
    count = lax.axis_size("ctx")
    pairs = []
    for source in range(count):
        target = target_of(source)
        if wrap:
            pairs.append((source, target % count))
        elif 0 <= target < count:
            pairs.append((source, target))
    return lax.ppermute(value, "ctx", pairs)


def swap(d):
    return d ^ 1


def outward(d):
    return d - 2 if d % 2 == 0 else d + 2


def inward(d):
    return d + 2 if d % 2 == 0 else d - 2


def across(d):
    return d - 1 if d % 2 == 0 else d + 1


def spec(rows, row_block=0, cols=HEAD_DIM):
    return pl.BlockSpec((rows, cols), lambda h, info: (row_block, h))


def own_spec(lead=()):
    zeros = (0,) * len(lead)
    return pl.BlockSpec(
        lead + (ROWS, HEAD_DIM), lambda h, info: zeros + (0, info[0] % 2 * HALF + h)
    )


def other_spec(lead=()):
    zeros = (0,) * len(lead)
    return pl.BlockSpec(
        lead + (ROWS, HEAD_DIM), lambda h, info: zeros + (0, (1 - info[0] % 2) * HALF + h)
    )


def whole_spec(shape, index=None):
    index = (0,) * len(shape) if index is None else index
    return pl.BlockSpec(shape, lambda h, *info: index)


def stat_spec(rows):
    return pl.BlockSpec((1, 8, rows), lambda h, info: (h, 0, 0))


def call(kernel, name, info, in_specs, inputs, out_specs, outs, steps=HALF, flops=0, prefetch=None):
    prefetch = (info,) if prefetch is None else prefetch
    return pl.pallas_call(
        kernel,
        name=name,
        grid_spec=pltpu.PrefetchScalarGridSpec(
            num_scalar_prefetch=len(prefetch),
            grid=(steps,),
            in_specs=in_specs,
            out_specs=out_specs,
        ),
        out_shape=[jax.ShapeDtypeStruct(shape, dtype) for shape, dtype in outs],
        compiler_params=pltpu.CompilerParams(vmem_limit_bytes=63 << 20),
        cost_estimate=pl.CostEstimate(flops=flops, transcendentals=0, bytes_accessed=0),
    )(*prefetch, *inputs)


def dot_last(a, b):
    return lax.dot_general(a, b, (((1,), (1,)), ((), ())), preferred_element_type=F32)


def dot_first(a, b):
    return lax.dot_general(a, b, (((0,), (0,)), ((), ())), preferred_element_type=F32)


def dot(a, b):
    return jnp.dot(a, b, preferred_element_type=F32)


def both(a, b):
    return jnp.concatenate([a, b], axis=0)


def weight_rows(times):
    log_two = jnp.where(times > 1.5, math.log(2.0), 0.0)
    return jnp.where(times < 0.5, MASKED, log_two)


def slot_pair(ref, first, core, second=None):
    times = ref[...].astype(F32)[:, :ROWS]
    low = times[first : first + 2]
    if second is None:
        return weight_rows(low)
    return weight_rows(jnp.where(core == 0, low, times[second : second + 2]))


def add_rows(s, rows):
    parts = [
        s[e * NBR_TOK : (e + 1) * NBR_TOK] + rows[e : e + 1] for e in range(s.shape[0] // NBR_TOK)
    ]
    return jnp.concatenate(parts, axis=0)


def partial_stats(s, dp):
    peak = jnp.max(s, axis=0, keepdims=True)
    e = jnp.exp(s - peak)
    return e, peak, jnp.sum(e, axis=0, keepdims=True), jnp.sum(e * dp, axis=0, keepdims=True)


def stat_rows(a, b, c):
    return jnp.concatenate([a, b, c, jnp.zeros((5, a.shape[1]), F32)], axis=0)[None]


def merge(stats, mine):
    t_peak, t_total, t_moment = stats[0, 0:1], stats[0, 1:2], stats[0, 2:3]
    peak, total, moment = mine
    top = jnp.maximum(t_peak, peak)
    t_scale = jnp.exp(t_peak - top)
    scale = jnp.exp(peak - top)
    full = t_total * t_scale + total * scale
    inverse = jnp.where(full > 0, 1.0 / full, 0.0)
    delta = (t_moment * t_scale + moment * scale) * inverse
    return top, inverse, delta, scale * inverse


def gradients(p, dp, delta, q, g, k):
    pb = p.astype(BF16)
    ds = (p * (dp - delta)).astype(BF16)
    return dot_first(ds, k) * FACTOR, dot(ds, q) * FACTOR, dot(pb, g)


def pack_cross_kernel(enc_dev, loop, info, ids_ref, qm, gm, q, g, pool, swap_ref, mine, other):
    shape = (EXTRA, mine.shape[1])
    row = lax.broadcasted_iota(jnp.int32, shape, 0)
    lane = lax.broadcasted_iota(jnp.int32, shape, 1) + pl.program_id(0) * shape[1]
    ids = ids_ref[...]
    owner = ids // enc_dev
    relative = owner - info[0] + 1
    relative = jnp.where(relative < 0, relative + loop, relative)
    relative = jnp.where(relative >= loop, relative - loop, relative)
    slots = relative * enc_dev + ids - owner * enc_dev
    times = jnp.zeros(shape, F32)
    for n in range(ids.shape[0]):
        for s in range(ids.shape[1]):
            hit = (row == slots[n : n + 1, s : s + 1]) & (lane // STRETCH == s)
            times = times + jnp.where(hit, 1.0, 0.0)
    times = times.astype(BF16)
    swap_ref[0:ROWS] = q[...]
    swap_ref[ROWS : 2 * ROWS] = g[...]
    swap_ref[2 * ROWS : 3 * ROWS] = pool[0]
    swap_ref[3 * ROWS : 4 * ROWS] = pool[1]
    swap_ref[4 * ROWS :] = times
    for out, first, second in ((mine, qm, gm), (other, q, g)):
        out[0:ROWS] = first[...]
        out[ROWS : 2 * ROWS] = second[...]
        out[2 * ROWS :] = times


def pack_self_kernel(info, qm, gm, q, g, k, v, swap_ref, mine, other):
    for index, ref in enumerate((q, g, k, v)):
        swap_ref[index * ROWS : (index + 1) * ROWS] = ref[...]
    for out, first, second in ((mine, qm, gm), (other, q, g)):
        out[0:ROWS] = first[...]
        out[ROWS : 2 * ROWS] = second[...]


def ordered(core, a, b):
    return jnp.where(core == 0, a, b), jnp.where(core == 0, b, a)


def wide_scores(keys_x, keys_y, values_x, values_y, qs, gs, bias):
    sx = dot_last(keys_x, qs) * FACTOR + bias[:ROWS]
    sy = dot_last(keys_y, qs[ROWS:]) * FACTOR + bias[ROWS:, ROWS:]
    return sx, sy, dot_last(values_x, gs), dot_last(values_y, gs[ROWS:])


def wide_stats(sx, sy, dpx, dpy):
    peak = jnp.max(sx, axis=0, keepdims=True)
    peak_y = jnp.maximum(peak[:, ROWS:], jnp.max(sy, axis=0, keepdims=True))
    peak = jnp.concatenate([peak[:, :ROWS], peak_y], axis=1)
    ex, ey = jnp.exp(sx - peak), jnp.exp(sy - peak_y)
    widen = lambda a, b: jnp.concatenate([a[:, :ROWS], a[:, ROWS:] + b], axis=1)
    add = lambda a: jnp.sum(a, axis=0, keepdims=True)
    return ex, ey, peak, widen(add(ex), add(ey)), widen(add(ex * dpx), add(ey * dpy))


def wide_gradients(px, py, dpx, dpy, delta, qs, gs, kx, ky):
    pbx, pby = px.astype(BF16), py.astype(BF16)
    dsx = (px * (dpx - delta)).astype(BF16)
    dsy = (py * (dpy - delta[:, ROWS:])).astype(BF16)
    dq_z = dot_first(dsx[:, :ROWS], kx) * FACTOR
    dq_y = dot_first(both(dsx[:, ROWS:], dsy), both(kx, ky)) * FACTOR
    dkx, dky = dot(dsx, qs) * FACTOR, dot(dsy, qs[ROWS:]) * FACTOR
    return dq_z, dq_y, dkx, dky, dot(pbx, gs), dot(pby, gs[ROWS:])


def local_self(core, bias, q, g, k, v, pq, pg, pk, pv):
    q0, q1 = ordered(core, q[...], pq[...])
    g0, g1 = ordered(core, g[...], pg[...])
    k0, k1 = ordered(core, k[...], pk[...])
    v0, v1 = ordered(core, v[...], pv[...])
    qs, gs = both(q0, q1), both(g0, g1)
    return wide_scores(k0, k1, v0, v1, qs, gs, bias[...]), qs, gs, k0, k1


def local_cross(core, w, pw, q, g, pool, pq, pg, pk, pv):
    qs, gs = both(q[...], pq[...]), both(g[...], pg[...])
    ks, vs = both(pool[0], pk[...]), both(pool[1], pv[...])
    own = both(slot_pair(w, 2, core), slot_pair(w, 4, core, 0))
    partner = both(slot_pair(pw, 0, core, 4), slot_pair(pw, 2, core))
    s = add_rows(dot_last(ks, qs) * FACTOR, jnp.concatenate([own, partner], axis=1))
    return s, dot_last(vs, gs), qs, gs, ks


def self_stats_kernel(info, *refs):
    scores = local_self(info[0] % 2, *refs[:-1])[0]
    refs[-1][...] = stat_rows(*wide_stats(*scores)[2:])


def cross_stats_kernel(info, *refs):
    s, dp, _, _, _ = local_cross(info[0] % 2, *refs[:-2])
    stats = stat_rows(*partial_stats(s, dp)[1:])
    refs[-2][...] = stats[:, :, :ROWS]
    refs[-1][...] = stats[:, :, ROWS:]


def self_remote_kernel(
    info, bias, sq, sg, cq, cg, k, v, pk, pv, stats, dq_same, dq_cross, kv_ref, out_stats
):
    core = info[0] % 2
    q0, q1 = ordered(core, sq[...], cq[...])
    g0, g1 = ordered(core, sg[...], cg[...])
    k0, k1 = ordered(core, k[...], pk[...])
    v0, v1 = ordered(core, v[...], pv[...])
    qs, gs = both(q1, q0), both(g1, g0)
    sx, sy, dpx, dpy = wide_scores(k1, k0, v1, v0, qs, gs, bias[...])
    ex, ey, *mine = wide_stats(sx, sy, dpx, dpy)
    known = stats[...]
    known = jnp.concatenate([known[:, :, ROWS:], known[:, :, :ROWS]], axis=2)
    top, inverse, delta, scale = merge(known, mine)
    px, py = ex * scale, ey * scale[:, ROWS:]
    dq1, dq0, dk1, dk0, dv1, dv0 = wide_gradients(px, py, dpx, dpy, delta, qs, gs, k1, k0)
    same, cross = ordered(core, dq0, dq1)
    dq_same[...] = same.astype(BF16)
    dq_cross[...] = cross.astype(BF16)
    for index, grad in enumerate(ordered(core, dk0, dk1) + ordered(core, dv0, dv1)):
        kv_ref[index * ROWS : (index + 1) * ROWS] = grad.astype(BF16)
    out_stats[...] = stat_rows(top, inverse, delta)


def cross_remote_kernel(
    info, sw, cw, sq, sg, cq, cg, pool, pk, pv, s_stats, c_stats, *outs
):
    dq_same, dq_cross, kv_ref, out_same, out_cross = outs
    core = info[0] % 2
    jobs = (
        (cq, cg, pool[0], pool[1], slot_pair(cw, 4, core, 0), c_stats, dq_cross, out_cross, 0),
        (sq, sg, pk[...], pv[...], slot_pair(sw, 0, core, 4), s_stats, dq_same, out_same, 1),
    )
    for q, g, k, v, rows, stats, dq_ref, out_stats, place in jobs:
        s, dp = add_rows(dot_last(k, q[...]) * FACTOR, rows), dot_last(v, g[...])
        e, *mine = partial_stats(s, dp)
        top, inverse, delta, scale = merge(stats[...], mine)
        dq, dk, dv = gradients(e * scale, dp, delta, q[...], g[...], k)
        dq_ref[...] = dq.astype(BF16)
        out_stats[...] = stat_rows(top, inverse, delta)
        kv_ref[place * ROWS : (place + 1) * ROWS] = dk.astype(BF16)
        kv_ref[(2 + place) * ROWS : (3 + place) * ROWS] = dv.astype(BF16)


def self_local_kernel(info, *refs):
    stats_ref, own_ref, kv_ref, mine, theirs = refs[-5:]
    local = own_ref[0]
    core = info[0] % 2
    first = info[0] < 2
    stats = stats_ref[0]
    stats = jnp.concatenate([stats[:, ROWS:], stats[:, :ROWS]], axis=1)
    inverse = 1.0 / local[1:2]
    top = jnp.where(first, local[0:1], stats[0:1])
    delta = jnp.where(first, local[2:3] * inverse, stats[2:3])
    inverse = jnp.where(first, inverse, stats[1:2])
    (sx, sy, dpx, dpy), qs, gs, k0, k1 = local_self(core, *refs[:-5])
    px = jnp.exp(sx - top) * inverse
    py = jnp.exp(sy - top[:, ROWS:]) * inverse[:, ROWS:]
    dq0, dq1, dk0, dk1, dv0, dv1 = wide_gradients(px, py, dpx, dpy, delta, qs, gs, k0, k1)
    grads = (ordered(core, dq0, dq1), ordered(core, dk0, dk1), ordered(core, dv0, dv1))
    for index, pair in enumerate(grads):
        for out, place, grad in ((mine, 0, pair[0]), (theirs, 1, pair[1])):
            if index > 0:
                low = (2 * index - 2 + place) * ROWS
                grad = grad + kv_ref[low : low + ROWS].astype(F32)
            out[index * ROWS : (index + 1) * ROWS] = grad.astype(BF16)


def cross_local_kernel(info, *refs):
    own_stats, partner_stats, kv_ref, mine, theirs = refs[-5:]
    stats = jnp.concatenate([own_stats[0], partner_stats[0]], axis=1)
    top, inverse, delta = stats[0:1], stats[1:2], stats[2:3]
    s, dp, qs, gs, ks = local_cross(info[0] % 2, *refs[:-5])
    dq, dk, dv = gradients(jnp.exp(s - top) * inverse, dp, delta, qs, gs, ks)
    dk = dk + kv_ref[: 2 * ROWS].astype(F32)
    dv = dv + kv_ref[2 * ROWS :].astype(F32)
    for index, grad in enumerate((dq, dk, dv)):
        mine[index * ROWS : (index + 1) * ROWS] = grad[:ROWS].astype(BF16)
        theirs[index * ROWS : (index + 1) * ROWS] = grad[ROWS:].astype(BF16)


def self_final_kernel(info, mine, theirs, dq_mine, dq_theirs, *outs):
    def write(source, extra):
        dq = source[:ROWS].astype(F32) + extra[...].astype(F32)
        outs[0][...] = dq.astype(BF16)
        outs[1][...] = source[ROWS : 2 * ROWS]
        outs[2][...] = source[2 * ROWS :]

    pl.when(pl.program_id(0) == 0)(lambda: write(mine, dq_mine))
    pl.when(pl.program_id(0) == 1)(lambda: write(theirs, dq_theirs))


def cross_final_kernel(info, mine, theirs, dq_mine, dq_theirs, dq_out, pool_out):
    def write(source, extra):
        dq = source[:ROWS].astype(F32) + extra[...].astype(F32)
        dq_out[...] = dq.astype(BF16)
        pool_out[0] = source[ROWS : 2 * ROWS]
        pool_out[1] = source[2 * ROWS :]

    pl.when(pl.program_id(0) == 0)(lambda: write(mine, dq_mine))
    pl.when(pl.program_id(0) == 1)(lambda: write(theirs, dq_theirs))


def assemble(kernel, name, info, inputs, pooled):
    half = lambda h, info: (info[0] + h) % 2
    rows_out = pl.BlockSpec((ROWS, WIDE), lambda h, info: (0, half(h, info)))
    pool_out = pl.BlockSpec((2, ROWS, WIDE), lambda h, info: (0, 0, half(h, info)))
    full = ((ROWS, 2 * WIDE), BF16)
    if pooled:
        out_specs, outs = [rows_out, pool_out], [full, ((2, ROWS, 2 * WIDE), BF16)]
    else:
        out_specs, outs = [rows_out] * 3, [full] * 3
    in_specs = [whole_spec(x.shape) for x in inputs]
    return call(kernel, name, info, in_specs, inputs, out_specs, outs, steps=2)


def body(
    queries, keys, values, grad_self, doc_ids, cross_queries, grad_cross, pool_kv, neighbour_ids
):
    loop = lax.axis_size("ctx")
    me = lax.axis_index("ctx").astype(jnp.int32)
    info = jnp.full((1,), me, jnp.int32)
    enc_dev = pool_kv.shape[1]
    width = queries.shape[1]
    pool = pool_kv.reshape(2, ROWS, width)

    cols = WIDE // 2
    block = lambda rows: pl.BlockSpec((rows, cols), lambda h, info: (0, h))
    mine_spec = pl.BlockSpec((ROWS, cols), lambda h, info: (0, info[0] % 2 * 2 + h))
    their_spec = pl.BlockSpec((ROWS, cols), lambda h, info: (0, (1 - info[0] % 2) * 2 + h))
    their_pool = pl.BlockSpec((2, ROWS, cols), lambda h, info: (0, 0, (1 - info[0] % 2) * 2 + h))
    sizes = (4 * ROWS + EXTRA, 2 * ROWS + EXTRA, 2 * ROWS + EXTRA)
    packed, x_mine, x_other = call(
        functools.partial(pack_cross_kernel, enc_dev, loop), "pack_cross", info,
        [whole_spec(neighbour_ids.shape[::-1])] + [mine_spec] * 2 + [their_spec] * 2 + [their_pool],
        (neighbour_ids.T, cross_queries, grad_cross, cross_queries, grad_cross, pool),
        [block(rows) for rows in sizes],
        [((rows, WIDE), BF16) for rows in sizes],
        steps=2,
    )
    x_same = send(x_mine, outward, True)
    x_cross = send(x_other, across, True)
    x_pair = send(packed, swap, False)
    queries_in, packed = lax.optimization_barrier((queries, packed))
    sizes = (4 * ROWS, 2 * ROWS, 2 * ROWS)
    packed, s_mine, s_other = call(
        pack_self_kernel, "pack_self", info,
        [mine_spec] * 2 + [their_spec] * 4,
        (queries_in, grad_self, queries_in, grad_self, keys, values),
        [block(rows) for rows in sizes],
        [((rows, WIDE), BF16) for rows in sizes],
        steps=2,
    )
    s_pair = send(packed, swap, False)

    ids_of = lambda d: lax.dynamic_slice_in_dim(doc_ids, d * ROWS, ROWS, 0)
    span = jnp.arange(ROWS, dtype=jnp.int32)
    base = me // 2 * 2
    places = jnp.concatenate([span + base * ROWS, span + (base + 1) * ROWS])
    near0, near1, far0, far1 = [ids_of(base + j) for j in range(4)]
    near = jnp.concatenate([near0, near1])
    near_flip = jnp.concatenate([near1, near0])
    far_flip = jnp.concatenate([far1, far0])
    local_ok = (near[:, None] == near[None, :]) & (places[:, None] <= places[None, :])
    far_ok = (near_flip[:, None] == far_flip[None, :]) & (base + 2 < loop)
    local_bias = jnp.where(local_ok, 0.0, MASKED).astype(F32)
    far_bias = jnp.where(far_ok, 0.0, MASKED).astype(F32)

    bias_spec = whole_spec((2 * ROWS, 2 * ROWS))
    local_bias, far_bias, x_pair = lax.optimization_barrier((local_bias, far_bias, x_pair))
    self_specs = [bias_spec] + [own_spec()] * 4 + [spec(ROWS, j) for j in range(4)]
    self_args = (local_bias, queries, grad_self, keys, values) + (s_pair,) * 4
    mine_w = whole_spec((EXTRA, WIDE), (2 * ROWS // EXTRA, 0))
    partner_w = whole_spec((EXTRA, WIDE), (4 * ROWS // EXTRA, 0))
    cross_specs = (
        [mine_w, partner_w, own_spec(), own_spec(), own_spec((2,))]
        + [spec(ROWS, j) for j in range(4)]
    )
    cross_args = (x_mine, x_pair, cross_queries, grad_cross, pool) + (x_pair,) * 4
    stat = lambda rows: ((HALF, 8, rows), F32)

    x_own, x_partner = call(
        cross_stats_kernel, "cross_stats", info, cross_specs, cross_args,
        [stat_spec(ROWS)] * 2, [stat(ROWS)] * 2, flops=0,
    )
    t_same = send(x_own, outward, True)
    t_cross = send(x_partner, inward, True)
    local_bias, x_own = lax.optimization_barrier((local_bias, x_own))
    self_args = (local_bias,) + self_args[1:]
    (s_own,) = call(
        self_stats_kernel, "self_stats", info, self_specs, self_args,
        [stat_spec(2 * ROWS)], [stat(2 * ROWS)], flops=0,
    )
    t_self = send(s_own, lambda d: d - 2, False)
    s_mine, x_same, x_cross, t_same, t_cross, s_own = lax.optimization_barrier(
        (s_mine, x_same, x_cross, t_same, t_cross, s_own)
    )
    s_same = send(s_mine, lambda d: d - 2, False)

    kv_out = spec(4 * ROWS)
    kv_shape = ((4 * ROWS, WIDE), BF16)
    q_shape = ((ROWS, WIDE), BF16)
    xd_same, xd_cross, x_kv, x_fin_same, x_fin_cross = call(
        cross_remote_kernel, "cross_remote", info,
        [mine_w, mine_w, spec(ROWS, 0), spec(ROWS, 1), spec(ROWS, 0), spec(ROWS, 1)]
        + [own_spec((2,)), spec(ROWS, 2), spec(ROWS, 3), stat_spec(ROWS), stat_spec(ROWS)],
        (x_same, x_cross, x_same, x_same, x_cross, x_cross, pool, x_pair, x_pair, t_same, t_cross),
        [spec(ROWS), spec(ROWS), kv_out, stat_spec(ROWS), stat_spec(ROWS)],
        [q_shape, q_shape, kv_shape, stat(ROWS), stat(ROWS)],
    )
    f_own = send(x_fin_same, inward, True)
    f_partner = send(x_fin_cross, outward, True)
    s_other, x_kv = lax.optimization_barrier((s_other, x_kv))
    s_cross = send(s_other, lambda d: (d - 2) ^ 1, False)
    xd_same, xd_cross, f_own, f_partner = lax.optimization_barrier(
        (xd_same, xd_cross, f_own, f_partner)
    )
    xr_same = send(xd_same, inward, True)
    xr_cross = send(xd_cross, across, True)

    x_kv, s_same, t_self = lax.optimization_barrier((x_kv, s_same, t_self))
    half_out = spec(3 * ROWS)
    half_shape = ((3 * ROWS, WIDE), BF16)
    x_keep, x_give = call(
        cross_local_kernel, "cross_local", info,
        cross_specs + [stat_spec(ROWS), stat_spec(ROWS), spec(4 * ROWS)],
        cross_args + (f_own, f_partner, x_kv),
        [half_out] * 2, [half_shape] * 2, flops=LONG,
    )

    far_bias, x_keep = lax.optimization_barrier((far_bias, x_keep))
    sd_same, sd_cross, s_kv, s_fin = call(
        self_remote_kernel, "self_remote", info,
        [bias_spec, spec(ROWS, 0), spec(ROWS, 1), spec(ROWS, 0), spec(ROWS, 1)]
        + [own_spec(), own_spec(), spec(ROWS, 2), spec(ROWS, 3), stat_spec(2 * ROWS)],
        (far_bias, s_same, s_same, s_cross, s_cross, keys, values, s_pair, s_pair, t_self),
        [spec(ROWS), spec(ROWS), kv_out, stat_spec(2 * ROWS)],
        [q_shape, q_shape, kv_shape, stat(2 * ROWS)], flops=LONG,
    )
    f_self = send(s_fin, lambda d: d + 2, False)
    sr_same = send(sd_same, lambda d: d + 2, False)
    sr_cross = send(sd_cross, lambda d: (d + 2) ^ 1, False)

    x_give, s_kv, xr_same, xr_cross, f_self = lax.optimization_barrier(
        (x_give, s_kv, xr_same, xr_cross, f_self)
    )
    x_take = send(x_give, swap, False)
    s_keep, s_give = call(
        self_local_kernel, "self_local", info,
        self_specs + [stat_spec(2 * ROWS), stat_spec(2 * ROWS), spec(4 * ROWS)],
        self_args + (f_self, s_own, s_kv),
        [half_out] * 2, [half_shape] * 2, flops=LONG,
    )
    grad_cq, grad_pool = assemble(
        cross_final_kernel, "cross_final", info, (x_keep, x_take, xr_same, xr_cross), True
    )
    s_give, sr_same, sr_cross, grad_cq = lax.optimization_barrier(
        (s_give, sr_same, sr_cross, grad_cq)
    )
    s_take = send(s_give, swap, False)
    grad_q, grad_k, grad_v = assemble(
        self_final_kernel, "self_final", info, (s_keep, s_take, sr_same, sr_cross), False
    )
    return grad_q, grad_k, grad_v, grad_cq, grad_pool.reshape(pool_kv.shape)


def solution(mesh):
    rows = P(("groups", "ctx"), None)
    pool = P(None, ("groups", "ctx"), None, None)
    return jax.shard_map(
        body,
        mesh=mesh,
        in_specs=(rows, rows, rows, rows, P("groups"), rows, rows, pool, rows),
        out_specs=(rows, rows, rows, rows, pool),
        check_vma=False,
    )
```

```python
import functools
import math

import jax
import jax.numpy as jnp
from jax import lax
from jax.experimental import pallas as pl
from jax.experimental.pallas import tpu as pltpu
from jax.sharding import PartitionSpec as P

HEADS = 8
HEAD_DIM = 128
HALF = HEADS // 2
WIDE = HALF * HEAD_DIM
STEP = 2
COLS = STEP * HEAD_DIM
STEPS = HALF // STEP
STRETCH = 64
NBR_TOK = 128
ROWS = 256
EXTRA = 16
LONG = 12 * 10**9
FACTOR = HEAD_DIM ** (-0.5)
MASKED = -1e30
BF16 = jnp.bfloat16
F32 = jnp.float32


def send(value, target_of, wrap):
    count = lax.axis_size("ctx")
    pairs = []
    for source in range(count):
        target = target_of(source)
        if wrap:
            pairs.append((source, target % count))
        elif 0 <= target < count:
            pairs.append((source, target))
    return lax.ppermute(value, "ctx", pairs)


def swap(d):
    return d ^ 1


def outward(d):
    return d - 2 if d % 2 == 0 else d + 2


def inward(d):
    return d + 2 if d % 2 == 0 else d - 2


def across(d):
    return d - 1 if d % 2 == 0 else d + 1


def spec(rows, row_block=0):
    return pl.BlockSpec((rows, COLS), lambda h, info: (row_block, h))


def own_spec(lead=()):
    zeros = (0,) * len(lead)
    return pl.BlockSpec(lead + (ROWS, COLS), lambda h, info: zeros + (0, info[0] % 2 * STEPS + h))


def other_spec(lead=()):
    zeros = (0,) * len(lead)
    return pl.BlockSpec(
        lead + (ROWS, COLS), lambda h, info: zeros + (0, (1 - info[0] % 2) * STEPS + h)
    )


def whole_spec(shape, index=None):
    index = (0,) * len(shape) if index is None else index
    return pl.BlockSpec(shape, lambda h, *info: index)


def stat_spec(rows):
    return pl.BlockSpec((STEP, 8, rows), lambda h, info: (h, 0, 0))


def call(kernel, name, info, in_specs, inputs, out_specs, outs, steps=STEPS, flops=0):
    return pl.pallas_call(
        kernel,
        name=name,
        grid_spec=pltpu.PrefetchScalarGridSpec(
            num_scalar_prefetch=1,
            grid=(steps,),
            in_specs=in_specs,
            out_specs=out_specs,
        ),
        out_shape=[jax.ShapeDtypeStruct(shape, dtype) for shape, dtype in outs],
        compiler_params=pltpu.CompilerParams(vmem_limit_bytes=63 << 20),
        cost_estimate=pl.CostEstimate(flops=flops, transcendentals=0, bytes_accessed=0),
    )(info, *inputs)


def head_of(ref, j):
    shape = ref.shape
    if len(shape) == 3 and shape[1] == 8:
        return ref.at[j : j + 1]
    if shape[-1] != COLS:
        return ref
    place = pl.ds(j * HEAD_DIM, HEAD_DIM)
    return ref.at[:, place] if len(shape) == 2 else ref.at[:, :, place]


def per_head(kernel):
    def run(info, *refs):
        for j in range(STEP):
            kernel(info, *[head_of(ref, j) for ref in refs])

    return run


def dot_last(a, b):
    return lax.dot_general(a, b, (((1,), (1,)), ((), ())), preferred_element_type=F32)


def dot_first(a, b):
    return lax.dot_general(a, b, (((0,), (0,)), ((), ())), preferred_element_type=F32)


def dot(a, b):
    return jnp.dot(a, b, preferred_element_type=F32)


def both(a, b):
    return jnp.concatenate([a, b], axis=0)


def weight_rows(times):
    log_two = jnp.where(times > 1.5, math.log(2.0), 0.0)
    return jnp.where(times < 0.5, MASKED, log_two)


def slot_pair(ref, first, core, second=None):
    times = ref[...].astype(F32)[:, :ROWS]
    low = times[first : first + 2]
    if second is None:
        return weight_rows(low)
    return weight_rows(jnp.where(core == 0, low, times[second : second + 2]))


def add_rows(s, rows):
    parts = [
        s[e * NBR_TOK : (e + 1) * NBR_TOK] + rows[e : e + 1] for e in range(s.shape[0] // NBR_TOK)
    ]
    return jnp.concatenate(parts, axis=0)


def partial_stats(s, dp):
    peak = jnp.max(s, axis=0, keepdims=True)
    e = jnp.exp(s - peak)
    return e, peak, jnp.sum(e, axis=0, keepdims=True), jnp.sum(e * dp, axis=0, keepdims=True)


def stat_rows(a, b, c):
    return jnp.concatenate([a, b, c, jnp.zeros((5, a.shape[1]), F32)], axis=0)[None]


def merge(stats, mine):
    t_peak, t_total, t_moment = stats[0, 0:1], stats[0, 1:2], stats[0, 2:3]
    peak, total, moment = mine
    top = jnp.maximum(t_peak, peak)
    t_scale = jnp.exp(t_peak - top)
    scale = jnp.exp(peak - top)
    full = t_total * t_scale + total * scale
    inverse = jnp.where(full > 0, 1.0 / full, 0.0)
    delta = (t_moment * t_scale + moment * scale) * inverse
    return top, inverse, delta, scale * inverse


def gradients(p, dp, delta, q, g, k):
    pb = p.astype(BF16)
    ds = (p * (dp - delta)).astype(BF16)
    return dot_first(ds, k) * FACTOR, dot(ds, q) * FACTOR, dot(pb, g)


def pack_cross_kernel(enc_dev, loop, info, ids_ref, qm, gm, q, g, pool, swap_ref, mine, other):
    shape = (EXTRA, mine.shape[1])
    row = lax.broadcasted_iota(jnp.int32, shape, 0)
    lane = lax.broadcasted_iota(jnp.int32, shape, 1) + pl.program_id(0) * shape[1]
    ids = ids_ref[...]
    owner = ids // enc_dev
    relative = owner - info[0] + 1
    relative = jnp.where(relative < 0, relative + loop, relative)
    relative = jnp.where(relative >= loop, relative - loop, relative)
    slots = relative * enc_dev + ids - owner * enc_dev
    times = jnp.zeros(shape, F32)
    for n in range(ids.shape[0]):
        for s in range(ids.shape[1]):
            hit = (row == slots[n : n + 1, s : s + 1]) & (lane // STRETCH == s)
            times = times + jnp.where(hit, 1.0, 0.0)
    times = times.astype(BF16)
    swap_ref[0:ROWS] = q[...]
    swap_ref[ROWS : 2 * ROWS] = g[...]
    swap_ref[2 * ROWS : 3 * ROWS] = pool[0]
    swap_ref[3 * ROWS : 4 * ROWS] = pool[1]
    swap_ref[4 * ROWS :] = times
    for out, first, second in ((mine, qm, gm), (other, q, g)):
        out[0:ROWS] = first[...]
        out[ROWS : 2 * ROWS] = second[...]
        out[2 * ROWS :] = times


def pack_self_kernel(info, qm, gm, q, g, k, v, swap_ref, mine, other):
    for index, ref in enumerate((q, g, k, v)):
        swap_ref[index * ROWS : (index + 1) * ROWS] = ref[...]
    for out, first, second in ((mine, qm, gm), (other, q, g)):
        out[0:ROWS] = first[...]
        out[ROWS : 2 * ROWS] = second[...]


def ordered(core, a, b):
    return jnp.where(core == 0, a, b), jnp.where(core == 0, b, a)


def wide_scores(keys_x, keys_y, values_x, values_y, qs, gs, bias):
    sx = dot_last(keys_x, qs) * FACTOR + bias[:ROWS]
    sy = dot_last(keys_y, qs[ROWS:]) * FACTOR + bias[ROWS:, ROWS:]
    return sx, sy, dot_last(values_x, gs), dot_last(values_y, gs[ROWS:])


def wide_stats(sx, sy, dpx, dpy):
    peak = jnp.max(sx, axis=0, keepdims=True)
    peak_y = jnp.maximum(peak[:, ROWS:], jnp.max(sy, axis=0, keepdims=True))
    peak = jnp.concatenate([peak[:, :ROWS], peak_y], axis=1)
    ex, ey = jnp.exp(sx - peak), jnp.exp(sy - peak_y)
    widen = lambda a, b: jnp.concatenate([a[:, :ROWS], a[:, ROWS:] + b], axis=1)
    add = lambda a: jnp.sum(a, axis=0, keepdims=True)
    return ex, ey, peak, widen(add(ex), add(ey)), widen(add(ex * dpx), add(ey * dpy))


def wide_gradients(px, py, dpx, dpy, delta, qs, gs, kx, ky):
    pbx, pby = px.astype(BF16), py.astype(BF16)
    dsx = (px * (dpx - delta)).astype(BF16)
    dsy = (py * (dpy - delta[:, ROWS:])).astype(BF16)
    dq_z = dot_first(dsx[:, :ROWS], kx) * FACTOR
    dq_y = dot_first(both(dsx[:, ROWS:], dsy), both(kx, ky)) * FACTOR
    dkx, dky = dot(dsx, qs) * FACTOR, dot(dsy, qs[ROWS:]) * FACTOR
    return dq_z, dq_y, dkx, dky, dot(pbx, gs), dot(pby, gs[ROWS:])


def local_self(core, bias, q, g, k, v, pq, pg, pk, pv):
    q0, q1 = ordered(core, q[...], pq[...])
    g0, g1 = ordered(core, g[...], pg[...])
    k0, k1 = ordered(core, k[...], pk[...])
    v0, v1 = ordered(core, v[...], pv[...])
    qs, gs = both(q0, q1), both(g0, g1)
    return wide_scores(k0, k1, v0, v1, qs, gs, bias[...]), qs, gs, k0, k1


def local_cross(core, w, pw, q, g, pool, pq, pg, pk, pv):
    qs, gs = both(q[...], pq[...]), both(g[...], pg[...])
    ks, vs = both(pool[0], pk[...]), both(pool[1], pv[...])
    own = both(slot_pair(w, 2, core), slot_pair(w, 4, core, 0))
    partner = both(slot_pair(pw, 0, core, 4), slot_pair(pw, 2, core))
    s = add_rows(dot_last(ks, qs) * FACTOR, jnp.concatenate([own, partner], axis=1))
    return s, dot_last(vs, gs), qs, gs, ks


def self_stats_kernel(info, *refs):
    scores = local_self(info[0] % 2, *refs[:-1])[0]
    refs[-1][...] = stat_rows(*wide_stats(*scores)[2:])


def cross_stats_kernel(info, *refs):
    s, dp, _, _, _ = local_cross(info[0] % 2, *refs[:-2])
    stats = stat_rows(*partial_stats(s, dp)[1:])
    refs[-2][...] = stats[:, :, :ROWS]
    refs[-1][...] = stats[:, :, ROWS:]


def self_remote_kernel(
    info, bias, sq, sg, cq, cg, k, v, pk, pv, stats, dq_same, dq_cross, kv_ref, out_stats
):
    core = info[0] % 2
    q0, q1 = ordered(core, sq[...], cq[...])
    g0, g1 = ordered(core, sg[...], cg[...])
    k0, k1 = ordered(core, k[...], pk[...])
    v0, v1 = ordered(core, v[...], pv[...])
    qs, gs = both(q1, q0), both(g1, g0)
    sx, sy, dpx, dpy = wide_scores(k1, k0, v1, v0, qs, gs, bias[...])
    ex, ey, *mine = wide_stats(sx, sy, dpx, dpy)
    known = stats[...]
    known = jnp.concatenate([known[:, :, ROWS:], known[:, :, :ROWS]], axis=2)
    top, inverse, delta, scale = merge(known, mine)
    px, py = ex * scale, ey * scale[:, ROWS:]
    dq1, dq0, dk1, dk0, dv1, dv0 = wide_gradients(px, py, dpx, dpy, delta, qs, gs, k1, k0)
    same, cross = ordered(core, dq0, dq1)
    dq_same[...] = same.astype(BF16)
    dq_cross[...] = cross.astype(BF16)
    for index, grad in enumerate(ordered(core, dk0, dk1) + ordered(core, dv0, dv1)):
        kv_ref[index * ROWS : (index + 1) * ROWS] = grad.astype(BF16)
    out_stats[...] = stat_rows(top, inverse, delta)


def cross_remote_kernel(
    info, sw, cw, sq, sg, cq, cg, pool, pk, pv, s_stats, c_stats, *outs
):
    dq_same, dq_cross, kv_ref, out_same, out_cross = outs
    core = info[0] % 2
    jobs = (
        (cq, cg, pool[0], pool[1], slot_pair(cw, 4, core, 0), c_stats, dq_cross, out_cross, 0),
        (sq, sg, pk[...], pv[...], slot_pair(sw, 0, core, 4), s_stats, dq_same, out_same, 1),
    )
    for q, g, k, v, rows, stats, dq_ref, out_stats, place in jobs:
        s, dp = add_rows(dot_last(k, q[...]) * FACTOR, rows), dot_last(v, g[...])
        e, *mine = partial_stats(s, dp)
        top, inverse, delta, scale = merge(stats[...], mine)
        dq, dk, dv = gradients(e * scale, dp, delta, q[...], g[...], k)
        dq_ref[...] = dq.astype(BF16)
        out_stats[...] = stat_rows(top, inverse, delta)
        kv_ref[place * ROWS : (place + 1) * ROWS] = dk.astype(BF16)
        kv_ref[(2 + place) * ROWS : (3 + place) * ROWS] = dv.astype(BF16)


def self_local_kernel(info, *refs):
    stats_ref, own_ref, kv_ref, mine, theirs = refs[-5:]
    local = own_ref[0]
    core = info[0] % 2
    first = info[0] < 2
    stats = stats_ref[0]
    stats = jnp.concatenate([stats[:, ROWS:], stats[:, :ROWS]], axis=1)
    inverse = 1.0 / local[1:2]
    top = jnp.where(first, local[0:1], stats[0:1])
    delta = jnp.where(first, local[2:3] * inverse, stats[2:3])
    inverse = jnp.where(first, inverse, stats[1:2])
    (sx, sy, dpx, dpy), qs, gs, k0, k1 = local_self(core, *refs[:-5])
    px = jnp.exp(sx - top) * inverse
    py = jnp.exp(sy - top[:, ROWS:]) * inverse[:, ROWS:]
    dq0, dq1, dk0, dk1, dv0, dv1 = wide_gradients(px, py, dpx, dpy, delta, qs, gs, k0, k1)
    grads = (ordered(core, dq0, dq1), ordered(core, dk0, dk1), ordered(core, dv0, dv1))
    for index, pair in enumerate(grads):
        for out, place, grad in ((mine, 0, pair[0]), (theirs, 1, pair[1])):
            if index > 0:
                low = (2 * index - 2 + place) * ROWS
                grad = grad + kv_ref[low : low + ROWS].astype(F32)
            out[index * ROWS : (index + 1) * ROWS] = grad.astype(BF16)


def cross_local_kernel(info, *refs):
    own_stats, partner_stats, kv_ref, mine, theirs = refs[-5:]
    stats = jnp.concatenate([own_stats[0], partner_stats[0]], axis=1)
    top, inverse, delta = stats[0:1], stats[1:2], stats[2:3]
    s, dp, qs, gs, ks = local_cross(info[0] % 2, *refs[:-5])
    dq, dk, dv = gradients(jnp.exp(s - top) * inverse, dp, delta, qs, gs, ks)
    dk = dk + kv_ref[: 2 * ROWS].astype(F32)
    dv = dv + kv_ref[2 * ROWS :].astype(F32)
    for index, grad in enumerate((dq, dk, dv)):
        mine[index * ROWS : (index + 1) * ROWS] = grad[:ROWS].astype(BF16)
        theirs[index * ROWS : (index + 1) * ROWS] = grad[ROWS:].astype(BF16)


def self_final_kernel(info, mine, theirs, dq_mine, dq_theirs, *outs):
    def write(source, extra):
        dq = source[:ROWS].astype(F32) + extra[...].astype(F32)
        outs[0][...] = dq.astype(BF16)
        outs[1][...] = source[ROWS : 2 * ROWS]
        outs[2][...] = source[2 * ROWS :]

    pl.when(pl.program_id(0) == 0)(lambda: write(mine, dq_mine))
    pl.when(pl.program_id(0) == 1)(lambda: write(theirs, dq_theirs))


def cross_final_kernel(info, mine, theirs, dq_mine, dq_theirs, dq_out, pool_out):
    def write(source, extra):
        dq = source[:ROWS].astype(F32) + extra[...].astype(F32)
        dq_out[...] = dq.astype(BF16)
        pool_out[0] = source[ROWS : 2 * ROWS]
        pool_out[1] = source[2 * ROWS :]

    pl.when(pl.program_id(0) == 0)(lambda: write(mine, dq_mine))
    pl.when(pl.program_id(0) == 1)(lambda: write(theirs, dq_theirs))


def assemble(kernel, name, info, inputs, pooled):
    half = lambda h, info: (info[0] + h) % 2
    rows_out = pl.BlockSpec((ROWS, WIDE), lambda h, info: (0, half(h, info)))
    pool_out = pl.BlockSpec((2, ROWS, WIDE), lambda h, info: (0, 0, half(h, info)))
    full = ((ROWS, 2 * WIDE), BF16)
    if pooled:
        out_specs, outs = [rows_out, pool_out], [full, ((2, ROWS, 2 * WIDE), BF16)]
    else:
        out_specs, outs = [rows_out] * 3, [full] * 3
    in_specs = [whole_spec(x.shape) for x in inputs]
    return call(kernel, name, info, in_specs, inputs, out_specs, outs, steps=2)


def body(
    queries, keys, values, grad_self, doc_ids, cross_queries, grad_cross, pool_kv, neighbour_ids
):
    loop = lax.axis_size("ctx")
    me = lax.axis_index("ctx").astype(jnp.int32)
    info = jnp.full((1,), me, jnp.int32)
    enc_dev = pool_kv.shape[1]
    width = queries.shape[1]
    pool = pool_kv.reshape(2, ROWS, width)

    mine_spec, their_spec, their_pool = own_spec(), other_spec(), other_spec((2,))
    sizes = (4 * ROWS + EXTRA, 2 * ROWS + EXTRA, 2 * ROWS + EXTRA)
    packed, x_mine, x_other = call(
        functools.partial(pack_cross_kernel, enc_dev, loop), "pack_cross", info,
        [whole_spec(neighbour_ids.shape[::-1])] + [mine_spec] * 2 + [their_spec] * 2 + [their_pool],
        (neighbour_ids.T, cross_queries, grad_cross, cross_queries, grad_cross, pool),
        [spec(rows) for rows in sizes],
        [((rows, WIDE), BF16) for rows in sizes],
    )
    x_same = send(x_mine, outward, True)
    x_cross = send(x_other, across, True)
    x_pair = send(packed, swap, False)
    queries_in, packed = lax.optimization_barrier((queries, packed))
    sizes = (4 * ROWS, 2 * ROWS, 2 * ROWS)
    packed, s_mine, s_other = call(
        pack_self_kernel, "pack_self", info,
        [mine_spec] * 2 + [their_spec] * 4,
        (queries_in, grad_self, queries_in, grad_self, keys, values),
        [spec(rows) for rows in sizes],
        [((rows, WIDE), BF16) for rows in sizes],
    )
    s_pair = send(packed, swap, False)

    ids_of = lambda d: lax.dynamic_slice_in_dim(doc_ids, d * ROWS, ROWS, 0)
    span = jnp.arange(ROWS, dtype=jnp.int32)
    base = me // 2 * 2
    places = jnp.concatenate([span + base * ROWS, span + (base + 1) * ROWS])
    near0, near1, far0, far1 = [ids_of(base + j) for j in range(4)]
    near = jnp.concatenate([near0, near1])
    near_flip = jnp.concatenate([near1, near0])
    far_flip = jnp.concatenate([far1, far0])
    local_ok = (near[:, None] == near[None, :]) & (places[:, None] <= places[None, :])
    far_ok = (near_flip[:, None] == far_flip[None, :]) & (base + 2 < loop)
    local_bias = jnp.where(local_ok, 0.0, MASKED).astype(F32)
    far_bias = jnp.where(far_ok, 0.0, MASKED).astype(F32)

    bias_spec = whole_spec((2 * ROWS, 2 * ROWS))
    local_bias, far_bias, x_pair = lax.optimization_barrier((local_bias, far_bias, x_pair))
    self_specs = [bias_spec] + [own_spec()] * 4 + [spec(ROWS, j) for j in range(4)]
    self_args = (local_bias, queries, grad_self, keys, values) + (s_pair,) * 4
    mine_w = whole_spec((EXTRA, WIDE), (2 * ROWS // EXTRA, 0))
    partner_w = whole_spec((EXTRA, WIDE), (4 * ROWS // EXTRA, 0))
    cross_specs = (
        [mine_w, partner_w, own_spec(), own_spec(), own_spec((2,))]
        + [spec(ROWS, j) for j in range(4)]
    )
    cross_args = (x_mine, x_pair, cross_queries, grad_cross, pool) + (x_pair,) * 4
    stat = lambda rows: ((HALF, 8, rows), F32)

    x_own, x_partner = call(
        per_head(cross_stats_kernel), "cross_stats", info, cross_specs, cross_args,
        [stat_spec(ROWS)] * 2, [stat(ROWS)] * 2, flops=0,
    )
    t_same = send(x_own, outward, True)
    t_cross = send(x_partner, inward, True)
    local_bias, x_own = lax.optimization_barrier((local_bias, x_own))
    self_args = (local_bias,) + self_args[1:]
    (s_own,) = call(
        per_head(self_stats_kernel), "self_stats", info, self_specs, self_args,
        [stat_spec(2 * ROWS)], [stat(2 * ROWS)], flops=0,
    )
    t_self = send(s_own, lambda d: d - 2, False)
    s_mine, x_same, x_cross, t_same, t_cross, s_own = lax.optimization_barrier(
        (s_mine, x_same, x_cross, t_same, t_cross, s_own)
    )
    s_same = send(s_mine, lambda d: d - 2, False)

    kv_out = spec(4 * ROWS)
    kv_shape = ((4 * ROWS, WIDE), BF16)
    q_shape = ((ROWS, WIDE), BF16)
    xd_same, xd_cross, x_kv, x_fin_same, x_fin_cross = call(
        per_head(cross_remote_kernel), "cross_remote", info,
        [mine_w, mine_w, spec(ROWS, 0), spec(ROWS, 1), spec(ROWS, 0), spec(ROWS, 1)]
        + [own_spec((2,)), spec(ROWS, 2), spec(ROWS, 3), stat_spec(ROWS), stat_spec(ROWS)],
        (x_same, x_cross, x_same, x_same, x_cross, x_cross, pool, x_pair, x_pair, t_same, t_cross),
        [spec(ROWS), spec(ROWS), kv_out, stat_spec(ROWS), stat_spec(ROWS)],
        [q_shape, q_shape, kv_shape, stat(ROWS), stat(ROWS)],
    )
    f_own = send(x_fin_same, inward, True)
    f_partner = send(x_fin_cross, outward, True)
    s_other, x_kv = lax.optimization_barrier((s_other, x_kv))
    s_cross = send(s_other, lambda d: (d - 2) ^ 1, False)
    xd_same, xd_cross, f_own, f_partner = lax.optimization_barrier(
        (xd_same, xd_cross, f_own, f_partner)
    )
    xr_same = send(xd_same, inward, True)
    xr_cross = send(xd_cross, across, True)

    x_kv, s_same, t_self = lax.optimization_barrier((x_kv, s_same, t_self))
    half_out = spec(3 * ROWS)
    half_shape = ((3 * ROWS, WIDE), BF16)
    x_keep, x_give = call(
        per_head(cross_local_kernel), "cross_local", info,
        cross_specs + [stat_spec(ROWS), stat_spec(ROWS), spec(4 * ROWS)],
        cross_args + (f_own, f_partner, x_kv),
        [half_out] * 2, [half_shape] * 2, flops=LONG,
    )

    far_bias, x_keep = lax.optimization_barrier((far_bias, x_keep))
    sd_same, sd_cross, s_kv, s_fin = call(
        per_head(self_remote_kernel), "self_remote", info,
        [bias_spec, spec(ROWS, 0), spec(ROWS, 1), spec(ROWS, 0), spec(ROWS, 1)]
        + [own_spec(), own_spec(), spec(ROWS, 2), spec(ROWS, 3), stat_spec(2 * ROWS)],
        (far_bias, s_same, s_same, s_cross, s_cross, keys, values, s_pair, s_pair, t_self),
        [spec(ROWS), spec(ROWS), kv_out, stat_spec(2 * ROWS)],
        [q_shape, q_shape, kv_shape, stat(2 * ROWS)], flops=LONG,
    )
    f_self = send(s_fin, lambda d: d + 2, False)
    sr_same = send(sd_same, lambda d: d + 2, False)
    sr_cross = send(sd_cross, lambda d: (d + 2) ^ 1, False)

    x_give, s_kv, xr_same, xr_cross, f_self = lax.optimization_barrier(
        (x_give, s_kv, xr_same, xr_cross, f_self)
    )
    x_take = send(x_give, swap, False)
    s_keep, s_give = call(
        per_head(self_local_kernel), "self_local", info,
        self_specs + [stat_spec(2 * ROWS), stat_spec(2 * ROWS), spec(4 * ROWS)],
        self_args + (f_self, s_own, s_kv),
        [half_out] * 2, [half_shape] * 2, flops=LONG,
    )
    grad_cq, grad_pool = assemble(
        cross_final_kernel, "cross_final", info, (x_keep, x_take, xr_same, xr_cross), True
    )
    s_give, sr_same, sr_cross, grad_cq = lax.optimization_barrier(
        (s_give, sr_same, sr_cross, grad_cq)
    )
    s_take = send(s_give, swap, False)
    grad_q, grad_k, grad_v = assemble(
        self_final_kernel, "self_final", info, (s_keep, s_take, sr_same, sr_cross), False
    )
    return grad_q, grad_k, grad_v, grad_cq, grad_pool.reshape(pool_kv.shape)


def solution(mesh):
    rows = P(("groups", "ctx"), None)
    pool = P(None, ("groups", "ctx"), None, None)
    return jax.shard_map(
        body,
        mesh=mesh,
        in_specs=(rows, rows, rows, rows, P("groups"), rows, rows, pool, rows),
        out_specs=(rows, rows, rows, rows, pool),
        check_vma=False,
    )
```

```python
import functools
import math

import jax
import jax.numpy as jnp
from jax import lax
from jax.experimental import pallas as pl
from jax.experimental.pallas import tpu as pltpu
from jax.sharding import PartitionSpec as P

HEADS = 8
HEAD_DIM = 128
HALF = HEADS // 2
WIDE = HALF * HEAD_DIM
STEP = 2
COLS = STEP * HEAD_DIM
STEPS = HALF // STEP
STRETCH = 64
NBR_TOK = 128
ROWS = 256
EXTRA = 16
LONG = 12 * 10**9
FACTOR = HEAD_DIM ** (-0.5)
MASKED = -1e30
BF16 = jnp.bfloat16
F32 = jnp.float32


def send(value, target_of, wrap):
    count = lax.axis_size("ctx")
    pairs = []
    for source in range(count):
        target = target_of(source)
        if wrap:
            pairs.append((source, target % count))
        elif 0 <= target < count:
            pairs.append((source, target))
    return lax.ppermute(value, "ctx", pairs)


def swap(d):
    return d ^ 1


def outward(d):
    return d - 2 if d % 2 == 0 else d + 2


def inward(d):
    return d + 2 if d % 2 == 0 else d - 2


def across(d):
    return d - 1 if d % 2 == 0 else d + 1


def spec(rows, row_block=0):
    return pl.BlockSpec((rows, COLS), lambda h, info: (row_block, h))


def own_spec(lead=()):
    zeros = (0,) * len(lead)
    return pl.BlockSpec(lead + (ROWS, COLS), lambda h, info: zeros + (0, info[0] % 2 * STEPS + h))


def other_spec(lead=()):
    zeros = (0,) * len(lead)
    return pl.BlockSpec(
        lead + (ROWS, COLS), lambda h, info: zeros + (0, (1 - info[0] % 2) * STEPS + h)
    )


def whole_spec(shape, index=None):
    index = (0,) * len(shape) if index is None else index
    return pl.BlockSpec(shape, lambda h, *info: index)


def stat_spec(rows):
    return pl.BlockSpec((STEP, 8, rows), lambda h, info: (h, 0, 0))


def call(kernel, name, info, in_specs, inputs, out_specs, outs, steps=STEPS, flops=0):
    return pl.pallas_call(
        kernel,
        name=name,
        grid_spec=pltpu.PrefetchScalarGridSpec(
            num_scalar_prefetch=1,
            grid=(steps,),
            in_specs=in_specs,
            out_specs=out_specs,
        ),
        out_shape=[jax.ShapeDtypeStruct(shape, dtype) for shape, dtype in outs],
        compiler_params=pltpu.CompilerParams(vmem_limit_bytes=63 << 20),
        cost_estimate=pl.CostEstimate(flops=flops, transcendentals=0, bytes_accessed=0),
    )(info, *[pltpu.with_memory_space_constraint(x, pltpu.HBM) for x in inputs])


def head_of(ref, j):
    shape = ref.shape
    if len(shape) == 3 and shape[1] == 8:
        return ref.at[j : j + 1]
    if shape[-1] != COLS:
        return ref
    place = pl.ds(j * HEAD_DIM, HEAD_DIM)
    return ref.at[:, place] if len(shape) == 2 else ref.at[:, :, place]


def per_head(kernel):
    def run(info, *refs):
        for j in range(STEP):
            kernel(info, *[head_of(ref, j) for ref in refs])

    return run


def dot_last(a, b):
    return lax.dot_general(a, b, (((1,), (1,)), ((), ())), preferred_element_type=F32)


def dot_first(a, b):
    return lax.dot_general(a, b, (((0,), (0,)), ((), ())), preferred_element_type=F32)


def dot(a, b):
    return jnp.dot(a, b, preferred_element_type=F32)


def both(a, b):
    return jnp.concatenate([a, b], axis=0)


def weight_rows(times):
    log_two = jnp.where(times > 1.5, math.log(2.0), 0.0)
    return jnp.where(times < 0.5, MASKED, log_two)


def slot_pair(ref, first, core, second=None):
    times = ref[...].astype(F32)[:, :ROWS]
    low = times[first : first + 2]
    if second is None:
        return weight_rows(low)
    return weight_rows(jnp.where(core == 0, low, times[second : second + 2]))


def add_rows(s, rows):
    parts = [
        s[e * NBR_TOK : (e + 1) * NBR_TOK] + rows[e : e + 1] for e in range(s.shape[0] // NBR_TOK)
    ]
    return jnp.concatenate(parts, axis=0)


def partial_stats(s, dp):
    peak = jnp.max(s, axis=0, keepdims=True)
    e = jnp.exp(s - peak)
    return e, peak, jnp.sum(e, axis=0, keepdims=True), jnp.sum(e * dp, axis=0, keepdims=True)


def stat_rows(a, b, c):
    return jnp.concatenate([a, b, c, jnp.zeros((5, a.shape[1]), F32)], axis=0)[None]


def merge(stats, mine):
    t_peak, t_total, t_moment = stats[0, 0:1], stats[0, 1:2], stats[0, 2:3]
    peak, total, moment = mine
    top = jnp.maximum(t_peak, peak)
    t_scale = jnp.exp(t_peak - top)
    scale = jnp.exp(peak - top)
    full = t_total * t_scale + total * scale
    inverse = jnp.where(full > 0, 1.0 / full, 0.0)
    delta = (t_moment * t_scale + moment * scale) * inverse
    return top, inverse, delta, scale * inverse


def gradients(p, dp, delta, q, g, k):
    pb = p.astype(BF16)
    ds = (p * (dp - delta)).astype(BF16)
    return dot_first(ds, k) * FACTOR, dot(ds, q) * FACTOR, dot(pb, g)


def pack_cross_kernel(enc_dev, loop, info, ids_ref, qm, gm, q, g, pool, swap_ref, mine, other):
    shape = (EXTRA, mine.shape[1])
    row = lax.broadcasted_iota(jnp.int32, shape, 0)
    lane = lax.broadcasted_iota(jnp.int32, shape, 1) + pl.program_id(0) * shape[1]
    ids = ids_ref[...]
    owner = ids // enc_dev
    relative = owner - info[0] + 1
    relative = jnp.where(relative < 0, relative + loop, relative)
    relative = jnp.where(relative >= loop, relative - loop, relative)
    slots = relative * enc_dev + ids - owner * enc_dev
    times = jnp.zeros(shape, F32)
    for n in range(ids.shape[0]):
        for s in range(ids.shape[1]):
            hit = (row == slots[n : n + 1, s : s + 1]) & (lane // STRETCH == s)
            times = times + jnp.where(hit, 1.0, 0.0)
    times = times.astype(BF16)
    swap_ref[0:ROWS] = q[...]
    swap_ref[ROWS : 2 * ROWS] = g[...]
    swap_ref[2 * ROWS : 3 * ROWS] = pool[0]
    swap_ref[3 * ROWS : 4 * ROWS] = pool[1]
    swap_ref[4 * ROWS :] = times
    for out, first, second in ((mine, qm, gm), (other, q, g)):
        out[0:ROWS] = first[...]
        out[ROWS : 2 * ROWS] = second[...]
        out[2 * ROWS :] = times


def pack_self_kernel(info, qm, gm, q, g, k, v, swap_ref, mine, other):
    for index, ref in enumerate((q, g, k, v)):
        swap_ref[index * ROWS : (index + 1) * ROWS] = ref[...]
    for out, first, second in ((mine, qm, gm), (other, q, g)):
        out[0:ROWS] = first[...]
        out[ROWS : 2 * ROWS] = second[...]


def ordered(core, a, b):
    return jnp.where(core == 0, a, b), jnp.where(core == 0, b, a)


def wide_scores(keys_x, keys_y, values_x, values_y, qs, gs, bias):
    sx = dot_last(keys_x, qs) * FACTOR + bias[:ROWS]
    sy = dot_last(keys_y, qs[ROWS:]) * FACTOR + bias[ROWS:, ROWS:]
    return sx, sy, dot_last(values_x, gs), dot_last(values_y, gs[ROWS:])


def wide_stats(sx, sy, dpx, dpy):
    peak = jnp.max(sx, axis=0, keepdims=True)
    peak_y = jnp.maximum(peak[:, ROWS:], jnp.max(sy, axis=0, keepdims=True))
    peak = jnp.concatenate([peak[:, :ROWS], peak_y], axis=1)
    ex, ey = jnp.exp(sx - peak), jnp.exp(sy - peak_y)
    widen = lambda a, b: jnp.concatenate([a[:, :ROWS], a[:, ROWS:] + b], axis=1)
    add = lambda a: jnp.sum(a, axis=0, keepdims=True)
    return ex, ey, peak, widen(add(ex), add(ey)), widen(add(ex * dpx), add(ey * dpy))


def wide_gradients(px, py, dpx, dpy, delta, qs, gs, kx, ky):
    pbx, pby = px.astype(BF16), py.astype(BF16)
    dsx = (px * (dpx - delta)).astype(BF16)
    dsy = (py * (dpy - delta[:, ROWS:])).astype(BF16)
    dq_z = dot_first(dsx[:, :ROWS], kx) * FACTOR
    dq_y = dot_first(both(dsx[:, ROWS:], dsy), both(kx, ky)) * FACTOR
    dkx, dky = dot(dsx, qs) * FACTOR, dot(dsy, qs[ROWS:]) * FACTOR
    return dq_z, dq_y, dkx, dky, dot(pbx, gs), dot(pby, gs[ROWS:])


def local_self(core, bias, q, g, k, v, pq, pg, pk, pv):
    q0, q1 = ordered(core, q[...], pq[...])
    g0, g1 = ordered(core, g[...], pg[...])
    k0, k1 = ordered(core, k[...], pk[...])
    v0, v1 = ordered(core, v[...], pv[...])
    qs, gs = both(q0, q1), both(g0, g1)
    return wide_scores(k0, k1, v0, v1, qs, gs, bias[...]), qs, gs, k0, k1


def local_cross(core, w, pw, q, g, pool, pq, pg, pk, pv):
    qs, gs = both(q[...], pq[...]), both(g[...], pg[...])
    ks, vs = both(pool[0], pk[...]), both(pool[1], pv[...])
    own = both(slot_pair(w, 2, core), slot_pair(w, 4, core, 0))
    partner = both(slot_pair(pw, 0, core, 4), slot_pair(pw, 2, core))
    s = add_rows(dot_last(ks, qs) * FACTOR, jnp.concatenate([own, partner], axis=1))
    return s, dot_last(vs, gs), qs, gs, ks


def self_stats_kernel(info, *refs):
    scores = local_self(info[0] % 2, *refs[:-1])[0]
    refs[-1][...] = stat_rows(*wide_stats(*scores)[2:])


def cross_stats_kernel(info, *refs):
    s, dp, _, _, _ = local_cross(info[0] % 2, *refs[:-2])
    stats = stat_rows(*partial_stats(s, dp)[1:])
    refs[-2][...] = stats[:, :, :ROWS]
    refs[-1][...] = stats[:, :, ROWS:]


def self_remote_kernel(
    info, bias, sq, sg, cq, cg, k, v, pk, pv, stats, dq_ref, kv_ref, out_stats
):
    core = info[0] % 2
    q0, q1 = ordered(core, sq[...], cq[...])
    g0, g1 = ordered(core, sg[...], cg[...])
    k0, k1 = ordered(core, k[...], pk[...])
    v0, v1 = ordered(core, v[...], pv[...])
    qs, gs = both(q1, q0), both(g1, g0)
    sx, sy, dpx, dpy = wide_scores(k1, k0, v1, v0, qs, gs, bias[...])
    ex, ey, *mine = wide_stats(sx, sy, dpx, dpy)
    known = stats[...]
    known = jnp.concatenate([known[:, :, ROWS:], known[:, :, :ROWS]], axis=2)
    top, inverse, delta, scale = merge(known, mine)
    px, py = ex * scale, ey * scale[:, ROWS:]
    dq1, dq0, dk1, dk0, dv1, dv0 = wide_gradients(px, py, dpx, dpy, delta, qs, gs, k1, k0)
    same, cross = ordered(core, dq0, dq1)
    dq_ref[:ROWS] = same.astype(BF16)
    dq_ref[ROWS:] = cross.astype(BF16)
    for index, grad in enumerate(ordered(core, dk0, dk1) + ordered(core, dv0, dv1)):
        kv_ref[index * ROWS : (index + 1) * ROWS] = grad.astype(BF16)
    out_stats[...] = stat_rows(top, inverse, delta)


def cross_remote_kernel(
    info, sw, cw, sq, sg, cq, cg, pool, pk, pv, s_stats, c_stats, *outs
):
    dq_same, dq_cross, kv_ref, out_same, out_cross = outs
    core = info[0] % 2
    jobs = (
        (cq, cg, pool[0], pool[1], slot_pair(cw, 4, core, 0), c_stats, dq_cross, out_cross, 0),
        (sq, sg, pk[...], pv[...], slot_pair(sw, 0, core, 4), s_stats, dq_same, out_same, 1),
    )
    for q, g, k, v, rows, stats, dq_ref, out_stats, place in jobs:
        s, dp = add_rows(dot_last(k, q[...]) * FACTOR, rows), dot_last(v, g[...])
        e, *mine = partial_stats(s, dp)
        top, inverse, delta, scale = merge(stats[...], mine)
        dq, dk, dv = gradients(e * scale, dp, delta, q[...], g[...], k)
        dq_ref[...] = dq.astype(BF16)
        out_stats[...] = stat_rows(top, inverse, delta)
        kv_ref[place * ROWS : (place + 1) * ROWS] = dk.astype(BF16)
        kv_ref[(2 + place) * ROWS : (3 + place) * ROWS] = dv.astype(BF16)


def self_local_kernel(info, *refs):
    stats_ref, own_ref, kv_ref, mine, theirs = refs[-5:]
    local = own_ref[0]
    core = info[0] % 2
    first = info[0] < 2
    stats = stats_ref[0]
    stats = jnp.concatenate([stats[:, ROWS:], stats[:, :ROWS]], axis=1)
    inverse = 1.0 / local[1:2]
    top = jnp.where(first, local[0:1], stats[0:1])
    delta = jnp.where(first, local[2:3] * inverse, stats[2:3])
    inverse = jnp.where(first, inverse, stats[1:2])
    (sx, sy, dpx, dpy), qs, gs, k0, k1 = local_self(core, *refs[:-5])
    px = jnp.exp(sx - top) * inverse
    py = jnp.exp(sy - top[:, ROWS:]) * inverse[:, ROWS:]
    dq0, dq1, dk0, dk1, dv0, dv1 = wide_gradients(px, py, dpx, dpy, delta, qs, gs, k0, k1)
    grads = (ordered(core, dq0, dq1), ordered(core, dk0, dk1), ordered(core, dv0, dv1))
    for index, pair in enumerate(grads):
        for out, place, grad in ((mine, 0, pair[0]), (theirs, 1, pair[1])):
            if index > 0:
                low = (2 * index - 2 + place) * ROWS
                grad = grad + kv_ref[low : low + ROWS].astype(F32)
            out[index * ROWS : (index + 1) * ROWS] = grad.astype(BF16)


def cross_local_kernel(info, *refs):
    own_stats, partner_stats, kv_ref, mine, theirs = refs[-5:]
    stats = jnp.concatenate([own_stats[0], partner_stats[0]], axis=1)
    top, inverse, delta = stats[0:1], stats[1:2], stats[2:3]
    s, dp, qs, gs, ks = local_cross(info[0] % 2, *refs[:-5])
    dq, dk, dv = gradients(jnp.exp(s - top) * inverse, dp, delta, qs, gs, ks)
    dk = dk + kv_ref[: 2 * ROWS].astype(F32)
    dv = dv + kv_ref[2 * ROWS :].astype(F32)
    for index, grad in enumerate((dq, dk, dv)):
        mine[index * ROWS : (index + 1) * ROWS] = grad[:ROWS].astype(BF16)
        theirs[index * ROWS : (index + 1) * ROWS] = grad[ROWS:].astype(BF16)


def self_final_kernel(info, mine, theirs, dq_mine, dq_theirs, *outs):
    def write(source, extra):
        dq = source[:ROWS].astype(F32) + extra[...].astype(F32)
        outs[0][...] = dq.astype(BF16)
        outs[1][...] = source[ROWS : 2 * ROWS]
        outs[2][...] = source[2 * ROWS :]

    pl.when(pl.program_id(0) == 0)(lambda: write(mine, dq_mine))
    pl.when(pl.program_id(0) == 1)(lambda: write(theirs, dq_theirs))


def cross_final_kernel(info, mine, theirs, dq_mine, dq_theirs, dq_out, pool_out):
    def write(source, extra):
        dq = source[:ROWS].astype(F32) + extra[...].astype(F32)
        dq_out[...] = dq.astype(BF16)
        pool_out[0] = source[ROWS : 2 * ROWS]
        pool_out[1] = source[2 * ROWS :]

    pl.when(pl.program_id(0) == 0)(lambda: write(mine, dq_mine))
    pl.when(pl.program_id(0) == 1)(lambda: write(theirs, dq_theirs))


def assemble(kernel, name, info, inputs, pooled):
    half = lambda h, info: (info[0] + h) % 2
    rows_out = pl.BlockSpec((ROWS, WIDE), lambda h, info: (0, half(h, info)))
    pool_out = pl.BlockSpec((2, ROWS, WIDE), lambda h, info: (0, 0, half(h, info)))
    full = ((ROWS, 2 * WIDE), BF16)
    if pooled:
        out_specs, outs = [rows_out, pool_out], [full, ((2, ROWS, 2 * WIDE), BF16)]
    else:
        out_specs, outs = [rows_out] * 3, [full] * 3
    in_specs = [whole_spec(x.shape) for x in inputs]
    if not pooled:
        in_specs[2:] = [whole_spec((ROWS, WIDE)), whole_spec((ROWS, WIDE), (1, 0))]
    return call(kernel, name, info, in_specs, inputs, out_specs, outs, steps=2)


def body(
    queries, keys, values, grad_self, doc_ids, cross_queries, grad_cross, pool_kv, neighbour_ids
):
    loop = lax.axis_size("ctx")
    me = lax.axis_index("ctx").astype(jnp.int32)
    info = jnp.full((1,), me, jnp.int32)
    enc_dev = pool_kv.shape[1]
    width = queries.shape[1]
    pool = pool_kv.reshape(2, ROWS, width)

    mine_spec, their_spec, their_pool = own_spec(), other_spec(), other_spec((2,))
    sizes = (4 * ROWS + EXTRA, 2 * ROWS + EXTRA, 2 * ROWS + EXTRA)
    packed, x_mine, x_other = call(
        functools.partial(pack_cross_kernel, enc_dev, loop), "pack_cross", info,
        [whole_spec(neighbour_ids.shape[::-1])] + [mine_spec] * 2 + [their_spec] * 2 + [their_pool],
        (neighbour_ids.T, cross_queries, grad_cross, cross_queries, grad_cross, pool),
        [spec(rows) for rows in sizes],
        [((rows, WIDE), BF16) for rows in sizes],
    )
    x_same = send(x_mine, outward, True)
    x_cross = send(x_other, across, True)
    x_pair = send(packed, swap, False)
    queries_in, packed = lax.optimization_barrier((queries, packed))
    sizes = (4 * ROWS, 2 * ROWS, 2 * ROWS)
    packed, s_mine, s_other = call(
        pack_self_kernel, "pack_self", info,
        [mine_spec] * 2 + [their_spec] * 4,
        (queries_in, grad_self, queries_in, grad_self, keys, values),
        [spec(rows) for rows in sizes],
        [((rows, WIDE), BF16) for rows in sizes],
    )
    s_pair = send(packed, swap, False)

    ids_of = lambda d: lax.dynamic_slice_in_dim(doc_ids, d * ROWS, ROWS, 0)
    span = jnp.arange(ROWS, dtype=jnp.int32)
    base = me // 2 * 2
    places = jnp.concatenate([span + base * ROWS, span + (base + 1) * ROWS])
    near0, near1, far0, far1 = [ids_of(base + j) for j in range(4)]
    near = jnp.concatenate([near0, near1])
    near_flip = jnp.concatenate([near1, near0])
    far_flip = jnp.concatenate([far1, far0])
    local_ok = (near[:, None] == near[None, :]) & (places[:, None] <= places[None, :])
    far_ok = (near_flip[:, None] == far_flip[None, :]) & (base + 2 < loop)
    local_bias = jnp.where(local_ok, 0.0, MASKED).astype(F32)
    far_bias = jnp.where(far_ok, 0.0, MASKED).astype(F32)

    bias_spec = whole_spec((2 * ROWS, 2 * ROWS))
    local_bias, far_bias, x_pair = lax.optimization_barrier((local_bias, far_bias, x_pair))
    self_specs = [bias_spec] + [own_spec()] * 4 + [spec(ROWS, j) for j in range(4)]
    self_args = (local_bias, queries, grad_self, keys, values) + (s_pair,) * 4
    mine_w = whole_spec((EXTRA, WIDE), (2 * ROWS // EXTRA, 0))
    partner_w = whole_spec((EXTRA, WIDE), (4 * ROWS // EXTRA, 0))
    cross_specs = (
        [mine_w, partner_w, own_spec(), own_spec(), own_spec((2,))]
        + [spec(ROWS, j) for j in range(4)]
    )
    cross_args = (x_mine, x_pair, cross_queries, grad_cross, pool) + (x_pair,) * 4
    stat = lambda rows: ((HALF, 8, rows), F32)

    x_own, x_partner = call(
        per_head(cross_stats_kernel), "cross_stats", info, cross_specs, cross_args,
        [stat_spec(ROWS)] * 2, [stat(ROWS)] * 2, flops=0,
    )
    t_same = send(x_own, outward, True)
    t_cross = send(x_partner, inward, True)
    local_bias, x_own = lax.optimization_barrier((local_bias, x_own))
    self_args = (local_bias,) + self_args[1:]
    (s_own,) = call(
        per_head(self_stats_kernel), "self_stats", info, self_specs, self_args,
        [stat_spec(2 * ROWS)], [stat(2 * ROWS)], flops=0,
    )
    t_self = send(s_own, lambda d: d - 2, False)
    s_mine, x_same, x_cross, t_same, t_cross, s_own = lax.optimization_barrier(
        (s_mine, x_same, x_cross, t_same, t_cross, s_own)
    )
    s_same = send(s_mine, lambda d: d - 2, False)

    kv_out = spec(4 * ROWS)
    kv_shape = ((4 * ROWS, WIDE), BF16)
    q_shape = ((ROWS, WIDE), BF16)
    xd_same, xd_cross, x_kv, x_fin_same, x_fin_cross = call(
        per_head(cross_remote_kernel), "cross_remote", info,
        [mine_w, mine_w, spec(ROWS, 0), spec(ROWS, 1), spec(ROWS, 0), spec(ROWS, 1)]
        + [own_spec((2,)), spec(ROWS, 2), spec(ROWS, 3), stat_spec(ROWS), stat_spec(ROWS)],
        (x_same, x_cross, x_same, x_same, x_cross, x_cross, pool, x_pair, x_pair, t_same, t_cross),
        [spec(ROWS), spec(ROWS), kv_out, stat_spec(ROWS), stat_spec(ROWS)],
        [q_shape, q_shape, kv_shape, stat(ROWS), stat(ROWS)],
    )
    f_own = send(x_fin_same, inward, True)
    f_partner = send(x_fin_cross, outward, True)
    s_other, x_kv = lax.optimization_barrier((s_other, x_kv))
    s_cross = send(s_other, lambda d: (d - 2) ^ 1, False)
    x_kv, s_same, t_self = lax.optimization_barrier((x_kv, s_same, t_self))
    half_out = spec(3 * ROWS)
    half_shape = ((3 * ROWS, WIDE), BF16)
    x_keep, x_give = call(
        per_head(cross_local_kernel), "cross_local", info,
        cross_specs + [stat_spec(ROWS), stat_spec(ROWS), spec(4 * ROWS)],
        cross_args + (f_own, f_partner, x_kv),
        [half_out] * 2, [half_shape] * 2, flops=LONG,
    )

    xd_same, xd_cross, s_cross, x_keep = lax.optimization_barrier(
        (xd_same, xd_cross, s_cross, x_keep)
    )
    xr_same = send(xd_same, inward, True)
    xr_cross = send(xd_cross, across, True)
    far_bias, x_keep = lax.optimization_barrier((far_bias, x_keep))
    sd, s_kv, s_fin = call(
        per_head(self_remote_kernel), "self_remote", info,
        [bias_spec, spec(ROWS, 0), spec(ROWS, 1), spec(ROWS, 0), spec(ROWS, 1)]
        + [own_spec(), own_spec(), spec(ROWS, 2), spec(ROWS, 3), stat_spec(2 * ROWS)],
        (far_bias, s_same, s_same, s_cross, s_cross, keys, values, s_pair, s_pair, t_self),
        [spec(2 * ROWS), kv_out, stat_spec(2 * ROWS)],
        [((2 * ROWS, WIDE), BF16), kv_shape, stat(2 * ROWS)], flops=LONG,
    )
    f_self = send(s_fin, lambda d: d + 2, False)
    sr = send(sd, lambda d: d + 2, False)

    x_give, s_kv, xr_same, xr_cross, f_self = lax.optimization_barrier(
        (x_give, s_kv, xr_same, xr_cross, f_self)
    )
    x_take = send(x_give, swap, False)
    s_keep, s_give = call(
        per_head(self_local_kernel), "self_local", info,
        self_specs + [stat_spec(2 * ROWS), stat_spec(2 * ROWS), spec(4 * ROWS)],
        self_args + (f_self, s_own, s_kv),
        [half_out] * 2, [half_shape] * 2, flops=LONG,
    )
    grad_cq, grad_pool = assemble(
        cross_final_kernel, "cross_final", info, (x_keep, x_take, xr_same, xr_cross), True
    )
    s_give, sr, grad_cq = lax.optimization_barrier((s_give, sr, grad_cq))
    s_take = send(s_give, swap, False)
    sr_take = send(sr, swap, False)
    grad_q, grad_k, grad_v = assemble(
        self_final_kernel, "self_final", info, (s_keep, s_take, sr, sr_take), False
    )
    return grad_q, grad_k, grad_v, grad_cq, grad_pool.reshape(pool_kv.shape)


def solution(mesh):
    rows = P(("groups", "ctx"), None)
    pool = P(None, ("groups", "ctx"), None, None)
    return jax.shard_map(
        body,
        mesh=mesh,
        in_specs=(rows, rows, rows, rows, P("groups"), rows, rows, pool, rows),
        out_specs=(rows, rows, rows, rows, pool),
        check_vma=False,
    )
```

```python
import functools
import math

import jax
import jax.numpy as jnp
from jax import lax
from jax.experimental import pallas as pl
from jax.experimental.pallas import tpu as pltpu
from jax.sharding import PartitionSpec as P

HEADS = 8
HEAD_DIM = 128
HALF = HEADS // 2
WIDE = HALF * HEAD_DIM
STEP = 2
COLS = STEP * HEAD_DIM
STEPS = HALF // STEP
STRETCH = 64
NBR_TOK = 128
ROWS = 256
EXTRA = 16
LONG = 12 * 10**9
FACTOR = HEAD_DIM ** (-0.5)
MASKED = -1e30
BF16 = jnp.bfloat16
F32 = jnp.float32


def send(value, target_of, wrap):
    count = lax.axis_size("ctx")
    pairs = []
    for source in range(count):
        target = target_of(source)
        if wrap:
            pairs.append((source, target % count))
        elif 0 <= target < count:
            pairs.append((source, target))
    return lax.ppermute(value, "ctx", pairs)


def swap(d):
    return d ^ 1


def outward(d):
    return d - 2 if d % 2 == 0 else d + 2


def inward(d):
    return d + 2 if d % 2 == 0 else d - 2


def across(d):
    return d - 1 if d % 2 == 0 else d + 1


def spec(rows, row_block=0):
    return pl.BlockSpec((rows, COLS), lambda h, info: (row_block, h))


def own_spec(lead=()):
    zeros = (0,) * len(lead)
    return pl.BlockSpec(lead + (ROWS, COLS), lambda h, info: zeros + (0, info[0] % 2 * STEPS + h))


def other_spec(lead=()):
    zeros = (0,) * len(lead)
    return pl.BlockSpec(
        lead + (ROWS, COLS), lambda h, info: zeros + (0, (1 - info[0] % 2) * STEPS + h)
    )


def whole_spec(shape, index=None):
    index = (0,) * len(shape) if index is None else index
    return pl.BlockSpec(shape, lambda h, *info: index)


def stat_spec(rows):
    return pl.BlockSpec((STEP, 8, rows), lambda h, info: (h, 0, 0))


def call(kernel, name, info, in_specs, inputs, out_specs, outs, steps=STEPS, flops=0):
    return pl.pallas_call(
        kernel,
        name=name,
        grid_spec=pltpu.PrefetchScalarGridSpec(
            num_scalar_prefetch=1,
            grid=(steps,),
            in_specs=in_specs,
            out_specs=out_specs,
        ),
        out_shape=[jax.ShapeDtypeStruct(shape, dtype) for shape, dtype in outs],
        compiler_params=pltpu.CompilerParams(vmem_limit_bytes=64 << 20),
        cost_estimate=pl.CostEstimate(flops=flops, transcendentals=0, bytes_accessed=0),
    )(info, *inputs)


def head_of(ref, j):
    shape = ref.shape
    if len(shape) == 3 and shape[1] == 8:
        return ref.at[j : j + 1]
    if shape[-1] != COLS:
        return ref
    place = pl.ds(j * HEAD_DIM, HEAD_DIM)
    return ref.at[:, place] if len(shape) == 2 else ref.at[:, :, place]


def per_head(kernel):
    def run(info, *refs):
        for j in range(STEP):
            kernel(info, *[head_of(ref, j) for ref in refs])

    return run


def dot_last(a, b):
    return lax.dot_general(a, b, (((1,), (1,)), ((), ())), preferred_element_type=F32)


def dot_first(a, b):
    return lax.dot_general(a, b, (((0,), (0,)), ((), ())), preferred_element_type=F32)


def dot(a, b):
    return jnp.dot(a, b, preferred_element_type=F32)


def both(a, b):
    return jnp.concatenate([a, b], axis=0)


def weight_rows(times):
    log_two = jnp.where(times > 1.5, math.log(2.0), 0.0)
    return jnp.where(times < 0.5, MASKED, log_two)


def slot_pair(ref, first, core, second=None):
    times = ref[...].astype(F32)[:, :ROWS]
    low = times[first : first + 2]
    if second is None:
        return weight_rows(low)
    return weight_rows(jnp.where(core == 0, low, times[second : second + 2]))


def add_rows(s, rows):
    parts = [
        s[e * NBR_TOK : (e + 1) * NBR_TOK] + rows[e : e + 1] for e in range(s.shape[0] // NBR_TOK)
    ]
    return jnp.concatenate(parts, axis=0)


def partial_stats(s, dp):
    peak = jnp.max(s, axis=0, keepdims=True)
    e = jnp.exp(s - peak)
    return e, peak, jnp.sum(e, axis=0, keepdims=True), jnp.sum(e * dp, axis=0, keepdims=True)


def stat_rows(a, b, c):
    return jnp.concatenate([a, b, c, jnp.zeros((5, a.shape[1]), F32)], axis=0)[None]


def merge(stats, mine):
    t_peak, t_total, t_moment = stats[0, 0:1], stats[0, 1:2], stats[0, 2:3]
    peak, total, moment = mine
    top = jnp.maximum(t_peak, peak)
    t_scale = jnp.exp(t_peak - top)
    scale = jnp.exp(peak - top)
    full = t_total * t_scale + total * scale
    inverse = jnp.where(full > 0, 1.0 / full, 0.0)
    delta = (t_moment * t_scale + moment * scale) * inverse
    return top, inverse, delta, scale * inverse


def gradients(p, dp, delta, q, g, k):
    pb = p.astype(BF16)
    ds = (p * (dp - delta)).astype(BF16)
    return dot_first(ds, k) * FACTOR, dot(ds, q) * FACTOR, dot(pb, g)


def pack_cross_kernel(enc_dev, loop, info, ids_ref, qm, gm, q, g, pool, swap_ref, mine, other):
    shape = (EXTRA, mine.shape[1])
    row = lax.broadcasted_iota(jnp.int32, shape, 0)
    lane = lax.broadcasted_iota(jnp.int32, shape, 1) + pl.program_id(0) * shape[1]
    ids = ids_ref[...]
    owner = ids // enc_dev
    relative = owner - info[0] + 1
    relative = jnp.where(relative < 0, relative + loop, relative)
    relative = jnp.where(relative >= loop, relative - loop, relative)
    slots = relative * enc_dev + ids - owner * enc_dev
    times = jnp.zeros(shape, F32)
    for n in range(ids.shape[0]):
        for s in range(ids.shape[1]):
            hit = (row == slots[n : n + 1, s : s + 1]) & (lane // STRETCH == s)
            times = times + jnp.where(hit, 1.0, 0.0)
    times = times.astype(BF16)
    swap_ref[0:ROWS] = q[...]
    swap_ref[ROWS : 2 * ROWS] = g[...]
    swap_ref[2 * ROWS : 3 * ROWS] = pool[0]
    swap_ref[3 * ROWS : 4 * ROWS] = pool[1]
    swap_ref[4 * ROWS :] = times
    for out, first, second in ((mine, qm, gm), (other, q, g)):
        out[0:ROWS] = first[...]
        out[ROWS : 2 * ROWS] = second[...]
        out[2 * ROWS :] = times


def pack_self_kernel(info, qm, gm, q, g, k, v, swap_ref, mine, other):
    for index, ref in enumerate((q, g, k, v)):
        swap_ref[index * ROWS : (index + 1) * ROWS] = ref[...]
    for out, first, second in ((mine, qm, gm), (other, q, g)):
        out[0:ROWS] = first[...]
        out[ROWS : 2 * ROWS] = second[...]


def ordered(core, a, b):
    return jnp.where(core == 0, a, b), jnp.where(core == 0, b, a)


def wide_scores(keys_x, keys_y, values_x, values_y, qs, gs, bias):
    sx = dot_last(keys_x, qs) * FACTOR + bias[:ROWS]
    sy = dot_last(keys_y, qs[ROWS:]) * FACTOR + bias[ROWS:, ROWS:]
    return sx, sy, dot_last(values_x, gs), dot_last(values_y, gs[ROWS:])


def wide_stats(sx, sy, dpx, dpy):
    peak = jnp.max(sx, axis=0, keepdims=True)
    peak_y = jnp.maximum(peak[:, ROWS:], jnp.max(sy, axis=0, keepdims=True))
    peak = jnp.concatenate([peak[:, :ROWS], peak_y], axis=1)
    ex, ey = jnp.exp(sx - peak), jnp.exp(sy - peak_y)
    widen = lambda a, b: jnp.concatenate([a[:, :ROWS], a[:, ROWS:] + b], axis=1)
    add = lambda a: jnp.sum(a, axis=0, keepdims=True)
    return ex, ey, peak, widen(add(ex), add(ey)), widen(add(ex * dpx), add(ey * dpy))


def wide_gradients(px, py, dpx, dpy, delta, qs, gs, kx, ky):
    pbx, pby = px.astype(BF16), py.astype(BF16)
    dsx = (px * (dpx - delta)).astype(BF16)
    dsy = (py * (dpy - delta[:, ROWS:])).astype(BF16)
    dq_z = dot_first(dsx[:, :ROWS], kx) * FACTOR
    dq_y = dot_first(both(dsx[:, ROWS:], dsy), both(kx, ky)) * FACTOR
    dkx, dky = dot(dsx, qs) * FACTOR, dot(dsy, qs[ROWS:]) * FACTOR
    return dq_z, dq_y, dkx, dky, dot(pbx, gs), dot(pby, gs[ROWS:])


def local_self(core, bias, q, g, k, v, pq, pg, pk, pv):
    q0, q1 = ordered(core, q[...], pq[...])
    g0, g1 = ordered(core, g[...], pg[...])
    k0, k1 = ordered(core, k[...], pk[...])
    v0, v1 = ordered(core, v[...], pv[...])
    qs, gs = both(q0, q1), both(g0, g1)
    return wide_scores(k0, k1, v0, v1, qs, gs, bias[...]), qs, gs, k0, k1


def local_cross(core, w, pw, q, g, pool, pq, pg, pk, pv):
    qs, gs = both(q[...], pq[...]), both(g[...], pg[...])
    ks, vs = both(pool[0], pk[...]), both(pool[1], pv[...])
    own = both(slot_pair(w, 2, core), slot_pair(w, 4, core, 0))
    partner = both(slot_pair(pw, 0, core, 4), slot_pair(pw, 2, core))
    s = add_rows(dot_last(ks, qs) * FACTOR, jnp.concatenate([own, partner], axis=1))
    return s, dot_last(vs, gs), qs, gs, ks


def self_stats_kernel(info, *refs):
    scores = local_self(info[0] % 2, *refs[:-1])[0]
    refs[-1][...] = stat_rows(*wide_stats(*scores)[2:])


def cross_stats_kernel(info, *refs):
    s, dp, _, _, _ = local_cross(info[0] % 2, *refs[:-2])
    stats = stat_rows(*partial_stats(s, dp)[1:])
    refs[-2][...] = stats[:, :, :ROWS]
    refs[-1][...] = stats[:, :, ROWS:]


def self_remote_kernel(
    info, bias, sq, sg, cq, cg, k, v, pk, pv, stats, dq_ref, kv_ref, out_stats
):
    core = info[0] % 2
    q0, q1 = ordered(core, sq[...], cq[...])
    g0, g1 = ordered(core, sg[...], cg[...])
    k0, k1 = ordered(core, k[...], pk[...])
    v0, v1 = ordered(core, v[...], pv[...])
    qs, gs = both(q1, q0), both(g1, g0)
    sx, sy, dpx, dpy = wide_scores(k1, k0, v1, v0, qs, gs, bias[...])
    ex, ey, *mine = wide_stats(sx, sy, dpx, dpy)
    known = stats[...]
    known = jnp.concatenate([known[:, :, ROWS:], known[:, :, :ROWS]], axis=2)
    top, inverse, delta, scale = merge(known, mine)
    px, py = ex * scale, ey * scale[:, ROWS:]
    dq1, dq0, dk1, dk0, dv1, dv0 = wide_gradients(px, py, dpx, dpy, delta, qs, gs, k1, k0)
    same, cross = ordered(core, dq0, dq1)
    dq_ref[:ROWS] = same.astype(BF16)
    dq_ref[ROWS:] = cross.astype(BF16)
    for index, grad in enumerate(ordered(core, dk0, dk1) + ordered(core, dv0, dv1)):
        kv_ref[index * ROWS : (index + 1) * ROWS] = grad.astype(BF16)
    out_stats[...] = stat_rows(top, inverse, delta)


def cross_remote_kernel(
    info, sw, cw, sq, sg, cq, cg, pool, pk, pv, s_stats, c_stats, *outs
):
    dq_same, dq_cross, kv_ref, out_same, out_cross = outs
    core = info[0] % 2
    jobs = (
        (cq, cg, pool[0], pool[1], slot_pair(cw, 4, core, 0), c_stats, dq_cross, out_cross, 0),
        (sq, sg, pk[...], pv[...], slot_pair(sw, 0, core, 4), s_stats, dq_same, out_same, 1),
    )
    for q, g, k, v, rows, stats, dq_ref, out_stats, place in jobs:
        s, dp = add_rows(dot_last(k, q[...]) * FACTOR, rows), dot_last(v, g[...])
        e, *mine = partial_stats(s, dp)
        top, inverse, delta, scale = merge(stats[...], mine)
        dq, dk, dv = gradients(e * scale, dp, delta, q[...], g[...], k)
        dq_ref[...] = dq.astype(BF16)
        out_stats[...] = stat_rows(top, inverse, delta)
        kv_ref[place * ROWS : (place + 1) * ROWS] = dk.astype(BF16)
        kv_ref[(2 + place) * ROWS : (3 + place) * ROWS] = dv.astype(BF16)


def self_local_kernel(info, *refs):
    stats_ref, own_ref, kv_ref, mine, theirs = refs[-5:]
    local = own_ref[0]
    core = info[0] % 2
    first = info[0] < 2
    stats = stats_ref[0]
    stats = jnp.concatenate([stats[:, ROWS:], stats[:, :ROWS]], axis=1)
    inverse = 1.0 / local[1:2]
    top = jnp.where(first, local[0:1], stats[0:1])
    delta = jnp.where(first, local[2:3] * inverse, stats[2:3])
    inverse = jnp.where(first, inverse, stats[1:2])
    (sx, sy, dpx, dpy), qs, gs, k0, k1 = local_self(core, *refs[:-5])
    px = jnp.exp(sx - top) * inverse
    py = jnp.exp(sy - top[:, ROWS:]) * inverse[:, ROWS:]
    dq0, dq1, dk0, dk1, dv0, dv1 = wide_gradients(px, py, dpx, dpy, delta, qs, gs, k0, k1)
    grads = (ordered(core, dq0, dq1), ordered(core, dk0, dk1), ordered(core, dv0, dv1))
    for index, pair in enumerate(grads):
        for out, place, grad in ((mine, 0, pair[0]), (theirs, 1, pair[1])):
            if index > 0:
                low = (2 * index - 2 + place) * ROWS
                grad = grad + kv_ref[low : low + ROWS].astype(F32)
            out[index * ROWS : (index + 1) * ROWS] = grad.astype(BF16)


def cross_local_kernel(info, *refs):
    own_stats, partner_stats, kv_ref, mine, theirs = refs[-5:]
    stats = jnp.concatenate([own_stats[0], partner_stats[0]], axis=1)
    top, inverse, delta = stats[0:1], stats[1:2], stats[2:3]
    s, dp, qs, gs, ks = local_cross(info[0] % 2, *refs[:-5])
    dq, dk, dv = gradients(jnp.exp(s - top) * inverse, dp, delta, qs, gs, ks)
    dk = dk + kv_ref[: 2 * ROWS].astype(F32)
    dv = dv + kv_ref[2 * ROWS :].astype(F32)
    for index, grad in enumerate((dq, dk, dv)):
        mine[index * ROWS : (index + 1) * ROWS] = grad[:ROWS].astype(BF16)
        theirs[index * ROWS : (index + 1) * ROWS] = grad[ROWS:].astype(BF16)


def self_final_kernel(info, mine, theirs, dq_mine, dq_theirs, *outs):
    def write(source, extra):
        dq = source[:ROWS].astype(F32) + extra[...].astype(F32)
        outs[0][...] = dq.astype(BF16)
        outs[1][...] = source[ROWS : 2 * ROWS]
        outs[2][...] = source[2 * ROWS :]

    pl.when(pl.program_id(0) == 0)(lambda: write(mine, dq_mine))
    pl.when(pl.program_id(0) == 1)(lambda: write(theirs, dq_theirs))


def cross_final_kernel(info, mine, theirs, dq_mine, dq_theirs, dq_out, pool_out):
    def write(source, extra):
        dq = source[:ROWS].astype(F32) + extra[...].astype(F32)
        dq_out[...] = dq.astype(BF16)
        pool_out[0] = source[ROWS : 2 * ROWS]
        pool_out[1] = source[2 * ROWS :]

    pl.when(pl.program_id(0) == 0)(lambda: write(mine, dq_mine))
    pl.when(pl.program_id(0) == 1)(lambda: write(theirs, dq_theirs))


def assemble(kernel, name, info, inputs, pooled):
    half = lambda h, info: (info[0] + h) % 2
    rows_out = pl.BlockSpec((ROWS, WIDE), lambda h, info: (0, half(h, info)))
    pool_out = pl.BlockSpec((2, ROWS, WIDE), lambda h, info: (0, 0, half(h, info)))
    full = ((ROWS, 2 * WIDE), BF16)
    if pooled:
        out_specs, outs = [rows_out, pool_out], [full, ((2, ROWS, 2 * WIDE), BF16)]
    else:
        out_specs, outs = [rows_out] * 3, [full] * 3
    in_specs = [whole_spec(x.shape) for x in inputs]
    if not pooled:
        in_specs[2:] = [whole_spec((ROWS, WIDE)), whole_spec((ROWS, WIDE), (1, 0))]
    return call(kernel, name, info, in_specs, inputs, out_specs, outs, steps=2)


def body(
    queries, keys, values, grad_self, doc_ids, cross_queries, grad_cross, pool_kv, neighbour_ids
):
    loop = lax.axis_size("ctx")
    me = lax.axis_index("ctx").astype(jnp.int32)
    info = jnp.full((1,), me, jnp.int32)
    enc_dev = pool_kv.shape[1]
    width = queries.shape[1]
    pool = pool_kv.reshape(2, ROWS, width)

    mine_spec, their_spec, their_pool = own_spec(), other_spec(), other_spec((2,))
    sizes = (4 * ROWS + EXTRA, 2 * ROWS + EXTRA, 2 * ROWS + EXTRA)
    packed, x_mine, x_other = call(
        functools.partial(pack_cross_kernel, enc_dev, loop), "pack_cross", info,
        [whole_spec(neighbour_ids.shape[::-1])] + [mine_spec] * 2 + [their_spec] * 2 + [their_pool],
        (neighbour_ids.T, cross_queries, grad_cross, cross_queries, grad_cross, pool),
        [spec(rows) for rows in sizes],
        [((rows, WIDE), BF16) for rows in sizes],
    )
    x_same = send(x_mine, outward, True)
    x_cross = send(x_other, across, True)
    x_pair = send(packed, swap, False)
    queries_in, packed = lax.optimization_barrier((queries, packed))
    sizes = (4 * ROWS, 2 * ROWS, 2 * ROWS)
    packed, s_mine, s_other = call(
        pack_self_kernel, "pack_self", info,
        [mine_spec] * 2 + [their_spec] * 4,
        (queries_in, grad_self, queries_in, grad_self, keys, values),
        [spec(rows) for rows in sizes],
        [((rows, WIDE), BF16) for rows in sizes],
    )
    s_pair = send(packed, swap, False)

    ids_of = lambda d: lax.dynamic_slice_in_dim(doc_ids, d * ROWS, ROWS, 0)
    span = jnp.arange(ROWS, dtype=jnp.int32)
    base = me // 2 * 2
    places = jnp.concatenate([span + base * ROWS, span + (base + 1) * ROWS])
    near0, near1, far0, far1 = [ids_of(base + j) for j in range(4)]
    near = jnp.concatenate([near0, near1])
    near_flip = jnp.concatenate([near1, near0])
    far_flip = jnp.concatenate([far1, far0])
    local_ok = (near[:, None] == near[None, :]) & (places[:, None] <= places[None, :])
    far_ok = (near_flip[:, None] == far_flip[None, :]) & (base + 2 < loop)
    local_bias = jnp.where(local_ok, 0.0, MASKED).astype(F32)
    far_bias = jnp.where(far_ok, 0.0, MASKED).astype(F32)

    bias_spec = whole_spec((2 * ROWS, 2 * ROWS))
    local_bias, far_bias, x_pair = lax.optimization_barrier((local_bias, far_bias, x_pair))
    self_specs = [bias_spec] + [own_spec()] * 4 + [spec(ROWS, j) for j in range(4)]
    self_args = (local_bias, queries, grad_self, keys, values) + (s_pair,) * 4
    mine_w = whole_spec((EXTRA, WIDE), (2 * ROWS // EXTRA, 0))
    partner_w = whole_spec((EXTRA, WIDE), (4 * ROWS // EXTRA, 0))
    cross_specs = (
        [mine_w, partner_w, own_spec(), own_spec(), own_spec((2,))]
        + [spec(ROWS, j) for j in range(4)]
    )
    cross_args = (x_mine, x_pair, cross_queries, grad_cross, pool) + (x_pair,) * 4
    stat = lambda rows: ((HALF, 8, rows), F32)

    x_own, x_partner = call(
        per_head(cross_stats_kernel), "cross_stats", info, cross_specs, cross_args,
        [stat_spec(ROWS)] * 2, [stat(ROWS)] * 2, flops=0,
    )
    t_same = send(x_own, outward, True)
    t_cross = send(x_partner, inward, True)
    local_bias, x_own = lax.optimization_barrier((local_bias, x_own))
    self_args = (local_bias,) + self_args[1:]
    (s_own,) = call(
        per_head(self_stats_kernel), "self_stats", info, self_specs, self_args,
        [stat_spec(2 * ROWS)], [stat(2 * ROWS)], flops=0,
    )
    t_self = send(s_own, lambda d: d - 2, False)
    s_mine, s_own = lax.optimization_barrier((s_mine, s_own))
    s_same = send(s_mine, lambda d: d - 2, False)
    s_other, x_same, x_cross, t_same, t_cross, s_own = lax.optimization_barrier(
        (s_other, x_same, x_cross, t_same, t_cross, s_own)
    )
    s_cross = send(s_other, lambda d: (d - 2) ^ 1, False)

    kv_out = spec(4 * ROWS)
    kv_shape = ((4 * ROWS, WIDE), BF16)
    q_shape = ((ROWS, WIDE), BF16)
    xd_same, xd_cross, x_kv, x_fin_same, x_fin_cross = call(
        per_head(cross_remote_kernel), "cross_remote", info,
        [mine_w, mine_w, spec(ROWS, 0), spec(ROWS, 1), spec(ROWS, 0), spec(ROWS, 1)]
        + [own_spec((2,)), spec(ROWS, 2), spec(ROWS, 3), stat_spec(ROWS), stat_spec(ROWS)],
        (x_same, x_cross, x_same, x_same, x_cross, x_cross, pool, x_pair, x_pair, t_same, t_cross),
        [spec(ROWS), spec(ROWS), kv_out, stat_spec(ROWS), stat_spec(ROWS)],
        [q_shape, q_shape, kv_shape, stat(ROWS), stat(ROWS)],
    )
    f_own = send(x_fin_same, inward, True)
    f_partner = send(x_fin_cross, outward, True)
    half_out = spec(3 * ROWS)
    half_shape = ((3 * ROWS, WIDE), BF16)
    x_keep, x_give = call(
        per_head(cross_local_kernel), "cross_local", info,
        cross_specs + [stat_spec(ROWS), stat_spec(ROWS), spec(4 * ROWS)],
        cross_args + (f_own, f_partner, x_kv),
        [half_out] * 2, [half_shape] * 2, flops=0,
    )

    xd_same, xd_cross, s_cross, x_keep = lax.optimization_barrier(
        (xd_same, xd_cross, s_cross, x_keep)
    )
    xr_same = send(xd_same, inward, True)
    xr_cross = send(xd_cross, across, True)
    far_bias, x_keep = lax.optimization_barrier((far_bias, x_keep))
    sd, s_kv, s_fin = call(
        per_head(self_remote_kernel), "self_remote", info,
        [bias_spec, spec(ROWS, 0), spec(ROWS, 1), spec(ROWS, 0), spec(ROWS, 1)]
        + [own_spec(), own_spec(), spec(ROWS, 2), spec(ROWS, 3), stat_spec(2 * ROWS)],
        (far_bias, s_same, s_same, s_cross, s_cross, keys, values, s_pair, s_pair, t_self),
        [spec(2 * ROWS), kv_out, stat_spec(2 * ROWS)],
        [((2 * ROWS, WIDE), BF16), kv_shape, stat(2 * ROWS)], flops=LONG,
    )
    f_self = send(s_fin, lambda d: d + 2, False)
    sr = send(sd, lambda d: d + 2, False)

    x_give, s_kv, xr_same, xr_cross, f_self = lax.optimization_barrier(
        (x_give, s_kv, xr_same, xr_cross, f_self)
    )
    x_take = send(x_give, swap, False)
    s_keep, s_give = call(
        per_head(self_local_kernel), "self_local", info,
        self_specs + [stat_spec(2 * ROWS), stat_spec(2 * ROWS), spec(4 * ROWS)],
        self_args + (f_self, s_own, s_kv),
        [half_out] * 2, [half_shape] * 2, flops=LONG,
    )
    grad_cq, grad_pool = assemble(
        cross_final_kernel, "cross_final", info, (x_keep, x_take, xr_same, xr_cross), True
    )
    s_give, sr, grad_cq = lax.optimization_barrier((s_give, sr, grad_cq))
    s_take = send(s_give, swap, False)
    sr_take = send(sr, swap, False)
    grad_q, grad_k, grad_v = assemble(
        self_final_kernel, "self_final", info, (s_keep, s_take, sr, sr_take), False
    )
    return grad_q, grad_k, grad_v, grad_cq, grad_pool.reshape(pool_kv.shape)


def solution(mesh):
    rows = P(("groups", "ctx"), None)
    pool = P(None, ("groups", "ctx"), None, None)
    return jax.shard_map(
        body,
        mesh=mesh,
        in_specs=(rows, rows, rows, rows, P("groups"), rows, rows, pool, rows),
        out_specs=(rows, rows, rows, rows, pool),
        check_vma=False,
    )
```

```python
import functools
import math

import jax
import jax.numpy as jnp
from jax import lax
from jax.experimental import pallas as pl
from jax.experimental.pallas import tpu as pltpu
from jax.sharding import PartitionSpec as P

HEADS = 8
HEAD_DIM = 128
HALF = HEADS // 2
WIDE = HALF * HEAD_DIM
STEP = 2
COLS = STEP * HEAD_DIM
STEPS = HALF // STEP
STRETCH = 64
NBR_TOK = 128
ROWS = 256
EXTRA = 16
LONG = 12 * 10**9
FACTOR = HEAD_DIM ** (-0.5)
MASKED = -1e30
BF16 = jnp.bfloat16
F32 = jnp.float32


def send(value, target_of, wrap):
    count = lax.axis_size("ctx")
    pairs = []
    for source in range(count):
        target = target_of(source)
        if wrap:
            pairs.append((source, target % count))
        elif 0 <= target < count:
            pairs.append((source, target))
    return lax.ppermute(value, "ctx", pairs)


def swap(d):
    return d ^ 1


def outward(d):
    return d - 2 if d % 2 == 0 else d + 2


def inward(d):
    return d + 2 if d % 2 == 0 else d - 2


def across(d):
    return d - 1 if d % 2 == 0 else d + 1


def spec(rows, row_block=0):
    return pl.BlockSpec((rows, COLS), lambda h, info: (row_block, h))


def own_spec(lead=()):
    zeros = (0,) * len(lead)
    return pl.BlockSpec(lead + (ROWS, COLS), lambda h, info: zeros + (0, info[0] % 2 * STEPS + h))


def other_spec(lead=()):
    zeros = (0,) * len(lead)
    return pl.BlockSpec(
        lead + (ROWS, COLS), lambda h, info: zeros + (0, (1 - info[0] % 2) * STEPS + h)
    )


def whole_spec(shape, index=None):
    index = (0,) * len(shape) if index is None else index
    return pl.BlockSpec(shape, lambda h, *info: index)


def stat_spec(rows):
    return pl.BlockSpec((STEP, 8, rows), lambda h, info: (h, 0, 0))


def call(kernel, name, info, in_specs, inputs, out_specs, outs, steps=STEPS, flops=0):
    return pl.pallas_call(
        kernel,
        name=name,
        grid_spec=pltpu.PrefetchScalarGridSpec(
            num_scalar_prefetch=1,
            grid=(steps,),
            in_specs=in_specs,
            out_specs=out_specs,
        ),
        out_shape=[jax.ShapeDtypeStruct(shape, dtype) for shape, dtype in outs],
        compiler_params=pltpu.CompilerParams(vmem_limit_bytes=64 << 20),
        cost_estimate=pl.CostEstimate(flops=flops, transcendentals=0, bytes_accessed=0),
    )(info, *inputs)


def head_of(ref, j):
    shape = ref.shape
    if len(shape) == 3 and shape[1] == 8:
        return ref.at[j : j + 1]
    if shape[-1] != COLS:
        return ref
    place = pl.ds(j * HEAD_DIM, HEAD_DIM)
    return ref.at[:, place] if len(shape) == 2 else ref.at[:, :, place]


def per_head(kernel):
    def run(info, *refs):
        for j in range(STEP):
            kernel(info, *[head_of(ref, j) for ref in refs])

    return run


def dot_last(a, b):
    return lax.dot_general(a, b, (((1,), (1,)), ((), ())), preferred_element_type=F32)


def dot_first(a, b):
    return lax.dot_general(a, b, (((0,), (0,)), ((), ())), preferred_element_type=F32)


def dot(a, b):
    return jnp.dot(a, b, preferred_element_type=F32)


def both(a, b):
    return jnp.concatenate([a, b], axis=0)


def weight_rows(times):
    log_two = jnp.where(times > 1.5, math.log(2.0), 0.0)
    return jnp.where(times < 0.5, MASKED, log_two)


def slot_pair(ref, first, core, second=None):
    times = ref[...].astype(F32)[:, :ROWS]
    low = times[first : first + 2]
    if second is None:
        return weight_rows(low)
    return weight_rows(jnp.where(core == 0, low, times[second : second + 2]))


def add_rows(s, rows):
    parts = [
        s[e * NBR_TOK : (e + 1) * NBR_TOK] + rows[e : e + 1] for e in range(s.shape[0] // NBR_TOK)
    ]
    return jnp.concatenate(parts, axis=0)


def partial_stats(s, dp):
    peak = jnp.max(s, axis=0, keepdims=True)
    e = jnp.exp(s - peak)
    return e, peak, jnp.sum(e, axis=0, keepdims=True), jnp.sum(e * dp, axis=0, keepdims=True)


def stat_rows(a, b, c):
    return jnp.concatenate([a, b, c, jnp.zeros((5, a.shape[1]), F32)], axis=0)[None]


def merge(stats, mine):
    t_peak, t_total, t_moment = stats[0, 0:1], stats[0, 1:2], stats[0, 2:3]
    peak, total, moment = mine
    top = jnp.maximum(t_peak, peak)
    t_scale = jnp.exp(t_peak - top)
    scale = jnp.exp(peak - top)
    full = t_total * t_scale + total * scale
    inverse = jnp.where(full > 0, 1.0 / full, 0.0)
    delta = (t_moment * t_scale + moment * scale) * inverse
    return top, inverse, delta, scale * inverse


def gradients(p, dp, delta, q, g, k):
    pb = p.astype(BF16)
    ds = (p * (dp - delta)).astype(BF16)
    return dot_first(ds, k) * FACTOR, dot(ds, q) * FACTOR, dot(pb, g)


def pack_cross_kernel(enc_dev, loop, info, ids_ref, qm, gm, q, g, pool, swap_ref, mine, other):
    shape = (EXTRA, mine.shape[1])
    row = lax.broadcasted_iota(jnp.int32, shape, 0)
    lane = lax.broadcasted_iota(jnp.int32, shape, 1) + pl.program_id(0) * shape[1]
    ids = ids_ref[...]
    owner = ids // enc_dev
    relative = owner - info[0] + 1
    relative = jnp.where(relative < 0, relative + loop, relative)
    relative = jnp.where(relative >= loop, relative - loop, relative)
    slots = relative * enc_dev + ids - owner * enc_dev
    times = jnp.zeros(shape, F32)
    for n in range(ids.shape[0]):
        for s in range(ids.shape[1]):
            hit = (row == slots[n : n + 1, s : s + 1]) & (lane // STRETCH == s)
            times = times + jnp.where(hit, 1.0, 0.0)
    times = times.astype(BF16)
    swap_ref[0:ROWS] = q[...]
    swap_ref[ROWS : 2 * ROWS] = g[...]
    swap_ref[2 * ROWS : 3 * ROWS] = pool[0]
    swap_ref[3 * ROWS : 4 * ROWS] = pool[1]
    swap_ref[4 * ROWS :] = times
    for out, first, second in ((mine, qm, gm), (other, q, g)):
        out[0:ROWS] = first[...]
        out[ROWS : 2 * ROWS] = second[...]
        out[2 * ROWS :] = times


def pack_self_kernel(info, qm, gm, q, g, k, v, swap_ref, mine, other):
    for index, ref in enumerate((q, g, k, v)):
        swap_ref[index * ROWS : (index + 1) * ROWS] = ref[...]
    for out, first, second in ((mine, qm, gm), (other, q, g)):
        out[0:ROWS] = first[...]
        out[ROWS : 2 * ROWS] = second[...]


def ordered(core, a, b):
    return jnp.where(core == 0, a, b), jnp.where(core == 0, b, a)


def wide_scores(keys_x, keys_y, values_x, values_y, qs, gs, bias):
    sx = dot_last(keys_x, qs) * FACTOR + bias[:ROWS]
    sy = dot_last(keys_y, qs[ROWS:]) * FACTOR + bias[ROWS:, ROWS:]
    return sx, sy, dot_last(values_x, gs), dot_last(values_y, gs[ROWS:])


def wide_stats(sx, sy, dpx, dpy):
    peak = jnp.max(sx, axis=0, keepdims=True)
    peak_y = jnp.maximum(peak[:, ROWS:], jnp.max(sy, axis=0, keepdims=True))
    peak = jnp.concatenate([peak[:, :ROWS], peak_y], axis=1)
    ex, ey = jnp.exp(sx - peak), jnp.exp(sy - peak_y)
    widen = lambda a, b: jnp.concatenate([a[:, :ROWS], a[:, ROWS:] + b], axis=1)
    add = lambda a: jnp.sum(a, axis=0, keepdims=True)
    return ex, ey, peak, widen(add(ex), add(ey)), widen(add(ex * dpx), add(ey * dpy))


def wide_gradients(px, py, dpx, dpy, delta, qs, gs, kx, ky):
    pbx, pby = px.astype(BF16), py.astype(BF16)
    dsx = (px * (dpx - delta)).astype(BF16)
    dsy = (py * (dpy - delta[:, ROWS:])).astype(BF16)
    dq_z = dot_first(dsx[:, :ROWS], kx) * FACTOR
    dq_y = dot_first(both(dsx[:, ROWS:], dsy), both(kx, ky)) * FACTOR
    dkx, dky = dot(dsx, qs) * FACTOR, dot(dsy, qs[ROWS:]) * FACTOR
    return dq_z, dq_y, dkx, dky, dot(pbx, gs), dot(pby, gs[ROWS:])


def local_self(core, bias, q, g, k, v, pq, pg, pk, pv):
    q0, q1 = ordered(core, q[...], pq[...])
    g0, g1 = ordered(core, g[...], pg[...])
    k0, k1 = ordered(core, k[...], pk[...])
    v0, v1 = ordered(core, v[...], pv[...])
    qs, gs = both(q0, q1), both(g0, g1)
    return wide_scores(k0, k1, v0, v1, qs, gs, bias[...]), qs, gs, k0, k1


def local_cross(core, w, pw, q, g, pool, pq, pg, pk, pv):
    qs, gs = both(q[...], pq[...]), both(g[...], pg[...])
    ks, vs = both(pool[0], pk[...]), both(pool[1], pv[...])
    own = both(slot_pair(w, 2, core), slot_pair(w, 4, core, 0))
    partner = both(slot_pair(pw, 0, core, 4), slot_pair(pw, 2, core))
    s = add_rows(dot_last(ks, qs) * FACTOR, jnp.concatenate([own, partner], axis=1))
    return s, dot_last(vs, gs), qs, gs, ks


def self_stats_kernel(info, *refs):
    scores = local_self(info[0] % 2, *refs[:-1])[0]
    refs[-1][...] = stat_rows(*wide_stats(*scores)[2:])


def cross_stats_kernel(info, *refs):
    s, dp, _, _, _ = local_cross(info[0] % 2, *refs[:-2])
    stats = stat_rows(*partial_stats(s, dp)[1:])
    refs[-2][...] = stats[:, :, :ROWS]
    refs[-1][...] = stats[:, :, ROWS:]


def self_remote_kernel(
    info, bias, sq, sg, cq, cg, k, v, pk, pv, stats, dq_ref, kv_ref, out_stats
):
    core = info[0] % 2
    q0, q1 = ordered(core, sq[...], cq[...])
    g0, g1 = ordered(core, sg[...], cg[...])
    k0, k1 = ordered(core, k[...], pk[...])
    v0, v1 = ordered(core, v[...], pv[...])
    qs, gs = both(q1, q0), both(g1, g0)
    sx, sy, dpx, dpy = wide_scores(k1, k0, v1, v0, qs, gs, bias[...])
    ex, ey, *mine = wide_stats(sx, sy, dpx, dpy)
    known = stats[...]
    known = jnp.concatenate([known[:, :, ROWS:], known[:, :, :ROWS]], axis=2)
    top, inverse, delta, scale = merge(known, mine)
    px, py = ex * scale, ey * scale[:, ROWS:]
    dq1, dq0, dk1, dk0, dv1, dv0 = wide_gradients(px, py, dpx, dpy, delta, qs, gs, k1, k0)
    same, cross = ordered(core, dq0, dq1)
    dq_ref[:ROWS] = same.astype(BF16)
    dq_ref[ROWS:] = cross.astype(BF16)
    for index, grad in enumerate(ordered(core, dk0, dk1) + ordered(core, dv0, dv1)):
        kv_ref[index * ROWS : (index + 1) * ROWS] = grad.astype(BF16)
    out_stats[...] = stat_rows(top, inverse, delta)


def cross_remote_kernel(
    info, sw, cw, sq, sg, cq, cg, pool, pk, pv, s_stats, c_stats, *outs
):
    dq_same, dq_cross, kv_ref, out_same, out_cross = outs
    core = info[0] % 2
    jobs = (
        (cq, cg, pool[0], pool[1], slot_pair(cw, 4, core, 0), c_stats, dq_cross, out_cross, 0),
        (sq, sg, pk[...], pv[...], slot_pair(sw, 0, core, 4), s_stats, dq_same, out_same, 1),
    )
    for q, g, k, v, rows, stats, dq_ref, out_stats, place in jobs:
        s, dp = add_rows(dot_last(k, q[...]) * FACTOR, rows), dot_last(v, g[...])
        e, *mine = partial_stats(s, dp)
        top, inverse, delta, scale = merge(stats[...], mine)
        dq, dk, dv = gradients(e * scale, dp, delta, q[...], g[...], k)
        dq_ref[...] = dq.astype(BF16)
        out_stats[...] = stat_rows(top, inverse, delta)
        kv_ref[place * ROWS : (place + 1) * ROWS] = dk.astype(BF16)
        kv_ref[(2 + place) * ROWS : (3 + place) * ROWS] = dv.astype(BF16)


def self_local_kernel(info, *refs):
    stats_ref, own_ref, kv_ref, mine, theirs = refs[-5:]
    local = own_ref[0]
    core = info[0] % 2
    first = info[0] < 2
    stats = stats_ref[0]
    stats = jnp.concatenate([stats[:, ROWS:], stats[:, :ROWS]], axis=1)
    inverse = 1.0 / local[1:2]
    top = jnp.where(first, local[0:1], stats[0:1])
    delta = jnp.where(first, local[2:3] * inverse, stats[2:3])
    inverse = jnp.where(first, inverse, stats[1:2])
    (sx, sy, dpx, dpy), qs, gs, k0, k1 = local_self(core, *refs[:-5])
    px = jnp.exp(sx - top) * inverse
    py = jnp.exp(sy - top[:, ROWS:]) * inverse[:, ROWS:]
    dq0, dq1, dk0, dk1, dv0, dv1 = wide_gradients(px, py, dpx, dpy, delta, qs, gs, k0, k1)
    grads = (ordered(core, dq0, dq1), ordered(core, dk0, dk1), ordered(core, dv0, dv1))
    for index, pair in enumerate(grads):
        for out, place, grad in ((mine, 0, pair[0]), (theirs, 1, pair[1])):
            if index > 0:
                low = (2 * index - 2 + place) * ROWS
                grad = grad + kv_ref[low : low + ROWS].astype(F32)
            out[index * ROWS : (index + 1) * ROWS] = grad.astype(BF16)


def cross_local_kernel(info, *refs):
    own_stats, partner_stats, kv_ref, mine, theirs = refs[-5:]
    stats = jnp.concatenate([own_stats[0], partner_stats[0]], axis=1)
    top, inverse, delta = stats[0:1], stats[1:2], stats[2:3]
    s, dp, qs, gs, ks = local_cross(info[0] % 2, *refs[:-5])
    dq, dk, dv = gradients(jnp.exp(s - top) * inverse, dp, delta, qs, gs, ks)
    dk = dk + kv_ref[: 2 * ROWS].astype(F32)
    dv = dv + kv_ref[2 * ROWS :].astype(F32)
    for index, grad in enumerate((dq, dk, dv)):
        mine[index * ROWS : (index + 1) * ROWS] = grad[:ROWS].astype(BF16)
        theirs[index * ROWS : (index + 1) * ROWS] = grad[ROWS:].astype(BF16)


def self_final_kernel(info, mine, theirs, dq_mine, dq_theirs, *outs):
    def write(source, extra):
        dq = source[:ROWS].astype(F32) + extra[...].astype(F32)
        outs[0][...] = dq.astype(BF16)
        outs[1][...] = source[ROWS : 2 * ROWS]
        outs[2][...] = source[2 * ROWS :]

    pl.when(pl.program_id(0) == 0)(lambda: write(mine, dq_mine))
    pl.when(pl.program_id(0) == 1)(lambda: write(theirs, dq_theirs))


def cross_final_kernel(info, mine, theirs, dq_mine, dq_theirs, dq_out, pool_out):
    def write(source, extra):
        dq = source[:ROWS].astype(F32) + extra[...].astype(F32)
        dq_out[...] = dq.astype(BF16)
        pool_out[0] = source[ROWS : 2 * ROWS]
        pool_out[1] = source[2 * ROWS :]

    pl.when(pl.program_id(0) == 0)(lambda: write(mine, dq_mine))
    pl.when(pl.program_id(0) == 1)(lambda: write(theirs, dq_theirs))


def assemble(kernel, name, info, inputs, pooled):
    half = lambda h, info: (info[0] + h) % 2
    rows_out = pl.BlockSpec((ROWS, WIDE), lambda h, info: (0, half(h, info)))
    pool_out = pl.BlockSpec((2, ROWS, WIDE), lambda h, info: (0, 0, half(h, info)))
    full = ((ROWS, 2 * WIDE), BF16)
    if pooled:
        out_specs, outs = [rows_out, pool_out], [full, ((2, ROWS, 2 * WIDE), BF16)]
    else:
        out_specs, outs = [rows_out] * 3, [full] * 3
    in_specs = [whole_spec(x.shape) for x in inputs]
    if not pooled:
        in_specs[2:] = [whole_spec((ROWS, WIDE)), whole_spec((ROWS, WIDE), (1, 0))]
    return call(kernel, name, info, in_specs, inputs, out_specs, outs, steps=2)


def body(
    queries, keys, values, grad_self, doc_ids, cross_queries, grad_cross, pool_kv, neighbour_ids
):
    loop = lax.axis_size("ctx")
    me = lax.axis_index("ctx").astype(jnp.int32)
    info = jnp.full((1,), me, jnp.int32)
    enc_dev = pool_kv.shape[1]
    width = queries.shape[1]
    pool = pool_kv.reshape(2, ROWS, width)

    mine_spec, their_spec, their_pool = own_spec(), other_spec(), other_spec((2,))
    sizes = (4 * ROWS + EXTRA, 2 * ROWS + EXTRA, 2 * ROWS + EXTRA)
    packed, x_mine, x_other = call(
        functools.partial(pack_cross_kernel, enc_dev, loop), "pack_cross", info,
        [whole_spec(neighbour_ids.shape[::-1])] + [mine_spec] * 2 + [their_spec] * 2 + [their_pool],
        (neighbour_ids.T, cross_queries, grad_cross, cross_queries, grad_cross, pool),
        [spec(rows) for rows in sizes],
        [((rows, WIDE), BF16) for rows in sizes],
    )
    x_same = send(x_mine, outward, True)
    x_cross = send(x_other, across, True)
    x_pair = send(packed, swap, False)
    queries_in, packed = lax.optimization_barrier((queries, packed))
    sizes = (4 * ROWS, 2 * ROWS, 2 * ROWS)
    packed, s_mine, s_other = call(
        pack_self_kernel, "pack_self", info,
        [mine_spec] * 2 + [their_spec] * 4,
        (queries_in, grad_self, queries_in, grad_self, keys, values),
        [spec(rows) for rows in sizes],
        [((rows, WIDE), BF16) for rows in sizes],
    )
    s_pair = send(packed, swap, False)

    ids_of = lambda d: lax.dynamic_slice_in_dim(doc_ids, d * ROWS, ROWS, 0)
    span = jnp.arange(ROWS, dtype=jnp.int32)
    base = me // 2 * 2
    places = jnp.concatenate([span + base * ROWS, span + (base + 1) * ROWS])
    near0, near1, far0, far1 = [ids_of(base + j) for j in range(4)]
    near = jnp.concatenate([near0, near1])
    near_flip = jnp.concatenate([near1, near0])
    far_flip = jnp.concatenate([far1, far0])
    local_ok = (near[:, None] == near[None, :]) & (places[:, None] <= places[None, :])
    far_ok = (near_flip[:, None] == far_flip[None, :]) & (base + 2 < loop)
    local_bias = jnp.where(local_ok, 0.0, MASKED).astype(F32)
    far_bias = jnp.where(far_ok, 0.0, MASKED).astype(F32)

    bias_spec = whole_spec((2 * ROWS, 2 * ROWS))
    local_bias, far_bias, x_pair = lax.optimization_barrier((local_bias, far_bias, x_pair))
    self_specs = [bias_spec] + [own_spec()] * 4 + [spec(ROWS, j) for j in range(4)]
    self_args = (local_bias, queries, grad_self, keys, values) + (s_pair,) * 4
    mine_w = whole_spec((EXTRA, WIDE), (2 * ROWS // EXTRA, 0))
    partner_w = whole_spec((EXTRA, WIDE), (4 * ROWS // EXTRA, 0))
    cross_specs = (
        [mine_w, partner_w, own_spec(), own_spec(), own_spec((2,))]
        + [spec(ROWS, j) for j in range(4)]
    )
    cross_args = (x_mine, x_pair, cross_queries, grad_cross, pool) + (x_pair,) * 4
    stat = lambda rows: ((HALF, 8, rows), F32)

    x_own, x_partner = call(
        per_head(cross_stats_kernel), "cross_stats", info, cross_specs, cross_args,
        [stat_spec(ROWS)] * 2, [stat(ROWS)] * 2, flops=0,
    )
    t_same = send(x_own, outward, True)
    t_cross = send(x_partner, inward, True)
    local_bias, x_own = lax.optimization_barrier((local_bias, x_own))
    self_args = (local_bias,) + self_args[1:]
    (s_own,) = call(
        per_head(self_stats_kernel), "self_stats", info, self_specs, self_args,
        [stat_spec(2 * ROWS)], [stat(2 * ROWS)], flops=0,
    )
    s_mine, x_same, x_cross, t_same, t_cross, s_own = lax.optimization_barrier(
        (s_mine, x_same, x_cross, t_same, t_cross, s_own)
    )
    s_same = send(s_mine, lambda d: d - 2, False)

    kv_out = spec(4 * ROWS)
    kv_shape = ((4 * ROWS, WIDE), BF16)
    q_shape = ((ROWS, WIDE), BF16)
    xd_same, xd_cross, x_kv, x_fin_same, x_fin_cross = call(
        per_head(cross_remote_kernel), "cross_remote", info,
        [mine_w, mine_w, spec(ROWS, 0), spec(ROWS, 1), spec(ROWS, 0), spec(ROWS, 1)]
        + [own_spec((2,)), spec(ROWS, 2), spec(ROWS, 3), stat_spec(ROWS), stat_spec(ROWS)],
        (x_same, x_cross, x_same, x_same, x_cross, x_cross, pool, x_pair, x_pair, t_same, t_cross),
        [spec(ROWS), spec(ROWS), kv_out, stat_spec(ROWS), stat_spec(ROWS)],
        [q_shape, q_shape, kv_shape, stat(ROWS), stat(ROWS)],
    )
    f_own = send(x_fin_same, inward, True)
    f_partner = send(x_fin_cross, outward, True)
    s_other, x_kv = lax.optimization_barrier((s_other, x_kv))
    s_cross = send(s_other, lambda d: (d - 2) ^ 1, False)
    s_own, f_own = lax.optimization_barrier((s_own, f_own))
    t_self = send(s_own, lambda d: d - 2, False)
    x_kv, s_same = lax.optimization_barrier((x_kv, s_same))
    half_out = spec(3 * ROWS)
    half_shape = ((3 * ROWS, WIDE), BF16)
    x_keep, x_give = call(
        per_head(cross_local_kernel), "cross_local", info,
        cross_specs + [stat_spec(ROWS), stat_spec(ROWS), spec(4 * ROWS)],
        cross_args + (f_own, f_partner, x_kv),
        [half_out] * 2, [half_shape] * 2, flops=LONG,
    )

    xd_same, xd_cross, s_cross, x_keep = lax.optimization_barrier(
        (xd_same, xd_cross, s_cross, x_keep)
    )
    xr_same = send(xd_same, inward, True)
    xr_cross = send(xd_cross, across, True)
    far_bias, x_keep = lax.optimization_barrier((far_bias, x_keep))
    sd, s_kv, s_fin = call(
        per_head(self_remote_kernel), "self_remote", info,
        [bias_spec, spec(ROWS, 0), spec(ROWS, 1), spec(ROWS, 0), spec(ROWS, 1)]
        + [own_spec(), own_spec(), spec(ROWS, 2), spec(ROWS, 3), stat_spec(2 * ROWS)],
        (far_bias, s_same, s_same, s_cross, s_cross, keys, values, s_pair, s_pair, t_self),
        [spec(2 * ROWS), kv_out, stat_spec(2 * ROWS)],
        [((2 * ROWS, WIDE), BF16), kv_shape, stat(2 * ROWS)], flops=LONG,
    )
    f_self = send(s_fin, lambda d: d + 2, False)
    sr = send(sd, lambda d: d + 2, False)

    x_give, s_kv, xr_same, xr_cross, f_self = lax.optimization_barrier(
        (x_give, s_kv, xr_same, xr_cross, f_self)
    )
    x_take = send(x_give, swap, False)
    s_keep, s_give = call(
        per_head(self_local_kernel), "self_local", info,
        self_specs + [stat_spec(2 * ROWS), stat_spec(2 * ROWS), spec(4 * ROWS)],
        self_args + (f_self, s_own, s_kv),
        [half_out] * 2, [half_shape] * 2, flops=LONG,
    )
    grad_cq, grad_pool = assemble(
        cross_final_kernel, "cross_final", info, (x_keep, x_take, xr_same, xr_cross), True
    )
    s_give, sr, grad_cq = lax.optimization_barrier((s_give, sr, grad_cq))
    s_take = send(s_give, swap, False)
    sr_take = send(sr, swap, False)
    grad_q, grad_k, grad_v = assemble(
        self_final_kernel, "self_final", info, (s_keep, s_take, sr, sr_take), False
    )
    return grad_q, grad_k, grad_v, grad_cq, grad_pool.reshape(pool_kv.shape)


def solution(mesh):
    rows = P(("groups", "ctx"), None)
    pool = P(None, ("groups", "ctx"), None, None)
    return jax.shard_map(
        body,
        mesh=mesh,
        in_specs=(rows, rows, rows, rows, P("groups"), rows, rows, pool, rows),
        out_specs=(rows, rows, rows, rows, pool),
        check_vma=False,
    )
```

```python
import functools
import math

import jax
import jax.numpy as jnp
from jax import lax
from jax.experimental import pallas as pl
from jax.experimental.pallas import tpu as pltpu
from jax.sharding import PartitionSpec as P

HEADS = 8
HEAD_DIM = 128
HALF = HEADS // 2
WIDE = HALF * HEAD_DIM
STEP = 2
COLS = STEP * HEAD_DIM
STEPS = HALF // STEP
STRETCH = 64
NBR_TOK = 128
ROWS = 256
EXTRA = 16
LONG = 12 * 10**9
FACTOR = HEAD_DIM ** (-0.5)
MASKED = -1e30
BF16 = jnp.bfloat16
F32 = jnp.float32


def send(value, target_of, wrap):
    count = lax.axis_size("ctx")
    pairs = []
    for source in range(count):
        target = target_of(source)
        if wrap:
            pairs.append((source, target % count))
        elif 0 <= target < count:
            pairs.append((source, target))
    return lax.ppermute(value, "ctx", pairs)


def swap(d):
    return d ^ 1


def outward(d):
    return d - 2 if d % 2 == 0 else d + 2


def inward(d):
    return d + 2 if d % 2 == 0 else d - 2


def across(d):
    return d - 1 if d % 2 == 0 else d + 1


def spec(rows, row_block=0):
    return pl.BlockSpec((rows, COLS), lambda h, info: (row_block, h))


def own_spec(lead=()):
    zeros = (0,) * len(lead)
    return pl.BlockSpec(lead + (ROWS, COLS), lambda h, info: zeros + (0, info[0] % 2 * STEPS + h))


def other_spec(lead=()):
    zeros = (0,) * len(lead)
    return pl.BlockSpec(
        lead + (ROWS, COLS), lambda h, info: zeros + (0, (1 - info[0] % 2) * STEPS + h)
    )


def whole_spec(shape, index=None):
    index = (0,) * len(shape) if index is None else index
    return pl.BlockSpec(shape, lambda h, *info: index)


def stat_spec(rows):
    return pl.BlockSpec((STEP, 8, rows), lambda h, info: (h, 0, 0))


def call(kernel, name, info, in_specs, inputs, out_specs, outs, steps=STEPS, flops=0):
    return pl.pallas_call(
        kernel,
        name=name,
        grid_spec=pltpu.PrefetchScalarGridSpec(
            num_scalar_prefetch=1,
            grid=(steps,),
            in_specs=in_specs,
            out_specs=out_specs,
        ),
        out_shape=[jax.ShapeDtypeStruct(shape, dtype) for shape, dtype in outs],
        compiler_params=pltpu.CompilerParams(vmem_limit_bytes=64 << 20),
        cost_estimate=pl.CostEstimate(flops=flops, transcendentals=0, bytes_accessed=0),
    )(info, *inputs)


def head_of(ref, j):
    shape = ref.shape
    if len(shape) == 3 and shape[1] == 8:
        return ref.at[j : j + 1]
    if shape[-1] != COLS:
        return ref
    place = pl.ds(j * HEAD_DIM, HEAD_DIM)
    return ref.at[:, place] if len(shape) == 2 else ref.at[:, :, place]


def per_head(kernel):
    def run(info, *refs):
        for j in range(STEP):
            kernel(info, *[head_of(ref, j) for ref in refs])

    return run


def dot_last(a, b):
    return lax.dot_general(a, b, (((1,), (1,)), ((), ())), preferred_element_type=F32)


def dot_first(a, b):
    return lax.dot_general(a, b, (((0,), (0,)), ((), ())), preferred_element_type=F32)


def dot(a, b):
    return jnp.dot(a, b, preferred_element_type=F32)


def both(a, b):
    return jnp.concatenate([a, b], axis=0)


def weight_rows(times):
    log_two = jnp.where(times > 1.5, math.log(2.0), 0.0)
    return jnp.where(times < 0.5, MASKED, log_two)


def slot_pair(ref, first, core, second=None):
    times = ref[...].astype(F32)[:, :ROWS]
    low = times[first : first + 2]
    if second is None:
        return weight_rows(low)
    return weight_rows(jnp.where(core == 0, low, times[second : second + 2]))


def add_rows(s, rows):
    parts = [
        s[e * NBR_TOK : (e + 1) * NBR_TOK] + rows[e : e + 1] for e in range(s.shape[0] // NBR_TOK)
    ]
    return jnp.concatenate(parts, axis=0)


def partial_stats(s, dp):
    peak = jnp.max(s, axis=0, keepdims=True)
    e = jnp.exp(s - peak)
    return e, peak, jnp.sum(e, axis=0, keepdims=True), jnp.sum(e * dp, axis=0, keepdims=True)


def stat_rows(a, b, c):
    return jnp.concatenate([a, b, c, jnp.zeros((5, a.shape[1]), F32)], axis=0)[None]


def merge(stats, mine):
    t_peak, t_total, t_moment = stats[0, 0:1], stats[0, 1:2], stats[0, 2:3]
    peak, total, moment = mine
    top = jnp.maximum(t_peak, peak)
    t_scale = jnp.exp(t_peak - top)
    scale = jnp.exp(peak - top)
    full = t_total * t_scale + total * scale
    inverse = jnp.where(full > 0, 1.0 / full, 0.0)
    delta = (t_moment * t_scale + moment * scale) * inverse
    return top, inverse, delta, scale * inverse


def gradients(p, dp, delta, q, g, k):
    pb = p.astype(BF16)
    ds = (p * (dp - delta)).astype(BF16)
    return dot_first(ds, k) * FACTOR, dot(ds, q) * FACTOR, dot(pb, g)


def pack_cross_kernel(enc_dev, loop, info, ids_ref, qm, gm, q, g, pool, swap_ref, mine, other):
    shape = (EXTRA, mine.shape[1])
    row = lax.broadcasted_iota(jnp.int32, shape, 0)
    lane = lax.broadcasted_iota(jnp.int32, shape, 1) + pl.program_id(0) * shape[1]
    ids = ids_ref[...]
    owner = ids // enc_dev
    relative = owner - info[0] + 1
    relative = jnp.where(relative < 0, relative + loop, relative)
    relative = jnp.where(relative >= loop, relative - loop, relative)
    slots = relative * enc_dev + ids - owner * enc_dev
    times = jnp.zeros(shape, F32)
    for n in range(ids.shape[0]):
        for s in range(ids.shape[1]):
            hit = (row == slots[n : n + 1, s : s + 1]) & (lane // STRETCH == s)
            times = times + jnp.where(hit, 1.0, 0.0)
    times = times.astype(BF16)
    swap_ref[0:ROWS] = q[...]
    swap_ref[ROWS : 2 * ROWS] = g[...]
    swap_ref[2 * ROWS : 3 * ROWS] = pool[0]
    swap_ref[3 * ROWS : 4 * ROWS] = pool[1]
    swap_ref[4 * ROWS :] = times
    for out, first, second in ((mine, qm, gm), (other, q, g)):
        out[0:ROWS] = first[...]
        out[ROWS : 2 * ROWS] = second[...]
        out[2 * ROWS :] = times


def pack_self_kernel(info, qm, gm, q, g, k, v, swap_ref, mine, other):
    for index, ref in enumerate((q, g, k, v)):
        swap_ref[index * ROWS : (index + 1) * ROWS] = ref[...]
    for out, first, second in ((mine, qm, gm), (other, q, g)):
        out[0:ROWS] = first[...]
        out[ROWS : 2 * ROWS] = second[...]


def ordered(core, a, b):
    return jnp.where(core == 0, a, b), jnp.where(core == 0, b, a)


def wide_scores(keys_x, keys_y, values_x, values_y, qs, gs, bias):
    sx = dot_last(keys_x, qs) * FACTOR + bias[:ROWS]
    sy = dot_last(keys_y, qs[ROWS:]) * FACTOR + bias[ROWS:, ROWS:]
    return sx, sy, dot_last(values_x, gs), dot_last(values_y, gs[ROWS:])


def wide_stats(sx, sy, dpx, dpy):
    peak = jnp.max(sx, axis=0, keepdims=True)
    peak_y = jnp.maximum(peak[:, ROWS:], jnp.max(sy, axis=0, keepdims=True))
    peak = jnp.concatenate([peak[:, :ROWS], peak_y], axis=1)
    ex, ey = jnp.exp(sx - peak), jnp.exp(sy - peak_y)
    widen = lambda a, b: jnp.concatenate([a[:, :ROWS], a[:, ROWS:] + b], axis=1)
    add = lambda a: jnp.sum(a, axis=0, keepdims=True)
    return ex, ey, peak, widen(add(ex), add(ey)), widen(add(ex * dpx), add(ey * dpy))


def wide_gradients(px, py, dpx, dpy, delta, qs, gs, kx, ky):
    pbx, pby = px.astype(BF16), py.astype(BF16)
    dsx = (px * (dpx - delta)).astype(BF16)
    dsy = (py * (dpy - delta[:, ROWS:])).astype(BF16)
    dq_z = dot_first(dsx[:, :ROWS], kx) * FACTOR
    dq_y = dot_first(both(dsx[:, ROWS:], dsy), both(kx, ky)) * FACTOR
    dkx, dky = dot(dsx, qs) * FACTOR, dot(dsy, qs[ROWS:]) * FACTOR
    return dq_z, dq_y, dkx, dky, dot(pbx, gs), dot(pby, gs[ROWS:])


def local_self(core, bias, q, g, k, v, pq, pg, pk, pv):
    q0, q1 = ordered(core, q[...], pq[...])
    g0, g1 = ordered(core, g[...], pg[...])
    k0, k1 = ordered(core, k[...], pk[...])
    v0, v1 = ordered(core, v[...], pv[...])
    qs, gs = both(q0, q1), both(g0, g1)
    return wide_scores(k0, k1, v0, v1, qs, gs, bias[...]), qs, gs, k0, k1


def local_cross(core, w, pw, q, g, pool, pq, pg, pk, pv):
    qs, gs = both(q[...], pq[...]), both(g[...], pg[...])
    ks, vs = both(pool[0], pk[...]), both(pool[1], pv[...])
    own = both(slot_pair(w, 2, core), slot_pair(w, 4, core, 0))
    partner = both(slot_pair(pw, 0, core, 4), slot_pair(pw, 2, core))
    s = add_rows(dot_last(ks, qs) * FACTOR, jnp.concatenate([own, partner], axis=1))
    return s, dot_last(vs, gs), qs, gs, ks


def self_stats_kernel(info, *refs):
    scores = local_self(info[0] % 2, *refs[:-1])[0]
    refs[-1][...] = stat_rows(*wide_stats(*scores)[2:])


def cross_stats_kernel(info, *refs):
    s, dp, _, _, _ = local_cross(info[0] % 2, *refs[:-2])
    stats = stat_rows(*partial_stats(s, dp)[1:])
    refs[-2][...] = stats[:, :, :ROWS]
    refs[-1][...] = stats[:, :, ROWS:]


def self_remote_kernel(
    info, bias, sq, sg, cq, cg, k, v, pk, pv, stats, dq_ref, kv_ref, out_stats
):
    core = info[0] % 2
    q0, q1 = ordered(core, sq[...], cq[...])
    g0, g1 = ordered(core, sg[...], cg[...])
    k0, k1 = ordered(core, k[...], pk[...])
    v0, v1 = ordered(core, v[...], pv[...])
    qs, gs = both(q1, q0), both(g1, g0)
    sx, sy, dpx, dpy = wide_scores(k1, k0, v1, v0, qs, gs, bias[...])
    ex, ey, *mine = wide_stats(sx, sy, dpx, dpy)
    known = stats[...]
    known = jnp.concatenate([known[:, :, ROWS:], known[:, :, :ROWS]], axis=2)
    top, inverse, delta, scale = merge(known, mine)
    px, py = ex * scale, ey * scale[:, ROWS:]
    dq1, dq0, dk1, dk0, dv1, dv0 = wide_gradients(px, py, dpx, dpy, delta, qs, gs, k1, k0)
    same, cross = ordered(core, dq0, dq1)
    dq_ref[:ROWS] = same.astype(BF16)
    dq_ref[ROWS:] = cross.astype(BF16)
    for index, grad in enumerate(ordered(core, dk0, dk1) + ordered(core, dv0, dv1)):
        kv_ref[index * ROWS : (index + 1) * ROWS] = grad.astype(BF16)
    out_stats[...] = stat_rows(top, inverse, delta)


def cross_remote_kernel(
    info, sw, cw, sq, sg, cq, cg, pool, pk, pv, s_stats, c_stats, *outs
):
    dq_same, dq_cross, kv_ref, out_same, out_cross = outs
    core = info[0] % 2
    jobs = (
        (cq, cg, pool[0], pool[1], slot_pair(cw, 4, core, 0), c_stats, dq_cross, out_cross, 0),
        (sq, sg, pk[...], pv[...], slot_pair(sw, 0, core, 4), s_stats, dq_same, out_same, 1),
    )
    for q, g, k, v, rows, stats, dq_ref, out_stats, place in jobs:
        s, dp = add_rows(dot_last(k, q[...]) * FACTOR, rows), dot_last(v, g[...])
        e, *mine = partial_stats(s, dp)
        top, inverse, delta, scale = merge(stats[...], mine)
        dq, dk, dv = gradients(e * scale, dp, delta, q[...], g[...], k)
        dq_ref[...] = dq.astype(BF16)
        out_stats[...] = stat_rows(top, inverse, delta)
        kv_ref[place * ROWS : (place + 1) * ROWS] = dk.astype(BF16)
        kv_ref[(2 + place) * ROWS : (3 + place) * ROWS] = dv.astype(BF16)


def self_local_kernel(info, *refs):
    stats_ref, own_ref, kv_ref, mine, theirs = refs[-5:]
    local = own_ref[0]
    core = info[0] % 2
    first = info[0] < 2
    stats = stats_ref[0]
    stats = jnp.concatenate([stats[:, ROWS:], stats[:, :ROWS]], axis=1)
    inverse = 1.0 / local[1:2]
    top = jnp.where(first, local[0:1], stats[0:1])
    delta = jnp.where(first, local[2:3] * inverse, stats[2:3])
    inverse = jnp.where(first, inverse, stats[1:2])
    (sx, sy, dpx, dpy), qs, gs, k0, k1 = local_self(core, *refs[:-5])
    px = jnp.exp(sx - top) * inverse
    py = jnp.exp(sy - top[:, ROWS:]) * inverse[:, ROWS:]
    dq0, dq1, dk0, dk1, dv0, dv1 = wide_gradients(px, py, dpx, dpy, delta, qs, gs, k0, k1)
    grads = (ordered(core, dq0, dq1), ordered(core, dk0, dk1), ordered(core, dv0, dv1))
    for index, pair in enumerate(grads):
        for out, place, grad in ((mine, 0, pair[0]), (theirs, 1, pair[1])):
            if index > 0:
                low = (2 * index - 2 + place) * ROWS
                grad = grad + kv_ref[low : low + ROWS].astype(F32)
            out[index * ROWS : (index + 1) * ROWS] = grad.astype(BF16)


def cross_local_kernel(info, *refs):
    own_stats, partner_stats, kv_ref, mine, theirs = refs[-5:]
    stats = jnp.concatenate([own_stats[0], partner_stats[0]], axis=1)
    top, inverse, delta = stats[0:1], stats[1:2], stats[2:3]
    s, dp, qs, gs, ks = local_cross(info[0] % 2, *refs[:-5])
    dq, dk, dv = gradients(jnp.exp(s - top) * inverse, dp, delta, qs, gs, ks)
    dk = dk + kv_ref[: 2 * ROWS].astype(F32)
    dv = dv + kv_ref[2 * ROWS :].astype(F32)
    for index, grad in enumerate((dq, dk, dv)):
        mine[index * ROWS : (index + 1) * ROWS] = grad[:ROWS].astype(BF16)
        theirs[index * ROWS : (index + 1) * ROWS] = grad[ROWS:].astype(BF16)


def self_final_kernel(info, mine, theirs, dq_mine, dq_theirs, *outs):
    def write(source, extra):
        dq = source[:ROWS].astype(F32) + extra[...].astype(F32)
        outs[0][...] = dq.astype(BF16)
        outs[1][...] = source[ROWS : 2 * ROWS]
        outs[2][...] = source[2 * ROWS :]

    pl.when(pl.program_id(0) == 0)(lambda: write(mine, dq_mine))
    pl.when(pl.program_id(0) == 1)(lambda: write(theirs, dq_theirs))


def cross_final_kernel(info, mine, theirs, dq_mine, dq_theirs, dq_out, pool_out):
    def write(source, extra):
        dq = source[:ROWS].astype(F32) + extra[...].astype(F32)
        dq_out[...] = dq.astype(BF16)
        pool_out[0] = source[ROWS : 2 * ROWS]
        pool_out[1] = source[2 * ROWS :]

    pl.when(pl.program_id(0) == 0)(lambda: write(mine, dq_mine))
    pl.when(pl.program_id(0) == 1)(lambda: write(theirs, dq_theirs))


def assemble(kernel, name, info, inputs, pooled):
    half = lambda h, info: (info[0] + h) % 2
    rows_out = pl.BlockSpec((ROWS, WIDE), lambda h, info: (0, half(h, info)))
    pool_out = pl.BlockSpec((2, ROWS, WIDE), lambda h, info: (0, 0, half(h, info)))
    full = ((ROWS, 2 * WIDE), BF16)
    if pooled:
        out_specs, outs = [rows_out, pool_out], [full, ((2, ROWS, 2 * WIDE), BF16)]
    else:
        out_specs, outs = [rows_out] * 3, [full] * 3
    in_specs = [whole_spec(x.shape) for x in inputs]
    if not pooled:
        in_specs[2:] = [whole_spec((ROWS, WIDE)), whole_spec((ROWS, WIDE), (1, 0))]
    return call(kernel, name, info, in_specs, inputs, out_specs, outs, steps=2)


def body(
    queries, keys, values, grad_self, doc_ids, cross_queries, grad_cross, pool_kv, neighbour_ids
):
    loop = lax.axis_size("ctx")
    me = lax.axis_index("ctx").astype(jnp.int32)
    info = jnp.full((1,), me, jnp.int32)
    enc_dev = pool_kv.shape[1]
    width = queries.shape[1]
    pool = pool_kv.reshape(2, ROWS, width)

    mine_spec, their_spec, their_pool = own_spec(), other_spec(), other_spec((2,))
    sizes = (4 * ROWS + EXTRA, 2 * ROWS + EXTRA, 2 * ROWS + EXTRA)
    packed, x_mine, x_other = call(
        functools.partial(pack_cross_kernel, enc_dev, loop), "pack_cross", info,
        [whole_spec(neighbour_ids.shape[::-1])] + [mine_spec] * 2 + [their_spec] * 2 + [their_pool],
        (neighbour_ids.T, cross_queries, grad_cross, cross_queries, grad_cross, pool),
        [spec(rows) for rows in sizes],
        [((rows, WIDE), BF16) for rows in sizes],
    )
    x_same = send(x_mine, outward, True)
    x_cross = send(x_other, across, True)
    x_pair = send(packed, swap, False)
    queries_in, packed = lax.optimization_barrier((queries, packed))
    sizes = (4 * ROWS, 2 * ROWS, 2 * ROWS)
    packed, s_mine, s_other = call(
        pack_self_kernel, "pack_self", info,
        [mine_spec] * 2 + [their_spec] * 4,
        (queries_in, grad_self, queries_in, grad_self, keys, values),
        [spec(rows) for rows in sizes],
        [((rows, WIDE), BF16) for rows in sizes],
    )
    s_pair = send(packed, swap, False)

    ids_of = lambda d: lax.dynamic_slice_in_dim(doc_ids, d * ROWS, ROWS, 0)
    span = jnp.arange(ROWS, dtype=jnp.int32)
    base = me // 2 * 2
    places = jnp.concatenate([span + base * ROWS, span + (base + 1) * ROWS])
    near0, near1, far0, far1 = [ids_of(base + j) for j in range(4)]
    near = jnp.concatenate([near0, near1])
    near_flip = jnp.concatenate([near1, near0])
    far_flip = jnp.concatenate([far1, far0])
    local_ok = (near[:, None] == near[None, :]) & (places[:, None] <= places[None, :])
    far_ok = (near_flip[:, None] == far_flip[None, :]) & (base + 2 < loop)
    local_bias = jnp.where(local_ok, 0.0, MASKED).astype(F32)
    far_bias = jnp.where(far_ok, 0.0, MASKED).astype(F32)

    bias_spec = whole_spec((2 * ROWS, 2 * ROWS))
    local_bias, far_bias, x_pair = lax.optimization_barrier((local_bias, far_bias, x_pair))
    self_specs = [bias_spec] + [own_spec()] * 4 + [spec(ROWS, j) for j in range(4)]
    self_args = (local_bias, queries, grad_self, keys, values) + (s_pair,) * 4
    mine_w = whole_spec((EXTRA, WIDE), (2 * ROWS // EXTRA, 0))
    partner_w = whole_spec((EXTRA, WIDE), (4 * ROWS // EXTRA, 0))
    cross_specs = (
        [mine_w, partner_w, own_spec(), own_spec(), own_spec((2,))]
        + [spec(ROWS, j) for j in range(4)]
    )
    cross_args = (x_mine, x_pair, cross_queries, grad_cross, pool) + (x_pair,) * 4
    stat = lambda rows: ((HALF, 8, rows), F32)

    x_own, x_partner = call(
        per_head(cross_stats_kernel), "cross_stats", info, cross_specs, cross_args,
        [stat_spec(ROWS)] * 2, [stat(ROWS)] * 2, flops=0,
    )
    t_same = send(x_own, outward, True)
    t_cross = send(x_partner, inward, True)
    local_bias, x_own = lax.optimization_barrier((local_bias, x_own))
    self_args = (local_bias,) + self_args[1:]
    (s_own,) = call(
        per_head(self_stats_kernel), "self_stats", info, self_specs, self_args,
        [stat_spec(2 * ROWS)], [stat(2 * ROWS)], flops=0,
    )
    t_self = send(s_own, lambda d: d - 2, False)
    s_mine, x_same, x_cross, t_same, t_cross, s_own = lax.optimization_barrier(
        (s_mine, x_same, x_cross, t_same, t_cross, s_own)
    )
    s_same = send(s_mine, lambda d: d - 2, False)

    kv_out = spec(4 * ROWS)
    kv_shape = ((4 * ROWS, WIDE), BF16)
    q_shape = ((ROWS, WIDE), BF16)
    xd_same, xd_cross, x_kv, x_fin_same, x_fin_cross = call(
        per_head(cross_remote_kernel), "cross_remote", info,
        [mine_w, mine_w, spec(ROWS, 0), spec(ROWS, 1), spec(ROWS, 0), spec(ROWS, 1)]
        + [own_spec((2,)), spec(ROWS, 2), spec(ROWS, 3), stat_spec(ROWS), stat_spec(ROWS)],
        (x_same, x_cross, x_same, x_same, x_cross, x_cross, pool, x_pair, x_pair, t_same, t_cross),
        [spec(ROWS), spec(ROWS), kv_out, stat_spec(ROWS), stat_spec(ROWS)],
        [q_shape, q_shape, kv_shape, stat(ROWS), stat(ROWS)],
    )
    f_own = send(x_fin_same, inward, True)
    f_partner = send(x_fin_cross, outward, True)
    s_other, x_kv = lax.optimization_barrier((s_other, x_kv))
    s_cross = send(s_other, lambda d: (d - 2) ^ 1, False)
    x_kv, s_same, t_self = lax.optimization_barrier((x_kv, s_same, t_self))
    half_out = spec(3 * ROWS)
    half_shape = ((3 * ROWS, WIDE), BF16)
    x_keep, x_give = call(
        per_head(cross_local_kernel), "cross_local", info,
        cross_specs + [stat_spec(ROWS), stat_spec(ROWS), spec(4 * ROWS)],
        cross_args + (f_own, f_partner, x_kv),
        [half_out] * 2, [half_shape] * 2, flops=LONG,
    )

    xd_same, xd_cross, s_cross, x_keep = lax.optimization_barrier(
        (xd_same, xd_cross, s_cross, x_keep)
    )
    xr_same = send(xd_same, inward, True)
    xr_cross = send(xd_cross, across, True)
    far_bias, x_keep = lax.optimization_barrier((far_bias, x_keep))
    sd, s_kv, s_fin = call(
        per_head(self_remote_kernel), "self_remote", info,
        [bias_spec, spec(ROWS, 0), spec(ROWS, 1), spec(ROWS, 0), spec(ROWS, 1)]
        + [own_spec(), own_spec(), spec(ROWS, 2), spec(ROWS, 3), stat_spec(2 * ROWS)],
        (far_bias, s_same, s_same, s_cross, s_cross, keys, values, s_pair, s_pair, t_self),
        [spec(2 * ROWS), kv_out, stat_spec(2 * ROWS)],
        [((2 * ROWS, WIDE), BF16), kv_shape, stat(2 * ROWS)], flops=LONG,
    )
    f_self = send(s_fin, lambda d: d + 2, False)
    sr = send(sd, lambda d: d + 2, False)

    x_give, s_kv, xr_same, xr_cross, f_self = lax.optimization_barrier(
        (x_give, s_kv, xr_same, xr_cross, f_self)
    )
    x_take = send(x_give, swap, False)
    s_keep, s_give = call(
        per_head(self_local_kernel), "self_local", info,
        self_specs + [stat_spec(2 * ROWS), stat_spec(2 * ROWS), spec(4 * ROWS)],
        self_args + (f_self, s_own, s_kv),
        [half_out] * 2, [half_shape] * 2, flops=LONG,
    )
    grad_cq, grad_pool = assemble(
        cross_final_kernel, "cross_final", info, (x_keep, x_take, xr_same, xr_cross), True
    )
    s_give, sr, grad_cq = lax.optimization_barrier((s_give, sr, grad_cq))
    s_take = send(s_give, swap, False)
    sr_take = send(sr, swap, False)
    grad_q, grad_k, grad_v = assemble(
        self_final_kernel, "self_final", info, (s_keep, s_take, sr, sr_take), False
    )
    return grad_q, grad_k, grad_v, grad_cq, grad_pool.reshape(pool_kv.shape)


def solution(mesh):
    rows = P(("groups", "ctx"), None)
    pool = P(None, ("groups", "ctx"), None, None)
    return jax.shard_map(
        body,
        mesh=mesh,
        in_specs=(rows, rows, rows, rows, P("groups"), rows, rows, pool, rows),
        out_specs=(rows, rows, rows, rows, pool),
        check_vma=False,
    )
```

```python
import functools
import math

import jax
import jax.numpy as jnp
from jax import lax
from jax.experimental import pallas as pl
from jax.experimental.pallas import tpu as pltpu
from jax.sharding import PartitionSpec as P

HEADS = 8
HEAD_DIM = 128
HALF = HEADS // 2
WIDE = HALF * HEAD_DIM
STEP = 2
COLS = STEP * HEAD_DIM
STEPS = HALF // STEP
STRETCH = 64
NBR_TOK = 128
ROWS = 256
EXTRA = 16
STATS = 64
LONG = 12 * 10**9
FACTOR = HEAD_DIM ** (-0.5)
MASKED = -1e30
BF16 = jnp.bfloat16
F32 = jnp.float32


def send(value, target_of, wrap):
    count = lax.axis_size("ctx")
    pairs = []
    for source in range(count):
        target = target_of(source)
        if wrap:
            pairs.append((source, target % count))
        elif 0 <= target < count:
            pairs.append((source, target))
    return lax.ppermute(value, "ctx", pairs)


def swap(d):
    return d ^ 1


def outward(d):
    return d - 2 if d % 2 == 0 else d + 2


def inward(d):
    return d + 2 if d % 2 == 0 else d - 2


def across(d):
    return d - 1 if d % 2 == 0 else d + 1


def spec(rows, row_block=0):
    return pl.BlockSpec((rows, COLS), lambda h, info: (row_block, h))


def own_spec(lead=()):
    zeros = (0,) * len(lead)
    return pl.BlockSpec(lead + (ROWS, COLS), lambda h, info: zeros + (0, info[0] % 2 * STEPS + h))


def other_spec(lead=()):
    zeros = (0,) * len(lead)
    return pl.BlockSpec(
        lead + (ROWS, COLS), lambda h, info: zeros + (0, (1 - info[0] % 2) * STEPS + h)
    )


def whole_spec(shape, index=None):
    index = (0,) * len(shape) if index is None else index
    return pl.BlockSpec(shape, lambda h, *info: index)


def stat_spec(rows):
    return pl.BlockSpec((STEP, 8, rows), lambda h, info: (h, 0, 0))


def call(kernel, name, info, in_specs, inputs, out_specs, outs, steps=STEPS, flops=0):
    return pl.pallas_call(
        kernel,
        name=name,
        grid_spec=pltpu.PrefetchScalarGridSpec(
            num_scalar_prefetch=1,
            grid=(steps,),
            in_specs=in_specs,
            out_specs=out_specs,
        ),
        out_shape=[jax.ShapeDtypeStruct(shape, dtype) for shape, dtype in outs],
        compiler_params=pltpu.CompilerParams(vmem_limit_bytes=64 << 20),
        cost_estimate=pl.CostEstimate(flops=flops, transcendentals=0, bytes_accessed=0),
    )(info, *inputs)


def head_of(ref, j):
    shape = ref.shape
    if len(shape) == 3 and shape[1] == 8:
        return ref.at[j : j + 1]
    if shape[-1] != COLS:
        return ref
    place = pl.ds(j * HEAD_DIM, HEAD_DIM)
    return ref.at[:, place] if len(shape) == 2 else ref.at[:, :, place]


def per_head(kernel):
    def run(info, *refs):
        for j in range(STEP):
            kernel(info, *[head_of(ref, j) for ref in refs])

    return run


def dot_last(a, b):
    return lax.dot_general(a, b, (((1,), (1,)), ((), ())), preferred_element_type=F32)


def dot_first(a, b):
    return lax.dot_general(a, b, (((0,), (0,)), ((), ())), preferred_element_type=F32)


def dot(a, b):
    return jnp.dot(a, b, preferred_element_type=F32)


def both(a, b):
    return jnp.concatenate([a, b], axis=0)


def weight_rows(times):
    log_two = jnp.where(times > 1.5, math.log(2.0), 0.0)
    return jnp.where(times < 0.5, MASKED, log_two)


def slot_pair(ref, first, core, second=None):
    times = ref[...].astype(F32)[:, :ROWS]
    low = times[first : first + 2]
    if second is None:
        return weight_rows(low)
    return weight_rows(jnp.where(core == 0, low, times[second : second + 2]))


def add_rows(s, rows):
    parts = [
        s[e * NBR_TOK : (e + 1) * NBR_TOK] + rows[e : e + 1] for e in range(s.shape[0] // NBR_TOK)
    ]
    return jnp.concatenate(parts, axis=0)


def partial_stats(s, dp):
    peak = jnp.max(s, axis=0, keepdims=True)
    e = jnp.exp(s - peak)
    return e, peak, jnp.sum(e, axis=0, keepdims=True), jnp.sum(e * dp, axis=0, keepdims=True)


def stat_rows(a, b, c):
    return jnp.concatenate([a, b, c, jnp.zeros((5, a.shape[1]), F32)], axis=0)[None]


def merge(stats, mine):
    t_peak, t_total, t_moment = stats
    peak, total, moment = mine
    top = jnp.maximum(t_peak, peak)
    t_scale = jnp.exp(t_peak - top)
    scale = jnp.exp(peak - top)
    full = t_total * t_scale + total * scale
    inverse = jnp.where(full > 0, 1.0 / full, 0.0)
    delta = (t_moment * t_scale + moment * scale) * inverse
    return top, inverse, delta, scale * inverse


def gradients(p, dp, delta, q, g, k):
    pb = p.astype(BF16)
    ds = (p * (dp - delta)).astype(BF16)
    return dot_first(ds, k) * FACTOR, dot(ds, q) * FACTOR, dot(pb, g)


def pack_cross_kernel(enc_dev, loop, info, ids_ref, qm, gm, q, g, pool, swap_ref, mine, other):
    shape = (EXTRA, mine.shape[1])
    row = lax.broadcasted_iota(jnp.int32, shape, 0)
    lane = lax.broadcasted_iota(jnp.int32, shape, 1) + pl.program_id(0) * shape[1]
    ids = ids_ref[...]
    owner = ids // enc_dev
    relative = owner - info[0] + 1
    relative = jnp.where(relative < 0, relative + loop, relative)
    relative = jnp.where(relative >= loop, relative - loop, relative)
    slots = relative * enc_dev + ids - owner * enc_dev
    times = jnp.zeros(shape, F32)
    for n in range(ids.shape[0]):
        for s in range(ids.shape[1]):
            hit = (row == slots[n : n + 1, s : s + 1]) & (lane // STRETCH == s)
            times = times + jnp.where(hit, 1.0, 0.0)
    times = times.astype(BF16)
    swap_ref[0:ROWS] = q[...]
    swap_ref[ROWS : 2 * ROWS] = g[...]
    swap_ref[2 * ROWS : 3 * ROWS] = pool[0]
    swap_ref[3 * ROWS : 4 * ROWS] = pool[1]
    swap_ref[4 * ROWS :] = times
    for out, first, second in ((mine, qm, gm), (other, q, g)):
        out[0:ROWS] = first[...]
        out[ROWS : 2 * ROWS] = second[...]
        out[2 * ROWS :] = times


def pack_self_kernel(info, q, g, k, v, swap_ref, other):
    for index, ref in enumerate((q, g, k, v)):
        swap_ref[index * ROWS : (index + 1) * ROWS] = ref[...]
    other[0:ROWS] = q[...]
    other[ROWS:] = g[...]


def ordered(core, a, b):
    return jnp.where(core == 0, a, b), jnp.where(core == 0, b, a)


def split3(x):
    high = x.astype(BF16)
    rest = x - high.astype(F32)
    middle = rest.astype(BF16)
    return [high, middle, (rest - middle.astype(F32)).astype(BF16)]


def packed_stats(stats):
    rows = []
    for low in range(0, stats[0].shape[1], HEAD_DIM):
        for x in stats:
            rows += split3(x[:, low : low + HEAD_DIM])
    rows.append(jnp.zeros((STATS - len(rows), HEAD_DIM), BF16))
    return jnp.concatenate(rows, axis=0)


def unpacked_stats(ref):
    x = ref[...].astype(F32)
    stats = []
    for index in range(3):
        parts = []
        for low in range(3 * index, 9 * (2 * ROWS // HEAD_DIM), 9):
            parts.append(x[low : low + 1] + x[low + 1 : low + 2] + x[low + 2 : low + 3])
        stats.append(jnp.concatenate(parts, axis=1))
    return stats


def wide_scores(keys_x, keys_y, values_x, values_y, qs, gs, bias):
    sx = dot_last(keys_x, qs) * FACTOR + bias[:ROWS]
    sy = dot_last(keys_y, qs[ROWS:]) * FACTOR + bias[ROWS:, ROWS:]
    return sx, sy, dot_last(values_x, gs), dot_last(values_y, gs[ROWS:])


def wide_stats(sx, sy, dpx, dpy):
    peak = jnp.max(sx, axis=0, keepdims=True)
    peak_y = jnp.maximum(peak[:, ROWS:], jnp.max(sy, axis=0, keepdims=True))
    peak = jnp.concatenate([peak[:, :ROWS], peak_y], axis=1)
    ex, ey = jnp.exp(sx - peak), jnp.exp(sy - peak_y)
    widen = lambda a, b: jnp.concatenate([a[:, :ROWS], a[:, ROWS:] + b], axis=1)
    add = lambda a: jnp.sum(a, axis=0, keepdims=True)
    return ex, ey, peak, widen(add(ex), add(ey)), widen(add(ex * dpx), add(ey * dpy))


def wide_gradients(px, py, dpx, dpy, delta, qs, gs, kx, ky):
    pbx, pby = px.astype(BF16), py.astype(BF16)
    dsx = (px * (dpx - delta)).astype(BF16)
    dsy = (py * (dpy - delta[:, ROWS:])).astype(BF16)
    dq_z = dot_first(dsx[:, :ROWS], kx) * FACTOR
    dq_y = dot_first(both(dsx[:, ROWS:], dsy), both(kx, ky)) * FACTOR
    dkx, dky = dot(dsx, qs) * FACTOR, dot(dsy, qs[ROWS:]) * FACTOR
    return dq_z, dq_y, dkx, dky, dot(pbx, gs), dot(pby, gs[ROWS:])


def local_self(core, bias, q, g, k, v, pq, pg, pk, pv):
    q0, q1 = ordered(core, q[...], pq[...])
    g0, g1 = ordered(core, g[...], pg[...])
    k0, k1 = ordered(core, k[...], pk[...])
    v0, v1 = ordered(core, v[...], pv[...])
    qs, gs = both(q0, q1), both(g0, g1)
    return wide_scores(k0, k1, v0, v1, qs, gs, bias[...]), qs, gs, k0, k1


def local_cross(core, w, pw, q, g, pool, pq, pg, pk, pv):
    qs, gs = both(q[...], pq[...]), both(g[...], pg[...])
    ks, vs = both(pool[0], pk[...]), both(pool[1], pv[...])
    own = both(slot_pair(w, 2, core), slot_pair(w, 4, core, 0))
    partner = both(slot_pair(pw, 0, core, 4), slot_pair(pw, 2, core))
    s = add_rows(dot_last(ks, qs) * FACTOR, jnp.concatenate([own, partner], axis=1))
    return s, dot_last(vs, gs), qs, gs, ks


def self_stats_kernel(info, *refs):
    scores = local_self(info[0] % 2, *refs[:-1])[0]
    out = refs[-1]
    out[:ROWS] = refs[1][...]
    out[ROWS : 2 * ROWS] = refs[2][...]
    out[2 * ROWS :] = packed_stats(wide_stats(*scores)[2:])


def cross_stats_kernel(info, *refs):
    s, dp, _, _, _ = local_cross(info[0] % 2, *refs[:-2])
    stats = stat_rows(*partial_stats(s, dp)[1:])
    refs[-2][...] = stats[:, :, :ROWS]
    refs[-1][...] = stats[:, :, ROWS:]


def self_remote_kernel(
    info, bias, sq, sg, cq, cg, k, v, pk, pv, stats, dq_ref, kv_ref, out_stats
):
    core = info[0] % 2
    q0, q1 = ordered(core, sq[...], cq[...])
    g0, g1 = ordered(core, sg[...], cg[...])
    k0, k1 = ordered(core, k[...], pk[...])
    v0, v1 = ordered(core, v[...], pv[...])
    qs, gs = both(q1, q0), both(g1, g0)
    sx, sy, dpx, dpy = wide_scores(k1, k0, v1, v0, qs, gs, bias[...])
    ex, ey, *mine = wide_stats(sx, sy, dpx, dpy)
    known = [jnp.concatenate([x[:, ROWS:], x[:, :ROWS]], axis=1) for x in unpacked_stats(stats)]
    top, inverse, delta, scale = merge(known, mine)
    px, py = ex * scale, ey * scale[:, ROWS:]
    dq1, dq0, dk1, dk0, dv1, dv0 = wide_gradients(px, py, dpx, dpy, delta, qs, gs, k1, k0)
    same, cross = ordered(core, dq0, dq1)
    dq_ref[:ROWS] = same.astype(BF16)
    dq_ref[ROWS:] = cross.astype(BF16)
    for index, grad in enumerate(ordered(core, dk0, dk1) + ordered(core, dv0, dv1)):
        kv_ref[index * ROWS : (index + 1) * ROWS] = grad.astype(BF16)
    out_stats[...] = stat_rows(top, inverse, delta)


def cross_remote_kernel(
    info, sw, cw, sq, sg, cq, cg, pool, pk, pv, s_stats, c_stats, *outs
):
    dq_same, dq_cross, kv_ref, out_same, out_cross = outs
    core = info[0] % 2
    jobs = (
        (cq, cg, pool[0], pool[1], slot_pair(cw, 4, core, 0), c_stats, dq_cross, out_cross, 0),
        (sq, sg, pk[...], pv[...], slot_pair(sw, 0, core, 4), s_stats, dq_same, out_same, 1),
    )
    for q, g, k, v, rows, stats, dq_ref, out_stats, place in jobs:
        s, dp = add_rows(dot_last(k, q[...]) * FACTOR, rows), dot_last(v, g[...])
        e, *mine = partial_stats(s, dp)
        known = [stats[0, row : row + 1] for row in range(3)]
        top, inverse, delta, scale = merge(known, mine)
        dq, dk, dv = gradients(e * scale, dp, delta, q[...], g[...], k)
        dq_ref[...] = dq.astype(BF16)
        out_stats[...] = stat_rows(top, inverse, delta)
        kv_ref[place * ROWS : (place + 1) * ROWS] = dk.astype(BF16)
        kv_ref[(2 + place) * ROWS : (3 + place) * ROWS] = dv.astype(BF16)


def self_local_kernel(info, *refs):
    stats_ref, own_ref, kv_ref, mine, theirs = refs[-5:]
    local_peak, local_total, local_moment = unpacked_stats(own_ref)
    core = info[0] % 2
    first = info[0] < 2
    stats = stats_ref[0]
    stats = jnp.concatenate([stats[:, ROWS:], stats[:, :ROWS]], axis=1)
    inverse = 1.0 / local_total
    top = jnp.where(first, local_peak, stats[0:1])
    delta = jnp.where(first, local_moment * inverse, stats[2:3])
    inverse = jnp.where(first, inverse, stats[1:2])
    (sx, sy, dpx, dpy), qs, gs, k0, k1 = local_self(core, *refs[:-5])
    px = jnp.exp(sx - top) * inverse
    py = jnp.exp(sy - top[:, ROWS:]) * inverse[:, ROWS:]
    dq0, dq1, dk0, dk1, dv0, dv1 = wide_gradients(px, py, dpx, dpy, delta, qs, gs, k0, k1)
    grads = (ordered(core, dq0, dq1), ordered(core, dk0, dk1), ordered(core, dv0, dv1))
    for index, pair in enumerate(grads):
        for out, place, grad in ((mine, 0, pair[0]), (theirs, 1, pair[1])):
            if index > 0:
                low = (2 * index - 2 + place) * ROWS
                grad = grad + kv_ref[low : low + ROWS].astype(F32)
            out[index * ROWS : (index + 1) * ROWS] = grad.astype(BF16)


def cross_local_kernel(info, *refs):
    own_stats, partner_stats, kv_ref, mine, theirs = refs[-5:]
    stats = jnp.concatenate([own_stats[0], partner_stats[0]], axis=1)
    top, inverse, delta = stats[0:1], stats[1:2], stats[2:3]
    s, dp, qs, gs, ks = local_cross(info[0] % 2, *refs[:-5])
    dq, dk, dv = gradients(jnp.exp(s - top) * inverse, dp, delta, qs, gs, ks)
    dk = dk + kv_ref[: 2 * ROWS].astype(F32)
    dv = dv + kv_ref[2 * ROWS :].astype(F32)
    for index, grad in enumerate((dq, dk, dv)):
        mine[index * ROWS : (index + 1) * ROWS] = grad[:ROWS].astype(BF16)
        theirs[index * ROWS : (index + 1) * ROWS] = grad[ROWS:].astype(BF16)


def self_final_kernel(info, mine, theirs, dq_mine, dq_theirs, *outs):
    def write(source, extra):
        dq = source[:ROWS].astype(F32) + extra[...].astype(F32)
        outs[0][...] = dq.astype(BF16)
        outs[1][...] = source[ROWS : 2 * ROWS]
        outs[2][...] = source[2 * ROWS :]

    pl.when(pl.program_id(0) == 0)(lambda: write(mine, dq_mine))
    pl.when(pl.program_id(0) == 1)(lambda: write(theirs, dq_theirs))


def cross_final_kernel(info, mine, theirs, dq_mine, dq_theirs, dq_out, pool_out):
    def write(source, extra):
        dq = source[:ROWS].astype(F32) + extra[...].astype(F32)
        dq_out[...] = dq.astype(BF16)
        pool_out[0] = source[ROWS : 2 * ROWS]
        pool_out[1] = source[2 * ROWS :]

    pl.when(pl.program_id(0) == 0)(lambda: write(mine, dq_mine))
    pl.when(pl.program_id(0) == 1)(lambda: write(theirs, dq_theirs))


def assemble(kernel, name, info, inputs, in_specs, pooled, count):
    half = lambda h, info: (info[0] + h) % 2
    rows_out = pl.BlockSpec((ROWS, WIDE), lambda h, info: (0, half(h, info)))
    pool_out = pl.BlockSpec((2, ROWS, WIDE), lambda h, info: (0, 0, half(h, info)))
    out_specs, outs = [rows_out] * count, [((ROWS, 2 * WIDE), BF16)] * count
    if pooled:
        out_specs, outs = out_specs + [pool_out], outs + [((2, ROWS, 2 * WIDE), BF16)]
    return call(kernel, name, info, in_specs, inputs, out_specs, outs, steps=2)


def body(
    queries, keys, values, grad_self, doc_ids, cross_queries, grad_cross, pool_kv, neighbour_ids
):
    loop = lax.axis_size("ctx")
    me = lax.axis_index("ctx").astype(jnp.int32)
    info = jnp.full((1,), me, jnp.int32)
    enc_dev = pool_kv.shape[1]
    width = queries.shape[1]
    pool = pool_kv.reshape(2, ROWS, width)

    mine_spec, their_spec, their_pool = own_spec(), other_spec(), other_spec((2,))
    sizes = (4 * ROWS + EXTRA, 2 * ROWS + EXTRA, 2 * ROWS + EXTRA)
    packed, x_mine, x_other = call(
        functools.partial(pack_cross_kernel, enc_dev, loop), "pack_cross", info,
        [whole_spec(neighbour_ids.shape[::-1])] + [mine_spec] * 2 + [their_spec] * 2 + [their_pool],
        (neighbour_ids.T, cross_queries, grad_cross, cross_queries, grad_cross, pool),
        [spec(rows) for rows in sizes],
        [((rows, WIDE), BF16) for rows in sizes],
    )
    x_same = send(x_mine, outward, True)
    x_cross = send(x_other, across, True)
    x_pair = send(packed, swap, False)
    queries_in, packed = lax.optimization_barrier((queries, packed))
    sizes = (4 * ROWS, 2 * ROWS)
    packed, s_other = call(
        pack_self_kernel, "pack_self", info,
        [their_spec] * 4,
        (queries_in, grad_self, keys, values),
        [spec(rows) for rows in sizes],
        [((rows, WIDE), BF16) for rows in sizes],
    )
    s_pair = send(packed, swap, False)

    ids_of = lambda d: lax.dynamic_slice_in_dim(doc_ids, d * ROWS, ROWS, 0)
    span = jnp.arange(ROWS, dtype=jnp.int32)
    base = me // 2 * 2
    places = jnp.concatenate([span + base * ROWS, span + (base + 1) * ROWS])
    near0, near1, far0, far1 = [ids_of(base + j) for j in range(4)]
    near = jnp.concatenate([near0, near1])
    near_flip = jnp.concatenate([near1, near0])
    far_flip = jnp.concatenate([far1, far0])
    local_ok = (near[:, None] == near[None, :]) & (places[:, None] <= places[None, :])
    far_ok = (near_flip[:, None] == far_flip[None, :]) & (base + 2 < loop)
    local_bias = jnp.where(local_ok, 0.0, MASKED).astype(F32)
    far_bias = jnp.where(far_ok, 0.0, MASKED).astype(F32)

    bias_spec = whole_spec((2 * ROWS, 2 * ROWS))
    local_bias, far_bias, x_pair = lax.optimization_barrier((local_bias, far_bias, x_pair))
    self_specs = [bias_spec] + [own_spec()] * 4 + [spec(ROWS, j) for j in range(4)]
    self_args = (local_bias, queries, grad_self, keys, values) + (s_pair,) * 4
    mine_w = whole_spec((EXTRA, WIDE), (2 * ROWS // EXTRA, 0))
    partner_w = whole_spec((EXTRA, WIDE), (4 * ROWS // EXTRA, 0))
    cross_specs = (
        [mine_w, partner_w, own_spec(), own_spec(), own_spec((2,))]
        + [spec(ROWS, j) for j in range(4)]
    )
    cross_args = (x_mine, x_pair, cross_queries, grad_cross, pool) + (x_pair,) * 4
    stat = lambda rows: ((HALF, 8, rows), F32)

    x_own, x_partner = call(
        per_head(cross_stats_kernel), "cross_stats", info, cross_specs, cross_args,
        [stat_spec(ROWS)] * 2, [stat(ROWS)] * 2, flops=0,
    )
    t_same = send(x_own, outward, True)
    t_cross = send(x_partner, inward, True)
    local_bias, x_own = lax.optimization_barrier((local_bias, x_own))
    self_args = (local_bias,) + self_args[1:]
    (s_mine,) = call(
        per_head(self_stats_kernel), "self_stats", info, self_specs, self_args,
        [spec(2 * ROWS + STATS)], [((2 * ROWS + STATS, WIDE), BF16)],
    )
    stats_block = spec(STATS, 2 * ROWS // STATS)
    s_mine, x_same, x_cross, t_same, t_cross = lax.optimization_barrier(
        (s_mine, x_same, x_cross, t_same, t_cross)
    )
    s_same = send(s_mine, lambda d: d - 2, False)

    kv_out = spec(4 * ROWS)
    kv_shape = ((4 * ROWS, WIDE), BF16)
    q_shape = ((ROWS, WIDE), BF16)
    xd_same, xd_cross, x_kv, x_fin_same, x_fin_cross = call(
        per_head(cross_remote_kernel), "cross_remote", info,
        [mine_w, mine_w, spec(ROWS, 0), spec(ROWS, 1), spec(ROWS, 0), spec(ROWS, 1)]
        + [own_spec((2,)), spec(ROWS, 2), spec(ROWS, 3), stat_spec(ROWS), stat_spec(ROWS)],
        (x_same, x_cross, x_same, x_same, x_cross, x_cross, pool, x_pair, x_pair, t_same, t_cross),
        [spec(ROWS), spec(ROWS), kv_out, stat_spec(ROWS), stat_spec(ROWS)],
        [q_shape, q_shape, kv_shape, stat(ROWS), stat(ROWS)],
    )
    f_own = send(x_fin_same, inward, True)
    f_partner = send(x_fin_cross, outward, True)
    s_other, x_kv = lax.optimization_barrier((s_other, x_kv))
    s_cross = send(s_other, lambda d: (d - 2) ^ 1, False)
    x_kv, s_same = lax.optimization_barrier((x_kv, s_same))
    half_out = spec(3 * ROWS)
    half_shape = ((3 * ROWS, WIDE), BF16)
    x_keep, x_give = call(
        per_head(cross_local_kernel), "cross_local", info,
        cross_specs + [stat_spec(ROWS), stat_spec(ROWS), spec(4 * ROWS)],
        cross_args + (f_own, f_partner, x_kv),
        [half_out] * 2, [half_shape] * 2, flops=LONG,
    )

    xd_same, xd_cross, s_cross, x_keep = lax.optimization_barrier(
        (xd_same, xd_cross, s_cross, x_keep)
    )
    xr_same = send(xd_same, inward, True)
    xr_cross = send(xd_cross, across, True)
    far_bias, x_keep = lax.optimization_barrier((far_bias, x_keep))
    sd, s_kv, s_fin = call(
        per_head(self_remote_kernel), "self_remote", info,
        [bias_spec, spec(ROWS, 0), spec(ROWS, 1), spec(ROWS, 0), spec(ROWS, 1)]
        + [own_spec(), own_spec(), spec(ROWS, 2), spec(ROWS, 3), stats_block],
        (far_bias, s_same, s_same, s_cross, s_cross, keys, values, s_pair, s_pair, s_same),
        [spec(2 * ROWS), kv_out, stat_spec(2 * ROWS)],
        [((2 * ROWS, WIDE), BF16), kv_shape, stat(2 * ROWS)], flops=LONG,
    )
    f_self = send(s_fin, lambda d: d + 2, False)
    sr = send(sd, lambda d: d + 2, False)

    x_give, s_kv, xr_same, xr_cross, f_self = lax.optimization_barrier(
        (x_give, s_kv, xr_same, xr_cross, f_self)
    )
    x_take = send(x_give, swap, False)
    s_keep, s_give = call(
        per_head(self_local_kernel), "self_local", info,
        self_specs + [stat_spec(2 * ROWS), stats_block, spec(4 * ROWS)],
        self_args + (f_self, s_mine, s_kv),
        [half_out] * 2, [half_shape] * 2, flops=LONG,
    )
    three, one = whole_spec((3 * ROWS, WIDE)), whole_spec((ROWS, WIDE))
    second = whole_spec((ROWS, WIDE), (1, 0))
    grad_cq, grad_pool = assemble(
        cross_final_kernel, "cross_final", info, (x_keep, x_take, xr_same, xr_cross),
        [three, three, one, one], True, 1,
    )
    s_give, sr, grad_cq = lax.optimization_barrier((s_give, sr, grad_cq))
    s_take = send(s_give, swap, False)
    sr_take = send(sr, swap, False)
    grad_q, grad_k, grad_v = assemble(
        self_final_kernel, "self_final", info, (s_keep, s_take, sr, sr_take),
        [three, three, one, second], False, 3,
    )
    return grad_q, grad_k, grad_v, grad_cq, grad_pool.reshape(pool_kv.shape)


def solution(mesh):
    rows = P(("groups", "ctx"), None)
    pool = P(None, ("groups", "ctx"), None, None)
    return jax.shard_map(
        body,
        mesh=mesh,
        in_specs=(rows, rows, rows, rows, P("groups"), rows, rows, pool, rows),
        out_specs=(rows, rows, rows, rows, pool),
        check_vma=False,
    )
```

```python
import functools
import math

import jax
import jax.numpy as jnp
from jax import lax
from jax.experimental import pallas as pl
from jax.experimental.pallas import tpu as pltpu
from jax.sharding import PartitionSpec as P

HEADS = 8
HEAD_DIM = 128
HALF = HEADS // 2
WIDE = HALF * HEAD_DIM
STEP = 2
COLS = STEP * HEAD_DIM
STEPS = HALF // STEP
STRETCH = 64
NBR_TOK = 128
ROWS = 256
EXTRA = 16
LONG = 12 * 10**9
FACTOR = HEAD_DIM ** (-0.5)
MASKED = -1e30
BF16 = jnp.bfloat16
F32 = jnp.float32


def send(value, target_of, wrap):
    count = lax.axis_size("ctx")
    pairs = []
    for source in range(count):
        target = target_of(source)
        if wrap:
            pairs.append((source, target % count))
        elif 0 <= target < count:
            pairs.append((source, target))
    return lax.ppermute(value, "ctx", pairs)


def swap(d):
    return d ^ 1


def outward(d):
    return d - 2 if d % 2 == 0 else d + 2


def inward(d):
    return d + 2 if d % 2 == 0 else d - 2


def across(d):
    return d - 1 if d % 2 == 0 else d + 1


def spec(rows, row_block=0):
    return pl.BlockSpec((rows, COLS), lambda h, info: (row_block, h))


def own_spec(lead=()):
    zeros = (0,) * len(lead)
    return pl.BlockSpec(lead + (ROWS, COLS), lambda h, info: zeros + (0, info[0] % 2 * STEPS + h))


def other_spec(lead=()):
    zeros = (0,) * len(lead)
    return pl.BlockSpec(
        lead + (ROWS, COLS), lambda h, info: zeros + (0, (1 - info[0] % 2) * STEPS + h)
    )


def whole_spec(shape, index=None):
    index = (0,) * len(shape) if index is None else index
    return pl.BlockSpec(shape, lambda h, *info: index)


def stat_spec(rows):
    return pl.BlockSpec((STEP, 8, rows), lambda h, info: (h, 0, 0))


def call(kernel, name, info, in_specs, inputs, out_specs, outs, steps=STEPS, flops=0):
    return pl.pallas_call(
        kernel,
        name=name,
        grid_spec=pltpu.PrefetchScalarGridSpec(
            num_scalar_prefetch=1,
            grid=(steps,),
            in_specs=in_specs,
            out_specs=out_specs,
        ),
        out_shape=[jax.ShapeDtypeStruct(shape, dtype) for shape, dtype in outs],
        compiler_params=pltpu.CompilerParams(vmem_limit_bytes=64 << 20),
        cost_estimate=pl.CostEstimate(flops=flops, transcendentals=0, bytes_accessed=0),
    )(info, *inputs)


def head_of(ref, j):
    shape = ref.shape
    if len(shape) == 3 and shape[1] == 8:
        return ref.at[j : j + 1]
    if shape[-1] != COLS:
        return ref
    place = pl.ds(j * HEAD_DIM, HEAD_DIM)
    return ref.at[:, place] if len(shape) == 2 else ref.at[:, :, place]


def per_head(kernel):
    def run(info, *refs):
        for j in range(STEP):
            kernel(info, *[head_of(ref, j) for ref in refs])

    return run


def dot_last(a, b):
    return lax.dot_general(a, b, (((1,), (1,)), ((), ())), preferred_element_type=F32)


def dot_first(a, b):
    return lax.dot_general(a, b, (((0,), (0,)), ((), ())), preferred_element_type=F32)


def dot(a, b):
    return jnp.dot(a, b, preferred_element_type=F32)


def both(a, b):
    return jnp.concatenate([a, b], axis=0)


def weight_rows(times):
    log_two = jnp.where(times > 1.5, math.log(2.0), 0.0)
    return jnp.where(times < 0.5, MASKED, log_two)


def slot_pair(ref, first, core, second=None):
    times = ref[...].astype(F32)[:, :ROWS]
    low = times[first : first + 2]
    if second is None:
        return weight_rows(low)
    return weight_rows(jnp.where(core == 0, low, times[second : second + 2]))


def add_rows(s, rows):
    parts = [
        s[e * NBR_TOK : (e + 1) * NBR_TOK] + rows[e : e + 1] for e in range(s.shape[0] // NBR_TOK)
    ]
    return jnp.concatenate(parts, axis=0)


def partial_stats(s, dp):
    peak = jnp.max(s, axis=0, keepdims=True)
    e = jnp.exp(s - peak)
    return e, peak, jnp.sum(e, axis=0, keepdims=True), jnp.sum(e * dp, axis=0, keepdims=True)


def stat_rows(a, b, c):
    return jnp.concatenate([a, b, c, jnp.zeros((5, a.shape[1]), F32)], axis=0)[None]


def merge(stats, mine):
    t_peak, t_total, t_moment = stats[0, 0:1], stats[0, 1:2], stats[0, 2:3]
    peak, total, moment = mine
    top = jnp.maximum(t_peak, peak)
    t_scale = jnp.exp(t_peak - top)
    scale = jnp.exp(peak - top)
    full = t_total * t_scale + total * scale
    inverse = jnp.where(full > 0, 1.0 / full, 0.0)
    delta = (t_moment * t_scale + moment * scale) * inverse
    return top, inverse, delta, scale * inverse


def gradients(p, dp, delta, q, g, k):
    pb = p.astype(BF16)
    ds = (p * (dp - delta)).astype(BF16)
    return dot_first(ds, k) * FACTOR, dot(ds, q) * FACTOR, dot(pb, g)


def pack_cross_kernel(enc_dev, loop, info, ids_ref, qm, gm, q, g, pool, swap_ref, mine, other):
    shape = (EXTRA, mine.shape[1])
    row = lax.broadcasted_iota(jnp.int32, shape, 0)
    lane = lax.broadcasted_iota(jnp.int32, shape, 1) + pl.program_id(0) * shape[1]
    ids = ids_ref[...]
    owner = ids // enc_dev
    relative = owner - info[0] + 1
    relative = jnp.where(relative < 0, relative + loop, relative)
    relative = jnp.where(relative >= loop, relative - loop, relative)
    slots = relative * enc_dev + ids - owner * enc_dev
    times = jnp.zeros(shape, F32)
    for n in range(ids.shape[0]):
        for s in range(ids.shape[1]):
            hit = (row == slots[n : n + 1, s : s + 1]) & (lane // STRETCH == s)
            times = times + jnp.where(hit, 1.0, 0.0)
    times = times.astype(BF16)
    swap_ref[0:ROWS] = q[...]
    swap_ref[ROWS : 2 * ROWS] = g[...]
    swap_ref[2 * ROWS : 3 * ROWS] = pool[0]
    swap_ref[3 * ROWS : 4 * ROWS] = pool[1]
    swap_ref[4 * ROWS :] = times
    for out, first, second in ((mine, qm, gm), (other, q, g)):
        out[0:ROWS] = first[...]
        out[ROWS : 2 * ROWS] = second[...]
        out[2 * ROWS :] = times


def pack_self_kernel(info, qm, gm, q, g, k, v, swap_ref, mine, other):
    for index, ref in enumerate((q, g, k, v)):
        swap_ref[index * ROWS : (index + 1) * ROWS] = ref[...]
    for out, first, second in ((mine, qm, gm), (other, q, g)):
        out[0:ROWS] = first[...]
        out[ROWS : 2 * ROWS] = second[...]


def ordered(core, a, b):
    return jnp.where(core == 0, a, b), jnp.where(core == 0, b, a)


def wide_scores(keys_x, keys_y, values_x, values_y, qs, gs, bias):
    sx = dot_last(keys_x, qs) * FACTOR + bias[:ROWS]
    sy = dot_last(keys_y, qs[ROWS:]) * FACTOR + bias[ROWS:, ROWS:]
    return sx, sy, dot_last(values_x, gs), dot_last(values_y, gs[ROWS:])


def wide_stats(sx, sy, dpx, dpy):
    peak = jnp.max(sx, axis=0, keepdims=True)
    peak_y = jnp.maximum(peak[:, ROWS:], jnp.max(sy, axis=0, keepdims=True))
    peak = jnp.concatenate([peak[:, :ROWS], peak_y], axis=1)
    ex, ey = jnp.exp(sx - peak), jnp.exp(sy - peak_y)
    widen = lambda a, b: jnp.concatenate([a[:, :ROWS], a[:, ROWS:] + b], axis=1)
    add = lambda a: jnp.sum(a, axis=0, keepdims=True)
    return ex, ey, peak, widen(add(ex), add(ey)), widen(add(ex * dpx), add(ey * dpy))


def wide_gradients(px, py, dpx, dpy, delta, qs, gs, kx, ky):
    pbx, pby = px.astype(BF16), py.astype(BF16)
    dsx = (px * (dpx - delta)).astype(BF16)
    dsy = (py * (dpy - delta[:, ROWS:])).astype(BF16)
    dq_z = dot_first(dsx[:, :ROWS], kx) * FACTOR
    dq_y = dot_first(both(dsx[:, ROWS:], dsy), both(kx, ky)) * FACTOR
    dkx, dky = dot(dsx, qs) * FACTOR, dot(dsy, qs[ROWS:]) * FACTOR
    return dq_z, dq_y, dkx, dky, dot(pbx, gs), dot(pby, gs[ROWS:])


def local_self(core, bias, q, g, k, v, pq, pg, pk, pv):
    q0, q1 = ordered(core, q[...], pq[...])
    g0, g1 = ordered(core, g[...], pg[...])
    k0, k1 = ordered(core, k[...], pk[...])
    v0, v1 = ordered(core, v[...], pv[...])
    qs, gs = both(q0, q1), both(g0, g1)
    return wide_scores(k0, k1, v0, v1, qs, gs, bias[...]), qs, gs, k0, k1


def local_cross(core, w, pw, q, g, pool, pq, pg, pk, pv):
    qs, gs = both(q[...], pq[...]), both(g[...], pg[...])
    ks, vs = both(pool[0], pk[...]), both(pool[1], pv[...])
    own = both(slot_pair(w, 2, core), slot_pair(w, 4, core, 0))
    partner = both(slot_pair(pw, 0, core, 4), slot_pair(pw, 2, core))
    s = add_rows(dot_last(ks, qs) * FACTOR, jnp.concatenate([own, partner], axis=1))
    return s, dot_last(vs, gs), qs, gs, ks


def self_stats_kernel(info, *refs):
    scores = local_self(info[0] % 2, *refs[:-1])[0]
    refs[-1][...] = stat_rows(*wide_stats(*scores)[2:])


def cross_stats_kernel(info, *refs):
    s, dp, _, _, _ = local_cross(info[0] % 2, *refs[:-2])
    stats = stat_rows(*partial_stats(s, dp)[1:])
    refs[-2][...] = stats[:, :, :ROWS]
    refs[-1][...] = stats[:, :, ROWS:]


def self_remote_kernel(
    info, bias, sq, sg, cq, cg, k, v, pk, pv, stats, dq_ref, kv_ref, out_stats
):
    core = info[0] % 2
    q0, q1 = ordered(core, sq[...], cq[...])
    g0, g1 = ordered(core, sg[...], cg[...])
    k0, k1 = ordered(core, k[...], pk[...])
    v0, v1 = ordered(core, v[...], pv[...])
    qs, gs = both(q1, q0), both(g1, g0)
    sx, sy, dpx, dpy = wide_scores(k1, k0, v1, v0, qs, gs, bias[...])
    ex, ey, *mine = wide_stats(sx, sy, dpx, dpy)
    known = stats[...]
    known = jnp.concatenate([known[:, :, ROWS:], known[:, :, :ROWS]], axis=2)
    top, inverse, delta, scale = merge(known, mine)
    px, py = ex * scale, ey * scale[:, ROWS:]
    dq1, dq0, dk1, dk0, dv1, dv0 = wide_gradients(px, py, dpx, dpy, delta, qs, gs, k1, k0)
    same, cross = ordered(core, dq0, dq1)
    dq_ref[:ROWS] = same.astype(BF16)
    dq_ref[ROWS:] = cross.astype(BF16)
    for index, grad in enumerate(ordered(core, dk0, dk1) + ordered(core, dv0, dv1)):
        kv_ref[index * ROWS : (index + 1) * ROWS] = grad.astype(BF16)
    out_stats[...] = stat_rows(top, inverse, delta)


def cross_remote_kernel(
    info, sw, cw, sq, sg, cq, cg, pool, pk, pv, s_stats, c_stats, *outs
):
    dq_same, dq_cross, kv_ref, out_same, out_cross = outs
    core = info[0] % 2
    jobs = (
        (cq, cg, pool[0], pool[1], slot_pair(cw, 4, core, 0), c_stats, dq_cross, out_cross, 0),
        (sq, sg, pk[...], pv[...], slot_pair(sw, 0, core, 4), s_stats, dq_same, out_same, 1),
    )
    for q, g, k, v, rows, stats, dq_ref, out_stats, place in jobs:
        s, dp = add_rows(dot_last(k, q[...]) * FACTOR, rows), dot_last(v, g[...])
        e, *mine = partial_stats(s, dp)
        top, inverse, delta, scale = merge(stats[...], mine)
        dq, dk, dv = gradients(e * scale, dp, delta, q[...], g[...], k)
        dq_ref[...] = dq.astype(BF16)
        out_stats[...] = stat_rows(top, inverse, delta)
        kv_ref[place * ROWS : (place + 1) * ROWS] = dk.astype(BF16)
        kv_ref[(2 + place) * ROWS : (3 + place) * ROWS] = dv.astype(BF16)


def self_local_kernel(info, *refs):
    stats_ref, own_ref, kv_ref, mine, theirs = refs[-5:]
    local = own_ref[0]
    core = info[0] % 2
    first = info[0] < 2
    stats = stats_ref[0]
    stats = jnp.concatenate([stats[:, ROWS:], stats[:, :ROWS]], axis=1)
    inverse = 1.0 / local[1:2]
    top = jnp.where(first, local[0:1], stats[0:1])
    delta = jnp.where(first, local[2:3] * inverse, stats[2:3])
    inverse = jnp.where(first, inverse, stats[1:2])
    (sx, sy, dpx, dpy), qs, gs, k0, k1 = local_self(core, *refs[:-5])
    px = jnp.exp(sx - top) * inverse
    py = jnp.exp(sy - top[:, ROWS:]) * inverse[:, ROWS:]
    dq0, dq1, dk0, dk1, dv0, dv1 = wide_gradients(px, py, dpx, dpy, delta, qs, gs, k0, k1)
    grads = (ordered(core, dq0, dq1), ordered(core, dk0, dk1), ordered(core, dv0, dv1))
    for index, pair in enumerate(grads):
        for out, place, grad in ((mine, 0, pair[0]), (theirs, 1, pair[1])):
            if index > 0:
                low = (2 * index - 2 + place) * ROWS
                grad = grad + kv_ref[low : low + ROWS].astype(F32)
            out[index * ROWS : (index + 1) * ROWS] = grad.astype(BF16)


def cross_local_kernel(info, *refs):
    own_stats, partner_stats, kv_ref, mine, theirs = refs[-5:]
    stats = jnp.concatenate([own_stats[0], partner_stats[0]], axis=1)
    top, inverse, delta = stats[0:1], stats[1:2], stats[2:3]
    s, dp, qs, gs, ks = local_cross(info[0] % 2, *refs[:-5])
    dq, dk, dv = gradients(jnp.exp(s - top) * inverse, dp, delta, qs, gs, ks)
    dk = dk + kv_ref[: 2 * ROWS].astype(F32)
    dv = dv + kv_ref[2 * ROWS :].astype(F32)
    for index, grad in enumerate((dq, dk, dv)):
        mine[index * ROWS : (index + 1) * ROWS] = grad[:ROWS].astype(BF16)
        theirs[index * ROWS : (index + 1) * ROWS] = grad[ROWS:].astype(BF16)


def kv_final_kernel(info, mine, theirs, *outs):
    def write(source):
        outs[0][...] = source[ROWS : 2 * ROWS]
        outs[1][...] = source[2 * ROWS :]

    pl.when(pl.program_id(0) == 0)(lambda: write(mine))
    pl.when(pl.program_id(0) == 1)(lambda: write(theirs))


def query_final_kernel(info, mine, theirs, dq_mine, dq_theirs, out):
    def write(source, extra):
        out[...] = (source[...].astype(F32) + extra[...].astype(F32)).astype(BF16)

    pl.when(pl.program_id(0) == 0)(lambda: write(mine, dq_mine))
    pl.when(pl.program_id(0) == 1)(lambda: write(theirs, dq_theirs))


def cross_final_kernel(info, mine, theirs, dq_mine, dq_theirs, dq_out, pool_out):
    def write(source, extra):
        dq = source[:ROWS].astype(F32) + extra[...].astype(F32)
        dq_out[...] = dq.astype(BF16)
        pool_out[0] = source[ROWS : 2 * ROWS]
        pool_out[1] = source[2 * ROWS :]

    pl.when(pl.program_id(0) == 0)(lambda: write(mine, dq_mine))
    pl.when(pl.program_id(0) == 1)(lambda: write(theirs, dq_theirs))


def assemble(kernel, name, info, inputs, in_specs, pooled, count):
    half = lambda h, info: (info[0] + h) % 2
    rows_out = pl.BlockSpec((ROWS, WIDE), lambda h, info: (0, half(h, info)))
    pool_out = pl.BlockSpec((2, ROWS, WIDE), lambda h, info: (0, 0, half(h, info)))
    out_specs, outs = [rows_out] * count, [((ROWS, 2 * WIDE), BF16)] * count
    if pooled:
        out_specs, outs = out_specs + [pool_out], outs + [((2, ROWS, 2 * WIDE), BF16)]
    return call(kernel, name, info, in_specs, inputs, out_specs, outs, steps=2)


def body(
    queries, keys, values, grad_self, doc_ids, cross_queries, grad_cross, pool_kv, neighbour_ids
):
    loop = lax.axis_size("ctx")
    me = lax.axis_index("ctx").astype(jnp.int32)
    info = jnp.full((1,), me, jnp.int32)
    enc_dev = pool_kv.shape[1]
    width = queries.shape[1]
    pool = pool_kv.reshape(2, ROWS, width)

    mine_spec, their_spec, their_pool = own_spec(), other_spec(), other_spec((2,))
    sizes = (4 * ROWS + EXTRA, 2 * ROWS + EXTRA, 2 * ROWS + EXTRA)
    packed, x_mine, x_other = call(
        functools.partial(pack_cross_kernel, enc_dev, loop), "pack_cross", info,
        [whole_spec(neighbour_ids.shape[::-1])] + [mine_spec] * 2 + [their_spec] * 2 + [their_pool],
        (neighbour_ids.T, cross_queries, grad_cross, cross_queries, grad_cross, pool),
        [spec(rows) for rows in sizes],
        [((rows, WIDE), BF16) for rows in sizes],
    )
    x_same = send(x_mine, outward, True)
    x_cross = send(x_other, across, True)
    x_pair = send(packed, swap, False)
    queries_in, packed = lax.optimization_barrier((queries, packed))
    sizes = (4 * ROWS, 2 * ROWS, 2 * ROWS)
    packed, s_mine, s_other = call(
        pack_self_kernel, "pack_self", info,
        [mine_spec] * 2 + [their_spec] * 4,
        (queries_in, grad_self, queries_in, grad_self, keys, values),
        [spec(rows) for rows in sizes],
        [((rows, WIDE), BF16) for rows in sizes],
    )
    s_pair = send(packed, swap, False)

    ids_of = lambda d: lax.dynamic_slice_in_dim(doc_ids, d * ROWS, ROWS, 0)
    span = jnp.arange(ROWS, dtype=jnp.int32)
    base = me // 2 * 2
    places = jnp.concatenate([span + base * ROWS, span + (base + 1) * ROWS])
    near0, near1, far0, far1 = [ids_of(base + j) for j in range(4)]
    near = jnp.concatenate([near0, near1])
    near_flip = jnp.concatenate([near1, near0])
    far_flip = jnp.concatenate([far1, far0])
    local_ok = (near[:, None] == near[None, :]) & (places[:, None] <= places[None, :])
    far_ok = (near_flip[:, None] == far_flip[None, :]) & (base + 2 < loop)
    local_bias = jnp.where(local_ok, 0.0, MASKED).astype(F32)
    far_bias = jnp.where(far_ok, 0.0, MASKED).astype(F32)

    bias_spec = whole_spec((2 * ROWS, 2 * ROWS))
    local_bias, far_bias, x_pair = lax.optimization_barrier((local_bias, far_bias, x_pair))
    self_specs = [bias_spec] + [own_spec()] * 4 + [spec(ROWS, j) for j in range(4)]
    self_args = (local_bias, queries, grad_self, keys, values) + (s_pair,) * 4
    mine_w = whole_spec((EXTRA, WIDE), (2 * ROWS // EXTRA, 0))
    partner_w = whole_spec((EXTRA, WIDE), (4 * ROWS // EXTRA, 0))
    cross_specs = (
        [mine_w, partner_w, own_spec(), own_spec(), own_spec((2,))]
        + [spec(ROWS, j) for j in range(4)]
    )
    cross_args = (x_mine, x_pair, cross_queries, grad_cross, pool) + (x_pair,) * 4
    stat = lambda rows: ((HALF, 8, rows), F32)

    x_own, x_partner = call(
        per_head(cross_stats_kernel), "cross_stats", info, cross_specs, cross_args,
        [stat_spec(ROWS)] * 2, [stat(ROWS)] * 2, flops=0,
    )
    t_same = send(x_own, outward, True)
    t_cross = send(x_partner, inward, True)
    local_bias, x_own = lax.optimization_barrier((local_bias, x_own))
    self_args = (local_bias,) + self_args[1:]
    (s_own,) = call(
        per_head(self_stats_kernel), "self_stats", info, self_specs, self_args,
        [stat_spec(2 * ROWS)], [stat(2 * ROWS)], flops=0,
    )
    t_self = send(s_own, lambda d: d - 2, False)
    s_mine, x_same, x_cross, t_same, t_cross, s_own = lax.optimization_barrier(
        (s_mine, x_same, x_cross, t_same, t_cross, s_own)
    )
    s_same = send(s_mine, lambda d: d - 2, False)

    kv_out = spec(4 * ROWS)
    kv_shape = ((4 * ROWS, WIDE), BF16)
    q_shape = ((ROWS, WIDE), BF16)
    xd_same, xd_cross, x_kv, x_fin_same, x_fin_cross = call(
        per_head(cross_remote_kernel), "cross_remote", info,
        [mine_w, mine_w, spec(ROWS, 0), spec(ROWS, 1), spec(ROWS, 0), spec(ROWS, 1)]
        + [own_spec((2,)), spec(ROWS, 2), spec(ROWS, 3), stat_spec(ROWS), stat_spec(ROWS)],
        (x_same, x_cross, x_same, x_same, x_cross, x_cross, pool, x_pair, x_pair, t_same, t_cross),
        [spec(ROWS), spec(ROWS), kv_out, stat_spec(ROWS), stat_spec(ROWS)],
        [q_shape, q_shape, kv_shape, stat(ROWS), stat(ROWS)],
    )
    f_own = send(x_fin_same, inward, True)
    f_partner = send(x_fin_cross, outward, True)
    s_other, x_kv = lax.optimization_barrier((s_other, x_kv))
    s_cross = send(s_other, lambda d: (d - 2) ^ 1, False)
    x_kv, s_same, t_self = lax.optimization_barrier((x_kv, s_same, t_self))
    half_out = spec(3 * ROWS)
    half_shape = ((3 * ROWS, WIDE), BF16)
    x_keep, x_give = call(
        per_head(cross_local_kernel), "cross_local", info,
        cross_specs + [stat_spec(ROWS), stat_spec(ROWS), spec(4 * ROWS)],
        cross_args + (f_own, f_partner, x_kv),
        [half_out] * 2, [half_shape] * 2, flops=LONG,
    )

    xd_same, xd_cross, s_cross, x_keep = lax.optimization_barrier(
        (xd_same, xd_cross, s_cross, x_keep)
    )
    xr_same = send(xd_same, inward, True)
    xr_cross = send(xd_cross, across, True)
    far_bias, x_keep = lax.optimization_barrier((far_bias, x_keep))
    sd, s_kv, s_fin = call(
        per_head(self_remote_kernel), "self_remote", info,
        [bias_spec, spec(ROWS, 0), spec(ROWS, 1), spec(ROWS, 0), spec(ROWS, 1)]
        + [own_spec(), own_spec(), spec(ROWS, 2), spec(ROWS, 3), stat_spec(2 * ROWS)],
        (far_bias, s_same, s_same, s_cross, s_cross, keys, values, s_pair, s_pair, t_self),
        [spec(2 * ROWS), kv_out, stat_spec(2 * ROWS)],
        [((2 * ROWS, WIDE), BF16), kv_shape, stat(2 * ROWS)], flops=LONG,
    )
    f_self = send(s_fin, lambda d: d + 2, False)
    sr = send(sd, lambda d: d + 2, False)

    x_give, s_kv, xr_same, xr_cross, f_self = lax.optimization_barrier(
        (x_give, s_kv, xr_same, xr_cross, f_self)
    )
    x_take = send(x_give, swap, False)
    s_keep, s_give = call(
        per_head(self_local_kernel), "self_local", info,
        self_specs + [stat_spec(2 * ROWS), stat_spec(2 * ROWS), spec(4 * ROWS)],
        self_args + (f_self, s_own, s_kv),
        [half_out] * 2, [half_shape] * 2, flops=LONG,
    )
    three, one = whole_spec((3 * ROWS, WIDE)), whole_spec((ROWS, WIDE))
    second = whole_spec((ROWS, WIDE), (1, 0))
    s_take = send(s_give, swap, False)
    grad_cq, grad_pool = assemble(
        cross_final_kernel, "cross_final", info, (x_keep, x_take, xr_same, xr_cross),
        [three, three, one, one], True, 1,
    )
    grad_k, grad_v = assemble(
        kv_final_kernel, "kv_final", info, (s_keep, s_take), [three, three], False, 2
    )
    sr, grad_cq = lax.optimization_barrier((sr, grad_cq))
    sr_take = send(sr, swap, False)
    (grad_q,) = assemble(
        query_final_kernel, "query_final", info, (s_keep, s_take, sr, sr_take),
        [one, one, one, second], False, 1,
    )
    return grad_q, grad_k, grad_v, grad_cq, grad_pool.reshape(pool_kv.shape)


def solution(mesh):
    rows = P(("groups", "ctx"), None)
    pool = P(None, ("groups", "ctx"), None, None)
    return jax.shard_map(
        body,
        mesh=mesh,
        in_specs=(rows, rows, rows, rows, P("groups"), rows, rows, pool, rows),
        out_specs=(rows, rows, rows, rows, pool),
        check_vma=False,
    )
```

```python
import functools
import math

import jax
import jax.numpy as jnp
from jax import lax
from jax.experimental import pallas as pl
from jax.experimental.pallas import tpu as pltpu
from jax.sharding import PartitionSpec as P

HEADS = 8
HEAD_DIM = 128
HALF = HEADS // 2
WIDE = HALF * HEAD_DIM
STEP = 2
COLS = STEP * HEAD_DIM
STEPS = HALF // STEP
STRETCH = 64
NBR_TOK = 128
ROWS = 256
EXTRA = 16
LONG = 12 * 10**9
FACTOR = HEAD_DIM ** (-0.5)
MASKED = -1e30
BF16 = jnp.bfloat16
F32 = jnp.float32


def send(value, target_of, wrap):
    count = lax.axis_size("ctx")
    pairs = []
    for source in range(count):
        target = target_of(source)
        if wrap:
            pairs.append((source, target % count))
        elif 0 <= target < count:
            pairs.append((source, target))
    return lax.ppermute(value, "ctx", pairs)


def swap(d):
    return d ^ 1


def outward(d):
    return d - 2 if d % 2 == 0 else d + 2


def inward(d):
    return d + 2 if d % 2 == 0 else d - 2


def across(d):
    return d - 1 if d % 2 == 0 else d + 1


def spec(rows, row_block=0):
    return pl.BlockSpec((rows, COLS), lambda h, info: (row_block, h))


def own_spec(lead=()):
    zeros = (0,) * len(lead)
    return pl.BlockSpec(lead + (ROWS, COLS), lambda h, info: zeros + (0, info[0] % 2 * STEPS + h))


def other_spec(lead=()):
    zeros = (0,) * len(lead)
    return pl.BlockSpec(
        lead + (ROWS, COLS), lambda h, info: zeros + (0, (1 - info[0] % 2) * STEPS + h)
    )


def whole_spec(shape, index=None):
    index = (0,) * len(shape) if index is None else index
    return pl.BlockSpec(shape, lambda h, *info: index)


def stat_spec(rows):
    return pl.BlockSpec((STEP, 8, rows), lambda h, info: (h, 0, 0))


def call(kernel, name, info, in_specs, inputs, out_specs, outs, steps=STEPS, flops=0):
    return pl.pallas_call(
        kernel,
        name=name,
        grid_spec=pltpu.PrefetchScalarGridSpec(
            num_scalar_prefetch=1,
            grid=(steps,),
            in_specs=in_specs,
            out_specs=out_specs,
        ),
        out_shape=[jax.ShapeDtypeStruct(shape, dtype) for shape, dtype in outs],
        compiler_params=pltpu.CompilerParams(vmem_limit_bytes=64 << 20),
        cost_estimate=pl.CostEstimate(flops=flops, transcendentals=0, bytes_accessed=0),
    )(info, *inputs)


def head_of(ref, j):
    shape = ref.shape
    if len(shape) == 3 and shape[1] == 8:
        return ref.at[j : j + 1]
    if shape[-1] != COLS:
        return ref
    place = pl.ds(j * HEAD_DIM, HEAD_DIM)
    return ref.at[:, place] if len(shape) == 2 else ref.at[:, :, place]


def per_head(kernel):
    def run(info, *refs):
        for j in range(STEP):
            kernel(info, *[head_of(ref, j) for ref in refs])

    return run


def dot_last(a, b):
    return lax.dot_general(a, b, (((1,), (1,)), ((), ())), preferred_element_type=F32)


def dot_first(a, b):
    return lax.dot_general(a, b, (((0,), (0,)), ((), ())), preferred_element_type=F32)


def dot(a, b):
    return jnp.dot(a, b, preferred_element_type=F32)


def both(a, b):
    return jnp.concatenate([a, b], axis=0)


def weight_rows(times):
    log_two = jnp.where(times > 1.5, math.log(2.0), 0.0)
    return jnp.where(times < 0.5, MASKED, log_two)


def slot_pair(ref, first, core, second=None):
    times = ref[...].astype(F32)[:, :ROWS]
    low = times[first : first + 2]
    if second is None:
        return weight_rows(low)
    return weight_rows(jnp.where(core == 0, low, times[second : second + 2]))


def add_rows(s, rows):
    parts = [
        s[e * NBR_TOK : (e + 1) * NBR_TOK] + rows[e : e + 1] for e in range(s.shape[0] // NBR_TOK)
    ]
    return jnp.concatenate(parts, axis=0)


def partial_stats(s, dp):
    peak = jnp.max(s, axis=0, keepdims=True)
    e = jnp.exp(s - peak)
    return e, peak, jnp.sum(e, axis=0, keepdims=True), jnp.sum(e * dp, axis=0, keepdims=True)


def stat_rows(a, b, c):
    return jnp.concatenate([a, b, c, jnp.zeros((5, a.shape[1]), F32)], axis=0)[None]


def merge(stats, mine):
    t_peak, t_total, t_moment = stats[0, 0:1], stats[0, 1:2], stats[0, 2:3]
    peak, total, moment = mine
    top = jnp.maximum(t_peak, peak)
    t_scale = jnp.exp(t_peak - top)
    scale = jnp.exp(peak - top)
    full = t_total * t_scale + total * scale
    inverse = jnp.where(full > 0, 1.0 / full, 0.0)
    delta = (t_moment * t_scale + moment * scale) * inverse
    return top, inverse, delta, scale * inverse


def gradients(p, dp, delta, q, g, k):
    pb = p.astype(BF16)
    ds = (p * (dp - delta)).astype(BF16)
    return dot_first(ds, k) * FACTOR, dot(ds, q) * FACTOR, dot(pb, g)


def naming(enc_dev, loop, me, ids, cols):
    shape = (EXTRA, cols)
    row = lax.broadcasted_iota(jnp.int32, shape, 0)
    lane = lax.broadcasted_iota(jnp.int32, shape, 1) + pl.program_id(0) * shape[1]
    owner = ids // enc_dev
    relative = owner - me + 1
    relative = jnp.where(relative < 0, relative + loop, relative)
    relative = jnp.where(relative >= loop, relative - loop, relative)
    slots = relative * enc_dev + ids - owner * enc_dev
    times = jnp.zeros(shape, F32)
    for n in range(ids.shape[0]):
        for s in range(ids.shape[1]):
            hit = (row == slots[n : n + 1, s : s + 1]) & (lane // STRETCH == s)
            times = times + jnp.where(hit, 1.0, 0.0)
    return times.astype(BF16)


def pack_cross_kernel(enc_dev, loop, info, ids_ref, qm, gm, q, g, mine, other):
    times = naming(enc_dev, loop, info[0], ids_ref[...], mine.shape[1])
    for out, first, second in ((mine, qm, gm), (other, q, g)):
        out[0:ROWS] = first[...]
        out[ROWS : 2 * ROWS] = second[...]
        out[2 * ROWS :] = times


def pack_swap_kernel(enc_dev, loop, info, ids_ref, q, g, pool, swap_ref):
    swap_ref[0:ROWS] = q[...]
    swap_ref[ROWS : 2 * ROWS] = g[...]
    swap_ref[2 * ROWS : 3 * ROWS] = pool[0]
    swap_ref[3 * ROWS : 4 * ROWS] = pool[1]
    swap_ref[4 * ROWS :] = naming(enc_dev, loop, info[0], ids_ref[...], swap_ref.shape[1])


def pack_self_kernel(info, qm, gm, q, g, k, v, swap_ref, mine, other):
    for index, ref in enumerate((q, g, k, v)):
        swap_ref[index * ROWS : (index + 1) * ROWS] = ref[...]
    for out, first, second in ((mine, qm, gm), (other, q, g)):
        out[0:ROWS] = first[...]
        out[ROWS : 2 * ROWS] = second[...]


def ordered(core, a, b):
    return jnp.where(core == 0, a, b), jnp.where(core == 0, b, a)


def wide_scores(keys_x, keys_y, values_x, values_y, qs, gs, bias):
    sx = dot_last(keys_x, qs) * FACTOR + bias[:ROWS]
    sy = dot_last(keys_y, qs[ROWS:]) * FACTOR + bias[ROWS:, ROWS:]
    return sx, sy, dot_last(values_x, gs), dot_last(values_y, gs[ROWS:])


def wide_stats(sx, sy, dpx, dpy):
    peak = jnp.max(sx, axis=0, keepdims=True)
    peak_y = jnp.maximum(peak[:, ROWS:], jnp.max(sy, axis=0, keepdims=True))
    peak = jnp.concatenate([peak[:, :ROWS], peak_y], axis=1)
    ex, ey = jnp.exp(sx - peak), jnp.exp(sy - peak_y)
    widen = lambda a, b: jnp.concatenate([a[:, :ROWS], a[:, ROWS:] + b], axis=1)
    add = lambda a: jnp.sum(a, axis=0, keepdims=True)
    return ex, ey, peak, widen(add(ex), add(ey)), widen(add(ex * dpx), add(ey * dpy))


def wide_gradients(px, py, dpx, dpy, delta, qs, gs, kx, ky):
    pbx, pby = px.astype(BF16), py.astype(BF16)
    dsx = (px * (dpx - delta)).astype(BF16)
    dsy = (py * (dpy - delta[:, ROWS:])).astype(BF16)
    dq_z = dot_first(dsx[:, :ROWS], kx) * FACTOR
    dq_y = dot_first(both(dsx[:, ROWS:], dsy), both(kx, ky)) * FACTOR
    dkx, dky = dot(dsx, qs) * FACTOR, dot(dsy, qs[ROWS:]) * FACTOR
    return dq_z, dq_y, dkx, dky, dot(pbx, gs), dot(pby, gs[ROWS:])


def local_self(core, bias, q, g, k, v, pq, pg, pk, pv):
    q0, q1 = ordered(core, q[...], pq[...])
    g0, g1 = ordered(core, g[...], pg[...])
    k0, k1 = ordered(core, k[...], pk[...])
    v0, v1 = ordered(core, v[...], pv[...])
    qs, gs = both(q0, q1), both(g0, g1)
    return wide_scores(k0, k1, v0, v1, qs, gs, bias[...]), qs, gs, k0, k1


def local_cross(core, w, pw, q, g, pool, pq, pg, pk, pv):
    qs, gs = both(q[...], pq[...]), both(g[...], pg[...])
    ks, vs = both(pool[0], pk[...]), both(pool[1], pv[...])
    own = both(slot_pair(w, 2, core), slot_pair(w, 4, core, 0))
    partner = both(slot_pair(pw, 0, core, 4), slot_pair(pw, 2, core))
    s = add_rows(dot_last(ks, qs) * FACTOR, jnp.concatenate([own, partner], axis=1))
    return s, dot_last(vs, gs), qs, gs, ks


def self_stats_kernel(info, *refs):
    scores = local_self(info[0] % 2, *refs[:-1])[0]
    refs[-1][...] = stat_rows(*wide_stats(*scores)[2:])


def cross_stats_kernel(info, *refs):
    s, dp, _, _, _ = local_cross(info[0] % 2, *refs[:-2])
    stats = stat_rows(*partial_stats(s, dp)[1:])
    refs[-2][...] = stats[:, :, :ROWS]
    refs[-1][...] = stats[:, :, ROWS:]


def self_remote_kernel(
    info, bias, sq, sg, cq, cg, k, v, pk, pv, stats, dq_ref, kv_ref, out_stats
):
    core = info[0] % 2
    q0, q1 = ordered(core, sq[...], cq[...])
    g0, g1 = ordered(core, sg[...], cg[...])
    k0, k1 = ordered(core, k[...], pk[...])
    v0, v1 = ordered(core, v[...], pv[...])
    qs, gs = both(q1, q0), both(g1, g0)
    sx, sy, dpx, dpy = wide_scores(k1, k0, v1, v0, qs, gs, bias[...])
    ex, ey, *mine = wide_stats(sx, sy, dpx, dpy)
    known = stats[...]
    known = jnp.concatenate([known[:, :, ROWS:], known[:, :, :ROWS]], axis=2)
    top, inverse, delta, scale = merge(known, mine)
    px, py = ex * scale, ey * scale[:, ROWS:]
    dq1, dq0, dk1, dk0, dv1, dv0 = wide_gradients(px, py, dpx, dpy, delta, qs, gs, k1, k0)
    same, cross = ordered(core, dq0, dq1)
    dq_ref[:ROWS] = same.astype(BF16)
    dq_ref[ROWS:] = cross.astype(BF16)
    for index, grad in enumerate(ordered(core, dk0, dk1) + ordered(core, dv0, dv1)):
        kv_ref[index * ROWS : (index + 1) * ROWS] = grad.astype(BF16)
    out_stats[...] = stat_rows(top, inverse, delta)


def cross_remote_kernel(
    info, sw, cw, sq, sg, cq, cg, pool, pk, pv, s_stats, c_stats, *outs
):
    dq_same, dq_cross, kv_ref, out_same, out_cross = outs
    core = info[0] % 2
    jobs = (
        (cq, cg, pool[0], pool[1], slot_pair(cw, 4, core, 0), c_stats, dq_cross, out_cross, 0),
        (sq, sg, pk[...], pv[...], slot_pair(sw, 0, core, 4), s_stats, dq_same, out_same, 1),
    )
    for q, g, k, v, rows, stats, dq_ref, out_stats, place in jobs:
        s, dp = add_rows(dot_last(k, q[...]) * FACTOR, rows), dot_last(v, g[...])
        e, *mine = partial_stats(s, dp)
        top, inverse, delta, scale = merge(stats[...], mine)
        dq, dk, dv = gradients(e * scale, dp, delta, q[...], g[...], k)
        dq_ref[...] = dq.astype(BF16)
        out_stats[...] = stat_rows(top, inverse, delta)
        kv_ref[place * ROWS : (place + 1) * ROWS] = dk.astype(BF16)
        kv_ref[(2 + place) * ROWS : (3 + place) * ROWS] = dv.astype(BF16)


def self_local_kernel(info, *refs):
    stats_ref, own_ref, kv_ref, mine, theirs = refs[-5:]
    local = own_ref[0]
    core = info[0] % 2
    first = info[0] < 2
    stats = stats_ref[0]
    stats = jnp.concatenate([stats[:, ROWS:], stats[:, :ROWS]], axis=1)
    inverse = 1.0 / local[1:2]
    top = jnp.where(first, local[0:1], stats[0:1])
    delta = jnp.where(first, local[2:3] * inverse, stats[2:3])
    inverse = jnp.where(first, inverse, stats[1:2])
    (sx, sy, dpx, dpy), qs, gs, k0, k1 = local_self(core, *refs[:-5])
    px = jnp.exp(sx - top) * inverse
    py = jnp.exp(sy - top[:, ROWS:]) * inverse[:, ROWS:]
    dq0, dq1, dk0, dk1, dv0, dv1 = wide_gradients(px, py, dpx, dpy, delta, qs, gs, k0, k1)
    grads = (ordered(core, dq0, dq1), ordered(core, dk0, dk1), ordered(core, dv0, dv1))
    for index, pair in enumerate(grads):
        for out, place, grad in ((mine, 0, pair[0]), (theirs, 1, pair[1])):
            if index > 0:
                low = (2 * index - 2 + place) * ROWS
                grad = grad + kv_ref[low : low + ROWS].astype(F32)
            out[index * ROWS : (index + 1) * ROWS] = grad.astype(BF16)


def cross_local_kernel(info, *refs):
    own_stats, partner_stats, kv_ref, mine, theirs = refs[-5:]
    stats = jnp.concatenate([own_stats[0], partner_stats[0]], axis=1)
    top, inverse, delta = stats[0:1], stats[1:2], stats[2:3]
    s, dp, qs, gs, ks = local_cross(info[0] % 2, *refs[:-5])
    dq, dk, dv = gradients(jnp.exp(s - top) * inverse, dp, delta, qs, gs, ks)
    dk = dk + kv_ref[: 2 * ROWS].astype(F32)
    dv = dv + kv_ref[2 * ROWS :].astype(F32)
    for index, grad in enumerate((dq, dk, dv)):
        mine[index * ROWS : (index + 1) * ROWS] = grad[:ROWS].astype(BF16)
        theirs[index * ROWS : (index + 1) * ROWS] = grad[ROWS:].astype(BF16)


def kv_final_kernel(info, mine, theirs, dq_mine, k_out, v_out, q_out):
    def write(source):
        k_out[...] = source[ROWS : 2 * ROWS]
        v_out[...] = source[2 * ROWS :]
        q_out[...] = (mine[:ROWS].astype(F32) + dq_mine[...].astype(F32)).astype(BF16)

    pl.when(pl.program_id(0) == 0)(lambda: write(mine))
    pl.when(pl.program_id(0) == 1)(lambda: write(theirs))


def query_final_kernel(info, theirs, dq_theirs, grad, out):
    out[...] = (theirs[...].astype(F32) + dq_theirs[...].astype(F32)).astype(BF16)


def cross_final_kernel(info, mine, theirs, dq_mine, dq_theirs, dq_out, pool_out):
    def write(source, extra):
        dq = source[:ROWS].astype(F32) + extra[...].astype(F32)
        dq_out[...] = dq.astype(BF16)
        pool_out[0] = source[ROWS : 2 * ROWS]
        pool_out[1] = source[2 * ROWS :]

    pl.when(pl.program_id(0) == 0)(lambda: write(mine, dq_mine))
    pl.when(pl.program_id(0) == 1)(lambda: write(theirs, dq_theirs))


def assemble(kernel, name, info, inputs, in_specs, pooled, count):
    half = lambda h, info: (info[0] + h) % 2
    rows_out = pl.BlockSpec((ROWS, WIDE), lambda h, info: (0, half(h, info)))
    pool_out = pl.BlockSpec((2, ROWS, WIDE), lambda h, info: (0, 0, half(h, info)))
    out_specs, outs = [rows_out] * count, [((ROWS, 2 * WIDE), BF16)] * count
    if pooled:
        out_specs, outs = out_specs + [pool_out], outs + [((2, ROWS, 2 * WIDE), BF16)]
    return call(kernel, name, info, in_specs, inputs, out_specs, outs, steps=2)


def body(
    queries, keys, values, grad_self, doc_ids, cross_queries, grad_cross, pool_kv, neighbour_ids
):
    loop = lax.axis_size("ctx")
    me = lax.axis_index("ctx").astype(jnp.int32)
    info = jnp.full((1,), me, jnp.int32)
    enc_dev = pool_kv.shape[1]
    width = queries.shape[1]
    pool = pool_kv.reshape(2, ROWS, width)

    mine_spec, their_spec, their_pool = own_spec(), other_spec(), other_spec((2,))
    names, names_spec = neighbour_ids.T, whole_spec(neighbour_ids.shape[::-1])
    x_mine, x_other = call(
        functools.partial(pack_cross_kernel, enc_dev, loop), "pack_cross", info,
        [names_spec] + [mine_spec] * 2 + [their_spec] * 2,
        (names, cross_queries, grad_cross, cross_queries, grad_cross),
        [spec(2 * ROWS + EXTRA)] * 2,
        [((2 * ROWS + EXTRA, WIDE), BF16)] * 2,
    )
    x_same = send(x_mine, outward, True)
    x_cross = send(x_other, across, True)
    names, x_mine = lax.optimization_barrier((names, x_mine))
    (packed,) = call(
        functools.partial(pack_swap_kernel, enc_dev, loop), "pack_swap", info,
        [names_spec] + [their_spec] * 2 + [their_pool],
        (names, cross_queries, grad_cross, pool),
        [spec(4 * ROWS + EXTRA)],
        [((4 * ROWS + EXTRA, WIDE), BF16)],
    )
    x_pair = send(packed, swap, False)
    queries_in, packed = lax.optimization_barrier((queries, packed))
    sizes = (4 * ROWS, 2 * ROWS, 2 * ROWS)
    packed, s_mine, s_other = call(
        pack_self_kernel, "pack_self", info,
        [mine_spec] * 2 + [their_spec] * 4,
        (queries_in, grad_self, queries_in, grad_self, keys, values),
        [spec(rows) for rows in sizes],
        [((rows, WIDE), BF16) for rows in sizes],
    )
    s_pair = send(packed, swap, False)

    ids_of = lambda d: lax.dynamic_slice_in_dim(doc_ids, d * ROWS, ROWS, 0)
    span = jnp.arange(ROWS, dtype=jnp.int32)
    base = me // 2 * 2
    places = jnp.concatenate([span + base * ROWS, span + (base + 1) * ROWS])
    near0, near1, far0, far1 = [ids_of(base + j) for j in range(4)]
    near = jnp.concatenate([near0, near1])
    near_flip = jnp.concatenate([near1, near0])
    far_flip = jnp.concatenate([far1, far0])
    local_ok = (near[:, None] == near[None, :]) & (places[:, None] <= places[None, :])
    far_ok = (near_flip[:, None] == far_flip[None, :]) & (base + 2 < loop)
    local_bias = jnp.where(local_ok, 0.0, MASKED).astype(F32)
    far_bias = jnp.where(far_ok, 0.0, MASKED).astype(F32)

    bias_spec = whole_spec((2 * ROWS, 2 * ROWS))
    local_bias, far_bias, x_pair = lax.optimization_barrier((local_bias, far_bias, x_pair))
    self_specs = [bias_spec] + [own_spec()] * 4 + [spec(ROWS, j) for j in range(4)]
    self_args = (local_bias, queries, grad_self, keys, values) + (s_pair,) * 4
    mine_w = whole_spec((EXTRA, WIDE), (2 * ROWS // EXTRA, 0))
    partner_w = whole_spec((EXTRA, WIDE), (4 * ROWS // EXTRA, 0))
    cross_specs = (
        [mine_w, partner_w, own_spec(), own_spec(), own_spec((2,))]
        + [spec(ROWS, j) for j in range(4)]
    )
    cross_args = (x_mine, x_pair, cross_queries, grad_cross, pool) + (x_pair,) * 4
    stat = lambda rows: ((HALF, 8, rows), F32)

    x_own, x_partner = call(
        per_head(cross_stats_kernel), "cross_stats", info, cross_specs, cross_args,
        [stat_spec(ROWS)] * 2, [stat(ROWS)] * 2, flops=0,
    )
    t_same = send(x_own, outward, True)
    t_cross = send(x_partner, inward, True)
    local_bias, x_own = lax.optimization_barrier((local_bias, x_own))
    self_args = (local_bias,) + self_args[1:]
    (s_own,) = call(
        per_head(self_stats_kernel), "self_stats", info, self_specs, self_args,
        [stat_spec(2 * ROWS)], [stat(2 * ROWS)], flops=0,
    )
    t_self = send(s_own, lambda d: d - 2, False)
    s_mine, x_same, x_cross, t_same, t_cross, s_own = lax.optimization_barrier(
        (s_mine, x_same, x_cross, t_same, t_cross, s_own)
    )
    s_same = send(s_mine, lambda d: d - 2, False)

    kv_out = spec(4 * ROWS)
    kv_shape = ((4 * ROWS, WIDE), BF16)
    q_shape = ((ROWS, WIDE), BF16)
    xd_same, xd_cross, x_kv, x_fin_same, x_fin_cross = call(
        per_head(cross_remote_kernel), "cross_remote", info,
        [mine_w, mine_w, spec(ROWS, 0), spec(ROWS, 1), spec(ROWS, 0), spec(ROWS, 1)]
        + [own_spec((2,)), spec(ROWS, 2), spec(ROWS, 3), stat_spec(ROWS), stat_spec(ROWS)],
        (x_same, x_cross, x_same, x_same, x_cross, x_cross, pool, x_pair, x_pair, t_same, t_cross),
        [spec(ROWS), spec(ROWS), kv_out, stat_spec(ROWS), stat_spec(ROWS)],
        [q_shape, q_shape, kv_shape, stat(ROWS), stat(ROWS)],
    )
    f_own = send(x_fin_same, inward, True)
    f_partner = send(x_fin_cross, outward, True)
    s_other, x_kv = lax.optimization_barrier((s_other, x_kv))
    s_cross = send(s_other, lambda d: (d - 2) ^ 1, False)
    x_kv, s_same, t_self = lax.optimization_barrier((x_kv, s_same, t_self))
    half_out = spec(3 * ROWS)
    half_shape = ((3 * ROWS, WIDE), BF16)
    x_keep, x_give = call(
        per_head(cross_local_kernel), "cross_local", info,
        cross_specs + [stat_spec(ROWS), stat_spec(ROWS), spec(4 * ROWS)],
        cross_args + (f_own, f_partner, x_kv),
        [half_out] * 2, [half_shape] * 2, flops=LONG,
    )

    xd_same, xd_cross, s_cross, x_keep = lax.optimization_barrier(
        (xd_same, xd_cross, s_cross, x_keep)
    )
    xr_same = send(xd_same, inward, True)
    xr_cross = send(xd_cross, across, True)
    far_bias, x_keep = lax.optimization_barrier((far_bias, x_keep))
    sd, s_kv, s_fin = call(
        per_head(self_remote_kernel), "self_remote", info,
        [bias_spec, spec(ROWS, 0), spec(ROWS, 1), spec(ROWS, 0), spec(ROWS, 1)]
        + [own_spec(), own_spec(), spec(ROWS, 2), spec(ROWS, 3), stat_spec(2 * ROWS)],
        (far_bias, s_same, s_same, s_cross, s_cross, keys, values, s_pair, s_pair, t_self),
        [spec(2 * ROWS), kv_out, stat_spec(2 * ROWS)],
        [((2 * ROWS, WIDE), BF16), kv_shape, stat(2 * ROWS)], flops=LONG,
    )
    f_self = send(s_fin, lambda d: d + 2, False)
    sr = send(sd, lambda d: d + 2, False)

    x_give, s_kv, xr_same, xr_cross, f_self = lax.optimization_barrier(
        (x_give, s_kv, xr_same, xr_cross, f_self)
    )
    x_take = send(x_give, swap, False)
    s_keep, s_give = call(
        per_head(self_local_kernel), "self_local", info,
        self_specs + [stat_spec(2 * ROWS), stat_spec(2 * ROWS), spec(4 * ROWS)],
        self_args + (f_self, s_own, s_kv),
        [half_out] * 2, [half_shape] * 2, flops=LONG,
    )
    three, one = whole_spec((3 * ROWS, WIDE)), whole_spec((ROWS, WIDE))
    s_take = send(s_give, swap, False)
    grad_cq, grad_pool = assemble(
        cross_final_kernel, "cross_final", info, (x_keep, x_take, xr_same, xr_cross),
        [three, three, one, one], True, 1,
    )
    sr, grad_cq = lax.optimization_barrier((sr, grad_cq))
    sr_take = send(sr, swap, False)
    grad_k, grad_v, grad_q = assemble(
        kv_final_kernel, "kv_final", info, (s_keep, s_take, sr), [three, three, one], False, 3
    )
    grad_q = pl.pallas_call(
        query_final_kernel,
        name="query_final",
        grid_spec=pltpu.PrefetchScalarGridSpec(
            num_scalar_prefetch=1,
            grid=(2,),
            in_specs=[
                pl.BlockSpec((ROWS // 2, WIDE), lambda h, info: (h, 0)),
                pl.BlockSpec((ROWS // 2, WIDE), lambda h, info: (2 + h, 0)),
                pl.BlockSpec(memory_space=pl.ANY),
            ],
            out_specs=pl.BlockSpec((ROWS // 2, WIDE), lambda h, info: (h, 1 - info[0] % 2)),
        ),
        out_shape=jax.ShapeDtypeStruct(grad_q.shape, BF16),
        input_output_aliases={3: 0},
        compiler_params=pltpu.CompilerParams(vmem_limit_bytes=64 << 20),
        cost_estimate=pl.CostEstimate(flops=0, transcendentals=0, bytes_accessed=0),
    )(info, s_take, sr_take, grad_q)
    return grad_q, grad_k, grad_v, grad_cq, grad_pool.reshape(pool_kv.shape)


def solution(mesh):
    rows = P(("groups", "ctx"), None)
    pool = P(None, ("groups", "ctx"), None, None)
    return jax.shard_map(
        body,
        mesh=mesh,
        in_specs=(rows, rows, rows, rows, P("groups"), rows, rows, pool, rows),
        out_specs=(rows, rows, rows, rows, pool),
        check_vma=False,
    )
```

```python
import functools
import math

import jax
import jax.numpy as jnp
from jax import lax
from jax.experimental import pallas as pl
from jax.experimental.pallas import tpu as pltpu
from jax.sharding import PartitionSpec as P

HEADS = 8
HEAD_DIM = 128
HALF = HEADS // 2
WIDE = HALF * HEAD_DIM
STEP = 2
COLS = STEP * HEAD_DIM
STEPS = HALF // STEP
STRETCH = 64
NBR_TOK = 128
ROWS = 256
EXTRA = 8
LONG = 12 * 10**9
FACTOR = HEAD_DIM ** (-0.5)
MASKED = -1e30
BF16 = jnp.bfloat16
F32 = jnp.float32


def send(value, target_of, wrap):
    count = lax.axis_size("ctx")
    pairs = []
    for source in range(count):
        target = target_of(source)
        if wrap:
            pairs.append((source, target % count))
        elif 0 <= target < count:
            pairs.append((source, target))
    return lax.ppermute(value, "ctx", pairs)


def swap(d):
    return d ^ 1


def outward(d):
    return d - 2 if d % 2 == 0 else d + 2


def inward(d):
    return d + 2 if d % 2 == 0 else d - 2


def across(d):
    return d - 1 if d % 2 == 0 else d + 1


def spec(rows, row_block=0):
    return pl.BlockSpec((rows, COLS), lambda h, info: (row_block, h))


def own_spec(lead=()):
    zeros = (0,) * len(lead)
    return pl.BlockSpec(lead + (ROWS, COLS), lambda h, info: zeros + (0, info[0] % 2 * STEPS + h))


def other_spec(lead=()):
    zeros = (0,) * len(lead)
    return pl.BlockSpec(
        lead + (ROWS, COLS), lambda h, info: zeros + (0, (1 - info[0] % 2) * STEPS + h)
    )


def whole_spec(shape, index=None):
    index = (0,) * len(shape) if index is None else index
    return pl.BlockSpec(shape, lambda h, *info: index)


def stat_spec(rows):
    return pl.BlockSpec((STEP, 8, rows), lambda h, info: (h, 0, 0))


def call(kernel, name, info, in_specs, inputs, out_specs, outs, steps=STEPS, flops=0):
    return pl.pallas_call(
        kernel,
        name=name,
        grid_spec=pltpu.PrefetchScalarGridSpec(
            num_scalar_prefetch=1,
            grid=(steps,),
            in_specs=in_specs,
            out_specs=out_specs,
        ),
        out_shape=[jax.ShapeDtypeStruct(shape, dtype) for shape, dtype in outs],
        compiler_params=pltpu.CompilerParams(vmem_limit_bytes=64 << 20),
        cost_estimate=pl.CostEstimate(flops=flops, transcendentals=0, bytes_accessed=0),
    )(info, *inputs)


def head_of(ref, j):
    shape = ref.shape
    if len(shape) == 3 and shape[1] == 8:
        return ref.at[j : j + 1]
    if shape[-1] != COLS:
        return ref
    place = pl.ds(j * HEAD_DIM, HEAD_DIM)
    return ref.at[:, place] if len(shape) == 2 else ref.at[:, :, place]


def per_head(kernel):
    def run(info, *refs):
        for j in range(STEP):
            kernel(info, *[head_of(ref, j) for ref in refs])

    return run


def dot_last(a, b):
    return lax.dot_general(a, b, (((1,), (1,)), ((), ())), preferred_element_type=F32)


def dot_first(a, b):
    return lax.dot_general(a, b, (((0,), (0,)), ((), ())), preferred_element_type=F32)


def dot(a, b):
    return jnp.dot(a, b, preferred_element_type=F32)


def both(a, b):
    return jnp.concatenate([a, b], axis=0)


def weight_rows(times):
    log_two = jnp.where(times > 1.5, math.log(2.0), 0.0)
    return jnp.where(times < 0.5, MASKED, log_two)


def slot_pair(ref, first, core, second=None):
    times = ref[...].astype(F32)[:, :ROWS]
    low = times[first : first + 2]
    if second is None:
        return weight_rows(low)
    return weight_rows(jnp.where(core == 0, low, times[second : second + 2]))


def add_rows(s, rows):
    parts = [
        s[e * NBR_TOK : (e + 1) * NBR_TOK] + rows[e : e + 1] for e in range(s.shape[0] // NBR_TOK)
    ]
    return jnp.concatenate(parts, axis=0)


def partial_stats(s, dp):
    peak = jnp.max(s, axis=0, keepdims=True)
    e = jnp.exp(s - peak)
    return e, peak, jnp.sum(e, axis=0, keepdims=True), jnp.sum(e * dp, axis=0, keepdims=True)


def stat_rows(a, b, c):
    return jnp.concatenate([a, b, c, jnp.zeros((5, a.shape[1]), F32)], axis=0)[None]


def merge(stats, mine):
    t_peak, t_total, t_moment = stats[0, 0:1], stats[0, 1:2], stats[0, 2:3]
    peak, total, moment = mine
    top = jnp.maximum(t_peak, peak)
    t_scale = jnp.exp(t_peak - top)
    scale = jnp.exp(peak - top)
    full = t_total * t_scale + total * scale
    inverse = jnp.where(full > 0, 1.0 / full, 0.0)
    delta = (t_moment * t_scale + moment * scale) * inverse
    return top, inverse, delta, scale * inverse


def gradients(p, dp, delta, q, g, k):
    pb = p.astype(BF16)
    ds = (p * (dp - delta)).astype(BF16)
    return dot_first(ds, k) * FACTOR, dot(ds, q) * FACTOR, dot(pb, g)


def naming(enc_dev, loop, me, ids, cols):
    shape = (EXTRA, cols)
    row = lax.broadcasted_iota(jnp.int32, shape, 0)
    lane = lax.broadcasted_iota(jnp.int32, shape, 1) + pl.program_id(0) * shape[1]
    owner = ids // enc_dev
    relative = owner - me + 1
    relative = jnp.where(relative < 0, relative + loop, relative)
    relative = jnp.where(relative >= loop, relative - loop, relative)
    slots = relative * enc_dev + ids - owner * enc_dev
    times = jnp.zeros(shape, F32)
    for n in range(ids.shape[0]):
        for s in range(ids.shape[1]):
            hit = (row == slots[n : n + 1, s : s + 1]) & (lane // STRETCH == s)
            times = times + jnp.where(hit, 1.0, 0.0)
    return times.astype(BF16)


def pack_cross_kernel(enc_dev, loop, info, ids_ref, qm, gm, q, g, mine, other):
    times = naming(enc_dev, loop, info[0], ids_ref[...], mine.shape[1])
    for out, first, second in ((mine, qm, gm), (other, q, g)):
        out[0:ROWS] = first[...]
        out[ROWS : 2 * ROWS] = second[...]
        out[2 * ROWS :] = times


def pack_swap_kernel(enc_dev, loop, info, ids_ref, q, g, pool, swap_ref):
    swap_ref[0:ROWS] = q[...]
    swap_ref[ROWS : 2 * ROWS] = g[...]
    swap_ref[2 * ROWS : 3 * ROWS] = pool[0]
    swap_ref[3 * ROWS : 4 * ROWS] = pool[1]
    swap_ref[4 * ROWS :] = naming(enc_dev, loop, info[0], ids_ref[...], swap_ref.shape[1])


def pack_self_kernel(info, qm, gm, q, g, k, v, swap_ref, mine, other):
    for index, ref in enumerate((q, g, k, v)):
        swap_ref[index * ROWS : (index + 1) * ROWS] = ref[...]
    for out, first, second in ((mine, qm, gm), (other, q, g)):
        out[0:ROWS] = first[...]
        out[ROWS : 2 * ROWS] = second[...]


def ordered(core, a, b):
    return jnp.where(core == 0, a, b), jnp.where(core == 0, b, a)


def wide_scores(keys_x, keys_y, values_x, values_y, qs, gs, bias):
    sx = dot_last(keys_x, qs) * FACTOR + bias[:ROWS]
    sy = dot_last(keys_y, qs[ROWS:]) * FACTOR + bias[ROWS:, ROWS:]
    return sx, sy, dot_last(values_x, gs), dot_last(values_y, gs[ROWS:])


def wide_stats(sx, sy, dpx, dpy):
    peak = jnp.max(sx, axis=0, keepdims=True)
    peak_y = jnp.maximum(peak[:, ROWS:], jnp.max(sy, axis=0, keepdims=True))
    peak = jnp.concatenate([peak[:, :ROWS], peak_y], axis=1)
    ex, ey = jnp.exp(sx - peak), jnp.exp(sy - peak_y)
    widen = lambda a, b: jnp.concatenate([a[:, :ROWS], a[:, ROWS:] + b], axis=1)
    add = lambda a: jnp.sum(a, axis=0, keepdims=True)
    return ex, ey, peak, widen(add(ex), add(ey)), widen(add(ex * dpx), add(ey * dpy))


def wide_gradients(px, py, dpx, dpy, delta, qs, gs, kx, ky):
    pbx, pby = px.astype(BF16), py.astype(BF16)
    dsx = (px * (dpx - delta)).astype(BF16)
    dsy = (py * (dpy - delta[:, ROWS:])).astype(BF16)
    dq_z = dot_first(dsx[:, :ROWS], kx) * FACTOR
    dq_y = dot_first(both(dsx[:, ROWS:], dsy), both(kx, ky)) * FACTOR
    dkx, dky = dot(dsx, qs) * FACTOR, dot(dsy, qs[ROWS:]) * FACTOR
    return dq_z, dq_y, dkx, dky, dot(pbx, gs), dot(pby, gs[ROWS:])


def local_self(core, bias, q, g, k, v, pq, pg, pk, pv):
    q0, q1 = ordered(core, q[...], pq[...])
    g0, g1 = ordered(core, g[...], pg[...])
    k0, k1 = ordered(core, k[...], pk[...])
    v0, v1 = ordered(core, v[...], pv[...])
    qs, gs = both(q0, q1), both(g0, g1)
    return wide_scores(k0, k1, v0, v1, qs, gs, bias[...]), qs, gs, k0, k1


def local_cross(core, w, pw, q, g, pool, pq, pg, pk, pv):
    qs, gs = both(q[...], pq[...]), both(g[...], pg[...])
    ks, vs = both(pool[0], pk[...]), both(pool[1], pv[...])
    own = both(slot_pair(w, 2, core), slot_pair(w, 4, core, 0))
    partner = both(slot_pair(pw, 0, core, 4), slot_pair(pw, 2, core))
    s = add_rows(dot_last(ks, qs) * FACTOR, jnp.concatenate([own, partner], axis=1))
    return s, dot_last(vs, gs), qs, gs, ks


def self_stats_kernel(info, *refs):
    scores = local_self(info[0] % 2, *refs[:-1])[0]
    refs[-1][...] = stat_rows(*wide_stats(*scores)[2:])


def cross_stats_kernel(info, *refs):
    s, dp, _, _, _ = local_cross(info[0] % 2, *refs[:-2])
    stats = stat_rows(*partial_stats(s, dp)[1:])
    refs[-2][...] = stats[:, :, :ROWS]
    refs[-1][...] = stats[:, :, ROWS:]


def self_remote_kernel(
    info, bias, sq, sg, cq, cg, k, v, pk, pv, stats, dq_ref, kv_ref, out_stats
):
    core = info[0] % 2
    q0, q1 = ordered(core, sq[...], cq[...])
    g0, g1 = ordered(core, sg[...], cg[...])
    k0, k1 = ordered(core, k[...], pk[...])
    v0, v1 = ordered(core, v[...], pv[...])
    qs, gs = both(q1, q0), both(g1, g0)
    sx, sy, dpx, dpy = wide_scores(k1, k0, v1, v0, qs, gs, bias[...])
    ex, ey, *mine = wide_stats(sx, sy, dpx, dpy)
    known = stats[...]
    known = jnp.concatenate([known[:, :, ROWS:], known[:, :, :ROWS]], axis=2)
    top, inverse, delta, scale = merge(known, mine)
    px, py = ex * scale, ey * scale[:, ROWS:]
    dq1, dq0, dk1, dk0, dv1, dv0 = wide_gradients(px, py, dpx, dpy, delta, qs, gs, k1, k0)
    same, cross = ordered(core, dq0, dq1)
    dq_ref[:ROWS] = same.astype(BF16)
    dq_ref[ROWS:] = cross.astype(BF16)
    for index, grad in enumerate(ordered(core, dk0, dk1) + ordered(core, dv0, dv1)):
        kv_ref[index * ROWS : (index + 1) * ROWS] = grad.astype(BF16)
    out_stats[...] = stat_rows(top, inverse, delta)


def cross_remote_kernel(
    info, sw, cw, sq, sg, cq, cg, pool, pk, pv, s_stats, c_stats, *outs
):
    dq_same, dq_cross, kv_ref, out_same, out_cross = outs
    core = info[0] % 2
    jobs = (
        (cq, cg, pool[0], pool[1], slot_pair(cw, 4, core, 0), c_stats, dq_cross, out_cross, 0),
        (sq, sg, pk[...], pv[...], slot_pair(sw, 0, core, 4), s_stats, dq_same, out_same, 1),
    )
    for q, g, k, v, rows, stats, dq_ref, out_stats, place in jobs:
        s, dp = add_rows(dot_last(k, q[...]) * FACTOR, rows), dot_last(v, g[...])
        e, *mine = partial_stats(s, dp)
        top, inverse, delta, scale = merge(stats[...], mine)
        dq, dk, dv = gradients(e * scale, dp, delta, q[...], g[...], k)
        dq_ref[...] = dq.astype(BF16)
        out_stats[...] = stat_rows(top, inverse, delta)
        kv_ref[place * ROWS : (place + 1) * ROWS] = dk.astype(BF16)
        kv_ref[(2 + place) * ROWS : (3 + place) * ROWS] = dv.astype(BF16)


def self_local_kernel(info, *refs):
    stats_ref, own_ref, kv_ref, mine, theirs = refs[-5:]
    local = own_ref[0]
    core = info[0] % 2
    first = info[0] < 2
    stats = stats_ref[0]
    stats = jnp.concatenate([stats[:, ROWS:], stats[:, :ROWS]], axis=1)
    inverse = 1.0 / local[1:2]
    top = jnp.where(first, local[0:1], stats[0:1])
    delta = jnp.where(first, local[2:3] * inverse, stats[2:3])
    inverse = jnp.where(first, inverse, stats[1:2])
    (sx, sy, dpx, dpy), qs, gs, k0, k1 = local_self(core, *refs[:-5])
    px = jnp.exp(sx - top) * inverse
    py = jnp.exp(sy - top[:, ROWS:]) * inverse[:, ROWS:]
    dq0, dq1, dk0, dk1, dv0, dv1 = wide_gradients(px, py, dpx, dpy, delta, qs, gs, k0, k1)
    grads = (ordered(core, dq0, dq1), ordered(core, dk0, dk1), ordered(core, dv0, dv1))
    for index, pair in enumerate(grads):
        for out, place, grad in ((mine, 0, pair[0]), (theirs, 1, pair[1])):
            if index > 0:
                low = (2 * index - 2 + place) * ROWS
                grad = grad + kv_ref[low : low + ROWS].astype(F32)
            out[index * ROWS : (index + 1) * ROWS] = grad.astype(BF16)


def cross_local_kernel(info, *refs):
    own_stats, partner_stats, kv_ref, mine, theirs = refs[-5:]
    stats = jnp.concatenate([own_stats[0], partner_stats[0]], axis=1)
    top, inverse, delta = stats[0:1], stats[1:2], stats[2:3]
    s, dp, qs, gs, ks = local_cross(info[0] % 2, *refs[:-5])
    dq, dk, dv = gradients(jnp.exp(s - top) * inverse, dp, delta, qs, gs, ks)
    dk = dk + kv_ref[: 2 * ROWS].astype(F32)
    dv = dv + kv_ref[2 * ROWS :].astype(F32)
    for index, grad in enumerate((dq, dk, dv)):
        mine[index * ROWS : (index + 1) * ROWS] = grad[:ROWS].astype(BF16)
        theirs[index * ROWS : (index + 1) * ROWS] = grad[ROWS:].astype(BF16)


def kv_final_kernel(info, mine, theirs, dq_mine, k_out, v_out, q_out):
    def write(source):
        k_out[...] = source[ROWS : 2 * ROWS]
        v_out[...] = source[2 * ROWS :]
        q_out[...] = (mine[:ROWS].astype(F32) + dq_mine[...].astype(F32)).astype(BF16)

    pl.when(pl.program_id(0) == 0)(lambda: write(mine))
    pl.when(pl.program_id(0) == 1)(lambda: write(theirs))


def query_final_kernel(info, theirs, dq_theirs, grad, out):
    out[...] = (theirs[...].astype(F32) + dq_theirs[...].astype(F32)).astype(BF16)


def cross_final_kernel(info, mine, theirs, dq_mine, dq_theirs, dq_out, pool_out):
    def write(source, extra):
        dq = source[:ROWS].astype(F32) + extra[...].astype(F32)
        dq_out[...] = dq.astype(BF16)
        pool_out[0] = source[ROWS : 2 * ROWS]
        pool_out[1] = source[2 * ROWS :]

    pl.when(pl.program_id(0) == 0)(lambda: write(mine, dq_mine))
    pl.when(pl.program_id(0) == 1)(lambda: write(theirs, dq_theirs))


def assemble(kernel, name, info, inputs, in_specs, pooled, count):
    half = lambda h, info: (info[0] + h) % 2
    rows_out = pl.BlockSpec((ROWS, WIDE), lambda h, info: (0, half(h, info)))
    pool_out = pl.BlockSpec((2, ROWS, WIDE), lambda h, info: (0, 0, half(h, info)))
    out_specs, outs = [rows_out] * count, [((ROWS, 2 * WIDE), BF16)] * count
    if pooled:
        out_specs, outs = out_specs + [pool_out], outs + [((2, ROWS, 2 * WIDE), BF16)]
    return call(kernel, name, info, in_specs, inputs, out_specs, outs, steps=2)


def body(
    queries, keys, values, grad_self, doc_ids, cross_queries, grad_cross, pool_kv, neighbour_ids
):
    loop = lax.axis_size("ctx")
    me = lax.axis_index("ctx").astype(jnp.int32)
    info = jnp.full((1,), me, jnp.int32)
    enc_dev = pool_kv.shape[1]
    width = queries.shape[1]
    pool = pool_kv.reshape(2, ROWS, width)

    mine_spec, their_spec, their_pool = own_spec(), other_spec(), other_spec((2,))
    names, names_spec = neighbour_ids.T, whole_spec(neighbour_ids.shape[::-1])
    x_mine, x_other = call(
        functools.partial(pack_cross_kernel, enc_dev, loop), "pack_cross", info,
        [names_spec] + [mine_spec] * 2 + [their_spec] * 2,
        (names, cross_queries, grad_cross, cross_queries, grad_cross),
        [spec(2 * ROWS + EXTRA)] * 2,
        [((2 * ROWS + EXTRA, WIDE), BF16)] * 2,
    )
    x_same = send(x_mine, outward, True)
    x_cross = send(x_other, across, True)
    names, x_mine = lax.optimization_barrier((names, x_mine))
    (packed,) = call(
        functools.partial(pack_swap_kernel, enc_dev, loop), "pack_swap", info,
        [names_spec] + [their_spec] * 2 + [their_pool],
        (names, cross_queries, grad_cross, pool),
        [spec(4 * ROWS + EXTRA)],
        [((4 * ROWS + EXTRA, WIDE), BF16)],
    )
    x_pair = send(packed, swap, False)
    queries_in, packed = lax.optimization_barrier((queries, packed))
    sizes = (4 * ROWS, 2 * ROWS, 2 * ROWS)
    packed, s_mine, s_other = call(
        pack_self_kernel, "pack_self", info,
        [mine_spec] * 2 + [their_spec] * 4,
        (queries_in, grad_self, queries_in, grad_self, keys, values),
        [spec(rows) for rows in sizes],
        [((rows, WIDE), BF16) for rows in sizes],
    )
    s_pair = send(packed, swap, False)

    ids_of = lambda d: lax.dynamic_slice_in_dim(doc_ids, d * ROWS, ROWS, 0)
    span = jnp.arange(ROWS, dtype=jnp.int32)
    base = me // 2 * 2
    places = jnp.concatenate([span + base * ROWS, span + (base + 1) * ROWS])
    near0, near1, far0, far1 = [ids_of(base + j) for j in range(4)]
    near = jnp.concatenate([near0, near1])
    near_flip = jnp.concatenate([near1, near0])
    far_flip = jnp.concatenate([far1, far0])
    local_ok = (near[:, None] == near[None, :]) & (places[:, None] <= places[None, :])
    far_ok = (near_flip[:, None] == far_flip[None, :]) & (base + 2 < loop)
    local_bias = jnp.where(local_ok, 0.0, MASKED).astype(F32)
    far_bias = jnp.where(far_ok, 0.0, MASKED).astype(F32)

    bias_spec = whole_spec((2 * ROWS, 2 * ROWS))
    local_bias, far_bias, x_pair = lax.optimization_barrier((local_bias, far_bias, x_pair))
    self_specs = [bias_spec] + [own_spec()] * 4 + [spec(ROWS, j) for j in range(4)]
    self_args = (local_bias, queries, grad_self, keys, values) + (s_pair,) * 4
    mine_w = whole_spec((EXTRA, WIDE), (2 * ROWS // EXTRA, 0))
    partner_w = whole_spec((EXTRA, WIDE), (4 * ROWS // EXTRA, 0))
    cross_specs = (
        [mine_w, partner_w, own_spec(), own_spec(), own_spec((2,))]
        + [spec(ROWS, j) for j in range(4)]
    )
    cross_args = (x_mine, x_pair, cross_queries, grad_cross, pool) + (x_pair,) * 4
    stat = lambda rows: ((HALF, 8, rows), F32)

    x_own, x_partner = call(
        per_head(cross_stats_kernel), "cross_stats", info, cross_specs, cross_args,
        [stat_spec(ROWS)] * 2, [stat(ROWS)] * 2, flops=0,
    )
    t_same = send(x_own, outward, True)
    t_cross = send(x_partner, inward, True)
    local_bias, x_own = lax.optimization_barrier((local_bias, x_own))
    self_args = (local_bias,) + self_args[1:]
    (s_own,) = call(
        per_head(self_stats_kernel), "self_stats", info, self_specs, self_args,
        [stat_spec(2 * ROWS)], [stat(2 * ROWS)], flops=0,
    )
    t_self = send(s_own, lambda d: d - 2, False)
    s_mine, x_same, x_cross, t_same, t_cross, s_own = lax.optimization_barrier(
        (s_mine, x_same, x_cross, t_same, t_cross, s_own)
    )
    s_same = send(s_mine, lambda d: d - 2, False)

    kv_out = spec(4 * ROWS)
    kv_shape = ((4 * ROWS, WIDE), BF16)
    q_shape = ((ROWS, WIDE), BF16)
    xd_same, xd_cross, x_kv, x_fin_same, x_fin_cross = call(
        per_head(cross_remote_kernel), "cross_remote", info,
        [mine_w, mine_w, spec(ROWS, 0), spec(ROWS, 1), spec(ROWS, 0), spec(ROWS, 1)]
        + [own_spec((2,)), spec(ROWS, 2), spec(ROWS, 3), stat_spec(ROWS), stat_spec(ROWS)],
        (x_same, x_cross, x_same, x_same, x_cross, x_cross, pool, x_pair, x_pair, t_same, t_cross),
        [spec(ROWS), spec(ROWS), kv_out, stat_spec(ROWS), stat_spec(ROWS)],
        [q_shape, q_shape, kv_shape, stat(ROWS), stat(ROWS)],
    )
    f_own = send(x_fin_same, inward, True)
    f_partner = send(x_fin_cross, outward, True)
    s_other, x_kv = lax.optimization_barrier((s_other, x_kv))
    s_cross = send(s_other, lambda d: (d - 2) ^ 1, False)
    x_kv, s_same, t_self = lax.optimization_barrier((x_kv, s_same, t_self))
    half_out = spec(3 * ROWS)
    half_shape = ((3 * ROWS, WIDE), BF16)
    x_keep, x_give = call(
        per_head(cross_local_kernel), "cross_local", info,
        cross_specs + [stat_spec(ROWS), stat_spec(ROWS), spec(4 * ROWS)],
        cross_args + (f_own, f_partner, x_kv),
        [half_out] * 2, [half_shape] * 2, flops=LONG,
    )

    xd_same, xd_cross, s_cross, x_keep = lax.optimization_barrier(
        (xd_same, xd_cross, s_cross, x_keep)
    )
    xr_same = send(xd_same, inward, True)
    xr_cross = send(xd_cross, across, True)
    far_bias, x_keep = lax.optimization_barrier((far_bias, x_keep))
    sd, s_kv, s_fin = call(
        per_head(self_remote_kernel), "self_remote", info,
        [bias_spec, spec(ROWS, 0), spec(ROWS, 1), spec(ROWS, 0), spec(ROWS, 1)]
        + [own_spec(), own_spec(), spec(ROWS, 2), spec(ROWS, 3), stat_spec(2 * ROWS)],
        (far_bias, s_same, s_same, s_cross, s_cross, keys, values, s_pair, s_pair, t_self),
        [spec(2 * ROWS), kv_out, stat_spec(2 * ROWS)],
        [((2 * ROWS, WIDE), BF16), kv_shape, stat(2 * ROWS)], flops=LONG,
    )
    f_self = send(s_fin, lambda d: d + 2, False)
    sr = send(sd, lambda d: d + 2, False)

    x_give, s_kv, xr_same, xr_cross, f_self = lax.optimization_barrier(
        (x_give, s_kv, xr_same, xr_cross, f_self)
    )
    x_take = send(x_give, swap, False)
    s_keep, s_give = call(
        per_head(self_local_kernel), "self_local", info,
        self_specs + [stat_spec(2 * ROWS), stat_spec(2 * ROWS), spec(4 * ROWS)],
        self_args + (f_self, s_own, s_kv),
        [half_out] * 2, [half_shape] * 2, flops=LONG,
    )
    three, one = whole_spec((3 * ROWS, WIDE)), whole_spec((ROWS, WIDE))
    s_take = send(s_give, swap, False)
    grad_cq, grad_pool = assemble(
        cross_final_kernel, "cross_final", info, (x_keep, x_take, xr_same, xr_cross),
        [three, three, one, one], True, 1,
    )
    sr, grad_cq = lax.optimization_barrier((sr, grad_cq))
    sr_take = send(sr, swap, False)
    grad_k, grad_v, grad_q = assemble(
        kv_final_kernel, "kv_final", info, (s_keep, s_take, sr), [three, three, one], False, 3
    )
    grad_q = pl.pallas_call(
        query_final_kernel,
        name="query_final",
        grid_spec=pltpu.PrefetchScalarGridSpec(
            num_scalar_prefetch=1,
            grid=(2,),
            in_specs=[
                pl.BlockSpec((ROWS // 2, WIDE), lambda h, info: (h, 0)),
                pl.BlockSpec((ROWS // 2, WIDE), lambda h, info: (2 + h, 0)),
                pl.BlockSpec(memory_space=pl.ANY),
            ],
            out_specs=pl.BlockSpec((ROWS // 2, WIDE), lambda h, info: (h, 1 - info[0] % 2)),
        ),
        out_shape=jax.ShapeDtypeStruct(grad_q.shape, BF16),
        input_output_aliases={3: 0},
        compiler_params=pltpu.CompilerParams(vmem_limit_bytes=64 << 20),
        cost_estimate=pl.CostEstimate(flops=0, transcendentals=0, bytes_accessed=0),
    )(info, s_take, sr_take, grad_q)
    return grad_q, grad_k, grad_v, grad_cq, grad_pool.reshape(pool_kv.shape)


def solution(mesh):
    rows = P(("groups", "ctx"), None)
    pool = P(None, ("groups", "ctx"), None, None)
    return jax.shard_map(
        body,
        mesh=mesh,
        in_specs=(rows, rows, rows, rows, P("groups"), rows, rows, pool, rows),
        out_specs=(rows, rows, rows, rows, pool),
        check_vma=False,
    )
```

```python
import functools
import math

import jax
import jax.numpy as jnp
from jax import lax
from jax.experimental import pallas as pl
from jax.experimental.pallas import tpu as pltpu
from jax.sharding import PartitionSpec as P

HEADS = 8
HEAD_DIM = 128
HALF = HEADS // 2
WIDE = HALF * HEAD_DIM
STEP = 2
COLS = STEP * HEAD_DIM
STEPS = HALF // STEP
STRETCH = 64
NBR_TOK = 128
ROWS = 256
EXTRA = 8
LONG = 12 * 10**9
FACTOR = HEAD_DIM ** (-0.5)
MASKED = -1e30
BF16 = jnp.bfloat16
F32 = jnp.float32


def send(value, target_of, wrap):
    count = lax.axis_size("ctx")
    pairs = []
    for source in range(count):
        target = target_of(source)
        if wrap:
            pairs.append((source, target % count))
        elif 0 <= target < count:
            pairs.append((source, target))
    return lax.ppermute(value, "ctx", pairs)


def swap(d):
    return d ^ 1


def outward(d):
    return d - 2 if d % 2 == 0 else d + 2


def inward(d):
    return d + 2 if d % 2 == 0 else d - 2


def across(d):
    return d - 1 if d % 2 == 0 else d + 1


def spec(rows, row_block=0):
    return pl.BlockSpec((rows, COLS), lambda h, info: (row_block, h))


def own_spec(lead=()):
    zeros = (0,) * len(lead)
    return pl.BlockSpec(lead + (ROWS, COLS), lambda h, info: zeros + (0, info[0] % 2 * STEPS + h))


def other_spec(lead=()):
    zeros = (0,) * len(lead)
    return pl.BlockSpec(
        lead + (ROWS, COLS), lambda h, info: zeros + (0, (1 - info[0] % 2) * STEPS + h)
    )


def whole_spec(shape, index=None):
    index = (0,) * len(shape) if index is None else index
    return pl.BlockSpec(shape, lambda h, *info: index)


def stat_spec(rows):
    return pl.BlockSpec((STEP, 8, rows), lambda h, info: (h, 0, 0))


def call(kernel, name, info, in_specs, inputs, out_specs, outs, steps=STEPS, flops=0):
    return pl.pallas_call(
        kernel,
        name=name,
        grid_spec=pltpu.PrefetchScalarGridSpec(
            num_scalar_prefetch=1,
            grid=(steps,),
            in_specs=in_specs,
            out_specs=out_specs,
        ),
        out_shape=[jax.ShapeDtypeStruct(shape, dtype) for shape, dtype in outs],
        compiler_params=pltpu.CompilerParams(vmem_limit_bytes=64 << 20),
        cost_estimate=pl.CostEstimate(flops=flops, transcendentals=0, bytes_accessed=0),
    )(info, *inputs)


def head_of(ref, j):
    shape = ref.shape
    if len(shape) == 3 and shape[1] == 8:
        return ref.at[j : j + 1]
    if shape[-1] != COLS:
        return ref
    place = pl.ds(j * HEAD_DIM, HEAD_DIM)
    return ref.at[:, place] if len(shape) == 2 else ref.at[:, :, place]


def per_head(kernel):
    def run(info, *refs):
        for j in range(STEP):
            kernel(info, *[head_of(ref, j) for ref in refs])

    return run


def dot_last(a, b):
    return lax.dot_general(a, b, (((1,), (1,)), ((), ())), preferred_element_type=F32)


def dot_first(a, b):
    return lax.dot_general(a, b, (((0,), (0,)), ((), ())), preferred_element_type=F32)


def dot(a, b):
    return jnp.dot(a, b, preferred_element_type=F32)


def both(a, b):
    return jnp.concatenate([a, b], axis=0)


def weight_rows(times):
    log_two = jnp.where(times > 1.5, math.log(2.0), 0.0)
    return jnp.where(times < 0.5, MASKED, log_two)


def slot_pair(ref, first, core, second=None):
    times = ref[...].astype(F32)[:, :ROWS]
    low = times[first : first + 2]
    if second is None:
        return weight_rows(low)
    return weight_rows(jnp.where(core == 0, low, times[second : second + 2]))


def add_rows(s, rows):
    parts = [
        s[e * NBR_TOK : (e + 1) * NBR_TOK] + rows[e : e + 1] for e in range(s.shape[0] // NBR_TOK)
    ]
    return jnp.concatenate(parts, axis=0)


def partial_stats(s, dp):
    peak = jnp.max(s, axis=0, keepdims=True)
    e = jnp.exp(s - peak)
    return e, peak, jnp.sum(e, axis=0, keepdims=True), jnp.sum(e * dp, axis=0, keepdims=True)


def stat_rows(a, b, c):
    return jnp.concatenate([a, b, c, jnp.zeros((5, a.shape[1]), F32)], axis=0)[None]


def merge(stats, mine):
    t_peak, t_total, t_moment = stats[0, 0:1], stats[0, 1:2], stats[0, 2:3]
    peak, total, moment = mine
    top = jnp.maximum(t_peak, peak)
    t_scale = jnp.exp(t_peak - top)
    scale = jnp.exp(peak - top)
    full = t_total * t_scale + total * scale
    inverse = jnp.where(full > 0, 1.0 / full, 0.0)
    delta = (t_moment * t_scale + moment * scale) * inverse
    return top, inverse, delta, scale * inverse


def gradients(p, dp, delta, q, g, k):
    pb = p.astype(BF16)
    ds = (p * (dp - delta)).astype(BF16)
    return dot_first(ds, k) * FACTOR, dot(ds, q) * FACTOR, dot(pb, g)


def naming(enc_dev, loop, me, ids, cols):
    shape = (EXTRA, cols)
    row = lax.broadcasted_iota(jnp.int32, shape, 0)
    lane = lax.broadcasted_iota(jnp.int32, shape, 1) + pl.program_id(0) * shape[1]
    owner = ids // enc_dev
    relative = owner - me + 1
    relative = jnp.where(relative < 0, relative + loop, relative)
    relative = jnp.where(relative >= loop, relative - loop, relative)
    slots = relative * enc_dev + ids - owner * enc_dev
    times = jnp.zeros(shape, F32)
    for n in range(ids.shape[0]):
        for s in range(ids.shape[1]):
            hit = (row == slots[n : n + 1, s : s + 1]) & (lane // STRETCH == s)
            times = times + jnp.where(hit, 1.0, 0.0)
    return times.astype(BF16)


def pack_cross_kernel(enc_dev, loop, info, ids_ref, qm, gm, q, g, mine, other):
    times = naming(enc_dev, loop, info[0], ids_ref[...], mine.shape[1])
    for out, first, second in ((mine, qm, gm), (other, q, g)):
        out[0:ROWS] = first[...]
        out[ROWS : 2 * ROWS] = second[...]
        out[2 * ROWS :] = times


def pack_swap_kernel(enc_dev, loop, info, ids_ref, q, g, pool, swap_ref):
    swap_ref[0:ROWS] = q[...]
    swap_ref[ROWS : 2 * ROWS] = g[...]
    swap_ref[2 * ROWS : 3 * ROWS] = pool[0]
    swap_ref[3 * ROWS : 4 * ROWS] = pool[1]
    swap_ref[4 * ROWS :] = naming(enc_dev, loop, info[0], ids_ref[...], swap_ref.shape[1])


def pack_self_kernel(info, qm, gm, q, g, k, v, swap_ref, mine, other):
    for index, ref in enumerate((q, g, k, v)):
        swap_ref[index * ROWS : (index + 1) * ROWS] = ref[...]
    for out, first, second in ((mine, qm, gm), (other, q, g)):
        out[0:ROWS] = first[...]
        out[ROWS : 2 * ROWS] = second[...]


def ordered(core, a, b):
    return jnp.where(core == 0, a, b), jnp.where(core == 0, b, a)


def wide_scores(keys_x, keys_y, values_x, values_y, qs, gs, bias):
    sx = dot_last(keys_x, qs) * FACTOR + bias[:ROWS]
    sy = dot_last(keys_y, qs[ROWS:]) * FACTOR + bias[ROWS:, ROWS:]
    return sx, sy, dot_last(values_x, gs), dot_last(values_y, gs[ROWS:])


def wide_stats(sx, sy, dpx, dpy):
    peak = jnp.max(sx, axis=0, keepdims=True)
    peak_y = jnp.maximum(peak[:, ROWS:], jnp.max(sy, axis=0, keepdims=True))
    peak = jnp.concatenate([peak[:, :ROWS], peak_y], axis=1)
    ex, ey = jnp.exp(sx - peak), jnp.exp(sy - peak_y)
    widen = lambda a, b: jnp.concatenate([a[:, :ROWS], a[:, ROWS:] + b], axis=1)
    add = lambda a: jnp.sum(a, axis=0, keepdims=True)
    return ex, ey, peak, widen(add(ex), add(ey)), widen(add(ex * dpx), add(ey * dpy))


def wide_gradients(px, py, dpx, dpy, delta, qs, gs, kx, ky):
    pbx, pby = px.astype(BF16), py.astype(BF16)
    dsx = (px * (dpx - delta)).astype(BF16)
    dsy = (py * (dpy - delta[:, ROWS:])).astype(BF16)
    dq_z = dot_first(dsx[:, :ROWS], kx) * FACTOR
    dq_y = dot_first(both(dsx[:, ROWS:], dsy), both(kx, ky)) * FACTOR
    dkx, dky = dot(dsx, qs) * FACTOR, dot(dsy, qs[ROWS:]) * FACTOR
    return dq_z, dq_y, dkx, dky, dot(pbx, gs), dot(pby, gs[ROWS:])


def local_self(core, bias, q, g, k, v, pq, pg, pk, pv):
    q0, q1 = ordered(core, q[...], pq[...])
    g0, g1 = ordered(core, g[...], pg[...])
    k0, k1 = ordered(core, k[...], pk[...])
    v0, v1 = ordered(core, v[...], pv[...])
    qs, gs = both(q0, q1), both(g0, g1)
    return wide_scores(k0, k1, v0, v1, qs, gs, bias[...]), qs, gs, k0, k1


def local_cross(core, w, pw, q, g, pool, pq, pg, pk, pv):
    qs, gs = both(q[...], pq[...]), both(g[...], pg[...])
    ks, vs = both(pool[0], pk[...]), both(pool[1], pv[...])
    own = both(slot_pair(w, 2, core), slot_pair(w, 4, core, 0))
    partner = both(slot_pair(pw, 0, core, 4), slot_pair(pw, 2, core))
    s = add_rows(dot_last(ks, qs) * FACTOR, jnp.concatenate([own, partner], axis=1))
    return s, dot_last(vs, gs), qs, gs, ks


def self_stats_kernel(info, *refs):
    scores = local_self(info[0] % 2, *refs[:-1])[0]
    refs[-1][...] = stat_rows(*wide_stats(*scores)[2:])


def cross_stats_kernel(info, *refs):
    s, dp, _, _, _ = local_cross(info[0] % 2, *refs[:-2])
    stats = stat_rows(*partial_stats(s, dp)[1:])
    refs[-2][...] = stats[:, :, :ROWS]
    refs[-1][...] = stats[:, :, ROWS:]


def self_remote_kernel(
    info, bias, sq, sg, cq, cg, k, v, pk, pv, stats, dq_ref, kv_ref, out_stats
):
    core = info[0] % 2
    q0, q1 = ordered(core, sq[...], cq[...])
    g0, g1 = ordered(core, sg[...], cg[...])
    k0, k1 = ordered(core, k[...], pk[...])
    v0, v1 = ordered(core, v[...], pv[...])
    qs, gs = both(q1, q0), both(g1, g0)
    sx, sy, dpx, dpy = wide_scores(k1, k0, v1, v0, qs, gs, bias[...])
    ex, ey, *mine = wide_stats(sx, sy, dpx, dpy)
    known = stats[...]
    known = jnp.concatenate([known[:, :, ROWS:], known[:, :, :ROWS]], axis=2)
    top, inverse, delta, scale = merge(known, mine)
    px, py = ex * scale, ey * scale[:, ROWS:]
    dq1, dq0, dk1, dk0, dv1, dv0 = wide_gradients(px, py, dpx, dpy, delta, qs, gs, k1, k0)
    same, cross = ordered(core, dq0, dq1)
    dq_ref[:ROWS] = same.astype(BF16)
    dq_ref[ROWS:] = cross.astype(BF16)
    for index, grad in enumerate(ordered(core, dk0, dk1) + ordered(core, dv0, dv1)):
        kv_ref[index * ROWS : (index + 1) * ROWS] = grad.astype(BF16)
    out_stats[...] = stat_rows(top, inverse, delta)


def cross_remote_kernel(
    info, sw, cw, sq, sg, cq, cg, pool, pk, pv, s_stats, c_stats, *outs
):
    dq_same, dq_cross, kv_ref, out_same, out_cross = outs
    core = info[0] % 2
    jobs = (
        (cq, cg, pool[0], pool[1], slot_pair(cw, 4, core, 0), c_stats, dq_cross, out_cross, 0),
        (sq, sg, pk[...], pv[...], slot_pair(sw, 0, core, 4), s_stats, dq_same, out_same, 1),
    )
    for q, g, k, v, rows, stats, dq_ref, out_stats, place in jobs:
        s, dp = add_rows(dot_last(k, q[...]) * FACTOR, rows), dot_last(v, g[...])
        e, *mine = partial_stats(s, dp)
        top, inverse, delta, scale = merge(stats[...], mine)
        dq, dk, dv = gradients(e * scale, dp, delta, q[...], g[...], k)
        dq_ref[...] = dq.astype(BF16)
        out_stats[...] = stat_rows(top, inverse, delta)
        kv_ref[place * ROWS : (place + 1) * ROWS] = dk.astype(BF16)
        kv_ref[(2 + place) * ROWS : (3 + place) * ROWS] = dv.astype(BF16)


def self_local_kernel(info, *refs):
    stats_ref, own_ref, kv_ref, mine, theirs = refs[-5:]
    local = own_ref[0]
    core = info[0] % 2
    first = info[0] < 2
    stats = stats_ref[0]
    stats = jnp.concatenate([stats[:, ROWS:], stats[:, :ROWS]], axis=1)
    inverse = 1.0 / local[1:2]
    top = jnp.where(first, local[0:1], stats[0:1])
    delta = jnp.where(first, local[2:3] * inverse, stats[2:3])
    inverse = jnp.where(first, inverse, stats[1:2])
    (sx, sy, dpx, dpy), qs, gs, k0, k1 = local_self(core, *refs[:-5])
    px = jnp.exp(sx - top) * inverse
    py = jnp.exp(sy - top[:, ROWS:]) * inverse[:, ROWS:]
    dq0, dq1, dk0, dk1, dv0, dv1 = wide_gradients(px, py, dpx, dpy, delta, qs, gs, k0, k1)
    grads = (ordered(core, dq0, dq1), ordered(core, dk0, dk1), ordered(core, dv0, dv1))
    for index, pair in enumerate(grads):
        for out, place, grad in ((mine, 0, pair[0]), (theirs, 1, pair[1])):
            if index > 0:
                low = (2 * index - 2 + place) * ROWS
                grad = grad + kv_ref[low : low + ROWS].astype(F32)
            out[index * ROWS : (index + 1) * ROWS] = grad.astype(BF16)


def cross_local_kernel(info, *refs):
    own_stats, partner_stats, kv_ref, mine, theirs = refs[-5:]
    stats = jnp.concatenate([own_stats[0], partner_stats[0]], axis=1)
    top, inverse, delta = stats[0:1], stats[1:2], stats[2:3]
    s, dp, qs, gs, ks = local_cross(info[0] % 2, *refs[:-5])
    dq, dk, dv = gradients(jnp.exp(s - top) * inverse, dp, delta, qs, gs, ks)
    dk = dk + kv_ref[: 2 * ROWS].astype(F32)
    dv = dv + kv_ref[2 * ROWS :].astype(F32)
    for index, grad in enumerate((dq, dk, dv)):
        mine[index * ROWS : (index + 1) * ROWS] = grad[:ROWS].astype(BF16)
        theirs[index * ROWS : (index + 1) * ROWS] = grad[ROWS:].astype(BF16)


def kv_final_kernel(info, mine, theirs, dq_mine, k_out, v_out, q_out):
    def write(source):
        k_out[...] = source[ROWS : 2 * ROWS]
        v_out[...] = source[2 * ROWS :]
        q_out[...] = (mine[:ROWS].astype(F32) + dq_mine[...].astype(F32)).astype(BF16)

    pl.when(pl.program_id(0) == 0)(lambda: write(mine))
    pl.when(pl.program_id(0) == 1)(lambda: write(theirs))


def query_final_kernel(info, theirs, dq_theirs, grad, out):
    out[...] = (theirs[...].astype(F32) + dq_theirs[...].astype(F32)).astype(BF16)


def cross_final_kernel(info, mine, theirs, dq_mine, dq_theirs, dq_out, pool_out):
    def write(source, extra):
        dq = source[:ROWS].astype(F32) + extra[...].astype(F32)
        dq_out[...] = dq.astype(BF16)
        pool_out[0] = source[ROWS : 2 * ROWS]
        pool_out[1] = source[2 * ROWS :]

    pl.when(pl.program_id(0) == 0)(lambda: write(mine, dq_mine))
    pl.when(pl.program_id(0) == 1)(lambda: write(theirs, dq_theirs))


def assemble(kernel, name, info, inputs, in_specs, pooled, count):
    half = lambda h, info: (info[0] + h) % 2
    rows_out = pl.BlockSpec((ROWS, WIDE), lambda h, info: (0, half(h, info)))
    pool_out = pl.BlockSpec((2, ROWS, WIDE), lambda h, info: (0, 0, half(h, info)))
    out_specs, outs = [rows_out] * count, [((ROWS, 2 * WIDE), BF16)] * count
    if pooled:
        out_specs, outs = out_specs + [pool_out], outs + [((2, ROWS, 2 * WIDE), BF16)]
    return call(kernel, name, info, in_specs, inputs, out_specs, outs, steps=2)


def body(
    queries, keys, values, grad_self, doc_ids, cross_queries, grad_cross, pool_kv, neighbour_ids
):
    loop = lax.axis_size("ctx")
    me = lax.axis_index("ctx").astype(jnp.int32)
    info = jnp.full((1,), me, jnp.int32)
    enc_dev = pool_kv.shape[1]
    width = queries.shape[1]
    pool = pool_kv.reshape(2, ROWS, width)

    mine_spec, their_spec, their_pool = own_spec(), other_spec(), other_spec((2,))
    names, names_spec = neighbour_ids.T, whole_spec(neighbour_ids.shape[::-1])
    x_mine, x_other = call(
        functools.partial(pack_cross_kernel, enc_dev, loop), "pack_cross", info,
        [names_spec] + [mine_spec] * 2 + [their_spec] * 2,
        (names, cross_queries, grad_cross, cross_queries, grad_cross),
        [spec(2 * ROWS + EXTRA)] * 2,
        [((2 * ROWS + EXTRA, WIDE), BF16)] * 2,
    )
    x_same = send(x_mine, outward, True)
    x_cross = send(x_other, across, True)
    names, x_mine = lax.optimization_barrier((names, x_mine))
    (packed,) = call(
        functools.partial(pack_swap_kernel, enc_dev, loop), "pack_swap", info,
        [names_spec] + [their_spec] * 2 + [their_pool],
        (names, cross_queries, grad_cross, pool),
        [spec(4 * ROWS + EXTRA)],
        [((4 * ROWS + EXTRA, WIDE), BF16)],
    )
    x_pair = send(packed, swap, False)
    queries_in, packed = lax.optimization_barrier((queries, packed))
    sizes = (4 * ROWS, 2 * ROWS, 2 * ROWS)
    packed, s_mine, s_other = call(
        pack_self_kernel, "pack_self", info,
        [mine_spec] * 2 + [their_spec] * 4,
        (queries_in, grad_self, queries_in, grad_self, keys, values),
        [spec(rows) for rows in sizes],
        [((rows, WIDE), BF16) for rows in sizes],
    )
    s_pair = send(packed, swap, False)

    ids_of = lambda d: lax.dynamic_slice_in_dim(doc_ids, d * ROWS, ROWS, 0)
    span = jnp.arange(ROWS, dtype=jnp.int32)
    base = me // 2 * 2
    places = jnp.concatenate([span + base * ROWS, span + (base + 1) * ROWS])
    near0, near1, far0, far1 = [ids_of(base + j) for j in range(4)]
    near = jnp.concatenate([near0, near1])
    near_flip = jnp.concatenate([near1, near0])
    far_flip = jnp.concatenate([far1, far0])
    local_ok = (near[:, None] == near[None, :]) & (places[:, None] <= places[None, :])
    far_ok = (near_flip[:, None] == far_flip[None, :]) & (base + 2 < loop)
    local_bias = jnp.where(local_ok, 0.0, MASKED).astype(F32)
    far_bias = jnp.where(far_ok, 0.0, MASKED).astype(F32)

    bias_spec = whole_spec((2 * ROWS, 2 * ROWS))
    local_bias, far_bias, x_pair = lax.optimization_barrier((local_bias, far_bias, x_pair))
    self_specs = [bias_spec] + [own_spec()] * 4 + [spec(ROWS, j) for j in range(4)]
    self_args = (local_bias, queries, grad_self, keys, values) + (s_pair,) * 4
    mine_w = whole_spec((EXTRA, WIDE), (2 * ROWS // EXTRA, 0))
    partner_w = whole_spec((EXTRA, WIDE), (4 * ROWS // EXTRA, 0))
    cross_specs = (
        [mine_w, partner_w, own_spec(), own_spec(), own_spec((2,))]
        + [spec(ROWS, j) for j in range(4)]
    )
    cross_args = (x_mine, x_pair, cross_queries, grad_cross, pool) + (x_pair,) * 4
    stat = lambda rows: ((HALF, 8, rows), F32)

    x_own, x_partner = call(
        per_head(cross_stats_kernel), "cross_stats", info, cross_specs, cross_args,
        [stat_spec(ROWS)] * 2, [stat(ROWS)] * 2, flops=0,
    )
    t_same = send(x_own, outward, True)
    t_cross = send(x_partner, inward, True)
    local_bias, x_own = lax.optimization_barrier((local_bias, x_own))
    self_args = (local_bias,) + self_args[1:]
    (s_own,) = call(
        per_head(self_stats_kernel), "self_stats", info, self_specs, self_args,
        [stat_spec(2 * ROWS)], [stat(2 * ROWS)], flops=0,
    )
    t_self = send(s_own, lambda d: d - 2, False)
    s_mine, x_same, x_cross, t_same, t_cross, s_own = lax.optimization_barrier(
        (s_mine, x_same, x_cross, t_same, t_cross, s_own)
    )
    s_same = send(s_mine, lambda d: d - 2, False)

    kv_out = spec(4 * ROWS)
    kv_shape = ((4 * ROWS, WIDE), BF16)
    q_shape = ((ROWS, WIDE), BF16)
    xd_same, xd_cross, x_kv, x_fin_same, x_fin_cross = call(
        per_head(cross_remote_kernel), "cross_remote", info,
        [mine_w, mine_w, spec(ROWS, 0), spec(ROWS, 1), spec(ROWS, 0), spec(ROWS, 1)]
        + [own_spec((2,)), spec(ROWS, 2), spec(ROWS, 3), stat_spec(ROWS), stat_spec(ROWS)],
        (x_same, x_cross, x_same, x_same, x_cross, x_cross, pool, x_pair, x_pair, t_same, t_cross),
        [spec(ROWS), spec(ROWS), kv_out, stat_spec(ROWS), stat_spec(ROWS)],
        [q_shape, q_shape, kv_shape, stat(ROWS), stat(ROWS)],
    )
    f_own = send(x_fin_same, inward, True)
    f_partner = send(x_fin_cross, outward, True)
    s_other, x_kv = lax.optimization_barrier((s_other, x_kv))
    s_cross = send(s_other, lambda d: (d - 2) ^ 1, False)
    x_kv, s_same, t_self = lax.optimization_barrier((x_kv, s_same, t_self))
    half_out = spec(3 * ROWS)
    half_shape = ((3 * ROWS, WIDE), BF16)
    x_keep, x_give = call(
        per_head(cross_local_kernel), "cross_local", info,
        cross_specs + [stat_spec(ROWS), stat_spec(ROWS), spec(4 * ROWS)],
        cross_args + (f_own, f_partner, x_kv),
        [half_out] * 2, [half_shape] * 2, flops=LONG,
    )

    xd_same, s_cross, x_keep = lax.optimization_barrier((xd_same, s_cross, x_keep))
    xr_same = send(xd_same, inward, True)
    far_bias, x_keep = lax.optimization_barrier((far_bias, x_keep))
    sd, s_kv, s_fin = call(
        per_head(self_remote_kernel), "self_remote", info,
        [bias_spec, spec(ROWS, 0), spec(ROWS, 1), spec(ROWS, 0), spec(ROWS, 1)]
        + [own_spec(), own_spec(), spec(ROWS, 2), spec(ROWS, 3), stat_spec(2 * ROWS)],
        (far_bias, s_same, s_same, s_cross, s_cross, keys, values, s_pair, s_pair, t_self),
        [spec(2 * ROWS), kv_out, stat_spec(2 * ROWS)],
        [((2 * ROWS, WIDE), BF16), kv_shape, stat(2 * ROWS)], flops=LONG,
    )
    f_self = send(s_fin, lambda d: d + 2, False)
    sr = send(sd, lambda d: d + 2, False)

    x_give, s_kv, xr_same, xd_cross, f_self = lax.optimization_barrier(
        (x_give, s_kv, xr_same, xd_cross, f_self)
    )
    xr_cross = send(xd_cross, across, True)
    x_take = send(x_give, swap, False)
    s_keep, s_give = call(
        per_head(self_local_kernel), "self_local", info,
        self_specs + [stat_spec(2 * ROWS), stat_spec(2 * ROWS), spec(4 * ROWS)],
        self_args + (f_self, s_own, s_kv),
        [half_out] * 2, [half_shape] * 2, flops=LONG,
    )
    three, one = whole_spec((3 * ROWS, WIDE)), whole_spec((ROWS, WIDE))
    s_take = send(s_give, swap, False)
    grad_cq, grad_pool = assemble(
        cross_final_kernel, "cross_final", info, (x_keep, x_take, xr_same, xr_cross),
        [three, three, one, one], True, 1,
    )
    sr, grad_cq = lax.optimization_barrier((sr, grad_cq))
    sr_take = send(sr, swap, False)
    grad_k, grad_v, grad_q = assemble(
        kv_final_kernel, "kv_final", info, (s_keep, s_take, sr), [three, three, one], False, 3
    )
    grad_q = pl.pallas_call(
        query_final_kernel,
        name="query_final",
        grid_spec=pltpu.PrefetchScalarGridSpec(
            num_scalar_prefetch=1,
            grid=(2,),
            in_specs=[
                pl.BlockSpec((ROWS // 2, WIDE), lambda h, info: (h, 0)),
                pl.BlockSpec((ROWS // 2, WIDE), lambda h, info: (2 + h, 0)),
                pl.BlockSpec(memory_space=pl.ANY),
            ],
            out_specs=pl.BlockSpec((ROWS // 2, WIDE), lambda h, info: (h, 1 - info[0] % 2)),
        ),
        out_shape=jax.ShapeDtypeStruct(grad_q.shape, BF16),
        input_output_aliases={3: 0},
        compiler_params=pltpu.CompilerParams(vmem_limit_bytes=64 << 20),
        cost_estimate=pl.CostEstimate(flops=0, transcendentals=0, bytes_accessed=0),
    )(info, s_take, sr_take, grad_q)
    return grad_q, grad_k, grad_v, grad_cq, grad_pool.reshape(pool_kv.shape)


def solution(mesh):
    rows = P(("groups", "ctx"), None)
    pool = P(None, ("groups", "ctx"), None, None)
    return jax.shard_map(
        body,
        mesh=mesh,
        in_specs=(rows, rows, rows, rows, P("groups"), rows, rows, pool, rows),
        out_specs=(rows, rows, rows, rows, pool),
        check_vma=False,
    )
```

```python
import functools
import math

import jax
import jax.numpy as jnp
from jax import lax
from jax.experimental import pallas as pl
from jax.experimental.pallas import tpu as pltpu
from jax.sharding import PartitionSpec as P

HEADS = 8
HEAD_DIM = 128
HALF = HEADS // 2
WIDE = HALF * HEAD_DIM
STEP = 2
COLS = STEP * HEAD_DIM
STEPS = HALF // STEP
STRETCH = 64
NBR_TOK = 128
ROWS = 256
EXTRA = 8
LONG = 12 * 10**9
FACTOR = HEAD_DIM ** (-0.5)
MASKED = -1e30
BF16 = jnp.bfloat16
F32 = jnp.float32


def send(value, target_of, wrap):
    count = lax.axis_size("ctx")
    pairs = []
    for source in range(count):
        target = target_of(source)
        if wrap:
            pairs.append((source, target % count))
        elif 0 <= target < count:
            pairs.append((source, target))
    return lax.ppermute(value, "ctx", pairs)


def swap(d):
    return d ^ 1


def outward(d):
    return d - 2 if d % 2 == 0 else d + 2


def inward(d):
    return d + 2 if d % 2 == 0 else d - 2


def across(d):
    return d - 1 if d % 2 == 0 else d + 1


def spec(rows, row_block=0):
    return pl.BlockSpec((rows, COLS), lambda h, info: (row_block, h))


def own_spec(lead=()):
    zeros = (0,) * len(lead)
    return pl.BlockSpec(lead + (ROWS, COLS), lambda h, info: zeros + (0, info[0] % 2 * STEPS + h))


def other_spec(lead=()):
    zeros = (0,) * len(lead)
    return pl.BlockSpec(
        lead + (ROWS, COLS), lambda h, info: zeros + (0, (1 - info[0] % 2) * STEPS + h)
    )


def whole_spec(shape, index=None):
    index = (0,) * len(shape) if index is None else index
    return pl.BlockSpec(shape, lambda h, *info: index)


def stat_spec(rows):
    return pl.BlockSpec((STEP, 8, rows), lambda h, info: (h, 0, 0))


def call(kernel, name, info, in_specs, inputs, out_specs, outs, steps=STEPS, flops=0):
    return pl.pallas_call(
        kernel,
        name=name,
        grid_spec=pltpu.PrefetchScalarGridSpec(
            num_scalar_prefetch=1,
            grid=(steps,),
            in_specs=in_specs,
            out_specs=out_specs,
        ),
        out_shape=[jax.ShapeDtypeStruct(shape, dtype) for shape, dtype in outs],
        compiler_params=pltpu.CompilerParams(vmem_limit_bytes=64 << 20),
        cost_estimate=pl.CostEstimate(flops=flops, transcendentals=0, bytes_accessed=0),
    )(info, *inputs)


def head_of(ref, j):
    shape = ref.shape
    if len(shape) == 3 and shape[1] == 8:
        return ref.at[j : j + 1]
    if shape[-1] != COLS:
        return ref
    place = pl.ds(j * HEAD_DIM, HEAD_DIM)
    return ref.at[:, place] if len(shape) == 2 else ref.at[:, :, place]


def per_head(kernel):
    def run(info, *refs):
        for j in range(STEP):
            kernel(info, *[head_of(ref, j) for ref in refs])

    return run


def dot_last(a, b):
    return lax.dot_general(a, b, (((1,), (1,)), ((), ())), preferred_element_type=F32)


def dot_first(a, b):
    return lax.dot_general(a, b, (((0,), (0,)), ((), ())), preferred_element_type=F32)


def dot(a, b):
    return jnp.dot(a, b, preferred_element_type=F32)


def both(a, b):
    return jnp.concatenate([a, b], axis=0)


def weight_rows(times):
    log_two = jnp.where(times > 1.5, math.log(2.0), 0.0)
    return jnp.where(times < 0.5, MASKED, log_two)


def slot_pair(ref, first, core, second=None):
    times = ref[...].astype(F32)[:, :ROWS]
    low = times[first : first + 2]
    if second is None:
        return weight_rows(low)
    return weight_rows(jnp.where(core == 0, low, times[second : second + 2]))


def add_rows(s, rows):
    parts = [
        s[e * NBR_TOK : (e + 1) * NBR_TOK] + rows[e : e + 1] for e in range(s.shape[0] // NBR_TOK)
    ]
    return jnp.concatenate(parts, axis=0)


def partial_stats(s, dp):
    peak = jnp.max(s, axis=0, keepdims=True)
    e = jnp.exp(s - peak)
    return e, peak, jnp.sum(e, axis=0, keepdims=True), jnp.sum(e * dp, axis=0, keepdims=True)


def stat_rows(a, b, c):
    return jnp.concatenate([a, b, c, jnp.zeros((5, a.shape[1]), F32)], axis=0)[None]


def merge(stats, mine):
    t_peak, t_total, t_moment = stats[0, 0:1], stats[0, 1:2], stats[0, 2:3]
    peak, total, moment = mine
    top = jnp.maximum(t_peak, peak)
    t_scale = jnp.exp(t_peak - top)
    scale = jnp.exp(peak - top)
    full = t_total * t_scale + total * scale
    inverse = jnp.where(full > 0, 1.0 / full, 0.0)
    delta = (t_moment * t_scale + moment * scale) * inverse
    return top, inverse, delta, scale * inverse


def gradients(p, dp, delta, q, g, k):
    pb = p.astype(BF16)
    ds = (p * (dp - delta)).astype(BF16)
    return dot_first(ds, k) * FACTOR, dot(ds, q) * FACTOR, dot(pb, g)


def naming(enc_dev, loop, me, ids, cols):
    shape = (EXTRA, cols)
    row = lax.broadcasted_iota(jnp.int32, shape, 0)
    lane = lax.broadcasted_iota(jnp.int32, shape, 1) + pl.program_id(0) * shape[1]
    owner = ids // enc_dev
    relative = owner - me + 1
    relative = jnp.where(relative < 0, relative + loop, relative)
    relative = jnp.where(relative >= loop, relative - loop, relative)
    slots = relative * enc_dev + ids - owner * enc_dev
    times = jnp.zeros(shape, F32)
    for n in range(ids.shape[0]):
        for s in range(ids.shape[1]):
            hit = (row == slots[n : n + 1, s : s + 1]) & (lane // STRETCH == s)
            times = times + jnp.where(hit, 1.0, 0.0)
    return times.astype(BF16)


def pack_cross_kernel(enc_dev, loop, info, ids_ref, qm, gm, q, g, mine, other):
    times = naming(enc_dev, loop, info[0], ids_ref[...], mine.shape[1])
    for out, first, second in ((mine, qm, gm), (other, q, g)):
        out[0:ROWS] = first[...]
        out[ROWS : 2 * ROWS] = second[...]
        out[2 * ROWS :] = times


def pack_swap_kernel(enc_dev, loop, info, ids_ref, q, g, pool, swap_ref):
    swap_ref[0:ROWS] = q[...]
    swap_ref[ROWS : 2 * ROWS] = g[...]
    swap_ref[2 * ROWS : 3 * ROWS] = pool[0]
    swap_ref[3 * ROWS : 4 * ROWS] = pool[1]
    swap_ref[4 * ROWS :] = naming(enc_dev, loop, info[0], ids_ref[...], swap_ref.shape[1])


def pack_self_kernel(info, qm, gm, q, g, k, v, swap_ref, mine, other):
    for index, ref in enumerate((q, g, k, v)):
        swap_ref[index * ROWS : (index + 1) * ROWS] = ref[...]
    for out, first, second in ((mine, qm, gm), (other, q, g)):
        out[0:ROWS] = first[...]
        out[ROWS : 2 * ROWS] = second[...]


def ordered(core, a, b):
    return jnp.where(core == 0, a, b), jnp.where(core == 0, b, a)


def wide_scores(keys_x, keys_y, values_x, values_y, qs, gs, bias):
    sx = dot_last(keys_x, qs) * FACTOR + bias[:ROWS]
    sy = dot_last(keys_y, qs[ROWS:]) * FACTOR + bias[ROWS:, ROWS:]
    return sx, sy, dot_last(values_x, gs), dot_last(values_y, gs[ROWS:])


def wide_stats(sx, sy, dpx, dpy):
    peak = jnp.max(sx, axis=0, keepdims=True)
    peak_y = jnp.maximum(peak[:, ROWS:], jnp.max(sy, axis=0, keepdims=True))
    peak = jnp.concatenate([peak[:, :ROWS], peak_y], axis=1)
    ex, ey = jnp.exp(sx - peak), jnp.exp(sy - peak_y)
    widen = lambda a, b: jnp.concatenate([a[:, :ROWS], a[:, ROWS:] + b], axis=1)
    add = lambda a: jnp.sum(a, axis=0, keepdims=True)
    return ex, ey, peak, widen(add(ex), add(ey)), widen(add(ex * dpx), add(ey * dpy))


def wide_gradients(px, py, dpx, dpy, delta, qs, gs, kx, ky):
    pbx, pby = px.astype(BF16), py.astype(BF16)
    dsx = (px * (dpx - delta)).astype(BF16)
    dsy = (py * (dpy - delta[:, ROWS:])).astype(BF16)
    dq_z = dot_first(dsx[:, :ROWS], kx) * FACTOR
    dq_y = dot_first(both(dsx[:, ROWS:], dsy), both(kx, ky)) * FACTOR
    dkx, dky = dot(dsx, qs) * FACTOR, dot(dsy, qs[ROWS:]) * FACTOR
    return dq_z, dq_y, dkx, dky, dot(pbx, gs), dot(pby, gs[ROWS:])


def local_self(core, bias, q, g, k, v, pq, pg, pk, pv):
    q0, q1 = ordered(core, q[...], pq[...])
    g0, g1 = ordered(core, g[...], pg[...])
    k0, k1 = ordered(core, k[...], pk[...])
    v0, v1 = ordered(core, v[...], pv[...])
    qs, gs = both(q0, q1), both(g0, g1)
    return wide_scores(k0, k1, v0, v1, qs, gs, bias[...]), qs, gs, k0, k1


def local_cross(core, w, pw, q, g, pool, pq, pg, pk, pv):
    qs, gs = both(q[...], pq[...]), both(g[...], pg[...])
    ks, vs = both(pool[0], pk[...]), both(pool[1], pv[...])
    own = both(slot_pair(w, 2, core), slot_pair(w, 4, core, 0))
    partner = both(slot_pair(pw, 0, core, 4), slot_pair(pw, 2, core))
    s = add_rows(dot_last(ks, qs) * FACTOR, jnp.concatenate([own, partner], axis=1))
    return s, dot_last(vs, gs), qs, gs, ks


def self_stats_kernel(info, *refs):
    scores = local_self(info[0] % 2, *refs[:-1])[0]
    refs[-1][...] = stat_rows(*wide_stats(*scores)[2:])


def cross_stats_kernel(info, *refs):
    s, dp, _, _, _ = local_cross(info[0] % 2, *refs[:-2])
    stats = stat_rows(*partial_stats(s, dp)[1:])
    refs[-2][...] = stats[:, :, :ROWS]
    refs[-1][...] = stats[:, :, ROWS:]


def self_remote_kernel(
    info, bias, sq, sg, cq, cg, k, v, pk, pv, stats, dq_ref, kv_ref, out_stats
):
    core = info[0] % 2
    q0, q1 = ordered(core, sq[...], cq[...])
    g0, g1 = ordered(core, sg[...], cg[...])
    k0, k1 = ordered(core, k[...], pk[...])
    v0, v1 = ordered(core, v[...], pv[...])
    qs, gs = both(q1, q0), both(g1, g0)
    sx, sy, dpx, dpy = wide_scores(k1, k0, v1, v0, qs, gs, bias[...])
    ex, ey, *mine = wide_stats(sx, sy, dpx, dpy)
    known = stats[...]
    known = jnp.concatenate([known[:, :, ROWS:], known[:, :, :ROWS]], axis=2)
    top, inverse, delta, scale = merge(known, mine)
    px, py = ex * scale, ey * scale[:, ROWS:]
    dq1, dq0, dk1, dk0, dv1, dv0 = wide_gradients(px, py, dpx, dpy, delta, qs, gs, k1, k0)
    same, cross = ordered(core, dq0, dq1)
    dq_ref[:ROWS] = same.astype(BF16)
    dq_ref[ROWS:] = cross.astype(BF16)
    for index, grad in enumerate(ordered(core, dk0, dk1) + ordered(core, dv0, dv1)):
        kv_ref[index * ROWS : (index + 1) * ROWS] = grad.astype(BF16)
    out_stats[...] = stat_rows(top, inverse, delta)


def cross_remote_kernel(
    info, sw, cw, sq, sg, cq, cg, pool, pk, pv, s_stats, c_stats, *outs
):
    dq_same, dq_cross, kv_ref, out_same, out_cross = outs
    core = info[0] % 2
    jobs = (
        (cq, cg, pool[0], pool[1], slot_pair(cw, 4, core, 0), c_stats, dq_cross, out_cross, 0),
        (sq, sg, pk[...], pv[...], slot_pair(sw, 0, core, 4), s_stats, dq_same, out_same, 1),
    )
    for q, g, k, v, rows, stats, dq_ref, out_stats, place in jobs:
        s, dp = add_rows(dot_last(k, q[...]) * FACTOR, rows), dot_last(v, g[...])
        e, *mine = partial_stats(s, dp)
        top, inverse, delta, scale = merge(stats[...], mine)
        dq, dk, dv = gradients(e * scale, dp, delta, q[...], g[...], k)
        dq_ref[...] = dq.astype(BF16)
        out_stats[...] = stat_rows(top, inverse, delta)
        kv_ref[place * ROWS : (place + 1) * ROWS] = dk.astype(BF16)
        kv_ref[(2 + place) * ROWS : (3 + place) * ROWS] = dv.astype(BF16)


def self_local_kernel(info, *refs):
    stats_ref, own_ref, kv_ref, mine, theirs = refs[-5:]
    local = own_ref[0]
    core = info[0] % 2
    first = info[0] < 2
    stats = stats_ref[0]
    stats = jnp.concatenate([stats[:, ROWS:], stats[:, :ROWS]], axis=1)
    inverse = 1.0 / local[1:2]
    top = jnp.where(first, local[0:1], stats[0:1])
    delta = jnp.where(first, local[2:3] * inverse, stats[2:3])
    inverse = jnp.where(first, inverse, stats[1:2])
    (sx, sy, dpx, dpy), qs, gs, k0, k1 = local_self(core, *refs[:-5])
    px = jnp.exp(sx - top) * inverse
    py = jnp.exp(sy - top[:, ROWS:]) * inverse[:, ROWS:]
    dq0, dq1, dk0, dk1, dv0, dv1 = wide_gradients(px, py, dpx, dpy, delta, qs, gs, k0, k1)
    grads = (ordered(core, dq0, dq1), ordered(core, dk0, dk1), ordered(core, dv0, dv1))
    for index, pair in enumerate(grads):
        for out, place, grad in ((mine, 0, pair[0]), (theirs, 1, pair[1])):
            if index > 0:
                low = (2 * index - 2 + place) * ROWS
                grad = grad + kv_ref[low : low + ROWS].astype(F32)
            out[index * ROWS : (index + 1) * ROWS] = grad.astype(BF16)


def cross_local_kernel(info, *refs):
    own_stats, partner_stats, kv_ref, mine, theirs = refs[-5:]
    stats = jnp.concatenate([own_stats[0], partner_stats[0]], axis=1)
    top, inverse, delta = stats[0:1], stats[1:2], stats[2:3]
    s, dp, qs, gs, ks = local_cross(info[0] % 2, *refs[:-5])
    dq, dk, dv = gradients(jnp.exp(s - top) * inverse, dp, delta, qs, gs, ks)
    dk = dk + kv_ref[: 2 * ROWS].astype(F32)
    dv = dv + kv_ref[2 * ROWS :].astype(F32)
    for index, grad in enumerate((dq, dk, dv)):
        mine[index * ROWS : (index + 1) * ROWS] = grad[:ROWS].astype(BF16)
        theirs[index * ROWS : (index + 1) * ROWS] = grad[ROWS:].astype(BF16)


def kv_final_kernel(info, mine, theirs, dq_mine, k_out, v_out, q_out):
    def write(source):
        k_out[...] = source[ROWS : 2 * ROWS]
        v_out[...] = source[2 * ROWS :]
        q_out[...] = (mine[:ROWS].astype(F32) + dq_mine[...].astype(F32)).astype(BF16)

    pl.when(pl.program_id(0) == 0)(lambda: write(mine))
    pl.when(pl.program_id(0) == 1)(lambda: write(theirs))


def query_final_kernel(info, theirs, dq_theirs, grad, out):
    out[...] = (theirs[...].astype(F32) + dq_theirs[...].astype(F32)).astype(BF16)


def cross_final_kernel(info, mine, theirs, dq_mine, dq_theirs, dq_out, pool_out):
    def write(source, extra):
        dq = source[:ROWS].astype(F32) + extra[...].astype(F32)
        dq_out[...] = dq.astype(BF16)
        pool_out[0] = source[ROWS : 2 * ROWS]
        pool_out[1] = source[2 * ROWS :]

    pl.when(pl.program_id(0) == 0)(lambda: write(mine, dq_mine))
    pl.when(pl.program_id(0) == 1)(lambda: write(theirs, dq_theirs))


def assemble(kernel, name, info, inputs, in_specs, pooled, count):
    half = lambda h, info: (info[0] + h) % 2
    rows_out = pl.BlockSpec((ROWS, WIDE), lambda h, info: (0, half(h, info)))
    pool_out = pl.BlockSpec((2, ROWS, WIDE), lambda h, info: (0, 0, half(h, info)))
    out_specs, outs = [rows_out] * count, [((ROWS, 2 * WIDE), BF16)] * count
    if pooled:
        out_specs, outs = out_specs + [pool_out], outs + [((2, ROWS, 2 * WIDE), BF16)]
    return call(kernel, name, info, in_specs, inputs, out_specs, outs, steps=2)


def body(
    queries, keys, values, grad_self, doc_ids, cross_queries, grad_cross, pool_kv, neighbour_ids
):
    loop = lax.axis_size("ctx")
    me = lax.axis_index("ctx").astype(jnp.int32)
    info = jnp.full((1,), me, jnp.int32)
    enc_dev = pool_kv.shape[1]
    width = queries.shape[1]
    pool = pool_kv.reshape(2, ROWS, width)

    mine_spec, their_spec, their_pool = own_spec(), other_spec(), other_spec((2,))
    names, names_spec = neighbour_ids.T, whole_spec(neighbour_ids.shape[::-1])
    x_mine, x_other = call(
        functools.partial(pack_cross_kernel, enc_dev, loop), "pack_cross", info,
        [names_spec] + [mine_spec] * 2 + [their_spec] * 2,
        (names, cross_queries, grad_cross, cross_queries, grad_cross),
        [spec(2 * ROWS + EXTRA)] * 2,
        [((2 * ROWS + EXTRA, WIDE), BF16)] * 2,
    )
    x_same = send(x_mine, outward, True)
    x_cross = send(x_other, across, True)
    names, x_mine = lax.optimization_barrier((names, x_mine))
    (packed,) = call(
        functools.partial(pack_swap_kernel, enc_dev, loop), "pack_swap", info,
        [names_spec] + [their_spec] * 2 + [their_pool],
        (names, cross_queries, grad_cross, pool),
        [spec(4 * ROWS + EXTRA)],
        [((4 * ROWS + EXTRA, WIDE), BF16)],
    )
    x_pair = send(packed, swap, False)
    queries_in, packed = lax.optimization_barrier((queries, packed))
    sizes = (4 * ROWS, 2 * ROWS, 2 * ROWS)
    packed, s_mine, s_other = call(
        pack_self_kernel, "pack_self", info,
        [mine_spec] * 2 + [their_spec] * 4,
        (queries_in, grad_self, queries_in, grad_self, keys, values),
        [spec(rows) for rows in sizes],
        [((rows, WIDE), BF16) for rows in sizes],
    )
    s_pair = send(packed, swap, False)

    ids_of = lambda d: lax.dynamic_slice_in_dim(doc_ids, d * ROWS, ROWS, 0)
    span = jnp.arange(ROWS, dtype=jnp.int32)
    base = me // 2 * 2
    places = jnp.concatenate([span + base * ROWS, span + (base + 1) * ROWS])
    near0, near1, far0, far1 = [ids_of(base + j) for j in range(4)]
    near = jnp.concatenate([near0, near1])
    near_flip = jnp.concatenate([near1, near0])
    far_flip = jnp.concatenate([far1, far0])
    local_ok = (near[:, None] == near[None, :]) & (places[:, None] <= places[None, :])
    far_ok = (near_flip[:, None] == far_flip[None, :]) & (base + 2 < loop)
    local_bias = jnp.where(local_ok, 0.0, MASKED).astype(F32)
    far_bias = jnp.where(far_ok, 0.0, MASKED).astype(F32)

    bias_spec = whole_spec((2 * ROWS, 2 * ROWS))
    local_bias, far_bias, x_pair = lax.optimization_barrier((local_bias, far_bias, x_pair))
    self_specs = [bias_spec] + [own_spec()] * 4 + [spec(ROWS, j) for j in range(4)]
    self_args = (local_bias, queries, grad_self, keys, values) + (s_pair,) * 4
    mine_w = whole_spec((EXTRA, WIDE), (2 * ROWS // EXTRA, 0))
    partner_w = whole_spec((EXTRA, WIDE), (4 * ROWS // EXTRA, 0))
    cross_specs = (
        [mine_w, partner_w, own_spec(), own_spec(), own_spec((2,))]
        + [spec(ROWS, j) for j in range(4)]
    )
    cross_args = (x_mine, x_pair, cross_queries, grad_cross, pool) + (x_pair,) * 4
    stat = lambda rows: ((HALF, 8, rows), F32)

    x_own, x_partner = call(
        per_head(cross_stats_kernel), "cross_stats", info, cross_specs, cross_args,
        [stat_spec(ROWS)] * 2, [stat(ROWS)] * 2, flops=0,
    )
    t_same = send(x_own, outward, True)
    t_cross = send(x_partner, inward, True)
    local_bias, x_own = lax.optimization_barrier((local_bias, x_own))
    self_args = (local_bias,) + self_args[1:]
    (s_own,) = call(
        per_head(self_stats_kernel), "self_stats", info, self_specs, self_args,
        [stat_spec(2 * ROWS)], [stat(2 * ROWS)], flops=0,
    )
    t_self = send(s_own, lambda d: d - 2, False)
    s_mine, x_same, x_cross, t_same, t_cross, s_own = lax.optimization_barrier(
        (s_mine, x_same, x_cross, t_same, t_cross, s_own)
    )
    s_same = send(s_mine, lambda d: d - 2, False)

    kv_out = spec(4 * ROWS)
    kv_shape = ((4 * ROWS, WIDE), BF16)
    q_shape = ((ROWS, WIDE), BF16)
    xd_same, xd_cross, x_kv, x_fin_same, x_fin_cross = call(
        per_head(cross_remote_kernel), "cross_remote", info,
        [mine_w, mine_w, spec(ROWS, 0), spec(ROWS, 1), spec(ROWS, 0), spec(ROWS, 1)]
        + [own_spec((2,)), spec(ROWS, 2), spec(ROWS, 3), stat_spec(ROWS), stat_spec(ROWS)],
        (x_same, x_cross, x_same, x_same, x_cross, x_cross, pool, x_pair, x_pair, t_same, t_cross),
        [spec(ROWS), spec(ROWS), kv_out, stat_spec(ROWS), stat_spec(ROWS)],
        [q_shape, q_shape, kv_shape, stat(ROWS), stat(ROWS)],
    )
    f_own = send(x_fin_same, inward, True)
    f_partner = send(x_fin_cross, outward, True)
    s_other, x_kv = lax.optimization_barrier((s_other, x_kv))
    s_cross = send(s_other, lambda d: (d - 2) ^ 1, False)
    x_kv, s_same, t_self = lax.optimization_barrier((x_kv, s_same, t_self))
    half_out = spec(3 * ROWS)
    half_shape = ((3 * ROWS, WIDE), BF16)
    x_keep, x_give = call(
        per_head(cross_local_kernel), "cross_local", info,
        cross_specs + [stat_spec(ROWS), stat_spec(ROWS), spec(4 * ROWS)],
        cross_args + (f_own, f_partner, x_kv),
        [half_out] * 2, [half_shape] * 2, flops=LONG,
    )

    xd_same, xd_cross, s_cross, x_keep = lax.optimization_barrier(
        (xd_same, xd_cross, s_cross, x_keep)
    )
    xr_same = send(xd_same, inward, True)
    xr_cross = send(xd_cross, across, True)
    far_bias, x_keep = lax.optimization_barrier((far_bias, x_keep))
    sd, s_kv, s_fin = call(
        per_head(self_remote_kernel), "self_remote", info,
        [bias_spec, spec(ROWS, 0), spec(ROWS, 1), spec(ROWS, 0), spec(ROWS, 1)]
        + [own_spec(), own_spec(), spec(ROWS, 2), spec(ROWS, 3), stat_spec(2 * ROWS)],
        (far_bias, s_same, s_same, s_cross, s_cross, keys, values, s_pair, s_pair, t_self),
        [spec(2 * ROWS), kv_out, stat_spec(2 * ROWS)],
        [((2 * ROWS, WIDE), BF16), kv_shape, stat(2 * ROWS)], flops=LONG,
    )
    f_self = send(s_fin, lambda d: d + 2, False)
    sr = send(sd, lambda d: d + 2, False)

    x_give, s_kv, xr_same, xr_cross, f_self = lax.optimization_barrier(
        (x_give, s_kv, xr_same, xr_cross, f_self)
    )
    x_take = send(x_give, swap, False)
    s_keep, s_give = call(
        per_head(self_local_kernel), "self_local", info,
        self_specs + [stat_spec(2 * ROWS), stat_spec(2 * ROWS), spec(4 * ROWS)],
        self_args + (f_self, s_own, s_kv),
        [half_out] * 2, [half_shape] * 2, flops=LONG,
    )
    three, one = whole_spec((3 * ROWS, WIDE)), whole_spec((ROWS, WIDE))
    s_take = send(s_give, swap, False)
    grad_cq, grad_pool = assemble(
        cross_final_kernel, "cross_final", info, (x_keep, x_take, xr_same, xr_cross),
        [three, three, one, one], True, 1,
    )
    sr, grad_cq = lax.optimization_barrier((sr, grad_cq))
    sr_take = send(sr, swap, False)
    grad_k, grad_v, grad_q = assemble(
        kv_final_kernel, "kv_final", info, (s_keep, s_take, sr), [three, three, one], False, 3
    )
    grad_q = pl.pallas_call(
        query_final_kernel,
        name="query_final",
        grid_spec=pltpu.PrefetchScalarGridSpec(
            num_scalar_prefetch=1,
            grid=(1,),
            in_specs=[
                pl.BlockSpec((ROWS, WIDE), lambda h, info: (0, 0)),
                pl.BlockSpec((ROWS, WIDE), lambda h, info: (1, 0)),
                pl.BlockSpec(memory_space=pl.ANY),
            ],
            out_specs=pl.BlockSpec((ROWS, WIDE), lambda h, info: (0, 1 - info[0] % 2)),
        ),
        out_shape=jax.ShapeDtypeStruct(grad_q.shape, BF16),
        input_output_aliases={3: 0},
        compiler_params=pltpu.CompilerParams(vmem_limit_bytes=64 << 20),
        cost_estimate=pl.CostEstimate(flops=0, transcendentals=0, bytes_accessed=0),
    )(info, s_take, sr_take, grad_q)
    return grad_q, grad_k, grad_v, grad_cq, grad_pool.reshape(pool_kv.shape)


def solution(mesh):
    rows = P(("groups", "ctx"), None)
    pool = P(None, ("groups", "ctx"), None, None)
    return jax.shard_map(
        body,
        mesh=mesh,
        in_specs=(rows, rows, rows, rows, P("groups"), rows, rows, pool, rows),
        out_specs=(rows, rows, rows, rows, pool),
        check_vma=False,
    )
```
